32 devices in a mesh: groups: 2 (over x), tile: 8 (over z, y), dp: 2 (over core).
Axes of the slice: x: 2, y: 2, z: 4, core: 2. Of those that a mesh axis runs over, the one named last changes fastest.
Arguments:
- initial_state: bfloat16 [4, 6, 24, 24, 256], P(('groups', 'dp'), None, 'tile'), parts along dimension 0, may hold values from -6 to 6
- state_cotangents: bfloat16 [1, 4, 6, 24, 24, 256], P(None, ('groups', 'dp'), None, 'tile'), parts along dimension 1, may hold values from -6 to 6
- w_first: bfloat16 [3, 3, 256, 256], replicated, may hold values from -0.125 to 0.125
- bias: float32 [256], replicated, may hold values from -3 to 3
- w_second: bfloat16 [3, 3, 256, 256], replicated, may hold values from -0.125 to 0.125
- edge_partner: int32 [6, 4], replicated, may hold values from 0 to 23, as said below
Outputs:
- final_state: bfloat16 [4, 6, 24, 24, 256], P(('groups', 'dp'), None, 'tile'), parts along dimension 0
- state_grad: float32 [4, 6, 24, 24, 256], P(('groups', 'dp'), None, 'tile'), parts along dimension 0
- w_first_step: float32 [6, 3, 256, 256], P('groups'), parts along dimension 0
- bias_step: float32 [512], P('groups'), parts along dimension 0
- w_second_step: float32 [6, 3, 256, 256], P('groups'), parts along dimension 0
The draws below stay inside these ranges and needn't reach their ends.
There are 2 independent parts, one for each index of `groups`. The reference program is written for one: setup_inputs(seed, part) draws one part's arguments, and reference() takes and returns one part's arrays. A program takes and returns all parts, laid end to end along the dimension named above; an argument that names none is the same for every part. Nothing has to cross between parts.
Inputs may be any that keep to these rules, and one draw needn't show every extreme that they name: `edge_partner`: entry [f, e] names edge e2 of face f2 as 4 * f2 + e2. The pairing is its own inverse, joins no edge to itself or to an edge of its own face, and glues the six faces into the surface of a cube with every face seen from outside.
All inputs are finite; a program needn't handle non-finite values.
Results may differ from the reference program's by a relative error of at most 0.005.
Values may be sent and summed in bfloat16 or wider, within the bound.
No kernel may reach another device: no remote copies, remote signals or barrier semaphores. Data moves between devices by JAX's collectives and lax.ppermute only.
A program may use at most 128 MiB of HBM per device.

```python
import jax
import jax.numpy as jnp
from jax import lax

CH = 256
STEPS = 1
FACE = 24
SAMPLES = 2


def draw_edge_partner(key, part):
    canonical = jnp.array([[18, 7, 20, 13], [17, 11, 21, 1], [16, 15, 22, 5], [19, 3, 23, 9], [8, 4, 0, 12], [2, 6, 10, 14]], dtype=jnp.int32)
    relabel = jax.random.permutation(jax.random.fold_in(key, 1), 6).astype(jnp.int32)
    rotation = jax.random.randint(jax.random.fold_in(key, 2), (6,), 0, 4, dtype=jnp.int32)
    face_ids = jnp.arange(24, dtype=jnp.int32) // 4
    edge_ids = jnp.arange(24, dtype=jnp.int32) % 4
    partner_flat = canonical.reshape(24)
    position = relabel[face_ids] * 4 + (edge_ids + rotation[face_ids]) % 4
    partner_value = relabel[partner_flat // 4] * 4 + (partner_flat % 4 + rotation[partner_flat // 4]) % 4
    paired = jnp.zeros((24,), jnp.int32).at[position].set(partner_value)
    return paired.reshape(6, 4)


def block_scale(own_key, extent, pieces, low, high):
    factor_of = 1.0
    for dim, parts in pieces:
        heights = jax.random.uniform(jax.random.fold_in(jax.random.fold_in(own_key, 6), dim), (parts,), jnp.float32, low / len(pieces), high / len(pieces))
        factor_of = factor_of * jnp.repeat(jnp.exp(heights), extent[dim] // parts).reshape((-1,) + (1,) * (len(extent) - 1 - dim))
    return factor_of


def scatter_about(key, extent, width, reach, shards=(), kind=jnp.bfloat16):
    values = jax.random.normal(key, extent, jnp.float32) * width
    if len(shards) > 0:
        values = block_scale(key, extent, shards, -0.22, 0.18) * values
    return jnp.clip(values, min=-reach, max=reach).astype(kind)


def setup_inputs(seed: int = 0, part: int = 0) -> dict:
    key_of = jax.random.split(jax.random.key(seed), 7)
    own_keys = jax.random.split(jax.random.fold_in(key_of[6], part), 7)
    return {
        "initial_state": scatter_about(own_keys[0], (SAMPLES, 6, FACE, FACE, CH), 1.0, 6.0, ((0, 2), (2, 8))),
        "state_cotangents": scatter_about(own_keys[1], (STEPS, SAMPLES, 6, FACE, FACE, CH), 1.0, 6.0, ((1, 2), (3, 8))),
        "w_first": scatter_about(key_of[2], (3, 3, CH, CH), (9 * CH) ** -0.5, 0.125),
        "bias": scatter_about(key_of[3], (CH,), 0.5, 3.0, (), jnp.float32),
        "w_second": scatter_about(key_of[4], (3, 3, CH, CH), (9 * CH) ** -0.5, 0.125),
        "edge_partner": draw_edge_partner(jax.random.fold_in(key_of[6], 71), part),
    }


def edge_rows(grid_field):
    return jnp.stack([grid_field[:, :, 0], grid_field[:, :, :, -1], grid_field[:, :, -1], grid_field[:, :, :, 0]], axis=2)

def edge_match(strip_table, edge_partner):
    samples_here = strip_table.shape[0]
    flat_rows = strip_table.reshape((samples_here, 24) + strip_table.shape[3:])
    partner_flat = edge_partner.reshape(24).astype(jnp.int32)
    moved_rows = jnp.take(flat_rows, partner_flat, axis=1)
    own_side = jnp.arange(24, dtype=jnp.int32) % 4 < 2
    far_side = partner_flat % 4 < 2
    flipped = own_side == far_side
    moved_rows = jnp.where(flipped[None, :, None, None], moved_rows[:, :, ::-1], moved_rows)
    return moved_rows.reshape(strip_table.shape)

def framed_field(grid_field, edge_partner):
    ghost_rows = edge_match(edge_rows(grid_field), edge_partner)
    middle = jnp.concatenate([ghost_rows[:, :, 3][:, :, :, None], grid_field, ghost_rows[:, :, 1][:, :, :, None]], axis=3)
    corner = jnp.zeros_like(ghost_rows[:, :, 0][:, :, :1])
    upper_row = jnp.concatenate([corner, ghost_rows[:, :, 0], corner], axis=2)
    lower_row = jnp.concatenate([corner, ghost_rows[:, :, 2], corner], axis=2)
    return jnp.concatenate([upper_row[:, :, None], middle, lower_row[:, :, None]], axis=2)

def convolve(framed, weights):
    row_count = framed.shape[2] - 2
    col_count = framed.shape[3] - 2
    channels = framed.shape[4]
    summed_taps = None
    for tap_row in range(3):
        for tap_col in range(3):
            window = framed[:, :, tap_row:tap_row + row_count, tap_col:tap_col + col_count].reshape(-1, channels)
            tap_term = jnp.dot(window, weights[tap_row, tap_col], preferred_element_type=jnp.float32)
            summed_taps = tap_term if summed_taps is None else summed_taps + tap_term
    return summed_taps.reshape(framed.shape[:2] + (row_count, col_count, weights.shape[3]))

def convolve_back(upstream, weights):
    row_count = upstream.shape[2]
    col_count = upstream.shape[3]
    flat_rows = upstream.reshape(-1, upstream.shape[4])
    framed = jnp.zeros(upstream.shape[:2] + (row_count + 2, col_count + 2, weights.shape[2]), jnp.float32)
    for tap_row in range(3):
        for tap_col in range(3):
            tap_term = lax.dot_general(flat_rows, weights[tap_row, tap_col], (((1,), (1,)), ((), ())), preferred_element_type=jnp.float32)
            framed = framed.at[:, :, tap_row:tap_row + row_count, tap_col:tap_col + col_count].add(tap_term.reshape(upstream.shape[:4] + (weights.shape[2],)))
    return framed

def weight_grad(framed, upstream):
    row_count = upstream.shape[2]
    col_count = upstream.shape[3]
    channels = framed.shape[4]
    flat_up = upstream.reshape(-1, upstream.shape[4])
    tap_grads = []
    for tap_row in range(3):
        for tap_col in range(3):
            window = framed[:, :, tap_row:tap_row + row_count, tap_col:tap_col + col_count].reshape(-1, channels)
            tap_grads.append(lax.dot_general(window, flat_up, (((0,), (0,)), ((), ())), preferred_element_type=jnp.float32))
    return jnp.stack(tap_grads).reshape(3, 3, channels, flat_up.shape[1])

def silu_slope(before):
    sigmoid_value = jax.nn.sigmoid(before)
    return sigmoid_value * (1.0 + before * (1.0 - sigmoid_value))

def normalized(gradient):
    return gradient / jnp.sqrt(jnp.mean(gradient * gradient) + 1e-06)

def reference(initial_state, state_cotangents, w_first, bias, w_second, edge_partner):
    current = initial_state
    history = []
    for rollout_step in range(STEPS):
        framed_state = framed_field(current, edge_partner)
        before = convolve(framed_state, w_first) + bias
        hidden = jax.nn.silu(before).astype(jnp.bfloat16)
        framed_hidden = framed_field(hidden, edge_partner)
        update = convolve(framed_hidden, w_second)
        history.append((framed_state, before, framed_hidden))
        current = (current.astype(jnp.float32) + update).astype(jnp.bfloat16)

    def unframe(framed):
        zero_field = jnp.zeros(initial_state.shape, jnp.float32)
        unused, pullback = jax.vjp(lambda grid_field: framed_field(grid_field, edge_partner), zero_field)
        return pullback(framed)[0]
    state_grad = state_cotangents[STEPS - 1].astype(jnp.float32)
    grad_first = jnp.zeros(w_first.shape, jnp.float32)
    grad_bias = jnp.zeros(bias.shape, jnp.float32)
    grad_second = jnp.zeros(w_second.shape, jnp.float32)
    for rollout_step in reversed(range(STEPS)):
        framed_state, before, framed_hidden = history[rollout_step]
        upstream = state_grad.astype(jnp.bfloat16)
        grad_second = grad_second + weight_grad(framed_hidden, upstream)
        hidden_grad = unframe(convolve_back(upstream, w_second))
        before_grad = hidden_grad * silu_slope(before)
        grad_bias = grad_bias + lax.optimization_barrier(jnp.sum(before_grad, axis=(0, 1, 2, 3)))
        inner_up = before_grad.astype(jnp.bfloat16)
        grad_first = grad_first + weight_grad(framed_state, inner_up)
        state_grad = state_grad + unframe(convolve_back(inner_up, w_first))
        if rollout_step > 0:
            state_grad = state_grad + state_cotangents[rollout_step - 1].astype(jnp.float32)
    return (current, state_grad, normalized(grad_first), normalized(grad_bias), normalized(grad_second))
```

```python
import functools

import jax
import jax.numpy as jnp
from jax import lax
from jax.experimental import pallas as pl
from jax.experimental.pallas import tpu as pltpu
from jax.sharding import PartitionSpec as P

BF = jnp.bfloat16
F32 = jnp.float32
EXTRA = 16


class Dims:
    def __init__(self, rows, face, tiles, channels):
        self.R, self.F, self.T, self.C = rows, face, tiles, channels
        self.N = 6 * rows * face
        self.ROW = 6 * face
        self.SLOT = -(-(2 * rows + 2) // 8) * 8
        self.RC = 6 * self.SLOT
        self.BASE = self.RC + 16
        self.MIR = 16 * rows
        self.row_ks = []
        k = 1
        while k < tiles:
            self.row_ks.append(k)
            k = 2 * k + 1
        self.o_msg = self.N
        self.o_mir = self.o_msg + tiles * self.BASE
        self.o_row = self.o_mir + self.MIR
        self.NT = self.o_row + len(self.row_ks) * self.ROW
        self.WE = 12 * 8
        self.S = self.WE + self.ROW

    def msg_rows(self, k):
        rows = self.BASE
        if k == self.T - 1:
            rows += self.MIR
        if k in self.row_ks:
            rows += self.ROW
        return rows


def col_iota(n):
    return lax.broadcasted_iota(jnp.int32, (n, 1), 0)


def one_hot(target, width):
    lanes = lax.broadcasted_iota(jnp.int32, (target.shape[0], width), 1)
    return jnp.where(lanes == target, 1.0, 0.0).astype(BF)


def edge_of(ep, strip):
    value = ep[strip]
    face = value // 4
    edge = value % 4
    own_low = (strip % 4) < 2
    far_low = edge < 2
    reverse = (far_low == own_low) if not isinstance(own_low, bool) else (far_low if own_low else edge >= 2)
    return face, edge, reverse


def message_targets(dm, ep, t, k):
    R, F, T = dm.R, dm.F, dm.T
    d = t ^ k
    parts = []
    i = col_iota(dm.SLOT)
    at_first = t == 0
    q = R * d - 1 + i
    inside = (q >= 0) & (q < F) & (i < R + 2)
    i2 = i - (R + 2)
    to_first = d == 0
    for f in range(6):
        strip = jnp.where(at_first, 4 * f, 4 * f + 2)
        value = ep[strip]
        far_low = (value % 4) < 2
        own_low = at_first
        reverse = far_low == own_low
        p0 = jnp.where(reverse, F - 1, 0)
        sgn = jnp.where(reverse, -1, 1)
        row = jnp.where(at_first, 0, R - 1)
        tgt_r = jnp.where(inside, (f * R + row) * F + p0 + sgn * q, -1)
        gvalue = ep[jnp.where(to_first, 4 * f, 4 * f + 2)]
        f2 = gvalue // 4
        column = jnp.where(gvalue % 4 == 1, F - 1, 0)
        tgt_c = f2 * (R * F) + column + F * i2
        parts.append(jnp.where(i2 < 0, tgt_r, jnp.where(i2 < R, tgt_c, -1)))
    s = col_iota(16)
    column_cells = (s // 2) * (R * F) + (s % 2) * (F - 1)
    row = jnp.where(d == T - 2 - t, R - 1, 0)
    parts.append(jnp.where(s < 12, column_cells + row * F, -1))
    if k == T - 1:
        for r in range(R):
            parts.append(jnp.where(s < 12, column_cells + r * F, -1))
    if k in dm.row_ks:
        row = jnp.where(d == (t + 1) % T, R - 1, 0)
        j = col_iota(F)
        for f in range(6):
            parts.append((f * R + row) * F + j)
    return jnp.concatenate(parts, axis=0)


def write_messages(dm, ep, t, sources, refs):
    for k in range(dm.T):
        hot = one_hot(message_targets(dm, ep, t, k), dm.N)
        for which, source in enumerate(sources):
            refs[k][which] = jnp.dot(hot, source, preferred_element_type=F32).astype(BF)


def pack_kernel(dm, sc, x_ref, up_ref, *refs):
    write_messages(dm, sc, sc[24], (x_ref[...], up_ref[...]), refs)


def ghost_targets(dm, ep, t):
    R, F, T = dm.R, dm.F, dm.T

    def o_row(k):
        out = dm.o_row
        for j, kk in enumerate(dm.row_ks):
            out = jnp.where(k == kk, dm.o_row + j * dm.ROW, out)
        return out

    parts = []
    m = col_iota(8)
    q = R * t - 1 + m
    inside = (q >= 0) & (q < F) & (m < R + 2)
    row_prev = o_row(t ^ (t - 1))
    row_next = o_row(t ^ (t + 1))
    ab_first = dm.o_msg + (t ^ (T - t)) * dm.BASE + dm.RC
    ab_last = dm.o_msg + (t ^ (T - 2 - t)) * dm.BASE + dm.RC
    for f in range(6):
        for edge in (3, 1):
            strip = 4 * f + edge
            value = ep[strip]
            f2, e2 = value // 4, value % 4
            far_low = e2 < 2
            reverse = far_low if edge < 2 else e2 >= 2
            is_col = (e2 % 2) == 1
            column = jnp.where(e2 == 1, F - 1, 0)
            s = 2 * f2 + jnp.where(e2 == 1, 1, 0)
            src_k = jnp.where(e2 == 0, t, t ^ (T - 1))
            slot = dm.o_msg + src_k * dm.BASE + f2 * dm.SLOT
            i0 = jnp.where(is_col, jnp.where(reverse, ab_first + s, row_prev + f2 * F + column), slot)
            i4 = jnp.where(is_col, jnp.where(reverse, ab_last + s, row_next + f2 * F + column), slot + R + 1)
            base = jnp.where(
                is_col, jnp.where(reverse, dm.o_mir + 16 * R + s, (f2 * R - 1) * F + column), slot
            )
            step = jnp.where(is_col, jnp.where(reverse, -16, F), 1)
            target = jnp.where(m == 0, i0, jnp.where(m == R + 1, i4, base + step * m))
            parts.append(jnp.where(inside, target, -1))
    j = col_iota(F)
    jt = jnp.zeros_like(j)
    for b in range(1, T):
        jt = jt + jnp.where(j >= b * R, 1, 0)
    jr = j - R * jt
    wrap = o_row(jnp.int32(T - 1))
    for edge in (0, 2):
        at_edge = (t == 0) if edge == 0 else (t == T - 1)
        inner_base = row_prev if edge == 0 else row_next
        own_row = 0 if edge == 0 else R - 1
        for f in range(6):
            value = ep[4 * f + edge]
            f2, e2 = value // 4, value % 4
            far_low = e2 < 2
            reverse = far_low if edge < 2 else e2 >= 2
            is_col = (e2 % 2) == 1
            same = e2 == edge
            row_base = jnp.where(same, (f2 * R + own_row) * F, wrap + f2 * F)
            lin_base = row_base + jnp.where(reverse, F - 1, 0)
            lin_step = jnp.where(reverse, -1, 1)
            k0 = jnp.where(reverse, T - 1, 0)
            ks = jnp.where(reverse, -1, 1)
            if edge == 2:
                k0 = T - 1 - k0
                ks = -ks
            col_base = dm.o_msg + k0 * dm.BASE + f * dm.SLOT + R + 2 + jnp.where(reverse, R - 1, 0)
            base = jnp.where(is_col, col_base, lin_base)
            sj = jnp.where(is_col, 0, lin_step)
            st = jnp.where(is_col, ks * dm.BASE, 0)
            sr = jnp.where(is_col, jnp.where(reverse, -1, 1), 0)
            base = jnp.where(at_edge, base, inner_base + f * F)
            sj = jnp.where(at_edge, sj, 1)
            st = jnp.where(at_edge, st, 0)
            sr = jnp.where(at_edge, sr, 0)
            parts.append(base + sj * j + st * jt + sr * jr)
    return jnp.concatenate(parts, axis=0)


def gather_ghosts(dm, ep, t, own, messages, table_ref):
    hot = one_hot(ghost_targets(dm, ep, t), dm.NT)
    out = []
    for which in range(2):
        table_ref[0 : dm.N] = own[which]
        for k in range(dm.T):
            ref = messages[k]
            at = dm.o_msg + k * dm.BASE
            table_ref[at : at + dm.BASE] = ref[which, 0 : dm.BASE]
            row = dm.BASE
            if k == dm.T - 1:
                table_ref[dm.o_mir : dm.o_mir + dm.MIR] = ref[which, row : row + dm.MIR]
                row += dm.MIR
            if k in dm.row_ks:
                at = dm.o_row + dm.row_ks.index(k) * dm.ROW
                table_ref[at : at + dm.ROW] = ref[which, row : row + dm.ROW]
        out.append(jnp.dot(hot, table_ref[...], preferred_element_type=F32))
    return out


def build_shifts(dm, field_ref, ghosts, top, bottom, frame_ref, shift_ref):
    R, F, C = dm.R, dm.F, dm.C
    for f in range(6):
        for r in range(R):
            frame_ref[r + 1, f, 8 : 8 + F] = field_ref[f * R + r].astype(F32)
    frame_ref[0, :, 8 : 8 + F] = top.reshape(6, F, C)
    frame_ref[R + 1, :, 8 : 8 + F] = bottom.reshape(6, F, C)
    for m in range(R + 2):
        for f in range(6):
            if ghosts is None:
                west = jnp.zeros((1, C), F32)
                east = west
            else:
                west = ghosts[16 * f + m : 16 * f + m + 1]
                east = ghosts[16 * f + 8 + m : 16 * f + 8 + m + 1]
            frame_ref[m, f, 7:8] = west
            frame_ref[m, f, 8 + F : 9 + F] = east
    for m in range(R + 2):
        for b in range(3):
            plane = frame_ref[m, :, 7 + b : 7 + b + F].reshape(dm.ROW, C)
            shift_ref[b, m * dm.ROW : (m + 1) * dm.ROW] = plane.astype(BF)


def build_strip_terms(dm, ep, t, ghosts, top, bottom, z_ref):
    R, F = dm.R, dm.F
    z_ref[...] = jnp.zeros(z_ref.shape, F32)

    def tap_of(strip, shift):
        value = ep[strip]
        e2 = value % 4
        far_low = e2 < 2
        own_low = (strip % 4) < 2
        reverse = far_low if own_low else jnp.logical_not(far_low)
        along = 1 - jnp.where(reverse, -shift, shift)
        return jnp.where(
            e2 == 0, along, jnp.where(e2 == 2, 6 + along, jnp.where(e2 == 1, 3 * along + 2, 3 * along))
        )

    live = lax.rem(lax.broadcasted_iota(jnp.int32, (dm.WE, 1), 0), 8) < R
    for shift in (-1, 0, 1):
        moved = pltpu.roll(ghosts, (dm.WE - 1 - shift) % dm.WE, 0) if shift > -1 else ghosts
        moved = jnp.where(live, moved, 0.0)
        for f in range(6):
            for side, edge in ((0, 3), (1, 1)):
                at = 16 * f + 8 * side
                z_ref[tap_of(4 * f + edge, shift), at : at + 8] = moved[at : at + 8]

    def add_rows(edge, rows):
        j = lax.rem(lax.broadcasted_iota(jnp.int32, (dm.ROW, 1), 0), F)
        for shift in (-1, 0, 1):
            if shift == 0:
                moved = rows
            else:
                moved = pltpu.roll(rows, (-shift) % dm.ROW, 0)
                moved = jnp.where((j + shift >= 0) & (j + shift < F), moved, 0.0)
            for f in range(6):
                at = dm.WE + F * f
                z_ref[tap_of(4 * f + edge, shift), at : at + F] = moved[F * f : F * (f + 1)]

    @pl.when(t == 0)
    def _():
        add_rows(0, top)

    @pl.when(t == dm.T - 1)
    def _():
        add_rows(2, bottom)


def adjoint(dm, t, u_ref, z_ref, w_ref, acc_ref):
    R, F = dm.R, dm.F
    total = None
    strips = None
    for a in range(3):
        for b in range(3):
            main = u_ref[2 - b, (2 - a) * dm.ROW : (2 - a + R) * dm.ROW]
            w = w_ref[3 * a + b]
            dims = (((1,), (1,)), ((), ()))
            term = lax.dot_general(main, w, dims, preferred_element_type=F32)
            strip = lax.dot_general(z_ref[3 * a + b].astype(BF), w, dims, preferred_element_type=F32)
            total = term if total is None else total + term
            strips = strip if strips is None else strips + strip
    acc_ref[...] = total
    for f in range(6):
        for side in range(2):
            for r in range(R):
                at = (r * 6 + f) * F + side * (F - 1)
                row = 16 * f + 8 * side + r
                acc_ref[at : at + 1] += strips[row : row + 1]

    @pl.when(t == 0)
    def _():
        acc_ref[0 : dm.ROW] += strips[dm.WE :]

    @pl.when(t == dm.T - 1)
    def _():
        acc_ref[(R - 1) * dm.ROW : R * dm.ROW] += strips[dm.WE :]


def put_tap(send_ref, keep_ref, p, tap, value):
    half = send_ref.shape[0] - EXTRA
    unit = value.shape[0] // 2
    for part in range(2):
        row = tap * 2 * unit + part * unit
        owner = row // half
        at = row - owner * half
        piece = value[part * unit : (part + 1) * unit]

        @pl.when(p == owner)
        def _():
            keep_ref[at : at + unit] = piece

        @pl.when(p != owner)
        def _():
            send_ref[at : at + unit] = piece.astype(BF)


def put_extra(send_ref, keep_ref, row):
    c = row.shape[1]
    n = send_ref.shape[0] - EXTRA
    i = lax.broadcasted_iota(jnp.int32, (EXTRA, c), 0)
    high = row.astype(BF)
    low = (row - high.astype(F32)).astype(BF).astype(F32)
    keep_ref[n:] = jnp.where(i == 0, row, 0.0)
    send_ref[n:] = jnp.where(i == 0, high.astype(F32), jnp.where(i == 1, low, 0.0)).astype(BF)


def first_kernel(dm, sc, x_ref, up_ref, w1_ref, bias_ref, w2_ref, *refs):
    T, R, F, N, C = dm.T, dm.R, dm.F, dm.N, dm.C
    messages = refs[:T]
    s1_ref, k1_ref, s2_ref, k2_ref, hid_ref, inner_ref = refs[T : T + 6]
    out_messages = refs[T + 6 : 2 * T + 6]
    table_ref, frame_ref, xs_ref, us_ref, z_ref, before_ref, acc_ref, hcat_ref = refs[2 * T + 6 :]
    t, p = sc[24], sc[25]
    own = (x_ref[...].reshape(N, C), up_ref[...].reshape(N, C))
    gx, gu = gather_ghosts(dm, sc, t, own, messages, table_ref)
    top, bottom = dm.WE, dm.WE + dm.ROW
    build_shifts(dm, x_ref, gx[:top], gx[top:bottom], gx[bottom:], frame_ref, xs_ref)
    total = None
    for a in range(3):
        for b in range(3):
            term = jnp.dot(
                xs_ref[b, a * dm.ROW : (a + R) * dm.ROW], w1_ref[3 * a + b], preferred_element_type=F32
            )
            total = term if total is None else total + term
    before = total + bias_ref[...]
    before_ref[...] = before
    sig = 1.0 / (1.0 + jnp.exp(-before))
    hidden = before * sig
    acc_ref[...] = hidden
    hidden_bf = hidden.astype(BF)
    up_top = jnp.where(t == 0, 0.0, gu[top:bottom])
    up_bottom = jnp.where(t == T - 1, 0.0, gu[bottom:])
    build_shifts(dm, up_ref, None, up_top, up_bottom, frame_ref, us_ref)
    build_strip_terms(dm, sc, t, gu[:top], gu[top:bottom], gu[bottom:], z_ref)
    hcat_ref[...] = jnp.zeros(hcat_ref.shape, F32)
    for f in range(6):
        for side in range(2):
            for r in range(R):
                at = (r * 6 + f) * F + side * (F - 1)
                row = 16 * f + 8 * side + r
                hcat_ref[row : row + 1] = acc_ref[at : at + 1]
    first_row = acc_ref[0 : dm.ROW]
    last_row = acc_ref[(R - 1) * dm.ROW : R * dm.ROW]
    hcat_ref[dm.WE :] = jnp.where(t == 0, first_row, last_row)
    hidden_t = hidden_bf.T
    edge_t = hcat_ref[...].astype(BF).T
    for a in range(3):
        for b in range(3):
            main = us_ref[2 - b, (2 - a) * dm.ROW : (2 - a + R) * dm.ROW]
            grad = jnp.dot(hidden_t, main, preferred_element_type=F32)
            grad = grad + jnp.dot(edge_t, z_ref[3 * a + b].astype(BF), preferred_element_type=F32)
            put_tap(s2_ref, k2_ref, p, 3 * a + b, grad)
    put_extra(s2_ref, k2_ref, jnp.zeros((1, C), F32))
    for r in range(R):
        for f in range(6):
            at = (r * 6 + f) * F
            hid_ref[f * R + r] = acc_ref[at : at + F].astype(BF)
    adjoint(dm, t, us_ref, z_ref, w2_ref, acc_ref)
    before = before_ref[...]
    sig = 1.0 / (1.0 + jnp.exp(-before))
    before_grad = acc_ref[...] * (sig * (1.0 + before * (1.0 - sig)))
    acc_ref[...] = before_grad
    inner = before_grad.astype(BF)
    for a in range(3):
        for b in range(3):
            grad = lax.dot_general(
                xs_ref[b, a * dm.ROW : (a + R) * dm.ROW],
                inner,
                (((0,), (0,)), ((), ())),
                preferred_element_type=F32,
            )
            put_tap(s1_ref, k1_ref, p, 3 * a + b, grad)
    put_extra(s1_ref, k1_ref, jnp.sum(before_grad, axis=0, keepdims=True))
    for r in range(R):
        for f in range(6):
            at = (r * 6 + f) * F
            inner_ref[f * R + r] = acc_ref[at : at + F].astype(BF)
    write_messages(
        dm, sc, t, (hid_ref[...].reshape(N, C), inner_ref[...].reshape(N, C)), out_messages
    )


def second_kernel(dm, sc, x_ref, d_ref, hid_ref, inner_ref, w1_ref, w2_ref, *refs):
    T, R, F, N, C = dm.T, dm.R, dm.F, dm.N, dm.C
    messages = refs[:T]
    state_ref, grad_ref = refs[T : T + 2]
    table_ref, frame_ref, shift_ref, z_ref, acc_ref = refs[T + 2 :]
    t = sc[24]
    own = (hid_ref[...].reshape(N, C), inner_ref[...].reshape(N, C))
    gh, gi = gather_ghosts(dm, sc, t, own, messages, table_ref)
    top, bottom = dm.WE, dm.WE + dm.ROW
    build_shifts(dm, hid_ref, gh[:top], gh[top:bottom], gh[bottom:], frame_ref, shift_ref)
    total = None
    for a in range(3):
        for b in range(3):
            term = jnp.dot(
                shift_ref[b, a * dm.ROW : (a + R) * dm.ROW],
                w2_ref[3 * a + b],
                preferred_element_type=F32,
            )
            total = term if total is None else total + term
    acc_ref[...] = total
    for r in range(R):
        for f in range(6):
            at = (r * 6 + f) * F
            value = x_ref[f * R + r].astype(F32) + acc_ref[at : at + F]
            state_ref[f * R + r] = value.astype(BF)
    in_top = jnp.where(t == 0, 0.0, gi[top:bottom])
    in_bottom = jnp.where(t == T - 1, 0.0, gi[bottom:])
    build_shifts(dm, inner_ref, None, in_top, in_bottom, frame_ref, shift_ref)
    build_strip_terms(dm, sc, t, gi[:top], gi[top:bottom], gi[bottom:], z_ref)
    adjoint(dm, t, shift_ref, z_ref, w1_ref, acc_ref)
    for r in range(R):
        for f in range(6):
            at = (r * 6 + f) * F
            grad_ref[f * R + r] = d_ref[f * R + r].astype(F32) + acc_ref[at : at + F]


def extra_sum(keep, recv, n):
    return keep[n : n + 1] + recv[n : n + 1].astype(F32) + recv[n + 1 : n + 2].astype(F32)


def halve_kernel(pieces, shift, sc, keep_ref, recv_ref, *refs):
    out_keep, out_sends, sum_ref = refs[0], refs[1:pieces], refs[pieces]
    n = keep_ref.shape[0] - EXTRA
    size = n // pieces
    own = sc[24] % 2 if shift == 0 else sc[24] // 2
    sum_ref[...] = keep_ref[0:n] + recv_ref[0:n].astype(F32)
    extra = extra_sum(keep_ref, recv_ref, n)
    out_keep[0:size] = sum_ref[pl.ds(pl.multiple_of(own * size, 8), size)]
    i = lax.broadcasted_iota(jnp.int32, (EXTRA, extra.shape[1]), 0)
    high = extra.astype(BF).astype(F32)
    out_keep[size:] = jnp.where(i == 0, extra, 0.0)
    tail = jnp.where(i == 0, high, jnp.where(i == 1, extra - high, 0.0)).astype(BF)
    for j in range(1, pieces):
        at = pl.multiple_of((own ^ j) * size, 8)
        out_sends[j - 1][0:size] = sum_ref[pl.ds(at, size)].astype(BF)
        out_sends[j - 1][size:] = tail


def last_kernel(keep_ref, *refs):
    recvs, (block_ref, extra_ref) = refs[:-2], refs[-2:]
    n = keep_ref.shape[0] - EXTRA
    total = keep_ref[0:n]
    extra = keep_ref[n : n + 1]
    for ref in recvs:
        total = total + ref[0:n].astype(F32)
        extra = extra + ref[n : n + 1].astype(F32) + ref[n + 1 : n + 2].astype(F32)
    block_ref[...] = total.astype(BF)
    extra_ref[...] = jnp.broadcast_to(extra, extra_ref.shape)


def normal_kernel(zcount, sc, a_ref, b_ref, c_ref, d_ref, extra_ref, out_ref, bias_ref):
    t, p = sc[24], sc[25]
    refs = (a_ref, b_ref, c_ref, d_ref)
    square = None
    for ref in refs:
        v = ref[...].astype(F32)
        s = jnp.sum(v * v, axis=0, keepdims=True)
        square = s if square is None else square + s
    mean = jnp.sum(square, keepdims=True) / (out_ref.shape[0] * out_ref.shape[1])
    scale = lax.rsqrt(mean + 1e-06)
    size = a_ref.shape[0] // zcount
    for index, ref in enumerate(refs):
        block = (p ^ (index // 2)) * 2 + ((t % 2) ^ (index % 2))
        for j in range(zcount):
            at = (block * zcount + ((t // 2) ^ j)) * size
            value = ref[j * size : (j + 1) * size].astype(F32) * scale
            out_ref[pl.ds(pl.multiple_of(at, 8), size)] = value
    extra = extra_ref[0:1]
    bias_mean = jnp.mean(extra * extra, keepdims=True)
    bias_ref[...] = jnp.broadcast_to(extra * lax.rsqrt(bias_mean + 1e-06), bias_ref.shape)


def call(kernel, out_shapes, scratch=(), smem_first=True):
    def run(*args):
        vmem = pl.BlockSpec(memory_space=pltpu.VMEM)
        smem = pl.BlockSpec(memory_space=pltpu.SMEM)
        specs = [smem if smem_first and i == 0 else vmem for i in range(len(args))]
        return pl.pallas_call(
            kernel,
            out_shape=[jax.ShapeDtypeStruct(s, dt) for s, dt in out_shapes],
            in_specs=specs,
            out_specs=[vmem] * len(out_shapes),
            scratch_shapes=[pltpu.VMEM(s, dt) for s, dt in scratch],
            compiler_params=pltpu.CompilerParams(vmem_limit_bytes=56 << 20),
        )(*args)

    return run


def exchange(tiles, messages):
    return [messages[0]] + [
        lax.ppermute(messages[k], "tile", [(i, i ^ k) for i in range(tiles)]) for k in range(1, tiles)
    ]


def swap_dp(v):
    count = lax.axis_size("dp")
    return lax.ppermute(v, "dp", [(i, count - 1 - i) for i in range(count)])


def on_device(initial_state, state_cotangents, w_first, bias, w_second, edge_partner):
    tiles = lax.axis_size("tile")
    _, _, rows, face, channels = initial_state.shape
    dm = Dims(rows, face, tiles, channels)
    planes = (6 * rows, face, channels)
    sc = jnp.concatenate(
        [
            edge_partner.reshape(24).astype(jnp.int32),
            lax.axis_index("tile")[None].astype(jnp.int32),
            lax.axis_index("dp")[None].astype(jnp.int32),
        ]
    )
    x = initial_state.reshape(planes)
    d = state_cotangents[state_cotangents.shape[0] - 1].reshape(planes)
    w1 = w_first.reshape(9, channels, channels)
    w2 = w_second.reshape(9, channels, channels)
    msg_shapes = [((2, dm.msg_rows(k), channels), BF) for k in range(tiles)]
    flat = (dm.N, channels)
    messages = call(functools.partial(pack_kernel, dm), msg_shapes)(sc, x.reshape(flat), d.reshape(flat))
    messages = exchange(tiles, messages)
    half = 9 * channels // 2 + EXTRA
    shift_rows = (3, (rows + 2) * dm.ROW, channels)
    frame = (rows + 2, 6, face + 16, channels)
    outs = call(
        functools.partial(first_kernel, dm),
        [((half, channels), BF), ((half, channels), F32)] * 2 + [(planes, BF)] * 2 + msg_shapes,
        [
            ((dm.NT, channels), BF),
            (frame, F32),
            (shift_rows, BF),
            (shift_rows, BF),
            ((9, dm.S, channels), F32),
            (flat, F32),
            (flat, F32),
            ((dm.S, channels), F32),
        ],
    )(sc, x, d, w1, bias.reshape(1, channels), w2, *messages)
    send_first, keep_first, send_second, keep_second, hidden, inner = outs[:6]

    zcount = tiles // 2

    def reduced(send, keep):
        recv = swap_dp(send)
        n = (half - EXTRA) // 2
        keep, send = call(
            functools.partial(halve_kernel, 2, 0),
            [((n + EXTRA, channels), F32), ((n + EXTRA, channels), BF)],
            [((2 * n, channels), F32)],
        )(sc, keep, recv)
        recv = lax.ppermute(send, "tile", [(i, i ^ 1) for i in range(tiles)])
        m = n // zcount
        keep, *sends = call(
            functools.partial(halve_kernel, zcount, 1),
            [((m + EXTRA, channels), F32)] + [((m + EXTRA, channels), BF)] * (zcount - 1),
            [((n, channels), F32)],
        )(sc, keep, recv)
        recvs = [
            lax.ppermute(v, "tile", [(i, i ^ (2 * (j + 1))) for i in range(tiles)])
            for j, v in enumerate(sends)
        ]
        block, extra = call(last_kernel, [((m, channels), BF), ((8, channels), F32)], smem_first=False)(
            keep, *recvs
        )
        blocks = [block] + [
            lax.ppermute(block, "tile", [(i, i ^ (2 * j)) for i in range(tiles)])
            for j in range(1, zcount)
        ]
        own = jnp.concatenate(blocks, axis=0)
        other = lax.ppermute(own, "tile", [(i, i ^ 1) for i in range(tiles)])
        far_own = swap_dp(own)
        far_other = swap_dp(other)
        return call(
            functools.partial(normal_kernel, zcount),
            [((9 * channels, channels), F32), ((8, channels), F32)],
        )(sc, own, other, far_own, far_other, extra)

    second_step, _ = reduced(send_second, keep_second)
    first_step, bias_step = reduced(send_first, keep_first)

    messages = exchange(tiles, outs[6:])
    state, grad = call(
        functools.partial(second_kernel, dm),
        [(planes, BF), (planes, F32)],
        [
            ((dm.NT, channels), BF),
            (frame, F32),
            (shift_rows, BF),
            ((9, dm.S, channels), F32),
            (flat, F32),
        ],
    )(sc, x, d, hidden, inner, w1, w2, *messages)
    return (
        state.reshape(initial_state.shape),
        grad.reshape(initial_state.shape),
        first_step.reshape(w_first.shape),
        bias_step[0],
        second_step.reshape(w_second.shape),
    )


def solution(mesh):
    return jax.shard_map(
        on_device,
        mesh=mesh,
        in_specs=(
            P(("groups", "dp"), None, "tile", None, None),
            P(None, ("groups", "dp"), None, "tile", None, None),
            P(),
            P(),
            P(),
            P(),
        ),
        out_specs=(
            P(("groups", "dp"), None, "tile", None, None),
            P(("groups", "dp"), None, "tile", None, None),
            P("groups", None, None, None),
            P("groups"),
            P("groups", None, None, None),
        ),
        check_vma=False,
    )
```

```python
import functools

import jax
import jax.numpy as jnp
from jax import lax
from jax.experimental import pallas as pl
from jax.experimental.pallas import tpu as pltpu
from jax.sharding import PartitionSpec as P

BF = jnp.bfloat16
F32 = jnp.float32
EXTRA = 16


class Dims:
    def __init__(self, rows, face, tiles, channels):
        self.R, self.F, self.T, self.C = rows, face, tiles, channels
        self.N = 6 * rows * face
        self.ROW = 6 * face
        self.SLOT = -(-(2 * rows + 2) // 8) * 8
        self.BASE = 6 * self.SLOT
        self.MIR = 16 * rows
        self.o_msg = self.N
        self.o_mir = self.o_msg + tiles * self.BASE
        self.o_row = self.o_mir + self.MIR
        self.NT = self.o_row + 2 * self.ROW
        self.WE = 12 * 8
        self.S = self.WE + self.ROW

    def messages(self):
        rows = [self.BASE] * (self.T - 1) + [self.MIR, self.BASE + self.ROW]
        rows[1] += self.ROW
        return rows

    def table_parts(self):
        parts = [(k, 0, self.BASE, self.o_msg + k * self.BASE) for k in range(self.T - 1)]
        parts.append((self.T, 0, self.BASE, self.o_msg + (self.T - 1) * self.BASE))
        parts.append((self.T - 1, 0, self.MIR, self.o_mir))
        parts.append((1, self.BASE, self.ROW, self.o_row))
        parts.append((self.T, self.BASE, self.ROW, self.o_row + self.ROW))
        return parts

    def pairs(self):
        T = self.T
        edges = (0, T - 1)

        def needed(i, d):
            return i in edges or d in edges or d in (T - 2 - i, T - i)

        out = [[(i, i ^ k) for i in range(T) if k == 1 or needed(i, i ^ k)] for k in range(T - 1)]
        out.append([(i, T - 1 - i) for i in range(T)])
        out.append([(i, (i + 1) % T if i % 2 else (i - 1) % T) for i in range(T)])
        return out


def col_iota(n):
    return lax.broadcasted_iota(jnp.int32, (n, 1), 0)


def one_hot(target, width):
    lanes = lax.broadcasted_iota(jnp.int32, (target.shape[0], width), 1)
    return jnp.where(lanes == target, 1.0, 0.0).astype(BF)


def strip_targets(dm, ep, t, d):
    R, F, T = dm.R, dm.F, dm.T
    at_edge = (t == 0) | (t == T - 1)
    to_edge = (d == 0) | (d == T - 1)
    own_edge = jnp.where(t == 0, 0, 2)
    far_edge = jnp.where(d == 0, 0, 2)
    side_row = jnp.where(d == T - 2 - t, R - 1, 0)
    i = col_iota(dm.SLOT)
    q = R * d - 1 + i
    inside = (q >= 0) & (q < F) & (i < R + 2)
    i2 = i - (R + 2)
    parts = []
    for f in range(6):
        far_low = (ep[f, own_edge] % 4) < 2
        reverse = far_low == (t == 0)
        p0 = jnp.where(reverse, F - 1, 0)
        sgn = jnp.where(reverse, -1, 1)
        row = jnp.where(t == 0, 0, R - 1)
        strip = jnp.where(inside, (f * R + row) * F + p0 + sgn * q, -1)
        sides = (f * R + side_row) * F
        low = jnp.where(at_edge, strip, sides + i * (F - 1))
        low = jnp.where(at_edge | (i < 2), low, -1)
        gvalue = ep[f, far_edge]
        column = jnp.where(gvalue % 4 == 1, F - 1, 0) + (gvalue // 4) * (R * F)
        high = jnp.where(to_edge, column + F * i2, jnp.where(i2 < 2, sides + i2 * (F - 1), -1))
        parts.append(jnp.where(i2 < 0, low, jnp.where(i2 < R, high, -1)))
    return parts


def row_targets(dm, row):
    j = col_iota(dm.F)
    return [(f * dm.R + row) * dm.F + j for f in range(6)]


def message_targets(dm, ep, t, k):
    R, F, T = dm.R, dm.F, dm.T
    if k == T - 1:
        s = col_iota(16)
        cells = (s // 2) * (R * F) + (s % 2) * (F - 1)
        parts = [jnp.where(s < 12, cells + r * F, -1) for r in range(R)]
    elif k == T:
        parts = strip_targets(dm, ep, t, T - 1 - t)
        parts += row_targets(dm, jnp.where(t % 2 == 1, R - 1, 0))
    else:
        parts = strip_targets(dm, ep, t, t ^ k)
        if k == 1:
            parts += row_targets(dm, jnp.where(t % 2 == 0, R - 1, 0))
    return jnp.concatenate(parts, axis=0)


def write_messages(dm, ep, t, sources, refs):
    for k in range(dm.T + 1):
        hot = one_hot(message_targets(dm, ep, t, k), dm.N)
        for which, source in enumerate(sources):
            refs[k][which] = jnp.dot(hot, source, preferred_element_type=F32).astype(BF)


def pack_kernel(dm, ep, x_ref, up_ref, *refs):
    write_messages(dm, ep, lax.axis_index("tile"), (x_ref[...], up_ref[...]), refs)


def ghost_targets(dm, ep, t):
    R, F, T = dm.R, dm.F, dm.T
    odd = t % 2
    parts = []
    m = col_iota(8)
    q = R * t - 1 + m
    inside = (q >= 0) & (q < F) & (m < R + 2)
    row_prev = dm.o_row + (1 - odd) * dm.ROW
    row_next = dm.o_row + odd * dm.ROW
    side_first = dm.o_msg + (t ^ (T - t)) * dm.BASE + jnp.where(t == 1, R + 2, 0)
    side_last = dm.o_msg + (t ^ (T - 2 - t)) * dm.BASE + jnp.where(t == T - 2, R + 2, 0)
    for f in range(6):
        for edge in (3, 1):
            value = ep[f, edge]
            f2, e2 = value // 4, value % 4
            far_low = e2 < 2
            reverse = far_low if edge < 2 else e2 >= 2
            is_col = (e2 % 2) == 1
            side = jnp.where(e2 == 1, 1, 0)
            column = side * (F - 1)
            s = 2 * f2 + side
            slot = f2 * dm.SLOT + side
            src_k = jnp.where(e2 == 0, t, t ^ (T - 1))
            row = dm.o_msg + src_k * dm.BASE + f2 * dm.SLOT
            i0 = jnp.where(is_col, jnp.where(reverse, side_first + slot, row_prev + f2 * F + column), row)
            i4 = jnp.where(
                is_col, jnp.where(reverse, side_last + slot, row_next + f2 * F + column), row + R + 1
            )
            base = jnp.where(
                is_col, jnp.where(reverse, dm.o_mir + 16 * R + s, (f2 * R - 1) * F + column), row
            )
            step = jnp.where(is_col, jnp.where(reverse, -16, F), 1)
            target = jnp.where(m == 0, i0, jnp.where(m == R + 1, i4, base + step * m))
            parts.append(jnp.where(inside, target, -1))
    j = col_iota(F)
    jt = jnp.zeros_like(j)
    for b in range(1, T):
        jt = jt + jnp.where(j >= b * R, 1, 0)
    jr = j - R * jt
    wrap = dm.o_row + dm.ROW
    for edge in (0, 2):
        at_edge = (t == 0) if edge == 0 else (t == T - 1)
        inner_base = row_prev if edge == 0 else row_next
        own_row = 0 if edge == 0 else R - 1
        for f in range(6):
            value = ep[f, edge]
            f2, e2 = value // 4, value % 4
            far_low = e2 < 2
            reverse = far_low if edge < 2 else e2 >= 2
            is_col = (e2 % 2) == 1
            same = e2 == edge
            row_base = jnp.where(same, (f2 * R + own_row) * F, wrap + f2 * F)
            lin_base = row_base + jnp.where(reverse, F - 1, 0)
            lin_step = jnp.where(reverse, -1, 1)
            k0 = jnp.where(reverse, T - 1, 0)
            ks = jnp.where(reverse, -1, 1)
            if edge == 2:
                k0 = T - 1 - k0
                ks = -ks
            col_base = dm.o_msg + k0 * dm.BASE + f * dm.SLOT + R + 2 + jnp.where(reverse, R - 1, 0)
            base = jnp.where(is_col, col_base, lin_base)
            sj = jnp.where(is_col, 0, lin_step)
            st = jnp.where(is_col, ks * dm.BASE, 0)
            sr = jnp.where(is_col, jnp.where(reverse, -1, 1), 0)
            base = jnp.where(at_edge, base, inner_base + f * F)
            sj = jnp.where(at_edge, sj, 1)
            st = jnp.where(at_edge, st, 0)
            sr = jnp.where(at_edge, sr, 0)
            parts.append(base + sj * j + st * jt + sr * jr)
    return jnp.concatenate(parts, axis=0)


def gather_ghosts(dm, ep, t, own, messages, table_ref):
    hot = one_hot(ghost_targets(dm, ep, t), dm.NT)
    out = []
    for which in range(2):
        table_ref[0 : dm.N] = own[which]
        for k, row, count, at in dm.table_parts():
            table_ref[at : at + count] = messages[k][which, row : row + count]
        out.append(jnp.dot(hot, table_ref[...], preferred_element_type=F32))
    return out


def build_shifts(dm, field_ref, ghosts, top, bottom, frame_ref, shift_ref):
    R, F, C = dm.R, dm.F, dm.C
    for f in range(6):
        for r in range(R):
            frame_ref[r + 1, f, 8 : 8 + F] = field_ref[f * R + r].astype(F32)
    frame_ref[0, :, 8 : 8 + F] = top.reshape(6, F, C)
    frame_ref[R + 1, :, 8 : 8 + F] = bottom.reshape(6, F, C)
    for m in range(R + 2):
        for f in range(6):
            if ghosts is None:
                west = jnp.zeros((1, C), F32)
                east = west
            else:
                west = ghosts[16 * f + m : 16 * f + m + 1]
                east = ghosts[16 * f + 8 + m : 16 * f + 8 + m + 1]
            frame_ref[m, f, 7:8] = west
            frame_ref[m, f, 8 + F : 9 + F] = east
    for m in range(R + 2):
        for b in range(3):
            plane = frame_ref[m, :, 7 + b : 7 + b + F].reshape(dm.ROW, C)
            shift_ref[b, m * dm.ROW : (m + 1) * dm.ROW] = plane.astype(BF)


def build_strip_terms(dm, ep, t, ghosts, top, bottom, z_ref):
    R, F = dm.R, dm.F
    z_ref[...] = jnp.zeros(z_ref.shape, F32)

    def tap_of(f, edge, shift):
        e2 = ep[f, edge] % 4
        reverse = e2 < 2 if edge < 2 else e2 >= 2
        along = 1 - jnp.where(reverse, -shift, shift)
        return jnp.where(
            e2 == 0, along, jnp.where(e2 == 2, 6 + along, jnp.where(e2 == 1, 3 * along + 2, 3 * along))
        )

    live = lax.rem(lax.broadcasted_iota(jnp.int32, (dm.WE, 1), 0), 8) < R
    for shift in (-1, 0, 1):
        moved = pltpu.roll(ghosts, (dm.WE - 1 - shift) % dm.WE, 0) if shift > -1 else ghosts
        moved = jnp.where(live, moved, 0.0)
        for f in range(6):
            for side, edge in ((0, 3), (1, 1)):
                at = 16 * f + 8 * side
                z_ref[tap_of(f, edge, shift), at : at + 8] = moved[at : at + 8]

    def add_rows(edge, rows):
        j = lax.rem(lax.broadcasted_iota(jnp.int32, (dm.ROW, 1), 0), F)
        for shift in (-1, 0, 1):
            if shift == 0:
                moved = rows
            else:
                moved = pltpu.roll(rows, (-shift) % dm.ROW, 0)
                moved = jnp.where((j + shift >= 0) & (j + shift < F), moved, 0.0)
            for f in range(6):
                at = dm.WE + F * f
                z_ref[tap_of(f, edge, shift), at : at + F] = moved[F * f : F * (f + 1)]

    @pl.when(t == 0)
    def _():
        add_rows(0, top)

    @pl.when(t == dm.T - 1)
    def _():
        add_rows(2, bottom)


def adjoint(dm, t, u_ref, z_ref, w_ref, acc_ref):
    R, F = dm.R, dm.F
    total = None
    strips = None
    for a in range(3):
        for b in range(3):
            main = u_ref[2 - b, (2 - a) * dm.ROW : (2 - a + R) * dm.ROW]
            w = w_ref[3 * a + b]
            dims = (((1,), (1,)), ((), ()))
            term = lax.dot_general(main, w, dims, preferred_element_type=F32)
            strip = lax.dot_general(z_ref[3 * a + b].astype(BF), w, dims, preferred_element_type=F32)
            total = term if total is None else total + term
            strips = strip if strips is None else strips + strip
    acc_ref[...] = total
    for f in range(6):
        for side in range(2):
            for r in range(R):
                at = (r * 6 + f) * F + side * (F - 1)
                row = 16 * f + 8 * side + r
                acc_ref[at : at + 1] += strips[row : row + 1]

    @pl.when(t == 0)
    def _():
        acc_ref[0 : dm.ROW] += strips[dm.WE :]

    @pl.when(t == dm.T - 1)
    def _():
        acc_ref[(R - 1) * dm.ROW : R * dm.ROW] += strips[dm.WE :]


def put_tap(send_ref, keep_ref, p, tap, value):
    half = send_ref.shape[0] - EXTRA
    unit = value.shape[0] // 2
    for part in range(2):
        row = tap * 2 * unit + part * unit
        owner = row // half
        at = row - owner * half
        piece = value[part * unit : (part + 1) * unit]

        @pl.when(p == owner)
        def _():
            keep_ref[at : at + unit] = piece

        @pl.when(p != owner)
        def _():
            send_ref[at : at + unit] = piece.astype(BF)


def put_extra(send_ref, keep_ref, row):
    c = row.shape[1]
    n = send_ref.shape[0] - EXTRA
    i = lax.broadcasted_iota(jnp.int32, (EXTRA, c), 0)
    high = row.astype(BF)
    low = (row - high.astype(F32)).astype(BF).astype(F32)
    keep_ref[n:] = jnp.where(i == 0, row, 0.0)
    send_ref[n:] = jnp.where(i == 0, high.astype(F32), jnp.where(i == 1, low, 0.0)).astype(BF)


def first_kernel(dm, ep, x_ref, up_ref, w1_ref, bias_ref, w2_ref, *refs):
    T, R, F, N, C = dm.T, dm.R, dm.F, dm.N, dm.C
    M = T + 1
    messages = refs[:M]
    s1_ref, k1_ref, s2_ref, k2_ref, hid_ref, inner_ref = refs[M : M + 6]
    out_messages = refs[M + 6 : 2 * M + 6]
    table_ref, frame_ref, xs_ref, us_ref, z_ref, before_ref, acc_ref, hcat_ref = refs[2 * M + 6 :]
    t, p = lax.axis_index("tile"), lax.axis_index("dp")
    own = (x_ref[...].reshape(N, C), up_ref[...].reshape(N, C))
    gx, gu = gather_ghosts(dm, ep, t, own, messages, table_ref)
    top, bottom = dm.WE, dm.WE + dm.ROW
    build_shifts(dm, x_ref, gx[:top], gx[top:bottom], gx[bottom:], frame_ref, xs_ref)
    total = None
    for a in range(3):
        for b in range(3):
            term = jnp.dot(
                xs_ref[b, a * dm.ROW : (a + R) * dm.ROW], w1_ref[3 * a + b], preferred_element_type=F32
            )
            total = term if total is None else total + term
    before = total + bias_ref[...]
    before_ref[...] = before
    sig = 1.0 / (1.0 + jnp.exp(-before))
    hidden = before * sig
    acc_ref[...] = hidden
    hidden_bf = hidden.astype(BF)
    up_top = jnp.where(t == 0, 0.0, gu[top:bottom])
    up_bottom = jnp.where(t == T - 1, 0.0, gu[bottom:])
    build_shifts(dm, up_ref, None, up_top, up_bottom, frame_ref, us_ref)
    build_strip_terms(dm, ep, t, gu[:top], gu[top:bottom], gu[bottom:], z_ref)
    hcat_ref[...] = jnp.zeros(hcat_ref.shape, F32)
    for f in range(6):
        for side in range(2):
            for r in range(R):
                at = (r * 6 + f) * F + side * (F - 1)
                row = 16 * f + 8 * side + r
                hcat_ref[row : row + 1] = acc_ref[at : at + 1]
    first_row = acc_ref[0 : dm.ROW]
    last_row = acc_ref[(R - 1) * dm.ROW : R * dm.ROW]
    hcat_ref[dm.WE :] = jnp.where(t == 0, first_row, last_row)
    hidden_t = hidden_bf.T
    edge_t = hcat_ref[...].astype(BF).T
    for a in range(3):
        for b in range(3):
            main = us_ref[2 - b, (2 - a) * dm.ROW : (2 - a + R) * dm.ROW]
            grad = jnp.dot(hidden_t, main, preferred_element_type=F32)
            grad = grad + jnp.dot(edge_t, z_ref[3 * a + b].astype(BF), preferred_element_type=F32)
            put_tap(s2_ref, k2_ref, p, 3 * a + b, grad)
    put_extra(s2_ref, k2_ref, jnp.zeros((1, C), F32))
    for r in range(R):
        for f in range(6):
            at = (r * 6 + f) * F
            hid_ref[f * R + r] = acc_ref[at : at + F].astype(BF)
    adjoint(dm, t, us_ref, z_ref, w2_ref, acc_ref)
    before = before_ref[...]
    sig = 1.0 / (1.0 + jnp.exp(-before))
    before_grad = acc_ref[...] * (sig * (1.0 + before * (1.0 - sig)))
    acc_ref[...] = before_grad
    inner = before_grad.astype(BF)
    for a in range(3):
        for b in range(3):
            grad = lax.dot_general(
                xs_ref[b, a * dm.ROW : (a + R) * dm.ROW],
                inner,
                (((0,), (0,)), ((), ())),
                preferred_element_type=F32,
            )
            put_tap(s1_ref, k1_ref, p, 3 * a + b, grad)
    put_extra(s1_ref, k1_ref, jnp.sum(before_grad, axis=0, keepdims=True))
    for r in range(R):
        for f in range(6):
            at = (r * 6 + f) * F
            inner_ref[f * R + r] = acc_ref[at : at + F].astype(BF)
    write_messages(
        dm, ep, t, (hid_ref[...].reshape(N, C), inner_ref[...].reshape(N, C)), out_messages
    )


def second_kernel(dm, ep, x_ref, d_ref, hid_ref, inner_ref, w1_ref, w2_ref, *refs):
    T, R, F, N, C = dm.T, dm.R, dm.F, dm.N, dm.C
    messages = refs[: T + 1]
    state_ref, grad_ref = refs[T + 1 : T + 3]
    table_ref, frame_ref, shift_ref, z_ref, acc_ref = refs[T + 3 :]
    t = lax.axis_index("tile")
    own = (hid_ref[...].reshape(N, C), inner_ref[...].reshape(N, C))
    gh, gi = gather_ghosts(dm, ep, t, own, messages, table_ref)
    top, bottom = dm.WE, dm.WE + dm.ROW
    build_shifts(dm, hid_ref, gh[:top], gh[top:bottom], gh[bottom:], frame_ref, shift_ref)
    total = None
    for a in range(3):
        for b in range(3):
            term = jnp.dot(
                shift_ref[b, a * dm.ROW : (a + R) * dm.ROW],
                w2_ref[3 * a + b],
                preferred_element_type=F32,
            )
            total = term if total is None else total + term
    acc_ref[...] = total
    for r in range(R):
        for f in range(6):
            at = (r * 6 + f) * F
            value = x_ref[f * R + r].astype(F32) + acc_ref[at : at + F]
            state_ref[f * R + r] = value.astype(BF)
    in_top = jnp.where(t == 0, 0.0, gi[top:bottom])
    in_bottom = jnp.where(t == T - 1, 0.0, gi[bottom:])
    build_shifts(dm, inner_ref, None, in_top, in_bottom, frame_ref, shift_ref)
    build_strip_terms(dm, ep, t, gi[:top], gi[top:bottom], gi[bottom:], z_ref)
    adjoint(dm, t, shift_ref, z_ref, w1_ref, acc_ref)
    for r in range(R):
        for f in range(6):
            at = (r * 6 + f) * F
            grad_ref[f * R + r] = d_ref[f * R + r].astype(F32) + acc_ref[at : at + F]


def extra_sum(keep, recv, n):
    return keep[n : n + 1] + recv[n : n + 1].astype(F32) + recv[n + 1 : n + 2].astype(F32)


def halve_kernel(pieces, shift, keep_ref, recv_ref, *refs):
    out_keep, out_sends, sum_ref = refs[0], refs[1:pieces], refs[pieces]
    n = keep_ref.shape[0] - EXTRA
    size = n // pieces
    t = lax.axis_index("tile")
    own = t % 2 if shift == 0 else t // 2
    sum_ref[...] = keep_ref[0:n] + recv_ref[0:n].astype(F32)
    extra = extra_sum(keep_ref, recv_ref, n)
    out_keep[0:size] = sum_ref[pl.ds(pl.multiple_of(own * size, 8), size)]
    i = lax.broadcasted_iota(jnp.int32, (EXTRA, extra.shape[1]), 0)
    high = extra.astype(BF).astype(F32)
    out_keep[size:] = jnp.where(i == 0, extra, 0.0)
    tail = jnp.where(i == 0, high, jnp.where(i == 1, extra - high, 0.0)).astype(BF)
    for j in range(1, pieces):
        at = pl.multiple_of((own ^ j) * size, 8)
        out_sends[j - 1][0:size] = sum_ref[pl.ds(at, size)].astype(BF)
        out_sends[j - 1][size:] = tail


def last_kernel(keep_ref, *refs):
    recvs, (block_ref, extra_ref) = refs[:-2], refs[-2:]
    n = keep_ref.shape[0] - EXTRA
    total = keep_ref[0:n]
    extra = keep_ref[n : n + 1]
    for ref in recvs:
        total = total + ref[0:n].astype(F32)
        extra = extra + ref[n : n + 1].astype(F32) + ref[n + 1 : n + 2].astype(F32)
    block_ref[...] = total.astype(BF)
    extra_ref[...] = jnp.broadcast_to(extra, extra_ref.shape)


def normal_kernel(zcount, a_ref, b_ref, c_ref, d_ref, extra_ref, out_ref, bias_ref):
    t, p = lax.axis_index("tile"), lax.axis_index("dp")
    refs = (a_ref, b_ref, c_ref, d_ref)
    square = None
    for ref in refs:
        v = ref[...].astype(F32)
        s = jnp.sum(v * v, axis=0, keepdims=True)
        square = s if square is None else square + s
    mean = jnp.sum(square, keepdims=True) / (out_ref.shape[0] * out_ref.shape[1])
    scale = lax.rsqrt(mean + 1e-06)
    size = a_ref.shape[0] // zcount
    for index, ref in enumerate(refs):
        block = (p ^ (index // 2)) * 2 + ((t % 2) ^ (index % 2))
        for j in range(zcount):
            at = (block * zcount + ((t // 2) ^ j)) * size
            value = ref[j * size : (j + 1) * size].astype(F32) * scale
            out_ref[pl.ds(pl.multiple_of(at, 8), size)] = value
    extra = extra_ref[0:1]
    bias_mean = jnp.mean(extra * extra, keepdims=True)
    bias_ref[...] = extra * lax.rsqrt(bias_mean + 1e-06)


def call(kernel, out_shapes, scratch=(), smem_first=False):
    def run(*args):
        vmem = pl.BlockSpec(memory_space=pltpu.VMEM)
        smem = pl.BlockSpec(memory_space=pltpu.SMEM)
        specs = [smem if smem_first and i == 0 else vmem for i in range(len(args))]
        return pl.pallas_call(
            kernel,
            out_shape=[jax.ShapeDtypeStruct(s, dt) for s, dt in out_shapes],
            in_specs=specs,
            out_specs=[vmem] * len(out_shapes),
            scratch_shapes=[pltpu.VMEM(s, dt) for s, dt in scratch],
            compiler_params=pltpu.CompilerParams(vmem_limit_bytes=56 << 20),
        )(*args)

    return run


def exchange(dm, messages):
    pairs = dm.pairs()
    return [messages[0]] + [lax.ppermute(messages[k], "tile", pairs[k]) for k in range(1, dm.T + 1)]


def swap_dp(v):
    count = lax.axis_size("dp")
    return lax.ppermute(v, "dp", [(i, count - 1 - i) for i in range(count)])


def on_device(initial_state, state_cotangents, w_first, bias, w_second, edge_partner):
    tiles = lax.axis_size("tile")
    _, _, rows, face, channels = initial_state.shape
    dm = Dims(rows, face, tiles, channels)
    planes = (6 * rows, face, channels)
    x = initial_state.reshape(planes)
    d = state_cotangents[state_cotangents.shape[0] - 1].reshape(planes)
    w1 = w_first.reshape(9, channels, channels)
    w2 = w_second.reshape(9, channels, channels)
    msg_shapes = [((2, n, channels), BF) for n in dm.messages()]
    flat = (dm.N, channels)
    messages = call(functools.partial(pack_kernel, dm), msg_shapes, smem_first=True)(
        edge_partner, x.reshape(flat), d.reshape(flat)
    )
    messages = exchange(dm, messages)
    half = 9 * channels // 2
    shift_rows = (3, (rows + 2) * dm.ROW, channels)
    frame = (rows + 2, 6, face + 16, channels)
    outs = call(
        functools.partial(first_kernel, dm),
        [((half + EXTRA, channels), BF), ((half + EXTRA, channels), F32)] * 2 + [(planes, BF)] * 2 + msg_shapes,
        [
            ((dm.NT, channels), BF),
            (frame, F32),
            (shift_rows, BF),
            (shift_rows, BF),
            ((9, dm.S, channels), F32),
            (flat, F32),
            (flat, F32),
            ((dm.S, channels), F32),
        ],
        smem_first=True,
    )(edge_partner, x, d, w1, bias.reshape(1, channels), w2, *messages)
    send_first, keep_first, send_second, keep_second, hidden, inner = outs[:6]

    zcount = tiles // 2
    n = half // 2
    m = n // zcount

    def along_z(v, j):
        return lax.ppermute(v, "tile", [(i, i ^ (2 * j)) for i in range(tiles)])

    def along_y(v):
        return lax.ppermute(v, "tile", [(i, i ^ 1) for i in range(tiles)])

    def reduce_y(keep, recv):
        keep, send = call(
            functools.partial(halve_kernel, 2, 0),
            [((n + EXTRA, channels), F32), ((n + EXTRA, channels), BF)],
            [((2 * n, channels), F32)],
        )(keep, recv)
        return keep, along_y(send)

    def reduce_z(keep, recv):
        keep, *sends = call(
            functools.partial(halve_kernel, zcount, 1),
            [((m + EXTRA, channels), F32)] + [((m + EXTRA, channels), BF)] * (zcount - 1),
            [((n, channels), F32)],
        )(keep, recv)
        return keep, [along_z(v, j + 1) for j, v in enumerate(sends)]

    def gather_z(keep, recvs):
        block, extra = call(last_kernel, [((m, channels), BF), ((8, channels), F32)])(keep, *recvs)
        return [block] + [along_z(block, j) for j in range(1, zcount)], extra

    def finish(own, other, extra):
        return call(
            functools.partial(normal_kernel, zcount),
            [((9 * channels, channels), F32), ((1, channels), F32)],
        )(own, other, swap_dp(own), swap_dp(other), extra)

    keep2, recv2 = reduce_y(keep_second, swap_dp(send_second))
    messages = exchange(dm, outs[6:])
    keep1, recv1 = reduce_y(keep_first, swap_dp(send_first))
    (keep2, recv2), messages = lax.optimization_barrier(((keep2, recv2), messages))
    keep2, recvs2 = reduce_z(keep2, recv2)
    keep1, recvs1 = reduce_z(keep1, recv1)
    blocks2, extra2 = gather_z(keep2, recvs2)
    blocks1, extra1 = gather_z(keep1, recvs1)
    own2 = jnp.concatenate(blocks2, axis=0)
    other2 = along_y(own2)
    own1 = jnp.concatenate(blocks1, axis=0)
    other1 = along_y(own1)
    messages, _ = lax.optimization_barrier((messages, own1))
    state, grad = call(
        functools.partial(second_kernel, dm),
        [(planes, BF), (planes, F32)],
        [
            ((dm.NT, channels), BF),
            (frame, F32),
            (shift_rows, BF),
            ((9, dm.S, channels), F32),
            (flat, F32),
        ],
        smem_first=True,
    )(edge_partner, x, d, hidden, inner, w1, w2, *messages)
    second_step, _ = finish(own2, other2, extra2)
    first_step, bias_step = finish(own1, other1, extra1)
    return (
        state.reshape(initial_state.shape),
        grad.reshape(initial_state.shape),
        first_step.reshape(w_first.shape),
        bias_step.reshape(channels),
        second_step.reshape(w_second.shape),
    )


def solution(mesh):
    return jax.shard_map(
        on_device,
        mesh=mesh,
        in_specs=(
            P(("groups", "dp"), None, "tile", None, None),
            P(None, ("groups", "dp"), None, "tile", None, None),
            P(),
            P(),
            P(),
            P(),
        ),
        out_specs=(
            P(("groups", "dp"), None, "tile", None, None),
            P(("groups", "dp"), None, "tile", None, None),
            P("groups", None, None, None),
            P("groups"),
            P("groups", None, None, None),
        ),
        check_vma=False,
    )
```

```python
import functools

import jax
import jax.numpy as jnp
from jax import lax
from jax.experimental import pallas as pl
from jax.experimental.pallas import tpu as pltpu
from jax.sharding import PartitionSpec as P

BF = jnp.bfloat16
F32 = jnp.float32
EXTRA = 16


class Dims:
    def __init__(self, rows, face, tiles, channels):
        self.R, self.F, self.T, self.C = rows, face, tiles, channels
        self.N = 6 * rows * face
        self.ROW = 6 * face
        self.SLOT = -(-(2 * rows + 2) // 8) * 8
        self.BASE = 6 * self.SLOT
        self.o_msg = self.N
        self.o_mir = self.o_msg + tiles * self.BASE
        self.o_row = self.o_mir + self.BASE
        self.NT = self.o_row + 2 * self.ROW
        self.WE = 12 * 8
        self.S = self.WE + self.ROW

    def messages(self):
        return [(self.T, 2, self.BASE, self.C), (2, self.ROW, self.C), (2, self.BASE + self.ROW, self.C)]


def col_iota(n):
    return lax.broadcasted_iota(jnp.int32, (n, 1), 0)


def one_hot(target, width):
    lanes = lax.broadcasted_iota(jnp.int32, (target.shape[0], width), 1)
    return jnp.where(lanes == target, 1.0, 0.0).astype(BF)


def strip_targets(dm, ep, t, d):
    R, F, T = dm.R, dm.F, dm.T
    at_edge = (t == 0) | (t == T - 1)
    to_edge = (d == 0) | (d == T - 1)
    own_edge = jnp.where(t == 0, 0, 2)
    far_edge = jnp.where(d == 0, 0, 2)
    side_row = jnp.where(d == T - 2 - t, R - 1, 0)
    i = col_iota(dm.SLOT)
    q = R * d - 1 + i
    inside = (q >= 0) & (q < F) & (i < R + 2)
    i2 = i - (R + 2)
    parts = []
    for f in range(6):
        far_low = (ep[f, own_edge] % 4) < 2
        reverse = far_low == (t == 0)
        p0 = jnp.where(reverse, F - 1, 0)
        sgn = jnp.where(reverse, -1, 1)
        row = jnp.where(t == 0, 0, R - 1)
        strip = jnp.where(inside, (f * R + row) * F + p0 + sgn * q, -1)
        sides = (f * R + side_row) * F
        low = jnp.where(at_edge, strip, sides + i * (F - 1))
        low = jnp.where(at_edge | (i < 2), low, -1)
        gvalue = ep[f, far_edge]
        column = jnp.where(gvalue % 4 == 1, F - 1, 0) + (gvalue // 4) * (R * F)
        high = jnp.where(to_edge, column + F * i2, jnp.where(i2 < 2, sides + i2 * (F - 1), -1))
        strips = jnp.where(i2 < 0, low, jnp.where(i2 < R, high, -1))
        mirror = (d == T - 1 - t) & jnp.logical_not(at_edge)
        parts.append(jnp.where(mirror, mirror_slot(dm, f), strips))
    return parts


def mirror_slot(dm, f):
    i = col_iota(dm.SLOT)
    return jnp.where(i < 2 * dm.R, (f * dm.R + i // 2) * dm.F + (i % 2) * (dm.F - 1), -1)


def row_targets(dm, row):
    j = col_iota(dm.F)
    return [(f * dm.R + row) * dm.F + j for f in range(6)]


def write_messages(dm, ep, t, sources, refs):
    R, T = dm.R, dm.T
    strips_ref, pair_ref, ring_ref = refs

    def pick(parts, which):
        hot = one_hot(jnp.concatenate(parts, axis=0), dm.N)
        return jnp.dot(hot, sources[which], preferred_element_type=F32).astype(BF)

    for which in range(2):
        for d in range(T):
            strips_ref[d, which] = pick(strip_targets(dm, ep, t, d), which)
        pair_ref[which] = pick(row_targets(dm, jnp.where(t % 2 == 0, R - 1, 0)), which)
        mirror = [mirror_slot(dm, f) for f in range(6)]
        ring_ref[which] = pick(mirror + row_targets(dm, jnp.where(t % 2 == 1, R - 1, 0)), which)


def pack_kernel(dm, ep, x_ref, up_ref, *refs):
    write_messages(dm, ep, lax.axis_index("tile"), (x_ref[...], up_ref[...]), refs)


def ghost_targets(dm, ep, t):
    R, F, T = dm.R, dm.F, dm.T
    odd = t % 2
    parts = []
    m = col_iota(8)
    q = R * t - 1 + m
    inside = (q >= 0) & (q < F) & (m < R + 2)
    row_prev = dm.o_row + (1 - odd) * dm.ROW
    row_next = dm.o_row + odd * dm.ROW
    side_first = dm.o_msg + (T - t) * dm.BASE + jnp.where(t == 1, R + 2, 0)
    side_last = dm.o_msg + (T - 2 - t) * dm.BASE + jnp.where(t == T - 2, R + 2, 0)
    mirror = jnp.where((t == 0) | (t == T - 1), dm.o_mir, dm.o_msg + (T - 1 - t) * dm.BASE)
    for f in range(6):
        for edge in (3, 1):
            value = ep[f, edge]
            f2, e2 = value // 4, value % 4
            far_low = e2 < 2
            reverse = far_low if edge < 2 else e2 >= 2
            is_col = (e2 % 2) == 1
            side = jnp.where(e2 == 1, 1, 0)
            column = side * (F - 1)
            slot = f2 * dm.SLOT + side
            row = dm.o_msg + jnp.where(e2 == 0, 0, T - 1) * dm.BASE + f2 * dm.SLOT
            i0 = jnp.where(is_col, jnp.where(reverse, side_first + slot, row_prev + f2 * F + column), row)
            i4 = jnp.where(
                is_col, jnp.where(reverse, side_last + slot, row_next + f2 * F + column), row + R + 1
            )
            base = jnp.where(
                is_col, jnp.where(reverse, mirror + 2 * R + slot, (f2 * R - 1) * F + column), row
            )
            step = jnp.where(is_col, jnp.where(reverse, -2, F), 1)
            target = jnp.where(m == 0, i0, jnp.where(m == R + 1, i4, base + step * m))
            parts.append(jnp.where(inside, target, -1))
    j = col_iota(F)
    jt = jnp.zeros_like(j)
    for b in range(1, T):
        jt = jt + jnp.where(j >= b * R, 1, 0)
    jr = j - R * jt
    wrap = dm.o_row + dm.ROW
    for edge in (0, 2):
        at_edge = (t == 0) if edge == 0 else (t == T - 1)
        inner_base = row_prev if edge == 0 else row_next
        own_row = 0 if edge == 0 else R - 1
        for f in range(6):
            value = ep[f, edge]
            f2, e2 = value // 4, value % 4
            far_low = e2 < 2
            reverse = far_low if edge < 2 else e2 >= 2
            is_col = (e2 % 2) == 1
            same = e2 == edge
            row_base = jnp.where(same, (f2 * R + own_row) * F, wrap + f2 * F)
            lin_base = row_base + jnp.where(reverse, F - 1, 0)
            lin_step = jnp.where(reverse, -1, 1)
            k0 = jnp.where(reverse, T - 1, 0)
            ks = jnp.where(reverse, -1, 1)
            col_base = dm.o_msg + k0 * dm.BASE + f * dm.SLOT + R + 2 + jnp.where(reverse, R - 1, 0)
            base = jnp.where(is_col, col_base, lin_base)
            sj = jnp.where(is_col, 0, lin_step)
            st = jnp.where(is_col, ks * dm.BASE, 0)
            sr = jnp.where(is_col, jnp.where(reverse, -1, 1), 0)
            base = jnp.where(at_edge, base, inner_base + f * F)
            sj = jnp.where(at_edge, sj, 1)
            st = jnp.where(at_edge, st, 0)
            sr = jnp.where(at_edge, sr, 0)
            parts.append(base + sj * j + st * jt + sr * jr)
    return jnp.concatenate(parts, axis=0)


def gather_ghosts(dm, ep, t, own, messages, table_ref):
    hot = one_hot(ghost_targets(dm, ep, t), dm.NT)
    out = []
    for which in range(2):
        table_ref[0 : dm.N] = own[which]
        for k in range(dm.T):
            at = dm.o_msg + k * dm.BASE
            table_ref[at : at + dm.BASE] = messages[0][k, which]
        table_ref[dm.o_mir : dm.o_row] = messages[2][which, : dm.BASE]
        table_ref[dm.o_row : dm.o_row + dm.ROW] = messages[1][which]
        table_ref[dm.o_row + dm.ROW :] = messages[2][which, dm.BASE :]
        out.append(jnp.dot(hot, table_ref[...], preferred_element_type=F32))
    return out


def build_shifts(dm, field_ref, ghosts, top, bottom, frame_ref, shift_ref):
    R, F, C = dm.R, dm.F, dm.C
    for f in range(6):
        for r in range(R):
            frame_ref[r + 1, f, 8 : 8 + F] = field_ref[f * R + r].astype(F32)
    frame_ref[0, :, 8 : 8 + F] = top.reshape(6, F, C)
    frame_ref[R + 1, :, 8 : 8 + F] = bottom.reshape(6, F, C)
    for m in range(R + 2):
        for f in range(6):
            if ghosts is None:
                west = jnp.zeros((1, C), F32)
                east = west
            else:
                west = ghosts[16 * f + m : 16 * f + m + 1]
                east = ghosts[16 * f + 8 + m : 16 * f + 8 + m + 1]
            frame_ref[m, f, 7:8] = west
            frame_ref[m, f, 8 + F : 9 + F] = east
    for m in range(R + 2):
        for b in range(3):
            plane = frame_ref[m, :, 7 + b : 7 + b + F].reshape(dm.ROW, C)
            shift_ref[b, m * dm.ROW : (m + 1) * dm.ROW] = plane.astype(BF)


def build_strip_terms(dm, ep, t, ghosts, top, bottom, z_ref):
    R, F = dm.R, dm.F
    z_ref[...] = jnp.zeros(z_ref.shape, F32)

    def tap_of(f, edge, shift):
        e2 = ep[f, edge] % 4
        reverse = e2 < 2 if edge < 2 else e2 >= 2
        along = 1 - jnp.where(reverse, -shift, shift)
        return jnp.where(
            e2 == 0, along, jnp.where(e2 == 2, 6 + along, jnp.where(e2 == 1, 3 * along + 2, 3 * along))
        )

    live = lax.rem(lax.broadcasted_iota(jnp.int32, (dm.WE, 1), 0), 8) < R
    for shift in (-1, 0, 1):
        moved = pltpu.roll(ghosts, (dm.WE - 1 - shift) % dm.WE, 0) if shift > -1 else ghosts
        moved = jnp.where(live, moved, 0.0)
        for f in range(6):
            for side, edge in ((0, 3), (1, 1)):
                at = 16 * f + 8 * side
                z_ref[tap_of(f, edge, shift), at : at + 8] = moved[at : at + 8]

    def add_rows(edge, rows):
        j = lax.rem(lax.broadcasted_iota(jnp.int32, (dm.ROW, 1), 0), F)
        for shift in (-1, 0, 1):
            if shift == 0:
                moved = rows
            else:
                moved = pltpu.roll(rows, (-shift) % dm.ROW, 0)
                moved = jnp.where((j + shift >= 0) & (j + shift < F), moved, 0.0)
            for f in range(6):
                at = dm.WE + F * f
                z_ref[tap_of(f, edge, shift), at : at + F] = moved[F * f : F * (f + 1)]

    @pl.when(t == 0)
    def _():
        add_rows(0, top)

    @pl.when(t == dm.T - 1)
    def _():
        add_rows(2, bottom)


def adjoint(dm, t, u_ref, z_ref, w_ref, acc_ref):
    R, F = dm.R, dm.F
    total = None
    strips = None
    for a in range(3):
        for b in range(3):
            main = u_ref[2 - b, (2 - a) * dm.ROW : (2 - a + R) * dm.ROW]
            w = w_ref[3 * a + b]
            dims = (((1,), (1,)), ((), ()))
            term = lax.dot_general(main, w, dims, preferred_element_type=F32)
            strip = lax.dot_general(z_ref[3 * a + b].astype(BF), w, dims, preferred_element_type=F32)
            total = term if total is None else total + term
            strips = strip if strips is None else strips + strip
    acc_ref[...] = total
    for f in range(6):
        for side in range(2):
            for r in range(R):
                at = (r * 6 + f) * F + side * (F - 1)
                row = 16 * f + 8 * side + r
                acc_ref[at : at + 1] += strips[row : row + 1]

    @pl.when(t == 0)
    def _():
        acc_ref[0 : dm.ROW] += strips[dm.WE :]

    @pl.when(t == dm.T - 1)
    def _():
        acc_ref[(R - 1) * dm.ROW : R * dm.ROW] += strips[dm.WE :]


def put_tap(dm, send_ref, keep_ref, p, which, tap, value):
    size = 9 * dm.C // (2 * dm.T)
    start, stop = tap * dm.C, (tap + 1) * dm.C
    for block in range(2 * dm.T):
        low, high = max(start, block * size), min(stop, (block + 1) * size)
        if low >= high:
            continue
        at = (block % dm.T) * 2 * size + which * size + low - block * size
        piece = value[low - start : high - start]

        @pl.when(p == block // dm.T)
        def _():
            keep_ref[at : at + high - low] = piece

        @pl.when(p != block // dm.T)
        def _():
            send_ref[at : at + high - low] = piece.astype(BF)


def put_extra(send_ref, keep_ref, row):
    c = row.shape[1]
    n = send_ref.shape[0] - EXTRA
    i = lax.broadcasted_iota(jnp.int32, (EXTRA, c), 0)
    high = row.astype(BF)
    low = (row - high.astype(F32)).astype(BF).astype(F32)
    keep_ref[n:] = jnp.where(i == 0, row, 0.0)
    send_ref[n:] = jnp.where(i == 0, high.astype(F32), jnp.where(i == 1, low, 0.0)).astype(BF)


def first_kernel(dm, ep, x_ref, up_ref, w1_ref, bias_ref, w2_ref, *refs):
    T, R, F, N, C = dm.T, dm.R, dm.F, dm.N, dm.C
    messages = refs[:3]
    send_ref, keep_ref, hid_ref, inner_ref = refs[3:7]
    out_messages = refs[7:10]
    table_ref, frame_ref, xs_ref, us_ref, z_ref, before_ref, acc_ref, hcat_ref = refs[10:]
    t, p = lax.axis_index("tile"), lax.axis_index("dp")
    own = (x_ref[...].reshape(N, C), up_ref[...].reshape(N, C))
    gx, gu = gather_ghosts(dm, ep, t, own, messages, table_ref)
    top, bottom = dm.WE, dm.WE + dm.ROW
    build_shifts(dm, x_ref, gx[:top], gx[top:bottom], gx[bottom:], frame_ref, xs_ref)
    total = None
    for a in range(3):
        for b in range(3):
            term = jnp.dot(
                xs_ref[b, a * dm.ROW : (a + R) * dm.ROW], w1_ref[3 * a + b], preferred_element_type=F32
            )
            total = term if total is None else total + term
    before = total + bias_ref[...]
    before_ref[...] = before
    sig = 1.0 / (1.0 + jnp.exp(-before))
    hidden = before * sig
    acc_ref[...] = hidden
    hidden_bf = hidden.astype(BF)
    up_top = jnp.where(t == 0, 0.0, gu[top:bottom])
    up_bottom = jnp.where(t == T - 1, 0.0, gu[bottom:])
    build_shifts(dm, up_ref, None, up_top, up_bottom, frame_ref, us_ref)
    build_strip_terms(dm, ep, t, gu[:top], gu[top:bottom], gu[bottom:], z_ref)
    hcat_ref[...] = jnp.zeros(hcat_ref.shape, F32)
    for f in range(6):
        for side in range(2):
            for r in range(R):
                at = (r * 6 + f) * F + side * (F - 1)
                row = 16 * f + 8 * side + r
                hcat_ref[row : row + 1] = acc_ref[at : at + 1]
    first_row = acc_ref[0 : dm.ROW]
    last_row = acc_ref[(R - 1) * dm.ROW : R * dm.ROW]
    hcat_ref[dm.WE :] = jnp.where(t == 0, first_row, last_row)
    hidden_t = hidden_bf.T
    edge_t = hcat_ref[...].astype(BF).T
    for a in range(3):
        for b in range(3):
            main = us_ref[2 - b, (2 - a) * dm.ROW : (2 - a + R) * dm.ROW]
            grad = jnp.dot(hidden_t, main, preferred_element_type=F32)
            grad = grad + jnp.dot(edge_t, z_ref[3 * a + b].astype(BF), preferred_element_type=F32)
            put_tap(dm, send_ref, keep_ref, p, 0, 3 * a + b, grad)
    for r in range(R):
        for f in range(6):
            at = (r * 6 + f) * F
            hid_ref[f * R + r] = acc_ref[at : at + F].astype(BF)
    adjoint(dm, t, us_ref, z_ref, w2_ref, acc_ref)
    before = before_ref[...]
    sig = 1.0 / (1.0 + jnp.exp(-before))
    before_grad = acc_ref[...] * (sig * (1.0 + before * (1.0 - sig)))
    acc_ref[...] = before_grad
    inner = before_grad.astype(BF)
    for a in range(3):
        for b in range(3):
            grad = lax.dot_general(
                xs_ref[b, a * dm.ROW : (a + R) * dm.ROW],
                inner,
                (((0,), (0,)), ((), ())),
                preferred_element_type=F32,
            )
            put_tap(dm, send_ref, keep_ref, p, 1, 3 * a + b, grad)
    put_extra(send_ref, keep_ref, jnp.sum(before_grad, axis=0, keepdims=True))
    for r in range(R):
        for f in range(6):
            at = (r * 6 + f) * F
            inner_ref[f * R + r] = acc_ref[at : at + F].astype(BF)
    write_messages(
        dm, ep, t, (hid_ref[...].reshape(N, C), inner_ref[...].reshape(N, C)), out_messages
    )


def second_kernel(dm, ep, x_ref, d_ref, hid_ref, inner_ref, w1_ref, w2_ref, *refs):
    T, R, F, N, C = dm.T, dm.R, dm.F, dm.N, dm.C
    messages = refs[:3]
    state_ref, grad_ref = refs[3:5]
    table_ref, frame_ref, shift_ref, z_ref, acc_ref = refs[5:]
    t = lax.axis_index("tile")
    own = (hid_ref[...].reshape(N, C), inner_ref[...].reshape(N, C))
    gh, gi = gather_ghosts(dm, ep, t, own, messages, table_ref)
    top, bottom = dm.WE, dm.WE + dm.ROW
    build_shifts(dm, hid_ref, gh[:top], gh[top:bottom], gh[bottom:], frame_ref, shift_ref)
    total = None
    for a in range(3):
        for b in range(3):
            term = jnp.dot(
                shift_ref[b, a * dm.ROW : (a + R) * dm.ROW],
                w2_ref[3 * a + b],
                preferred_element_type=F32,
            )
            total = term if total is None else total + term
    acc_ref[...] = total
    for r in range(R):
        for f in range(6):
            at = (r * 6 + f) * F
            value = x_ref[f * R + r].astype(F32) + acc_ref[at : at + F]
            state_ref[f * R + r] = value.astype(BF)
    in_top = jnp.where(t == 0, 0.0, gi[top:bottom])
    in_bottom = jnp.where(t == T - 1, 0.0, gi[bottom:])
    build_shifts(dm, inner_ref, None, in_top, in_bottom, frame_ref, shift_ref)
    build_strip_terms(dm, ep, t, gi[:top], gi[top:bottom], gi[bottom:], z_ref)
    adjoint(dm, t, shift_ref, z_ref, w1_ref, acc_ref)
    for r in range(R):
        for f in range(6):
            at = (r * 6 + f) * F
            grad_ref[f * R + r] = d_ref[f * R + r].astype(F32) + acc_ref[at : at + F]


def extra_sum(keep, recv, n):
    return keep[n : n + 1] + recv[n : n + 1].astype(F32) + recv[n + 1 : n + 2].astype(F32)


def extra_rows(extra):
    i = lax.broadcasted_iota(jnp.int32, (EXTRA, extra.shape[1]), 0)
    high = extra.astype(BF).astype(F32)
    tail = jnp.where(i == 0, high, jnp.where(i == 1, extra - high, 0.0)).astype(BF)
    return jnp.where(i == 0, extra, 0.0), tail


def half_kernel(keep_ref, recv_ref, out_keep, out_send):
    n = keep_ref.shape[0] - EXTRA
    size = n // 2
    own = lax.axis_index("tile") % 2
    mine = pl.multiple_of(own * size, 8)
    far = pl.multiple_of((1 - own) * size, 8)
    out_keep[0:size] = keep_ref[pl.ds(mine, size)] + recv_ref[pl.ds(mine, size)].astype(F32)
    out_send[0:size] = (keep_ref[pl.ds(far, size)] + recv_ref[pl.ds(far, size)].astype(F32)).astype(BF)
    keep, tail = extra_rows(extra_sum(keep_ref, recv_ref, n))
    out_keep[size:] = keep
    out_send[size:] = tail


def block_kernel(zcount, keep_ref, recv_ref, out_keep, out_sends):
    n = keep_ref.shape[0] - EXTRA
    size = n // zcount
    own = lax.axis_index("tile") // 2
    keep, tail = extra_rows(extra_sum(keep_ref, recv_ref, n))
    for j in range(zcount):
        at = slice(j * size, (j + 1) * size)
        total = keep_ref[at] + recv_ref[at].astype(F32)
        out_sends[j, 0:size] = total.astype(BF)
        out_sends[j, size:] = tail

        @pl.when(own == j)
        def _():
            out_keep[0:size] = total

    out_keep[size:] = keep


def last_kernel(zcount, keep_ref, recv_ref, block_ref, extra_ref):
    n = keep_ref.shape[0] - EXTRA
    own = lax.axis_index("tile") // 2
    total = keep_ref[0:n]
    extra = keep_ref[n : n + 1]
    for j in range(zcount):
        far = own != j
        total = total + jnp.where(far, recv_ref[j, 0:n].astype(F32), 0.0)
        parts = recv_ref[j, n : n + 2].astype(F32)
        extra = extra + jnp.where(far, parts[0:1] + parts[1:2], 0.0)
    for j in range(zcount):
        block_ref[j] = total.astype(BF)
    extra_ref[...] = extra


def normal_kernel(zcount, a_ref, b_ref, c_ref, d_ref, extra_ref, second_ref, first_ref, bias_ref):
    t, p = lax.axis_index("tile"), lax.axis_index("dp")
    refs = (a_ref, b_ref, c_ref, d_ref)
    size = a_ref.shape[1] // 2
    for which, out_ref in enumerate((second_ref, first_ref)):
        rows = slice(which * size, (which + 1) * size)
        square = None
        for ref in refs:
            for j in range(zcount):
                v = ref[j, rows].astype(F32)
                s = jnp.sum(v * v, axis=0, keepdims=True)
                square = s if square is None else square + s
        mean = jnp.sum(square, keepdims=True) / (out_ref.shape[0] * out_ref.shape[1])
        scale = lax.rsqrt(mean + 1e-06)
        for index, ref in enumerate(refs):
            block = (p ^ (index // 2)) * 2 + ((t % 2) ^ (index % 2))
            for j in range(zcount):
                at = pl.multiple_of((block * zcount + j) * size, 8)
                out_ref[pl.ds(at, size)] = ref[j, rows].astype(F32) * scale
    extra = extra_ref[...]
    bias_mean = jnp.mean(extra * extra, keepdims=True)
    bias_ref[...] = extra * lax.rsqrt(bias_mean + 1e-06)


def call(kernel, out_shapes, scratch=(), smem_first=False):
    def run(*args):
        vmem = pl.BlockSpec(memory_space=pltpu.VMEM)
        smem = pl.BlockSpec(memory_space=pltpu.SMEM)
        specs = [smem if smem_first and i == 0 else vmem for i in range(len(args))]
        return pl.pallas_call(
            kernel,
            out_shape=[jax.ShapeDtypeStruct(s, dt) for s, dt in out_shapes],
            in_specs=specs,
            out_specs=[vmem] * len(out_shapes),
            scratch_shapes=[pltpu.VMEM(s, dt) for s, dt in scratch],
            compiler_params=pltpu.CompilerParams(vmem_limit_bytes=56 << 20),
        )(*args)

    return run


def exchange(tiles, messages):
    strips, pair, ring = messages
    other = [(i, (i + 1) % tiles if i % 2 else (i - 1) % tiles) for i in range(tiles)]
    return [
        lax.all_to_all(strips, "tile", 0, 0),
        lax.ppermute(pair, "tile", [(i, i ^ 1) for i in range(tiles)]),
        lax.ppermute(ring, "tile", other),
    ]


def swap_dp(v):
    count = lax.axis_size("dp")
    return lax.ppermute(v, "dp", [(i, count - 1 - i) for i in range(count)])


def on_device(initial_state, state_cotangents, w_first, bias, w_second, edge_partner):
    tiles = lax.axis_size("tile")
    _, _, rows, face, channels = initial_state.shape
    dm = Dims(rows, face, tiles, channels)
    planes = (6 * rows, face, channels)
    x = initial_state.reshape(planes)
    d = state_cotangents[state_cotangents.shape[0] - 1].reshape(planes)
    w1 = w_first.reshape(9, channels, channels)
    w2 = w_second.reshape(9, channels, channels)
    msg_shapes = [(shape, BF) for shape in dm.messages()]
    flat = (dm.N, channels)
    messages = call(functools.partial(pack_kernel, dm), msg_shapes, smem_first=True)(
        edge_partner, x.reshape(flat), d.reshape(flat)
    )
    messages = exchange(tiles, messages)
    half = 9 * channels
    shift_rows = (3, (rows + 2) * dm.ROW, channels)
    frame = (rows + 2, 6, face + 16, channels)
    outs = call(
        functools.partial(first_kernel, dm),
        [((half + EXTRA, channels), BF), ((half + EXTRA, channels), F32)] + [(planes, BF)] * 2 + msg_shapes,
        [
            ((dm.NT, channels), BF),
            (frame, F32),
            (shift_rows, BF),
            (shift_rows, BF),
            ((9, dm.S, channels), F32),
            (flat, F32),
            (flat, F32),
            ((dm.S, channels), F32),
        ],
        smem_first=True,
    )(edge_partner, x, d, w1, bias.reshape(1, channels), w2, *messages)
    send, keep, hidden, inner = outs[:4]

    zcount = tiles // 2
    n = half // 2
    m = n // zcount
    groups = [[h + 2 * z for z in range(zcount)] for h in range(2)]

    def along_y(v):
        return lax.ppermute(v, "tile", [(i, i ^ 1) for i in range(tiles)])

    def along_z(v):
        return lax.all_to_all(v, "tile", 0, 0, axis_index_groups=groups)

    keep, send = call(half_kernel, [((n + EXTRA, channels), F32), ((n + EXTRA, channels), BF)])(
        keep, swap_dp(send)
    )
    recv = along_y(send)
    messages = exchange(tiles, outs[4:])
    recv, messages = lax.optimization_barrier((recv, messages))
    keep, sends = call(
        functools.partial(block_kernel, zcount),
        [((m + EXTRA, channels), F32), ((zcount, m + EXTRA, channels), BF)],
    )(keep, recv)
    blocks, extra = call(
        functools.partial(last_kernel, zcount), [((zcount, m, channels), BF), ((1, channels), F32)]
    )(keep, along_z(sends))
    own = along_z(blocks)
    other = along_y(own)
    messages, _ = lax.optimization_barrier((messages, own))
    state, grad = call(
        functools.partial(second_kernel, dm),
        [(planes, BF), (planes, F32)],
        [
            ((dm.NT, channels), BF),
            (frame, F32),
            (shift_rows, BF),
            ((9, dm.S, channels), F32),
            (flat, F32),
        ],
        smem_first=True,
    )(edge_partner, x, d, hidden, inner, w1, w2, *messages)
    second_step, first_step, bias_step = call(
        functools.partial(normal_kernel, zcount),
        [((half, channels), F32)] * 2 + [((1, channels), F32)],
    )(own, other, swap_dp(own), swap_dp(other), extra)
    return (
        state.reshape(initial_state.shape),
        grad.reshape(initial_state.shape),
        first_step.reshape(w_first.shape),
        bias_step.reshape(channels),
        second_step.reshape(w_second.shape),
    )


def solution(mesh):
    return jax.shard_map(
        on_device,
        mesh=mesh,
        in_specs=(
            P(("groups", "dp"), None, "tile", None, None),
            P(None, ("groups", "dp"), None, "tile", None, None),
            P(),
            P(),
            P(),
            P(),
        ),
        out_specs=(
            P(("groups", "dp"), None, "tile", None, None),
            P(("groups", "dp"), None, "tile", None, None),
            P("groups", None, None, None),
            P("groups"),
            P("groups", None, None, None),
        ),
        check_vma=False,
    )
```

```python
import functools

import jax
import jax.numpy as jnp
from jax import lax
from jax.experimental import pallas as pl
from jax.experimental.pallas import tpu as pltpu
from jax.sharding import PartitionSpec as P

BF = jnp.bfloat16
F32 = jnp.float32
EXTRA = 16


class Dims:
    def __init__(self, rows, face, tiles, channels):
        self.R, self.F, self.T, self.C = rows, face, tiles, channels
        self.N = 6 * rows * face
        self.ROW = 6 * face
        self.SLOT = -(-(2 * rows + 2) // 8) * 8
        self.BASE = 6 * self.SLOT
        self.o_msg = self.N
        self.o_row = self.o_msg + tiles * self.BASE
        self.NT = self.o_row + 2 * self.ROW
        self.WE = 12 * 8
        self.S = self.WE + self.ROW

    def messages(self):
        return [(self.T, 2, self.BASE, self.C), (2, self.ROW, self.C), (2, self.ROW, self.C)]


def col_iota(n):
    return lax.broadcasted_iota(jnp.int32, (n, 1), 0)


def one_hot(target, width):
    lanes = lax.broadcasted_iota(jnp.int32, (target.shape[0], width), 1)
    return jnp.where(lanes == target, 1.0, 0.0).astype(BF)


def strip_targets(dm, ep, t, d):
    R, F, T = dm.R, dm.F, dm.T
    at_edge = (t == 0) | (t == T - 1)
    to_edge = (d == 0) | (d == T - 1)
    own_edge = jnp.where(t == 0, 0, 2)
    far_edge = jnp.where(d == 0, 0, 2)
    side_row = jnp.where(d == T - 2 - t, R - 1, 0)
    i = col_iota(dm.SLOT)
    q = R * d - 1 + i
    inside = (q >= 0) & (q < F) & (i < R + 2)
    i2 = i - (R + 2)
    parts = []
    for f in range(6):
        far_low = (ep[f, own_edge] % 4) < 2
        reverse = far_low == (t == 0)
        p0 = jnp.where(reverse, F - 1, 0)
        sgn = jnp.where(reverse, -1, 1)
        row = jnp.where(t == 0, 0, R - 1)
        strip = jnp.where(inside, (f * R + row) * F + p0 + sgn * q, -1)
        sides = (f * R + side_row) * F
        low = jnp.where(at_edge, strip, sides + i * (F - 1))
        low = jnp.where(at_edge | (i < 2), low, -1)
        gvalue = ep[f, far_edge]
        column = jnp.where(gvalue % 4 == 1, F - 1, 0) + (gvalue // 4) * (R * F)
        high = jnp.where(to_edge, column + F * i2, jnp.where(i2 < 2, sides + i2 * (F - 1), -1))
        strips = jnp.where(i2 < 0, low, jnp.where(i2 < R, high, -1))
        parts.append(jnp.where(d == T - 1 - t, mirror_slot(dm, f), strips))
    return parts


def mirror_slot(dm, f):
    i = col_iota(dm.SLOT)
    return jnp.where(i < 2 * dm.R, (f * dm.R + i // 2) * dm.F + (i % 2) * (dm.F - 1), -1)


def row_targets(dm, row):
    j = col_iota(dm.F)
    return [(f * dm.R + row) * dm.F + j for f in range(6)]


def write_messages(dm, ep, t, sources, refs):
    R, T = dm.R, dm.T
    strips_ref, pair_ref, ring_ref = refs

    def pick(parts, which):
        hot = one_hot(jnp.concatenate(parts, axis=0), dm.N)
        return jnp.dot(hot, sources[which], preferred_element_type=F32).astype(BF)

    for which in range(2):
        for d in range(T):
            strips_ref[d, which] = pick(strip_targets(dm, ep, t, d), which)
        pair_ref[which] = pick(row_targets(dm, jnp.where(t % 2 == 0, R - 1, 0)), which)
        ring_ref[which] = pick(row_targets(dm, jnp.where(t % 2 == 1, R - 1, 0)), which)


def pack_kernel(dm, ep, x_ref, up_ref, *refs):
    write_messages(dm, ep, lax.axis_index("tile"), (x_ref[...], up_ref[...]), refs)


def ghost_targets(dm, ep, t):
    R, F, T = dm.R, dm.F, dm.T
    odd = t % 2
    parts = []
    m = col_iota(8)
    q = R * t - 1 + m
    inside = (q >= 0) & (q < F) & (m < R + 2)
    row_prev = dm.o_row + (1 - odd) * dm.ROW
    row_next = dm.o_row + odd * dm.ROW
    side_first = dm.o_msg + (T - t) * dm.BASE + jnp.where(t == 1, R + 2, 0)
    side_last = dm.o_msg + (T - 2 - t) * dm.BASE + jnp.where(t == T - 2, R + 2, 0)
    mirror = dm.o_msg + (T - 1 - t) * dm.BASE
    for f in range(6):
        for edge in (3, 1):
            value = ep[f, edge]
            f2, e2 = value // 4, value % 4
            far_low = e2 < 2
            reverse = far_low if edge < 2 else e2 >= 2
            is_col = (e2 % 2) == 1
            side = jnp.where(e2 == 1, 1, 0)
            column = side * (F - 1)
            slot = f2 * dm.SLOT + side
            row = dm.o_msg + jnp.where(e2 == 0, 0, T - 1) * dm.BASE + f2 * dm.SLOT
            facing = jnp.where(e2 == 0, t == T - 1, t == 0)
            whole = dm.o_row + dm.ROW + f2 * F + jnp.where(reverse, F - R * t, R * t - 1)
            row = jnp.where(facing, whole, row)
            along = jnp.where(facing & reverse, -1, 1)
            i0 = jnp.where(is_col, jnp.where(reverse, side_first + slot, row_prev + f2 * F + column), row)
            i4 = jnp.where(
                is_col, jnp.where(reverse, side_last + slot, row_next + f2 * F + column), row + along * (R + 1)
            )
            base = jnp.where(
                is_col, jnp.where(reverse, mirror + 2 * R + slot, (f2 * R - 1) * F + column), row
            )
            step = jnp.where(is_col, jnp.where(reverse, -2, F), along)
            target = jnp.where(m == 0, i0, jnp.where(m == R + 1, i4, base + step * m))
            parts.append(jnp.where(inside, target, -1))
    j = col_iota(F)
    jt = jnp.zeros_like(j)
    for b in range(1, T):
        jt = jt + jnp.where(j >= b * R, 1, 0)
    jr = j - R * jt
    wrap = dm.o_row + dm.ROW
    for edge in (0, 2):
        at_edge = (t == 0) if edge == 0 else (t == T - 1)
        inner_base = row_prev if edge == 0 else row_next
        own_row = 0 if edge == 0 else R - 1
        for f in range(6):
            value = ep[f, edge]
            f2, e2 = value // 4, value % 4
            far_low = e2 < 2
            reverse = far_low if edge < 2 else e2 >= 2
            is_col = (e2 % 2) == 1
            same = e2 == edge
            row_base = jnp.where(same, (f2 * R + own_row) * F, wrap + f2 * F)
            lin_base = row_base + jnp.where(reverse, F - 1, 0)
            lin_step = jnp.where(reverse, -1, 1)
            k0 = jnp.where(reverse, T - 1, 0)
            ks = jnp.where(reverse, -1, 1)
            col_base = dm.o_msg + k0 * dm.BASE + f * dm.SLOT + R + 2 + jnp.where(reverse, R - 1, 0)
            base = jnp.where(is_col, col_base, lin_base)
            sj = jnp.where(is_col, 0, lin_step)
            st = jnp.where(is_col, ks * dm.BASE, 0)
            sr = jnp.where(is_col, jnp.where(reverse, -1, 1), 0)
            base = jnp.where(at_edge, base, inner_base + f * F)
            sj = jnp.where(at_edge, sj, 1)
            st = jnp.where(at_edge, st, 0)
            sr = jnp.where(at_edge, sr, 0)
            target = base + sj * j + st * jt + sr * jr
            far_tile = T - 1 if edge == 0 else 0
            from_mirror = is_col & at_edge & (jnp.where(reverse, T - 1 - jt, jt) == far_tile)
            side = jnp.where(e2 == 1, 1, 0)
            cells = mirror + f2 * dm.SLOT + side + 2 * jnp.where(reverse, R - 1 - jr, jr)
            parts.append(jnp.where(from_mirror, cells, target))
    return jnp.concatenate(parts, axis=0)


def gather_ghosts(dm, ep, t, own, messages, table_ref):
    hot = one_hot(ghost_targets(dm, ep, t), dm.NT)
    out = []
    for which in range(2):
        table_ref[0 : dm.N] = own[which]
        for k in range(dm.T):
            at = dm.o_msg + k * dm.BASE
            table_ref[at : at + dm.BASE] = messages[0][k, which]
        table_ref[dm.o_row : dm.o_row + dm.ROW] = messages[1][which]
        table_ref[dm.o_row + dm.ROW :] = messages[2][which]
        out.append(jnp.dot(hot, table_ref[...], preferred_element_type=F32))
    return out


def build_taps(dm, field_ref, ghosts, top, bottom, frame_ref, taps_ref, adjoint):
    R, F, C = dm.R, dm.F, dm.C
    for f in range(6):
        for r in range(R):
            frame_ref[r + 1, f, 8 : 8 + F] = field_ref[f * R + r].astype(F32)
    frame_ref[0, :, 8 : 8 + F] = top.reshape(6, F, C)
    frame_ref[R + 1, :, 8 : 8 + F] = bottom.reshape(6, F, C)
    for m in range(R + 2):
        for f in range(6):
            if ghosts is None:
                west = jnp.zeros((1, C), F32)
                east = west
            else:
                west = ghosts[16 * f + m : 16 * f + m + 1]
                east = ghosts[16 * f + 8 + m : 16 * f + 8 + m + 1]
            frame_ref[m, f, 7:8] = west
            frame_ref[m, f, 8 + F : 9 + F] = east
    for m in range(R + 2):
        for b in range(3):
            plane = frame_ref[m, :, 7 + b : 7 + b + F].reshape(dm.ROW, C).astype(BF)
            for a in range(3):
                r = m - 2 + a if adjoint else m - a
                tap = 3 * a + (2 - b if adjoint else b)
                if 0 <= r < R:
                    taps_ref[r * dm.ROW : (r + 1) * dm.ROW, tap * C : (tap + 1) * C] = plane


def build_strip_terms(dm, ep, t, ghosts, top, bottom, z_ref):
    R, F = dm.R, dm.F
    z_ref[...] = jnp.zeros(z_ref.shape, F32)

    def tap_of(f, edge, shift):
        e2 = ep[f, edge] % 4
        reverse = e2 < 2 if edge < 2 else e2 >= 2
        along = 1 - jnp.where(reverse, -shift, shift)
        return jnp.where(
            e2 == 0, along, jnp.where(e2 == 2, 6 + along, jnp.where(e2 == 1, 3 * along + 2, 3 * along))
        )

    live = lax.rem(lax.broadcasted_iota(jnp.int32, (dm.WE, 1), 0), 8) < R
    for shift in (-1, 0, 1):
        moved = pltpu.roll(ghosts, (dm.WE - 1 - shift) % dm.WE, 0) if shift > -1 else ghosts
        moved = jnp.where(live, moved, 0.0)
        for f in range(6):
            for side, edge in ((0, 3), (1, 1)):
                at = 16 * f + 8 * side
                z_ref[tap_of(f, edge, shift), at : at + 8] = moved[at : at + 8]

    def add_rows(edge, rows):
        j = lax.rem(lax.broadcasted_iota(jnp.int32, (dm.ROW, 1), 0), F)
        for shift in (-1, 0, 1):
            if shift == 0:
                moved = rows
            else:
                moved = pltpu.roll(rows, (-shift) % dm.ROW, 0)
                moved = jnp.where((j + shift >= 0) & (j + shift < F), moved, 0.0)
            for f in range(6):
                at = dm.WE + F * f
                z_ref[tap_of(f, edge, shift), at : at + F] = moved[F * f : F * (f + 1)]

    @pl.when(t == 0)
    def _():
        add_rows(0, top)

    @pl.when(t == dm.T - 1)
    def _():
        add_rows(2, bottom)


def adjoint(dm, t, taps_ref, z_ref, wt_ref, acc_ref):
    R, F, C, N = dm.R, dm.F, dm.C, dm.N
    for tap in range(9):
        taps_ref[N:, tap * C : (tap + 1) * C] = z_ref[tap].astype(BF)
    total = jnp.dot(taps_ref[...], wt_ref[...], preferred_element_type=F32)
    acc_ref[...] = total[:N]
    strips = total[N:]
    for f in range(6):
        for side in range(2):
            for r in range(R):
                at = (r * 6 + f) * F + side * (F - 1)
                row = 16 * f + 8 * side + r
                acc_ref[at : at + 1] += strips[row : row + 1]

    @pl.when(t == 0)
    def _():
        acc_ref[0 : dm.ROW] += strips[dm.WE :]

    @pl.when(t == dm.T - 1)
    def _():
        acc_ref[(R - 1) * dm.ROW : R * dm.ROW] += strips[dm.WE :]


def turn_kernel(w1_ref, w2_ref, w1t_ref, w2t_ref):
    for w_ref, wt_ref in ((w1_ref, w1t_ref), (w2_ref, w2t_ref)):
        for tap in range(9):
            wt_ref[tap] = w_ref[tap].T


def put_tap(dm, send_ref, keep_ref, p, which, tap, value):
    size = 9 * dm.C // (2 * dm.T)
    start, stop = tap * dm.C, (tap + 1) * dm.C
    for block in range(2 * dm.T):
        low, high = max(start, block * size), min(stop, (block + 1) * size)
        if low >= high:
            continue
        at = (block % dm.T) * 2 * size + which * size + low - block * size
        piece = value[low - start : high - start]

        @pl.when(p == block // dm.T)
        def _():
            keep_ref[at : at + high - low] = piece

        @pl.when(p != block // dm.T)
        def _():
            send_ref[at : at + high - low] = piece.astype(BF)


def put_extra(send_ref, keep_ref, row):
    c = row.shape[1]
    n = send_ref.shape[0] - EXTRA
    i = lax.broadcasted_iota(jnp.int32, (EXTRA, c), 0)
    high = row.astype(BF)
    low = (row - high.astype(F32)).astype(BF).astype(F32)
    keep_ref[n:] = jnp.where(i == 0, row, 0.0)
    send_ref[n:] = jnp.where(i == 0, high.astype(F32), jnp.where(i == 1, low, 0.0)).astype(BF)


def first_kernel(dm, ep, x_ref, up_ref, w1_ref, bias_ref, w2t_ref, *refs):
    T, R, F, N, C = dm.T, dm.R, dm.F, dm.N, dm.C
    messages = refs[:3]
    send_ref, keep_ref, hid_ref, inner_ref = refs[3:7]
    out_messages = refs[7:10]
    table_ref, frame_ref, xs_ref, us_ref, z_ref, before_ref, acc_ref, hcat_ref = refs[10:]
    t, p = lax.axis_index("tile"), lax.axis_index("dp")
    own = (x_ref[...].reshape(N, C), up_ref[...].reshape(N, C))
    gx, gu = gather_ghosts(dm, ep, t, own, messages, table_ref)
    top, bottom = dm.WE, dm.WE + dm.ROW
    build_taps(dm, x_ref, gx[:top], gx[top:bottom], gx[bottom:], frame_ref, xs_ref, False)
    before = jnp.dot(xs_ref[...], w1_ref[...], preferred_element_type=F32) + bias_ref[...]
    before_ref[...] = before
    sig = 1.0 / (1.0 + jnp.exp(-before))
    acc_ref[...] = before * sig
    up_top = jnp.where(t == 0, 0.0, gu[top:bottom])
    up_bottom = jnp.where(t == T - 1, 0.0, gu[bottom:])
    build_taps(dm, up_ref, None, up_top, up_bottom, frame_ref, us_ref, True)
    build_strip_terms(dm, ep, t, gu[:top], gu[top:bottom], gu[bottom:], z_ref)
    hcat_ref[0:N] = acc_ref[...]
    hcat_ref[N:] = jnp.zeros((dm.S, C), F32)
    for f in range(6):
        for side in range(2):
            for r in range(R):
                at = (r * 6 + f) * F + side * (F - 1)
                row = N + 16 * f + 8 * side + r
                hcat_ref[row : row + 1] = acc_ref[at : at + 1]
    first_row = acc_ref[0 : dm.ROW]
    last_row = acc_ref[(R - 1) * dm.ROW : R * dm.ROW]
    hcat_ref[N + dm.WE :] = jnp.where(t == 0, first_row, last_row)
    for r in range(R):
        for f in range(6):
            at = (r * 6 + f) * F
            hid_ref[f * R + r] = acc_ref[at : at + F].astype(BF)
    adjoint(dm, t, us_ref, z_ref, w2t_ref, acc_ref)
    hidden_t = hcat_ref[...].astype(BF).T
    for tap in range(9):
        grad = jnp.dot(hidden_t, us_ref[:, tap * C : (tap + 1) * C], preferred_element_type=F32)
        put_tap(dm, send_ref, keep_ref, p, 0, tap, grad)
    before = before_ref[...]
    sig = 1.0 / (1.0 + jnp.exp(-before))
    before_grad = acc_ref[...] * (sig * (1.0 + before * (1.0 - sig)))
    acc_ref[...] = before_grad
    inner = before_grad.astype(BF)
    for tap in range(9):
        grad = lax.dot_general(
            xs_ref[:, tap * C : (tap + 1) * C],
            inner,
            (((0,), (0,)), ((), ())),
            preferred_element_type=F32,
        )
        put_tap(dm, send_ref, keep_ref, p, 1, tap, grad)
    put_extra(send_ref, keep_ref, jnp.sum(before_grad, axis=0, keepdims=True))
    for r in range(R):
        for f in range(6):
            at = (r * 6 + f) * F
            inner_ref[f * R + r] = acc_ref[at : at + F].astype(BF)
    write_messages(
        dm, ep, t, (hid_ref[...].reshape(N, C), inner_ref[...].reshape(N, C)), out_messages
    )


def second_kernel(dm, ep, x_ref, d_ref, hid_ref, inner_ref, w1t_ref, w2_ref, *refs):
    T, R, F, N, C = dm.T, dm.R, dm.F, dm.N, dm.C
    messages = refs[:3]
    state_ref, grad_ref = refs[3:5]
    table_ref, frame_ref, hs_ref, is_ref, z_ref, acc_ref = refs[5:]
    t = lax.axis_index("tile")
    own = (hid_ref[...].reshape(N, C), inner_ref[...].reshape(N, C))
    gh, gi = gather_ghosts(dm, ep, t, own, messages, table_ref)
    top, bottom = dm.WE, dm.WE + dm.ROW
    build_taps(dm, hid_ref, gh[:top], gh[top:bottom], gh[bottom:], frame_ref, hs_ref, False)
    acc_ref[...] = jnp.dot(hs_ref[...], w2_ref[...], preferred_element_type=F32)
    for r in range(R):
        for f in range(6):
            at = (r * 6 + f) * F
            value = x_ref[f * R + r].astype(F32) + acc_ref[at : at + F]
            state_ref[f * R + r] = value.astype(BF)
    in_top = jnp.where(t == 0, 0.0, gi[top:bottom])
    in_bottom = jnp.where(t == T - 1, 0.0, gi[bottom:])
    build_taps(dm, inner_ref, None, in_top, in_bottom, frame_ref, is_ref, True)
    build_strip_terms(dm, ep, t, gi[:top], gi[top:bottom], gi[bottom:], z_ref)
    adjoint(dm, t, is_ref, z_ref, w1t_ref, acc_ref)
    for r in range(R):
        for f in range(6):
            at = (r * 6 + f) * F
            grad_ref[f * R + r] = d_ref[f * R + r].astype(F32) + acc_ref[at : at + F]


def extra_sum(keep, recv, n):
    return keep[n : n + 1] + recv[n : n + 1].astype(F32) + recv[n + 1 : n + 2].astype(F32)


def extra_rows(extra):
    i = lax.broadcasted_iota(jnp.int32, (EXTRA, extra.shape[1]), 0)
    high = extra.astype(BF).astype(F32)
    tail = jnp.where(i == 0, high, jnp.where(i == 1, extra - high, 0.0)).astype(BF)
    return jnp.where(i == 0, extra, 0.0), tail


def half_kernel(keep_ref, recv_ref, out_keep, out_send):
    n = keep_ref.shape[0] - EXTRA
    size = n // 2
    own = lax.axis_index("tile") % 2
    mine = pl.multiple_of(own * size, 8)
    far = pl.multiple_of((1 - own) * size, 8)
    out_keep[0:size] = keep_ref[pl.ds(mine, size)] + recv_ref[pl.ds(mine, size)].astype(F32)
    out_send[0:size] = (keep_ref[pl.ds(far, size)] + recv_ref[pl.ds(far, size)].astype(F32)).astype(BF)
    keep, tail = extra_rows(extra_sum(keep_ref, recv_ref, n))
    out_keep[size:] = keep
    out_send[size:] = tail


def block_kernel(zcount, keep_ref, recv_ref, out_keep, out_sends):
    n = keep_ref.shape[0] - EXTRA
    size = n // zcount
    own = lax.axis_index("tile") // 2
    keep, tail = extra_rows(extra_sum(keep_ref, recv_ref, n))
    for j in range(zcount):
        at = slice(j * size, (j + 1) * size)
        total = keep_ref[at] + recv_ref[at].astype(F32)
        out_sends[j, 0:size] = total.astype(BF)
        out_sends[j, size:] = tail

        @pl.when(own == j)
        def _():
            out_keep[0:size] = total

    out_keep[size:] = keep


def last_kernel(zcount, keep_ref, recv_ref, block_ref, extra_ref):
    n = keep_ref.shape[0] - EXTRA
    own = lax.axis_index("tile") // 2
    total = keep_ref[0:n]
    extra = keep_ref[n : n + 1]
    for j in range(zcount):
        far = own != j
        total = total + jnp.where(far, recv_ref[j, 0:n].astype(F32), 0.0)
        parts = recv_ref[j, n : n + 2].astype(F32)
        extra = extra + jnp.where(far, parts[0:1] + parts[1:2], 0.0)
    for j in range(zcount):
        block_ref[j] = total.astype(BF)
    extra_ref[...] = extra


def normal_kernel(zcount, a_ref, b_ref, c_ref, d_ref, extra_ref, second_ref, first_ref, bias_ref):
    t, p = lax.axis_index("tile"), lax.axis_index("dp")
    refs = (a_ref, b_ref, c_ref, d_ref)
    size = a_ref.shape[1] // 2
    for which, out_ref in enumerate((second_ref, first_ref)):
        rows = slice(which * size, (which + 1) * size)
        square = None
        for ref in refs:
            for j in range(zcount):
                v = ref[j, rows].astype(F32)
                s = jnp.sum(v * v, axis=0, keepdims=True)
                square = s if square is None else square + s
        mean = jnp.sum(square, keepdims=True) / (out_ref.shape[0] * out_ref.shape[1])
        scale = lax.rsqrt(mean + 1e-06)
        for index, ref in enumerate(refs):
            block = (p ^ (index // 2)) * 2 + ((t % 2) ^ (index % 2))
            for j in range(zcount):
                at = pl.multiple_of((block * zcount + j) * size, 8)
                out_ref[pl.ds(at, size)] = ref[j, rows].astype(F32) * scale
    extra = extra_ref[...]
    bias_mean = jnp.mean(extra * extra, keepdims=True)
    bias_ref[...] = extra * lax.rsqrt(bias_mean + 1e-06)


def call(kernel, out_shapes, scratch=(), smem_first=False):
    def run(*args):
        vmem = pl.BlockSpec(memory_space=pltpu.VMEM)
        smem = pl.BlockSpec(memory_space=pltpu.SMEM)
        specs = [smem if smem_first and i == 0 else vmem for i in range(len(args))]
        return pl.pallas_call(
            kernel,
            out_shape=[jax.ShapeDtypeStruct(s, dt) for s, dt in out_shapes],
            in_specs=specs,
            out_specs=[vmem] * len(out_shapes),
            scratch_shapes=[pltpu.VMEM(s, dt) for s, dt in scratch],
            compiler_params=pltpu.CompilerParams(vmem_limit_bytes=56 << 20),
        )(*args)

    return run


def exchange(tiles, messages):
    strips, pair, ring = messages
    other = [(i, (i + 1) % tiles if i % 2 else (i - 1) % tiles) for i in range(tiles)]
    return [
        lax.all_to_all(strips, "tile", 0, 0),
        lax.ppermute(pair, "tile", [(i, i ^ 1) for i in range(tiles)]),
        lax.ppermute(ring, "tile", other),
    ]


def swap_dp(v):
    count = lax.axis_size("dp")
    return lax.ppermute(v, "dp", [(i, count - 1 - i) for i in range(count)])


def on_device(initial_state, state_cotangents, w_first, bias, w_second, edge_partner):
    tiles = lax.axis_size("tile")
    _, _, rows, face, channels = initial_state.shape
    dm = Dims(rows, face, tiles, channels)
    planes = (6 * rows, face, channels)
    x = initial_state.reshape(planes)
    d = state_cotangents[state_cotangents.shape[0] - 1].reshape(planes)
    taps = (9, channels, channels)
    w1 = w_first.reshape(9 * channels, channels)
    w2 = w_second.reshape(9 * channels, channels)
    w1t, w2t = call(turn_kernel, [(taps, BF)] * 2)(w_first.reshape(taps), w_second.reshape(taps))
    w1t = w1t.reshape(w1.shape)
    w2t = w2t.reshape(w2.shape)
    msg_shapes = [(shape, BF) for shape in dm.messages()]
    flat = (dm.N, channels)
    messages = call(functools.partial(pack_kernel, dm), msg_shapes, smem_first=True)(
        edge_partner, x.reshape(flat), d.reshape(flat)
    )
    messages = exchange(tiles, messages)
    half = 9 * channels
    wide = 9 * channels
    frame = (rows + 2, 6, face + 16, channels)
    outs = call(
        functools.partial(first_kernel, dm),
        [((half + EXTRA, channels), BF), ((half + EXTRA, channels), F32)] + [(planes, BF)] * 2 + msg_shapes,
        [
            ((dm.NT, channels), BF),
            (frame, F32),
            ((dm.N, wide), BF),
            ((dm.N + dm.S, wide), BF),
            ((9, dm.S, channels), F32),
            (flat, F32),
            (flat, F32),
            ((dm.N + dm.S, channels), F32),
        ],
        smem_first=True,
    )(edge_partner, x, d, w1, bias.reshape(1, channels), w2t, *messages)
    send, keep, hidden, inner = outs[:4]

    zcount = tiles // 2
    n = half // 2
    m = n // zcount
    groups = [[h + 2 * z for z in range(zcount)] for h in range(2)]

    def along_y(v):
        return lax.ppermute(v, "tile", [(i, i ^ 1) for i in range(tiles)])

    def along_z(v):
        return lax.all_to_all(v, "tile", 0, 0, axis_index_groups=groups)

    keep, send = call(half_kernel, [((n + EXTRA, channels), F32), ((n + EXTRA, channels), BF)])(
        keep, swap_dp(send)
    )
    recv = along_y(send)
    messages = exchange(tiles, outs[4:])
    recv, messages = lax.optimization_barrier((recv, messages))
    keep, sends = call(
        functools.partial(block_kernel, zcount),
        [((m + EXTRA, channels), F32), ((zcount, m + EXTRA, channels), BF)],
    )(keep, recv)
    blocks, extra = call(
        functools.partial(last_kernel, zcount), [((zcount, m, channels), BF), ((1, channels), F32)]
    )(keep, along_z(sends))
    own = along_z(blocks)
    other = along_y(own)
    messages, _ = lax.optimization_barrier((messages, own))
    state, grad = call(
        functools.partial(second_kernel, dm),
        [(planes, BF), (planes, F32)],
        [
            ((dm.NT, channels), BF),
            (frame, F32),
            ((dm.N, wide), BF),
            ((dm.N + dm.S, wide), BF),
            ((9, dm.S, channels), F32),
            (flat, F32),
        ],
        smem_first=True,
    )(edge_partner, x, d, hidden, inner, w1t, w2, *messages)
    other, state, grad = lax.optimization_barrier((other, state, grad))
    second_step, first_step, bias_step = call(
        functools.partial(normal_kernel, zcount),
        [((half, channels), F32)] * 2 + [((1, channels), F32)],
    )(own, other, swap_dp(own), swap_dp(other), extra)
    return (
        state.reshape(initial_state.shape),
        grad.reshape(initial_state.shape),
        first_step.reshape(w_first.shape),
        bias_step.reshape(channels),
        second_step.reshape(w_second.shape),
    )


def solution(mesh):
    return jax.shard_map(
        on_device,
        mesh=mesh,
        in_specs=(
            P(("groups", "dp"), None, "tile", None, None),
            P(None, ("groups", "dp"), None, "tile", None, None),
            P(),
            P(),
            P(),
            P(),
        ),
        out_specs=(
            P(("groups", "dp"), None, "tile", None, None),
            P(("groups", "dp"), None, "tile", None, None),
            P("groups", None, None, None),
            P("groups"),
            P("groups", None, None, None),
        ),
        check_vma=False,
    )
```

```python
import functools

import jax
import jax.numpy as jnp
from jax import lax
from jax.experimental import pallas as pl
from jax.experimental.pallas import tpu as pltpu
from jax.sharding import PartitionSpec as P

BF = jnp.bfloat16
F32 = jnp.float32
EXTRA = 16
LIMIT = 40


class Dims:
    def __init__(self, rows, face, tiles, channels):
        self.R, self.F, self.T, self.C = rows, face, tiles, channels
        self.N = 6 * rows * face
        self.ROW = 6 * face
        self.SLOT = -(-(2 * rows + 2) // 8) * 8
        self.BASE = 6 * self.SLOT
        self.o_msg = self.N
        self.o_row = self.o_msg + tiles * self.BASE
        self.NT = self.o_row + 2 * self.ROW
        self.WE = 12 * 8
        self.S = self.WE + self.ROW

    def messages(self):
        return [(self.T, 2, self.BASE, self.C), (2, self.ROW, self.C), (2, self.ROW, self.C)]


def col_iota(n):
    return lax.broadcasted_iota(jnp.int32, (n, 1), 0)


def one_hot(target, width):
    lanes = lax.broadcasted_iota(jnp.int32, (target.shape[0], width), 1)
    return jnp.where(lanes == target, 1.0, 0.0).astype(BF)


def strip_targets(dm, ep, t, d):
    R, F, T = dm.R, dm.F, dm.T
    at_edge = (t == 0) | (t == T - 1)
    to_edge = (d == 0) | (d == T - 1)
    own_edge = jnp.where(t == 0, 0, 2)
    far_edge = jnp.where(d == 0, 0, 2)
    side_row = jnp.where(d == T - 2 - t, R - 1, 0)
    i = col_iota(dm.SLOT)
    q = R * d - 1 + i
    inside = (q >= 0) & (q < F) & (i < R + 2)
    i2 = i - (R + 2)
    parts = []
    for f in range(6):
        far_low = (ep[f, own_edge] % 4) < 2
        reverse = far_low == (t == 0)
        p0 = jnp.where(reverse, F - 1, 0)
        sgn = jnp.where(reverse, -1, 1)
        row = jnp.where(t == 0, 0, R - 1)
        strip = jnp.where(inside, (f * R + row) * F + p0 + sgn * q, -1)
        sides = (f * R + side_row) * F
        low = jnp.where(at_edge, strip, sides + i * (F - 1))
        low = jnp.where(at_edge | (i < 2), low, -1)
        gvalue = ep[f, far_edge]
        column = jnp.where(gvalue % 4 == 1, F - 1, 0) + (gvalue // 4) * (R * F)
        high = jnp.where(to_edge, column + F * i2, jnp.where(i2 < 2, sides + i2 * (F - 1), -1))
        strips = jnp.where(i2 < 0, low, jnp.where(i2 < R, high, -1))
        parts.append(jnp.where(d == T - 1 - t, mirror_slot(dm, f), strips))
    return parts


def mirror_slot(dm, f):
    i = col_iota(dm.SLOT)
    return jnp.where(i < 2 * dm.R, (f * dm.R + i // 2) * dm.F + (i % 2) * (dm.F - 1), -1)


def row_targets(dm, row):
    j = col_iota(dm.F)
    return [(f * dm.R + row) * dm.F + j for f in range(6)]


def write_messages(dm, ep, t, sources, refs):
    R, T = dm.R, dm.T
    strips_ref, pair_ref, ring_ref = refs

    def pick(parts, which):
        hot = one_hot(jnp.concatenate(parts, axis=0), dm.N)
        return jnp.dot(hot, sources[which], preferred_element_type=F32).astype(BF)

    for which in range(2):
        for d in range(T):
            strips_ref[d, which] = pick(strip_targets(dm, ep, t, d), which)
        pair_ref[which] = pick(row_targets(dm, jnp.where(t % 2 == 0, R - 1, 0)), which)
        ring_ref[which] = pick(row_targets(dm, jnp.where(t % 2 == 1, R - 1, 0)), which)


def pack_kernel(dm, ep, x_ref, up_ref, *refs):
    write_messages(dm, ep, lax.axis_index("tile"), (x_ref[...], up_ref[...]), refs)


def ghost_targets(dm, ep, t):
    R, F, T = dm.R, dm.F, dm.T
    odd = t % 2
    parts = []
    m = col_iota(8)
    q = R * t - 1 + m
    inside = (q >= 0) & (q < F) & (m < R + 2)
    row_prev = dm.o_row + (1 - odd) * dm.ROW
    row_next = dm.o_row + odd * dm.ROW
    side_first = dm.o_msg + (T - t) * dm.BASE + jnp.where(t == 1, R + 2, 0)
    side_last = dm.o_msg + (T - 2 - t) * dm.BASE + jnp.where(t == T - 2, R + 2, 0)
    mirror = dm.o_msg + (T - 1 - t) * dm.BASE
    for f in range(6):
        for edge in (3, 1):
            value = ep[f, edge]
            f2, e2 = value // 4, value % 4
            far_low = e2 < 2
            reverse = far_low if edge < 2 else e2 >= 2
            is_col = (e2 % 2) == 1
            side = jnp.where(e2 == 1, 1, 0)
            column = side * (F - 1)
            slot = f2 * dm.SLOT + side
            row = dm.o_msg + jnp.where(e2 == 0, 0, T - 1) * dm.BASE + f2 * dm.SLOT
            facing = jnp.where(e2 == 0, t == T - 1, t == 0)
            whole = dm.o_row + dm.ROW + f2 * F + jnp.where(reverse, F - R * t, R * t - 1)
            row = jnp.where(facing, whole, row)
            along = jnp.where(facing & reverse, -1, 1)
            i0 = jnp.where(is_col, jnp.where(reverse, side_first + slot, row_prev + f2 * F + column), row)
            i4 = jnp.where(
                is_col, jnp.where(reverse, side_last + slot, row_next + f2 * F + column), row + along * (R + 1)
            )
            base = jnp.where(
                is_col, jnp.where(reverse, mirror + 2 * R + slot, (f2 * R - 1) * F + column), row
            )
            step = jnp.where(is_col, jnp.where(reverse, -2, F), along)
            target = jnp.where(m == 0, i0, jnp.where(m == R + 1, i4, base + step * m))
            parts.append(jnp.where(inside, target, -1))
    j = col_iota(F)
    jt = jnp.zeros_like(j)
    for b in range(1, T):
        jt = jt + jnp.where(j >= b * R, 1, 0)
    jr = j - R * jt
    wrap = dm.o_row + dm.ROW
    for edge in (0, 2):
        at_edge = (t == 0) if edge == 0 else (t == T - 1)
        inner_base = row_prev if edge == 0 else row_next
        own_row = 0 if edge == 0 else R - 1
        for f in range(6):
            value = ep[f, edge]
            f2, e2 = value // 4, value % 4
            far_low = e2 < 2
            reverse = far_low if edge < 2 else e2 >= 2
            is_col = (e2 % 2) == 1
            same = e2 == edge
            row_base = jnp.where(same, (f2 * R + own_row) * F, wrap + f2 * F)
            lin_base = row_base + jnp.where(reverse, F - 1, 0)
            lin_step = jnp.where(reverse, -1, 1)
            k0 = jnp.where(reverse, T - 1, 0)
            ks = jnp.where(reverse, -1, 1)
            col_base = dm.o_msg + k0 * dm.BASE + f * dm.SLOT + R + 2 + jnp.where(reverse, R - 1, 0)
            base = jnp.where(is_col, col_base, lin_base)
            sj = jnp.where(is_col, 0, lin_step)
            st = jnp.where(is_col, ks * dm.BASE, 0)
            sr = jnp.where(is_col, jnp.where(reverse, -1, 1), 0)
            base = jnp.where(at_edge, base, inner_base + f * F)
            sj = jnp.where(at_edge, sj, 1)
            st = jnp.where(at_edge, st, 0)
            sr = jnp.where(at_edge, sr, 0)
            target = base + sj * j + st * jt + sr * jr
            far_tile = T - 1 if edge == 0 else 0
            from_mirror = is_col & at_edge & (jnp.where(reverse, T - 1 - jt, jt) == far_tile)
            side = jnp.where(e2 == 1, 1, 0)
            cells = mirror + f2 * dm.SLOT + side + 2 * jnp.where(reverse, R - 1 - jr, jr)
            parts.append(jnp.where(from_mirror, cells, target))
    return jnp.concatenate(parts, axis=0)


def gather_ghosts(dm, ep, t, own, messages, table_ref):
    hot = one_hot(ghost_targets(dm, ep, t), dm.NT)
    out = []
    for which in range(2):
        table_ref[0 : dm.N] = own[which]
        for k in range(dm.T):
            at = dm.o_msg + k * dm.BASE
            table_ref[at : at + dm.BASE] = messages[0][k, which]
        table_ref[dm.o_row : dm.o_row + dm.ROW] = messages[1][which]
        table_ref[dm.o_row + dm.ROW :] = messages[2][which]
        out.append(jnp.dot(hot, table_ref[...], preferred_element_type=F32))
    return out


def own_first(value, p):
    half = value.shape[1] // 2
    low, high = value[:, :half], value[:, half:]
    return jnp.concatenate([jnp.where(p == 0, low, high), jnp.where(p == 0, high, low)], axis=1)


def build_taps(dm, field_ref, ghosts, top, bottom, frame_ref, taps_ref, adjoint, p=None):
    R, F, C = dm.R, dm.F, dm.C
    for f in range(6):
        for r in range(R):
            frame_ref[r + 1, f, 8 : 8 + F] = field_ref[f * R + r].astype(F32)
    frame_ref[0, :, 8 : 8 + F] = top.reshape(6, F, C)
    frame_ref[R + 1, :, 8 : 8 + F] = bottom.reshape(6, F, C)
    for m in range(R + 2):
        for f in range(6):
            if ghosts is None:
                west = jnp.zeros((1, C), F32)
                east = west
            else:
                west = ghosts[16 * f + m : 16 * f + m + 1]
                east = ghosts[16 * f + 8 + m : 16 * f + 8 + m + 1]
            frame_ref[m, f, 7:8] = west
            frame_ref[m, f, 8 + F : 9 + F] = east
    for m in range(R + 2):
        for b in range(3):
            plane = frame_ref[m, :, 7 + b : 7 + b + F].reshape(dm.ROW, C)
            if p is not None:
                plane = own_first(plane, p)
            plane = plane.astype(BF)
            for a in range(3):
                r = m - 2 + a if adjoint else m - a
                tap = 3 * a + (2 - b if adjoint else b)
                if 0 <= r < R:
                    taps_ref[r * dm.ROW : (r + 1) * dm.ROW, tap * C : (tap + 1) * C] = plane


def build_strip_terms(dm, ep, t, ghosts, top, bottom, z_ref):
    R, F = dm.R, dm.F
    z_ref[...] = jnp.zeros(z_ref.shape, F32)

    def tap_of(f, edge, shift):
        e2 = ep[f, edge] % 4
        reverse = e2 < 2 if edge < 2 else e2 >= 2
        along = 1 - jnp.where(reverse, -shift, shift)
        return jnp.where(
            e2 == 0, along, jnp.where(e2 == 2, 6 + along, jnp.where(e2 == 1, 3 * along + 2, 3 * along))
        )

    live = lax.rem(lax.broadcasted_iota(jnp.int32, (dm.WE, 1), 0), 8) < R
    for shift in (-1, 0, 1):
        moved = pltpu.roll(ghosts, (dm.WE - 1 - shift) % dm.WE, 0) if shift > -1 else ghosts
        moved = jnp.where(live, moved, 0.0)
        for f in range(6):
            for side, edge in ((0, 3), (1, 1)):
                at = 16 * f + 8 * side
                z_ref[tap_of(f, edge, shift), at : at + 8] = moved[at : at + 8]

    def add_rows(edge, rows):
        j = lax.rem(lax.broadcasted_iota(jnp.int32, (dm.ROW, 1), 0), F)
        for shift in (-1, 0, 1):
            if shift == 0:
                moved = rows
            else:
                moved = pltpu.roll(rows, (-shift) % dm.ROW, 0)
                moved = jnp.where((j + shift >= 0) & (j + shift < F), moved, 0.0)
            for f in range(6):
                at = dm.WE + F * f
                z_ref[tap_of(f, edge, shift), at : at + F] = moved[F * f : F * (f + 1)]

    @pl.when(t == 0)
    def _():
        add_rows(0, top)

    @pl.when(t == dm.T - 1)
    def _():
        add_rows(2, bottom)


def adjoint(dm, t, taps_ref, z_ref, wt_ref, acc_ref):
    R, F, C, N = dm.R, dm.F, dm.C, dm.N
    for tap in range(9):
        taps_ref[N:, tap * C : (tap + 1) * C] = z_ref[tap].astype(BF)
    total = jnp.dot(taps_ref[...], wt_ref[...], preferred_element_type=F32)
    acc_ref[...] = total[:N]
    strips = total[N:]
    for f in range(6):
        for side in range(2):
            for r in range(R):
                at = (r * 6 + f) * F + side * (F - 1)
                row = 16 * f + 8 * side + r
                acc_ref[at : at + 1] += strips[row : row + 1]

    @pl.when(t == 0)
    def _():
        acc_ref[0 : dm.ROW] += strips[dm.WE :]

    @pl.when(t == dm.T - 1)
    def _():
        acc_ref[(R - 1) * dm.ROW : R * dm.ROW] += strips[dm.WE :]


def turn_kernel(w1_ref, w2_ref, w1s_ref, w1t_ref, w2t_ref):
    p = lax.axis_index("dp")
    half = w1_ref.shape[1] // 2
    for tap in range(9):
        w1t_ref[tap] = w1_ref[tap].T
        w2t_ref[tap] = w2_ref[tap].T
        w1s_ref[tap, :half] = w1_ref[tap, pl.ds(pl.multiple_of(p * half, half), half)]
        w1s_ref[tap, half:] = w1_ref[tap, pl.ds(pl.multiple_of((1 - p) * half, half), half)]


def put_taps(send_ref, keep_ref, which, taps, value):
    half = value.shape[0] // (2 * len(taps))
    for i, tap in enumerate(taps):
        keep_ref[which, tap] = value[2 * i * half : (2 * i + 1) * half]
        send_ref[which, tap] = value[(2 * i + 1) * half : (2 * i + 2) * half].astype(BF)


def high_low(row):
    i = lax.broadcasted_iota(jnp.int32, (EXTRA, row.shape[1]), 0)
    high = row.astype(BF).astype(F32)
    return jnp.where(i == 0, high, jnp.where(i == 1, row - high, 0.0)).astype(BF)


def first_kernel(dm, ep, x_ref, up_ref, w1_ref, bias_ref, w2t_ref, *refs):
    T, R, F, N, C = dm.T, dm.R, dm.F, dm.N, dm.C
    messages = refs[:3]
    send_ref, send_bias_ref, keep_ref, bias_sum_ref, hid_ref, inner_ref = refs[3:9]
    out_messages = refs[9:12]
    table_ref, frame_ref, xs_ref, us_ref, z_ref, before_ref, acc_ref, hcat_ref = refs[12:]
    t, p = lax.axis_index("tile"), lax.axis_index("dp")
    own = (x_ref[...].reshape(N, C), up_ref[...].reshape(N, C))
    gx, gu = gather_ghosts(dm, ep, t, own, messages, table_ref)
    top, bottom = dm.WE, dm.WE + dm.ROW
    build_taps(dm, x_ref, gx[:top], gx[top:bottom], gx[bottom:], frame_ref, xs_ref, False, p)
    before = jnp.dot(xs_ref[...], w1_ref[...], preferred_element_type=F32) + bias_ref[...]
    before_ref[...] = before
    sig = 1.0 / (1.0 + jnp.exp(-before))
    acc_ref[...] = before * sig
    up_top = jnp.where(t == 0, 0.0, gu[top:bottom])
    up_bottom = jnp.where(t == T - 1, 0.0, gu[bottom:])
    build_taps(dm, up_ref, None, up_top, up_bottom, frame_ref, us_ref, True)
    build_strip_terms(dm, ep, t, gu[:top], gu[top:bottom], gu[bottom:], z_ref)
    hcat_ref[0:N] = acc_ref[...]
    hcat_ref[N:] = jnp.zeros((dm.S, C), F32)
    for f in range(6):
        for side in range(2):
            for r in range(R):
                at = (r * 6 + f) * F + side * (F - 1)
                row = N + 16 * f + 8 * side + r
                hcat_ref[row : row + 1] = acc_ref[at : at + 1]
    first_row = acc_ref[0 : dm.ROW]
    last_row = acc_ref[(R - 1) * dm.ROW : R * dm.ROW]
    hcat_ref[N + dm.WE :] = jnp.where(t == 0, first_row, last_row)
    for r in range(R):
        for f in range(6):
            at = (r * 6 + f) * F
            hid_ref[f * R + r] = acc_ref[at : at + F].astype(BF)
    adjoint(dm, t, us_ref, z_ref, w2t_ref, acc_ref)
    hidden_t = own_first(hcat_ref[...], p).astype(BF).T
    for tap in range(9):
        grad = jnp.dot(hidden_t, us_ref[:, tap * C : (tap + 1) * C], preferred_element_type=F32)
        put_taps(send_ref, keep_ref, 0, [tap], grad)
    before = before_ref[...]
    sig = 1.0 / (1.0 + jnp.exp(-before))
    before_grad = acc_ref[...] * (sig * (1.0 + before * (1.0 - sig)))
    acc_ref[...] = before_grad
    inner = before_grad.astype(BF)
    for taps in ((0, 1, 2), (3, 4, 5), (6, 7, 8)):
        grad = lax.dot_general(
            xs_ref[:, taps[0] * C : (taps[-1] + 1) * C],
            inner,
            (((0,), (0,)), ((), ())),
            preferred_element_type=F32,
        )
        put_taps(send_ref, keep_ref, 1, taps, grad)
    bias_sum = jnp.sum(before_grad, axis=0, keepdims=True)
    bias_sum_ref[...] = bias_sum
    send_bias_ref[...] = high_low(bias_sum)
    for r in range(R):
        for f in range(6):
            at = (r * 6 + f) * F
            inner_ref[f * R + r] = acc_ref[at : at + F].astype(BF)
    write_messages(
        dm, ep, t, (hid_ref[...].reshape(N, C), inner_ref[...].reshape(N, C)), out_messages
    )


def second_kernel(dm, ep, x_ref, d_ref, hid_ref, inner_ref, w1t_ref, w2_ref, *refs):
    T, R, F, N, C = dm.T, dm.R, dm.F, dm.N, dm.C
    messages = refs[:3]
    state_ref, grad_ref = refs[3:5]
    table_ref, frame_ref, hs_ref, is_ref, z_ref, acc_ref = refs[5:]
    t = lax.axis_index("tile")
    own = (hid_ref[...].reshape(N, C), inner_ref[...].reshape(N, C))
    gh, gi = gather_ghosts(dm, ep, t, own, messages, table_ref)
    top, bottom = dm.WE, dm.WE + dm.ROW
    build_taps(dm, hid_ref, gh[:top], gh[top:bottom], gh[bottom:], frame_ref, hs_ref, False)
    acc_ref[...] = jnp.dot(hs_ref[...], w2_ref[...], preferred_element_type=F32)
    for r in range(R):
        for f in range(6):
            at = (r * 6 + f) * F
            value = x_ref[f * R + r].astype(F32) + acc_ref[at : at + F]
            state_ref[f * R + r] = value.astype(BF)
    in_top = jnp.where(t == 0, 0.0, gi[top:bottom])
    in_bottom = jnp.where(t == T - 1, 0.0, gi[bottom:])
    build_taps(dm, inner_ref, None, in_top, in_bottom, frame_ref, is_ref, True)
    build_strip_terms(dm, ep, t, gi[:top], gi[top:bottom], gi[bottom:], z_ref)
    adjoint(dm, t, is_ref, z_ref, w1t_ref, acc_ref)
    for r in range(R):
        for f in range(6):
            at = (r * 6 + f) * F
            grad_ref[f * R + r] = d_ref[f * R + r].astype(F32) + acc_ref[at : at + F]


def both(pair):
    return pair[0:1].astype(F32) + pair[1:2].astype(F32)


def half_kernel(keep_ref, bias_ref, recv_ref, recv_bias_ref, out_keep, out_bias, out_send, out_send_bias):
    size = keep_ref.shape[2] // 2
    own = lax.axis_index("tile") % 2
    mine = pl.ds(pl.multiple_of(own * size, size), size)
    far = pl.ds(pl.multiple_of((1 - own) * size, size), size)
    for which in range(2):
        for tap in range(9):
            out_keep[which, tap] = keep_ref[which, tap, mine] + recv_ref[which, tap, mine].astype(F32)
            out = keep_ref[which, tap, far] + recv_ref[which, tap, far].astype(F32)
            out_send[which, tap] = out.astype(BF)
    bias = bias_ref[...] + both(recv_bias_ref)
    out_bias[...] = bias
    out_send_bias[...] = high_low(bias)


def block_kernel(zcount, keep_ref, bias_ref, recv_ref, recv_bias_ref, out_keep, out_bias, out_sends):
    size = keep_ref.shape[2] // zcount
    own = lax.axis_index("tile") // 2
    bias = bias_ref[...] + both(recv_bias_ref)
    out_bias[...] = bias
    tail = high_low(bias)
    for j in range(zcount):
        rows = slice(j * size, (j + 1) * size)
        for which in range(2):
            for tap in range(9):
                total = keep_ref[which, tap, rows] + recv_ref[which, tap, rows].astype(F32)
                at = (9 * which + tap) * size
                out_sends[j, at : at + size] = total.astype(BF)
        out_sends[j, 18 * size :] = tail
    mine = pl.ds(pl.multiple_of(own * size, size), size)
    for which in range(2):
        for tap in range(9):
            at = (9 * which + tap) * size
            out_keep[at : at + size] = keep_ref[which, tap, mine] + recv_ref[which, tap, mine].astype(F32)


def last_kernel(zcount, keep_ref, bias_ref, recv_ref, block_ref, bias_sum_ref):
    n = keep_ref.shape[0]
    own = lax.axis_index("tile") // 2
    total = keep_ref[...]
    bias = bias_ref[...]
    for j in range(zcount):
        far = own != j
        total = total + jnp.where(far, recv_ref[j, 0:n].astype(F32), 0.0)
        bias = bias + jnp.where(far, both(recv_ref[j, n : n + 2]), 0.0)
    for j in range(zcount):
        block_ref[j] = total.astype(BF)
    bias_sum_ref[...] = bias


def normal_kernel(zcount, a_ref, b_ref, c_ref, d_ref, bias_sum_ref, second_ref, first_ref, bias_ref):
    t, p = lax.axis_index("tile"), lax.axis_index("dp")
    refs = (a_ref, b_ref, c_ref, d_ref)
    size = a_ref.shape[1] // 18
    for which, out_ref in enumerate((second_ref, first_ref)):
        rows = slice(which * 9 * size, (which + 1) * 9 * size)
        square = None
        for ref in refs:
            for j in range(zcount):
                v = ref[j, rows].astype(F32)
                s = jnp.sum(v * v, axis=0, keepdims=True)
                square = s if square is None else square + s
        mean = jnp.sum(square, keepdims=True) / (9 * out_ref.shape[1] * out_ref.shape[2])
        scale = lax.rsqrt(mean + 1e-06)
        for index, ref in enumerate(refs):
            block = (p ^ (index // 2)) * 2 + ((t % 2) ^ (index % 2))
            for j in range(zcount):
                at = pl.ds(pl.multiple_of((block * zcount + j) * size, size), size)
                for tap in range(9):
                    row = (9 * which + tap) * size
                    out_ref[tap, at] = ref[j, row : row + size].astype(F32) * scale
    total = bias_sum_ref[...]
    bias_mean = jnp.mean(total * total, keepdims=True)
    bias_ref[...] = total * lax.rsqrt(bias_mean + 1e-06)


def call(kernel, out_shapes, scratch=(), smem_first=False, limit=16):
    def run(*args):
        vmem = pl.BlockSpec(memory_space=pltpu.VMEM)
        smem = pl.BlockSpec(memory_space=pltpu.SMEM)
        specs = [smem if smem_first and i == 0 else vmem for i in range(len(args))]
        return pl.pallas_call(
            kernel,
            out_shape=[jax.ShapeDtypeStruct(s, dt) for s, dt in out_shapes],
            in_specs=specs,
            out_specs=[vmem] * len(out_shapes),
            scratch_shapes=[pltpu.VMEM(s, dt) for s, dt in scratch],
            compiler_params=pltpu.CompilerParams(vmem_limit_bytes=limit << 20),
        )(*args)

    return run


def exchange(tiles, messages):
    strips, pair, ring = messages
    other = [(i, (i + 1) % tiles if i % 2 else (i - 1) % tiles) for i in range(tiles)]
    return [
        lax.all_to_all(strips, "tile", 0, 0),
        lax.ppermute(pair, "tile", [(i, i ^ 1) for i in range(tiles)]),
        lax.ppermute(ring, "tile", other),
    ]


def swap_dp(v):
    count = lax.axis_size("dp")
    return lax.ppermute(v, "dp", [(i, count - 1 - i) for i in range(count)])


def on_device(initial_state, state_cotangents, w_first, bias, w_second, edge_partner):
    tiles = lax.axis_size("tile")
    _, _, rows, face, channels = initial_state.shape
    dm = Dims(rows, face, tiles, channels)
    planes = (6 * rows, face, channels)
    x = initial_state.reshape(planes)
    d = state_cotangents[state_cotangents.shape[0] - 1].reshape(planes)
    taps = (9, channels, channels)
    w1 = w_first.reshape(9 * channels, channels)
    w2 = w_second.reshape(9 * channels, channels)
    w1s, w1t, w2t = call(turn_kernel, [(taps, BF)] * 3)(w_first.reshape(taps), w_second.reshape(taps))
    w1s = w1s.reshape(w1.shape)
    w1t = w1t.reshape(w1.shape)
    w2t = w2t.reshape(w2.shape)
    msg_shapes = [(shape, BF) for shape in dm.messages()]
    flat = (dm.N, channels)
    messages = call(functools.partial(pack_kernel, dm), msg_shapes, smem_first=True)(
        edge_partner, x.reshape(flat), d.reshape(flat)
    )
    messages = exchange(tiles, messages)
    half = channels // 2
    wide = 9 * channels
    frame = (rows + 2, 6, face + 16, channels)
    outs = call(
        functools.partial(first_kernel, dm),
        [
            ((2, 9, half, channels), BF),
            ((EXTRA, channels), BF),
            ((2, 9, half, channels), F32),
            ((1, channels), F32),
            (planes, BF),
            (planes, BF),
        ]
        + msg_shapes,
        [
            ((dm.NT, channels), BF),
            (frame, F32),
            ((dm.N, wide), BF),
            ((dm.N + dm.S, wide), BF),
            ((9, dm.S, channels), F32),
            (flat, F32),
            (flat, F32),
            ((dm.N + dm.S, channels), F32),
        ],
        smem_first=True,
        limit=LIMIT,
    )(edge_partner, x, d, w1s, bias.reshape(1, channels), w2t, *messages)
    send, send_bias, keep, bias_sum, hidden, inner = outs[:6]

    zcount = tiles // 2
    n = half // 2
    m = n // zcount
    groups = [[h + 2 * z for z in range(zcount)] for h in range(2)]

    def along_y(v):
        return lax.ppermute(v, "tile", [(i, i ^ 1) for i in range(tiles)])

    def along_z(v):
        return lax.all_to_all(v, "tile", 0, 0, axis_index_groups=groups)

    keep, bias_sum, send, send_bias = call(
        half_kernel,
        [
            ((2, 9, n, channels), F32),
            ((1, channels), F32),
            ((2, 9, n, channels), BF),
            ((EXTRA, channels), BF),
        ],
    )(keep, bias_sum, swap_dp(send), swap_dp(send_bias))
    recv, recv_bias = along_y(send), along_y(send_bias)
    messages = exchange(tiles, outs[6:])
    recv, messages = lax.optimization_barrier((recv, messages))
    keep, bias_sum, sends = call(
        functools.partial(block_kernel, zcount),
        [((18 * m, channels), F32), ((1, channels), F32), ((zcount, 18 * m + EXTRA, channels), BF)],
    )(keep, bias_sum, recv, recv_bias)
    blocks, bias_sum = call(
        functools.partial(last_kernel, zcount), [((zcount, 18 * m, channels), BF), ((1, channels), F32)]
    )(keep, bias_sum, along_z(sends))
    own = along_z(blocks)
    other = along_y(own)
    messages, _ = lax.optimization_barrier((messages, own))
    state, grad = call(
        functools.partial(second_kernel, dm),
        [(planes, BF), (planes, F32)],
        [
            ((dm.NT, channels), BF),
            (frame, F32),
            ((dm.N, wide), BF),
            ((dm.N + dm.S, wide), BF),
            ((9, dm.S, channels), F32),
            (flat, F32),
        ],
        smem_first=True,
        limit=LIMIT,
    )(edge_partner, x, d, hidden, inner, w1t, w2, *messages)
    other, state, grad = lax.optimization_barrier((other, state, grad))
    second_step, first_step, bias_step = call(
        functools.partial(normal_kernel, zcount),
        [(taps, F32)] * 2 + [((1, channels), F32)],
        limit=24,
    )(own, other, swap_dp(own), swap_dp(other), bias_sum)
    return (
        state.reshape(initial_state.shape),
        grad.reshape(initial_state.shape),
        first_step.reshape(w_first.shape),
        bias_step.reshape(channels),
        second_step.reshape(w_second.shape),
    )


def solution(mesh):
    return jax.shard_map(
        on_device,
        mesh=mesh,
        in_specs=(
            P(("groups", "dp"), None, "tile", None, None),
            P(None, ("groups", "dp"), None, "tile", None, None),
            P(),
            P(),
            P(),
            P(),
        ),
        out_specs=(
            P(("groups", "dp"), None, "tile", None, None),
            P(("groups", "dp"), None, "tile", None, None),
            P("groups", None, None, None),
            P("groups"),
            P("groups", None, None, None),
        ),
        check_vma=False,
    )
```

```python
import functools

import jax
import jax.numpy as jnp
from jax import lax
from jax.experimental import pallas as pl
from jax.experimental.pallas import tpu as pltpu
from jax.sharding import PartitionSpec as P

BF = jnp.bfloat16
F32 = jnp.float32
LIMIT = 40


class Dims:
    def __init__(self, rows, face, tiles, channels):
        self.R, self.F, self.T, self.C = rows, face, tiles, channels
        self.N = 6 * rows * face
        self.ROW = 6 * face
        self.SLOT = -(-(2 * rows + 2) // 8) * 8
        self.BASE = 6 * self.SLOT
        self.o_msg = self.N
        self.o_row = self.o_msg + tiles * self.BASE
        self.NT = self.o_row + 2 * self.ROW
        self.WE = 12 * 8
        self.S = self.WE + self.ROW

    def messages(self):
        rows = [self.BASE] * self.T + [self.ROW]
        rows[1] += self.ROW
        return [(2, n, self.C) for n in rows]

    def pairs(self):
        T = self.T

        def needed(i, d):
            return i in (0, T - 1) or d in (0, T - 1) or d in (T - 2 - i, T - i)

        out = [[(i, i ^ k) for i in range(T) if k in (1, T - 1) or needed(i, i ^ k)] for k in range(T)]
        out.append([(i, (i + 1) % T if i % 2 else (i - 1) % T) for i in range(T)])
        return out


def col_iota(n):
    return lax.broadcasted_iota(jnp.int32, (n, 1), 0)


def one_hot(target, width):
    lanes = lax.broadcasted_iota(jnp.int32, (target.shape[0], width), 1)
    return jnp.where(lanes == target, 1.0, 0.0).astype(BF)


def strip_targets(dm, ep, t, d):
    R, F, T = dm.R, dm.F, dm.T
    at_edge = (t == 0) | (t == T - 1)
    to_edge = (d == 0) | (d == T - 1)
    own_edge = jnp.where(t == 0, 0, 2)
    far_edge = jnp.where(d == 0, 0, 2)
    side_row = jnp.where(d == T - 2 - t, R - 1, 0)
    i = col_iota(dm.SLOT)
    q = R * d - 1 + i
    inside = (q >= 0) & (q < F) & (i < R + 2)
    i2 = i - (R + 2)
    parts = []
    for f in range(6):
        far_low = (ep[f, own_edge] % 4) < 2
        reverse = far_low == (t == 0)
        p0 = jnp.where(reverse, F - 1, 0)
        sgn = jnp.where(reverse, -1, 1)
        row = jnp.where(t == 0, 0, R - 1)
        strip = jnp.where(inside, (f * R + row) * F + p0 + sgn * q, -1)
        sides = (f * R + side_row) * F
        low = jnp.where(at_edge, strip, sides + i * (F - 1))
        low = jnp.where(at_edge | (i < 2), low, -1)
        gvalue = ep[f, far_edge]
        column = jnp.where(gvalue % 4 == 1, F - 1, 0) + (gvalue // 4) * (R * F)
        high = jnp.where(to_edge, column + F * i2, jnp.where(i2 < 2, sides + i2 * (F - 1), -1))
        strips = jnp.where(i2 < 0, low, jnp.where(i2 < R, high, -1))
        parts.append(jnp.where(d == T - 1 - t, mirror_slot(dm, f), strips))
    return parts


def mirror_slot(dm, f):
    i = col_iota(dm.SLOT)
    return jnp.where(i < 2 * dm.R, (f * dm.R + i // 2) * dm.F + (i % 2) * (dm.F - 1), -1)


def row_targets(dm, row):
    j = col_iota(dm.F)
    return [(f * dm.R + row) * dm.F + j for f in range(6)]


def write_messages(dm, ep, t, sources, refs):
    R = dm.R
    for k in range(dm.T + 1):
        parts = strip_targets(dm, ep, t, t ^ k) if k < dm.T else []
        if k == 1:
            parts = parts + row_targets(dm, jnp.where(t % 2 == 0, R - 1, 0))
        if k == dm.T:
            parts = row_targets(dm, jnp.where(t % 2 == 1, R - 1, 0))
        hot = one_hot(jnp.concatenate(parts, axis=0), dm.N)
        for which in range(2):
            refs[k][which] = jnp.dot(hot, sources[which], preferred_element_type=F32).astype(BF)


def pack_kernel(dm, ep, x_ref, up_ref, *refs):
    write_messages(dm, ep, lax.axis_index("tile"), (x_ref[...], up_ref[...]), refs)


def ghost_targets(dm, ep, t):
    R, F, T = dm.R, dm.F, dm.T
    odd = t % 2
    parts = []
    m = col_iota(8)
    q = R * t - 1 + m
    inside = (q >= 0) & (q < F) & (m < R + 2)
    row_prev = dm.o_row + (1 - odd) * dm.ROW
    row_next = dm.o_row + odd * dm.ROW
    side_first = dm.o_msg + (t ^ (T - t)) * dm.BASE + jnp.where(t == 1, R + 2, 0)
    side_last = dm.o_msg + (t ^ (T - 2 - t)) * dm.BASE + jnp.where(t == T - 2, R + 2, 0)
    mirror = dm.o_msg + (T - 1) * dm.BASE
    for f in range(6):
        for edge in (3, 1):
            value = ep[f, edge]
            f2, e2 = value // 4, value % 4
            far_low = e2 < 2
            reverse = far_low if edge < 2 else e2 >= 2
            is_col = (e2 % 2) == 1
            side = jnp.where(e2 == 1, 1, 0)
            column = side * (F - 1)
            slot = f2 * dm.SLOT + side
            row = dm.o_msg + (t ^ jnp.where(e2 == 0, 0, T - 1)) * dm.BASE + f2 * dm.SLOT
            facing = jnp.where(e2 == 0, t == T - 1, t == 0)
            whole = dm.o_row + dm.ROW + f2 * F + jnp.where(reverse, F - R * t, R * t - 1)
            row = jnp.where(facing, whole, row)
            along = jnp.where(facing & reverse, -1, 1)
            i0 = jnp.where(is_col, jnp.where(reverse, side_first + slot, row_prev + f2 * F + column), row)
            i4 = jnp.where(
                is_col, jnp.where(reverse, side_last + slot, row_next + f2 * F + column), row + along * (R + 1)
            )
            base = jnp.where(
                is_col, jnp.where(reverse, mirror + 2 * R + slot, (f2 * R - 1) * F + column), row
            )
            step = jnp.where(is_col, jnp.where(reverse, -2, F), along)
            target = jnp.where(m == 0, i0, jnp.where(m == R + 1, i4, base + step * m))
            parts.append(jnp.where(inside, target, -1))
    j = col_iota(F)
    jt = jnp.zeros_like(j)
    for b in range(1, T):
        jt = jt + jnp.where(j >= b * R, 1, 0)
    jr = j - R * jt
    wrap = dm.o_row + dm.ROW
    for edge in (0, 2):
        at_edge = (t == 0) if edge == 0 else (t == T - 1)
        inner_base = row_prev if edge == 0 else row_next
        own_row = 0 if edge == 0 else R - 1
        for f in range(6):
            value = ep[f, edge]
            f2, e2 = value // 4, value % 4
            far_low = e2 < 2
            reverse = far_low if edge < 2 else e2 >= 2
            is_col = (e2 % 2) == 1
            same = e2 == edge
            row_base = jnp.where(same, (f2 * R + own_row) * F, wrap + f2 * F)
            lin_base = row_base + jnp.where(reverse, F - 1, 0)
            lin_step = jnp.where(reverse, -1, 1)
            k0 = jnp.where(reverse, T - 1, 0)
            ks = jnp.where(reverse, -1, 1)
            if edge == 2:
                k0 = T - 1 - k0
                ks = -ks
            col_base = dm.o_msg + k0 * dm.BASE + f * dm.SLOT + R + 2 + jnp.where(reverse, R - 1, 0)
            base = jnp.where(is_col, col_base, lin_base)
            sj = jnp.where(is_col, 0, lin_step)
            st = jnp.where(is_col, ks * dm.BASE, 0)
            sr = jnp.where(is_col, jnp.where(reverse, -1, 1), 0)
            base = jnp.where(at_edge, base, inner_base + f * F)
            sj = jnp.where(at_edge, sj, 1)
            st = jnp.where(at_edge, st, 0)
            sr = jnp.where(at_edge, sr, 0)
            target = base + sj * j + st * jt + sr * jr
            far_tile = T - 1 if edge == 0 else 0
            from_mirror = is_col & at_edge & (jnp.where(reverse, T - 1 - jt, jt) == far_tile)
            side = jnp.where(e2 == 1, 1, 0)
            cells = mirror + f2 * dm.SLOT + side + 2 * jnp.where(reverse, R - 1 - jr, jr)
            parts.append(jnp.where(from_mirror, cells, target))
    return jnp.concatenate(parts, axis=0)


def gather_ghosts(dm, ep, t, own, messages, table_ref):
    hot = one_hot(ghost_targets(dm, ep, t), dm.NT)
    out = []
    for which in range(2):
        table_ref[0 : dm.N] = own[which]
        for k in range(dm.T):
            at = dm.o_msg + k * dm.BASE
            table_ref[at : at + dm.BASE] = messages[k][which, : dm.BASE]
        table_ref[dm.o_row : dm.o_row + dm.ROW] = messages[1][which, dm.BASE :]
        table_ref[dm.o_row + dm.ROW :] = messages[dm.T][which]
        out.append(jnp.dot(hot, table_ref[...], preferred_element_type=F32))
    return out


def own_first(value, p):
    half = value.shape[1] // 2
    low, high = value[:, :half], value[:, half:]
    return jnp.concatenate([jnp.where(p == 0, low, high), jnp.where(p == 0, high, low)], axis=1)


def build_taps(dm, field_ref, ghosts, top, bottom, frame_ref, taps_ref, adjoint, p=None):
    R, F, C = dm.R, dm.F, dm.C
    for f in range(6):
        for r in range(R):
            frame_ref[r + 1, f, 8 : 8 + F] = field_ref[f * R + r].astype(F32)
    frame_ref[0, :, 8 : 8 + F] = top.reshape(6, F, C)
    frame_ref[R + 1, :, 8 : 8 + F] = bottom.reshape(6, F, C)
    for m in range(R + 2):
        for f in range(6):
            if ghosts is None:
                west = jnp.zeros((1, C), F32)
                east = west
            else:
                west = ghosts[16 * f + m : 16 * f + m + 1]
                east = ghosts[16 * f + 8 + m : 16 * f + 8 + m + 1]
            frame_ref[m, f, 7:8] = west
            frame_ref[m, f, 8 + F : 9 + F] = east
    for m in range(R + 2):
        for b in range(3):
            plane = frame_ref[m, :, 7 + b : 7 + b + F].reshape(dm.ROW, C)
            if p is not None:
                plane = own_first(plane, p)
            plane = plane.astype(BF)
            for a in range(3):
                r = m - 2 + a if adjoint else m - a
                tap = 3 * a + (2 - b if adjoint else b)
                if 0 <= r < R:
                    taps_ref[r * dm.ROW : (r + 1) * dm.ROW, tap * C : (tap + 1) * C] = plane


def build_strip_terms(dm, ep, t, ghosts, top, bottom, z_ref):
    R, F = dm.R, dm.F
    z_ref[...] = jnp.zeros(z_ref.shape, F32)

    def tap_of(f, edge, shift):
        e2 = ep[f, edge] % 4
        reverse = e2 < 2 if edge < 2 else e2 >= 2
        along = 1 - jnp.where(reverse, -shift, shift)
        return jnp.where(
            e2 == 0, along, jnp.where(e2 == 2, 6 + along, jnp.where(e2 == 1, 3 * along + 2, 3 * along))
        )

    live = lax.rem(lax.broadcasted_iota(jnp.int32, (dm.WE, 1), 0), 8) < R
    for shift in (-1, 0, 1):
        moved = pltpu.roll(ghosts, (dm.WE - 1 - shift) % dm.WE, 0) if shift > -1 else ghosts
        moved = jnp.where(live, moved, 0.0)
        for f in range(6):
            for side, edge in ((0, 3), (1, 1)):
                at = 16 * f + 8 * side
                z_ref[tap_of(f, edge, shift), at : at + 8] = moved[at : at + 8]

    def add_rows(edge, rows):
        j = lax.rem(lax.broadcasted_iota(jnp.int32, (dm.ROW, 1), 0), F)
        for shift in (-1, 0, 1):
            if shift == 0:
                moved = rows
            else:
                moved = pltpu.roll(rows, (-shift) % dm.ROW, 0)
                moved = jnp.where((j + shift >= 0) & (j + shift < F), moved, 0.0)
            for f in range(6):
                at = dm.WE + F * f
                z_ref[tap_of(f, edge, shift), at : at + F] = moved[F * f : F * (f + 1)]

    @pl.when(t == 0)
    def _():
        add_rows(0, top)

    @pl.when(t == dm.T - 1)
    def _():
        add_rows(2, bottom)


def adjoint(dm, t, taps_ref, z_ref, wt_ref, acc_ref):
    R, F, C, N = dm.R, dm.F, dm.C, dm.N
    for tap in range(9):
        taps_ref[N:, tap * C : (tap + 1) * C] = z_ref[tap].astype(BF)
    total = jnp.dot(taps_ref[...], wt_ref[...], preferred_element_type=F32)
    acc_ref[...] = total[:N]
    strips = total[N:]
    for f in range(6):
        for side in range(2):
            for r in range(R):
                at = (r * 6 + f) * F + side * (F - 1)
                row = 16 * f + 8 * side + r
                acc_ref[at : at + 1] += strips[row : row + 1]

    @pl.when(t == 0)
    def _():
        acc_ref[0 : dm.ROW] += strips[dm.WE :]

    @pl.when(t == dm.T - 1)
    def _():
        acc_ref[(R - 1) * dm.ROW : R * dm.ROW] += strips[dm.WE :]


def turn_kernel(w1_ref, w2_ref, w1s_ref, w1t_ref, w2t_ref):
    p = lax.axis_index("dp")
    half = w1_ref.shape[1] // 2
    for tap in range(9):
        w1t_ref[tap] = w1_ref[tap].T
        w2t_ref[tap] = w2_ref[tap].T
        w1s_ref[tap, :half] = w1_ref[tap, pl.ds(pl.multiple_of(p * half, half), half)]
        w1s_ref[tap, half:] = w1_ref[tap, pl.ds(pl.multiple_of((1 - p) * half, half), half)]


def put_taps(send_ref, keep_ref, first_tap, value):
    half = keep_ref.shape[1]
    for i in range(value.shape[0] // (2 * half)):
        keep_ref[first_tap + i] = value[2 * i * half : (2 * i + 1) * half]
        send_ref[first_tap + i] = value[(2 * i + 1) * half : (2 * i + 2) * half].astype(BF)


def first_kernel(dm, ep, x_ref, up_ref, w1_ref, bias_ref, w2t_ref, *refs):
    T, R, F, N, C = dm.T, dm.R, dm.F, dm.N, dm.C
    M = T + 1
    messages = refs[:M]
    send1_ref, keep1_ref, send2_ref, keep2_ref, bias_sum_ref, hid_ref, inner_ref = refs[M : M + 7]
    out_messages = refs[M + 7 : 2 * M + 7]
    table_ref, frame_ref, xs_ref, us_ref, z_ref, before_ref, acc_ref, hcat_ref = refs[2 * M + 7 :]
    t, p = lax.axis_index("tile"), lax.axis_index("dp")
    own = (x_ref[...].reshape(N, C), up_ref[...].reshape(N, C))
    gx, gu = gather_ghosts(dm, ep, t, own, messages, table_ref)
    top, bottom = dm.WE, dm.WE + dm.ROW
    build_taps(dm, x_ref, gx[:top], gx[top:bottom], gx[bottom:], frame_ref, xs_ref, False, p)
    before = jnp.dot(xs_ref[...], w1_ref[...], preferred_element_type=F32) + bias_ref[...]
    before_ref[...] = before
    sig = 1.0 / (1.0 + jnp.exp(-before))
    acc_ref[...] = before * sig
    up_top = jnp.where(t == 0, 0.0, gu[top:bottom])
    up_bottom = jnp.where(t == T - 1, 0.0, gu[bottom:])
    build_taps(dm, up_ref, None, up_top, up_bottom, frame_ref, us_ref, True)
    build_strip_terms(dm, ep, t, gu[:top], gu[top:bottom], gu[bottom:], z_ref)
    hcat_ref[0:N] = acc_ref[...]
    hcat_ref[N:] = jnp.zeros((dm.S, C), F32)
    for f in range(6):
        for side in range(2):
            for r in range(R):
                at = (r * 6 + f) * F + side * (F - 1)
                row = N + 16 * f + 8 * side + r
                hcat_ref[row : row + 1] = acc_ref[at : at + 1]
    first_row = acc_ref[0 : dm.ROW]
    last_row = acc_ref[(R - 1) * dm.ROW : R * dm.ROW]
    hcat_ref[N + dm.WE :] = jnp.where(t == 0, first_row, last_row)
    for r in range(R):
        for f in range(6):
            at = (r * 6 + f) * F
            hid_ref[f * R + r] = acc_ref[at : at + F].astype(BF)
    adjoint(dm, t, us_ref, z_ref, w2t_ref, acc_ref)
    hidden_t = own_first(hcat_ref[...], p).astype(BF).T
    for tap in range(9):
        grad = jnp.dot(hidden_t, us_ref[:, tap * C : (tap + 1) * C], preferred_element_type=F32)
        put_taps(send2_ref, keep2_ref, tap, grad)
    before = before_ref[...]
    sig = 1.0 / (1.0 + jnp.exp(-before))
    before_grad = acc_ref[...] * (sig * (1.0 + before * (1.0 - sig)))
    acc_ref[...] = before_grad
    inner = before_grad.astype(BF)
    for tap in (0, 3, 6):
        grad = lax.dot_general(
            xs_ref[:, tap * C : (tap + 3) * C],
            inner,
            (((0,), (0,)), ((), ())),
            preferred_element_type=F32,
        )
        put_taps(send1_ref, keep1_ref, tap, grad)
    bias_sum_ref[...] = jnp.sum(before_grad, axis=0, keepdims=True)
    for r in range(R):
        for f in range(6):
            at = (r * 6 + f) * F
            inner_ref[f * R + r] = acc_ref[at : at + F].astype(BF)
    write_messages(
        dm, ep, t, (hid_ref[...].reshape(N, C), inner_ref[...].reshape(N, C)), out_messages
    )


def second_kernel(dm, ep, x_ref, d_ref, hid_ref, inner_ref, w1t_ref, w2_ref, *refs):
    T, R, F, N, C = dm.T, dm.R, dm.F, dm.N, dm.C
    messages = refs[: T + 1]
    state_ref, grad_ref = refs[T + 1 : T + 3]
    table_ref, frame_ref, hs_ref, is_ref, z_ref, acc_ref = refs[T + 3 :]
    t = lax.axis_index("tile")
    own = (hid_ref[...].reshape(N, C), inner_ref[...].reshape(N, C))
    gh, gi = gather_ghosts(dm, ep, t, own, messages, table_ref)
    top, bottom = dm.WE, dm.WE + dm.ROW
    build_taps(dm, hid_ref, gh[:top], gh[top:bottom], gh[bottom:], frame_ref, hs_ref, False)
    acc_ref[...] = jnp.dot(hs_ref[...], w2_ref[...], preferred_element_type=F32)
    for r in range(R):
        for f in range(6):
            at = (r * 6 + f) * F
            value = x_ref[f * R + r].astype(F32) + acc_ref[at : at + F]
            state_ref[f * R + r] = value.astype(BF)
    in_top = jnp.where(t == 0, 0.0, gi[top:bottom])
    in_bottom = jnp.where(t == T - 1, 0.0, gi[bottom:])
    build_taps(dm, inner_ref, None, in_top, in_bottom, frame_ref, is_ref, True)
    build_strip_terms(dm, ep, t, gi[:top], gi[top:bottom], gi[bottom:], z_ref)
    adjoint(dm, t, is_ref, z_ref, w1t_ref, acc_ref)
    for r in range(R):
        for f in range(6):
            at = (r * 6 + f) * F
            grad_ref[f * R + r] = d_ref[f * R + r].astype(F32) + acc_ref[at : at + F]


def half_kernel(zcount, keep2_ref, keep1_ref, recv2_ref, recv1_ref, out_keep, *out_sends):
    size = keep1_ref.shape[1] // 2
    own = lax.axis_index("tile") % 2
    mine = pl.ds(pl.multiple_of(own * size, size), size)
    far = pl.ds(pl.multiple_of((1 - own) * size, size), size)
    part = size // zcount
    for which, (keep_ref, recv_ref) in enumerate(((keep2_ref, recv2_ref), (keep1_ref, recv1_ref))):
        for tap in range(9):
            kept = keep_ref[tap, mine] + recv_ref[tap, mine].astype(F32)
            sent = keep_ref[tap, far] + recv_ref[tap, far].astype(F32)
            at = (9 * which + tap) * part
            for j in range(zcount):
                out_keep[j, at : at + part] = kept[j * part : (j + 1) * part]
                out_sends[j][at : at + part] = sent[j * part : (j + 1) * part].astype(BF)


def block_kernel(zcount, keep_ref, *refs):
    recvs, (out_keep, *out_sends), sum_ref = refs[:zcount], refs[zcount : 2 * zcount], refs[2 * zcount]
    own = lax.axis_index("tile") // 2
    for j in range(zcount):
        sum_ref[j] = keep_ref[j] + recvs[j][...].astype(F32)
    out_keep[...] = sum_ref[own]
    for j in range(1, zcount):
        out_sends[j - 1][...] = sum_ref[own ^ j].astype(BF)


def last_kernel(keep_ref, *refs):
    total = keep_ref[...]
    for ref in refs[:-1]:
        total = total + ref[...].astype(F32)
    refs[-1][...] = total.astype(BF)


def normal_kernel(zcount, bias_sum_ref, *refs):
    blocks, (second_ref, first_ref, bias_ref) = refs[: 4 * zcount], refs[4 * zcount :]
    t, p = lax.axis_index("tile"), lax.axis_index("dp")
    n = blocks[0].shape[0] // 2
    size = n // 9
    for which, out_ref in enumerate((second_ref, first_ref)):
        square = None
        for ref in blocks:
            v = ref[which * n : (which + 1) * n].astype(F32)
            square = v * v if square is None else square + v * v
        mean = jnp.sum(square, keepdims=True) / (9 * out_ref.shape[1] * out_ref.shape[2])
        scale = lax.rsqrt(mean + 1e-06)
        for index, ref in enumerate(blocks):
            group, j = index // zcount, index % zcount
            block = (p ^ (group // 2)) * 2 + ((t % 2) ^ (group % 2))
            at = pl.ds(pl.multiple_of((block * zcount + ((t // 2) ^ j)) * size, size), size)
            for tap in range(9):
                row = which * n + tap * size
                out_ref[tap, at] = ref[row : row + size].astype(F32) * scale
    total = bias_sum_ref[...]
    bias_mean = jnp.mean(total * total, keepdims=True)
    bias_ref[...] = total * lax.rsqrt(bias_mean + 1e-06)


def call(kernel, out_shapes, scratch=(), smem_first=False, limit=16):
    def run(*args):
        vmem = pl.BlockSpec(memory_space=pltpu.VMEM)
        smem = pl.BlockSpec(memory_space=pltpu.SMEM)
        specs = [smem if smem_first and i == 0 else vmem for i in range(len(args))]
        return pl.pallas_call(
            kernel,
            out_shape=[jax.ShapeDtypeStruct(s, dt) for s, dt in out_shapes],
            in_specs=specs,
            out_specs=[vmem] * len(out_shapes),
            scratch_shapes=[pltpu.VMEM(s, dt) for s, dt in scratch],
            compiler_params=pltpu.CompilerParams(vmem_limit_bytes=limit << 20),
        )(*args)

    return run


def swap_dp(v):
    count = lax.axis_size("dp")
    return lax.ppermute(v, "dp", [(i, count - 1 - i) for i in range(count)])


def on_device(initial_state, state_cotangents, w_first, bias, w_second, edge_partner):
    tiles = lax.axis_size("tile")
    _, _, rows, face, channels = initial_state.shape
    dm = Dims(rows, face, tiles, channels)
    planes = (6 * rows, face, channels)
    x = initial_state.reshape(planes)
    d = state_cotangents[state_cotangents.shape[0] - 1].reshape(planes)
    taps = (9, channels, channels)
    w1 = w_first.reshape(9 * channels, channels)
    w2 = w_second.reshape(9 * channels, channels)
    w1s, w1t, w2t = call(turn_kernel, [(taps, BF)] * 3)(w_first.reshape(taps), w_second.reshape(taps))
    w1s = w1s.reshape(w1.shape)
    w1t = w1t.reshape(w1.shape)
    w2t = w2t.reshape(w2.shape)
    msg_shapes = [(shape, BF) for shape in dm.messages()]
    flat = (dm.N, channels)
    messages = call(functools.partial(pack_kernel, dm), msg_shapes, smem_first=True)(
        edge_partner, x.reshape(flat), d.reshape(flat)
    )
    pairs = dm.pairs()

    def send_message(messages, k):
        return messages[k] if k == 0 else lax.ppermute(messages[k], "tile", pairs[k])

    messages = [send_message(messages, k) for k in range(tiles + 1)]
    half = channels // 2
    wide = 9 * channels
    frame = (rows + 2, 6, face + 16, channels)
    outs = call(
        functools.partial(first_kernel, dm),
        [
            ((9, half, channels), BF),
            ((9, half, channels), F32),
            ((9, half, channels), BF),
            ((9, half, channels), F32),
            ((1, channels), F32),
            (planes, BF),
            (planes, BF),
        ]
        + msg_shapes,
        [
            ((dm.NT, channels), BF),
            (frame, F32),
            ((dm.N, wide), BF),
            ((dm.N + dm.S, wide), BF),
            ((9, dm.S, channels), F32),
            (flat, F32),
            (flat, F32),
            ((dm.N + dm.S, channels), F32),
        ],
        smem_first=True,
        limit=LIMIT,
    )(edge_partner, x, d, w1s, bias.reshape(1, channels), w2t, *messages)
    send1, keep1, send2, keep2, bias_sum, hidden, inner = outs[:7]
    packed = list(outs[7:])
    bias_sum = lax.psum(bias_sum, ("tile", "dp"))

    zcount = tiles // 2
    block = (18 * half // tiles, channels)
    barrier = lax.optimization_barrier

    def along_y(v):
        return lax.ppermute(v, "tile", [(i, i ^ 1) for i in range(tiles)])

    def along_z(v, j):
        return lax.ppermute(v, "tile", [(i, i ^ (2 * j)) for i in range(tiles)])

    early = [k for k in range(2, tiles - 1) if k % 2 == 0]
    middle = [k for k in range(1, tiles - 1) if k % 2 == 1]
    late = [tiles - 1, tiles]
    messages = list(packed)

    keep, *sends = call(
        functools.partial(half_kernel, zcount), [((zcount,) + block, F32)] + [(block, BF)] * zcount
    )(keep2, keep1, swap_dp(send2), swap_dp(send1))
    recvs = [along_y(v) for v in sends]
    got = [send_message(packed, k) for k in early]
    recvs, got = barrier((recvs, got))
    for k, v in zip(early, got):
        messages[k] = v

    keep, *sends = call(
        functools.partial(block_kernel, zcount),
        [(block, F32)] + [(block, BF)] * (zcount - 1),
        [((zcount,) + block, F32)],
    )(keep, *recvs)
    sends, todo = barrier((sends, [packed[k] for k in middle]))
    recvs = [along_z(v, j + 1) for j, v in enumerate(sends)]
    got = [lax.ppermute(v, "tile", pairs[k]) for k, v in zip(middle, todo)]
    recvs, got = barrier((recvs, got))
    for k, v in zip(middle, got):
        messages[k] = v

    (own,) = call(last_kernel, [(block, BF)])(keep, *recvs)
    own, todo = barrier((own, [packed[k] for k in late]))
    own = [own] + [along_z(own, j) for j in range(1, zcount)]
    got = [lax.ppermute(v, "tile", pairs[k]) for k, v in zip(late, todo)]
    own[-1], got = barrier((own[-1], got))
    for k, v in zip(late, got):
        messages[k] = v
    other = [along_y(v) for v in own]
    blocks = own + other
    blocks = blocks + [swap_dp(v) for v in blocks]
    state, grad = call(
        functools.partial(second_kernel, dm),
        [(planes, BF), (planes, F32)],
        [
            ((dm.NT, channels), BF),
            (frame, F32),
            ((dm.N, wide), BF),
            ((dm.N + dm.S, wide), BF),
            ((9, dm.S, channels), F32),
            (flat, F32),
        ],
        smem_first=True,
        limit=LIMIT,
    )(edge_partner, x, d, hidden, inner, w1t, w2, *messages)
    second_step, first_step, bias_step = call(
        functools.partial(normal_kernel, zcount),
        [(taps, F32)] * 2 + [((1, channels), F32)],
        limit=24,
    )(bias_sum, *blocks)
    return (
        state.reshape(initial_state.shape),
        grad.reshape(initial_state.shape),
        first_step.reshape(w_first.shape),
        bias_step.reshape(channels),
        second_step.reshape(w_second.shape),
    )


def solution(mesh):
    return jax.shard_map(
        on_device,
        mesh=mesh,
        in_specs=(
            P(("groups", "dp"), None, "tile", None, None),
            P(None, ("groups", "dp"), None, "tile", None, None),
            P(),
            P(),
            P(),
            P(),
        ),
        out_specs=(
            P(("groups", "dp"), None, "tile", None, None),
            P(("groups", "dp"), None, "tile", None, None),
            P("groups", None, None, None),
            P("groups"),
            P("groups", None, None, None),
        ),
        check_vma=False,
    )
```

```python
import functools

import jax
import jax.numpy as jnp
from jax import lax
from jax.experimental import pallas as pl
from jax.experimental.pallas import tpu as pltpu
from jax.sharding import PartitionSpec as P

BF = jnp.bfloat16
F32 = jnp.float32
EXTRA = 8
LIMIT = 24


class Dims:
    def __init__(self, rows, face, tiles, channels):
        self.R, self.F, self.T, self.C = rows, face, tiles, channels
        self.N = 6 * rows * face
        self.ROW = 6 * face
        self.SLOT = -(-(2 * rows + 2) // 8) * 8
        self.BASE = 6 * self.SLOT
        self.o_msg = self.N
        self.o_row = self.o_msg + tiles * self.BASE
        self.NT = self.o_row + 2 * self.ROW
        self.WE = 12 * 8
        self.S = self.WE + self.ROW

    def messages(self, extra=0):
        rows = [self.BASE + extra] * self.T + [self.ROW]
        rows[1] += self.ROW
        return [(2, n, self.C) for n in rows]

    def pairs(self, every=False):
        T = self.T

        def needed(i, d):
            return i in (0, T - 1) or d in (0, T - 1) or d in (T - 2 - i, T - i)

        out = [[(i, i ^ k) for i in range(T) if every or k in (1, T - 1) or needed(i, i ^ k)] for k in range(T)]
        out.append([(i, (i + 1) % T if i % 2 else (i - 1) % T) for i in range(T)])
        return out


def col_iota(n):
    return lax.broadcasted_iota(jnp.int32, (n, 1), 0)


def one_hot(target, width):
    lanes = lax.broadcasted_iota(jnp.int32, (target.shape[0], width), 1)
    return jnp.where(lanes == target, 1.0, 0.0).astype(BF)


def strip_targets(dm, ep, t, d):
    R, F, T = dm.R, dm.F, dm.T
    at_edge = (t == 0) | (t == T - 1)
    to_edge = (d == 0) | (d == T - 1)
    own_edge = jnp.where(t == 0, 0, 2)
    far_edge = jnp.where(d == 0, 0, 2)
    side_row = jnp.where(d == T - 2 - t, R - 1, 0)
    i = col_iota(dm.SLOT)
    q = R * d - 1 + i
    inside = (q >= 0) & (q < F) & (i < R + 2)
    i2 = i - (R + 2)
    parts = []
    for f in range(6):
        far_low = (ep[f, own_edge] % 4) < 2
        reverse = far_low == (t == 0)
        p0 = jnp.where(reverse, F - 1, 0)
        sgn = jnp.where(reverse, -1, 1)
        row = jnp.where(t == 0, 0, R - 1)
        strip = jnp.where(inside, (f * R + row) * F + p0 + sgn * q, -1)
        sides = (f * R + side_row) * F
        low = jnp.where(at_edge, strip, sides + i * (F - 1))
        low = jnp.where(at_edge | (i < 2), low, -1)
        gvalue = ep[f, far_edge]
        column = jnp.where(gvalue % 4 == 1, F - 1, 0) + (gvalue // 4) * (R * F)
        high = jnp.where(to_edge, column + F * i2, jnp.where(i2 < 2, sides + i2 * (F - 1), -1))
        strips = jnp.where(i2 < 0, low, jnp.where(i2 < R, high, -1))
        parts.append(jnp.where(d == T - 1 - t, mirror_slot(dm, f), strips))
    return parts


def mirror_slot(dm, f):
    i = col_iota(dm.SLOT)
    return jnp.where(i < 2 * dm.R, (f * dm.R + i // 2) * dm.F + (i % 2) * (dm.F - 1), -1)


def row_targets(dm, row):
    j = col_iota(dm.F)
    return [(f * dm.R + row) * dm.F + j for f in range(6)]


def write_messages(dm, ep, t, sources, refs):
    R = dm.R
    for k in range(dm.T + 1):
        parts = strip_targets(dm, ep, t, t ^ k) if k < dm.T else []
        if k == 1:
            parts = parts + row_targets(dm, jnp.where(t % 2 == 0, R - 1, 0))
        if k == dm.T:
            parts = row_targets(dm, jnp.where(t % 2 == 1, R - 1, 0))
        hot = one_hot(jnp.concatenate(parts, axis=0), dm.N)
        for which in range(2):
            rows = jnp.dot(hot, sources[which], preferred_element_type=F32).astype(BF)
            refs[k][which, : rows.shape[0]] = rows


def pack_kernel(dm, ep, x_ref, up_ref, *refs):
    write_messages(dm, ep, lax.axis_index("tile"), (x_ref[...], up_ref[...]), refs)


def ghost_targets(dm, ep, t):
    R, F, T = dm.R, dm.F, dm.T
    odd = t % 2
    parts = []
    m = col_iota(8)
    q = R * t - 1 + m
    inside = (q >= 0) & (q < F) & (m < R + 2)
    row_prev = dm.o_row + (1 - odd) * dm.ROW
    row_next = dm.o_row + odd * dm.ROW
    side_first = dm.o_msg + (t ^ (T - t)) * dm.BASE + jnp.where(t == 1, R + 2, 0)
    side_last = dm.o_msg + (t ^ (T - 2 - t)) * dm.BASE + jnp.where(t == T - 2, R + 2, 0)
    mirror = dm.o_msg + (T - 1) * dm.BASE
    for f in range(6):
        for edge in (3, 1):
            value = ep[f, edge]
            f2, e2 = value // 4, value % 4
            far_low = e2 < 2
            reverse = far_low if edge < 2 else e2 >= 2
            is_col = (e2 % 2) == 1
            side = jnp.where(e2 == 1, 1, 0)
            column = side * (F - 1)
            slot = f2 * dm.SLOT + side
            row = dm.o_msg + (t ^ jnp.where(e2 == 0, 0, T - 1)) * dm.BASE + f2 * dm.SLOT
            facing = jnp.where(e2 == 0, t == T - 1, t == 0)
            whole = dm.o_row + dm.ROW + f2 * F + jnp.where(reverse, F - R * t, R * t - 1)
            row = jnp.where(facing, whole, row)
            along = jnp.where(facing & reverse, -1, 1)
            i0 = jnp.where(is_col, jnp.where(reverse, side_first + slot, row_prev + f2 * F + column), row)
            i4 = jnp.where(
                is_col, jnp.where(reverse, side_last + slot, row_next + f2 * F + column), row + along * (R + 1)
            )
            base = jnp.where(
                is_col, jnp.where(reverse, mirror + 2 * R + slot, (f2 * R - 1) * F + column), row
            )
            step = jnp.where(is_col, jnp.where(reverse, -2, F), along)
            target = jnp.where(m == 0, i0, jnp.where(m == R + 1, i4, base + step * m))
            parts.append(jnp.where(inside, target, -1))
    j = col_iota(F)
    jt = jnp.zeros_like(j)
    for b in range(1, T):
        jt = jt + jnp.where(j >= b * R, 1, 0)
    jr = j - R * jt
    wrap = dm.o_row + dm.ROW
    for edge in (0, 2):
        at_edge = (t == 0) if edge == 0 else (t == T - 1)
        inner_base = row_prev if edge == 0 else row_next
        own_row = 0 if edge == 0 else R - 1
        for f in range(6):
            value = ep[f, edge]
            f2, e2 = value // 4, value % 4
            far_low = e2 < 2
            reverse = far_low if edge < 2 else e2 >= 2
            is_col = (e2 % 2) == 1
            same = e2 == edge
            row_base = jnp.where(same, (f2 * R + own_row) * F, wrap + f2 * F)
            lin_base = row_base + jnp.where(reverse, F - 1, 0)
            lin_step = jnp.where(reverse, -1, 1)
            k0 = jnp.where(reverse, T - 1, 0)
            ks = jnp.where(reverse, -1, 1)
            if edge == 2:
                k0 = T - 1 - k0
                ks = -ks
            col_base = dm.o_msg + k0 * dm.BASE + f * dm.SLOT + R + 2 + jnp.where(reverse, R - 1, 0)
            base = jnp.where(is_col, col_base, lin_base)
            sj = jnp.where(is_col, 0, lin_step)
            st = jnp.where(is_col, ks * dm.BASE, 0)
            sr = jnp.where(is_col, jnp.where(reverse, -1, 1), 0)
            base = jnp.where(at_edge, base, inner_base + f * F)
            sj = jnp.where(at_edge, sj, 1)
            st = jnp.where(at_edge, st, 0)
            sr = jnp.where(at_edge, sr, 0)
            target = base + sj * j + st * jt + sr * jr
            far_tile = T - 1 if edge == 0 else 0
            from_mirror = is_col & at_edge & (jnp.where(reverse, T - 1 - jt, jt) == far_tile)
            side = jnp.where(e2 == 1, 1, 0)
            cells = mirror + f2 * dm.SLOT + side + 2 * jnp.where(reverse, R - 1 - jr, jr)
            parts.append(jnp.where(from_mirror, cells, target))
    return jnp.concatenate(parts, axis=0)


def gather_ghosts(dm, ep, t, own, messages, table_ref):
    hot = one_hot(ghost_targets(dm, ep, t), dm.NT)
    out = []
    for which in range(2):
        table_ref[0 : dm.N] = own[which]
        for k in range(dm.T):
            at = dm.o_msg + k * dm.BASE
            table_ref[at : at + dm.BASE] = messages[k][which, : dm.BASE]
        table_ref[dm.o_row : dm.o_row + dm.ROW] = messages[1][which, dm.BASE : dm.BASE + dm.ROW]
        table_ref[dm.o_row + dm.ROW :] = messages[dm.T][which]
        out.append(jnp.dot(hot, table_ref[...], preferred_element_type=F32))
    return out


def own_first(value, p):
    half = value.shape[1] // 2
    low, high = value[:, :half], value[:, half:]
    return jnp.concatenate([jnp.where(p == 0, low, high), jnp.where(p == 0, high, low)], axis=1)


def build_taps(dm, field_ref, ghosts, top, bottom, frame_ref, taps_ref, adjoint, p=None):
    R, F, C = dm.R, dm.F, dm.C
    for f in range(6):
        for r in range(R):
            frame_ref[r + 1, f, 8 : 8 + F] = field_ref[f * R + r].astype(F32)
    frame_ref[0, :, 8 : 8 + F] = top.reshape(6, F, C)
    frame_ref[R + 1, :, 8 : 8 + F] = bottom.reshape(6, F, C)
    for m in range(R + 2):
        for f in range(6):
            if ghosts is None:
                west = jnp.zeros((1, C), F32)
                east = west
            else:
                west = ghosts[16 * f + m : 16 * f + m + 1]
                east = ghosts[16 * f + 8 + m : 16 * f + 8 + m + 1]
            frame_ref[m, f, 7:8] = west
            frame_ref[m, f, 8 + F : 9 + F] = east
    for m in range(R + 2):
        for b in range(3):
            plane = frame_ref[m, :, 7 + b : 7 + b + F].reshape(dm.ROW, C)
            if p is not None:
                plane = own_first(plane, p)
            plane = plane.astype(BF)
            for a in range(3):
                r = m - 2 + a if adjoint else m - a
                tap = 3 * a + (2 - b if adjoint else b)
                if 0 <= r < R:
                    taps_ref[r * dm.ROW : (r + 1) * dm.ROW, tap * C : (tap + 1) * C] = plane


def build_strip_terms(dm, ep, t, ghosts, top, bottom, z_ref):
    R, F = dm.R, dm.F
    z_ref[...] = jnp.zeros(z_ref.shape, F32)

    def tap_of(f, edge, shift):
        e2 = ep[f, edge] % 4
        reverse = e2 < 2 if edge < 2 else e2 >= 2
        along = 1 - jnp.where(reverse, -shift, shift)
        return jnp.where(
            e2 == 0, along, jnp.where(e2 == 2, 6 + along, jnp.where(e2 == 1, 3 * along + 2, 3 * along))
        )

    live = lax.rem(lax.broadcasted_iota(jnp.int32, (dm.WE, 1), 0), 8) < R
    for shift in (-1, 0, 1):
        moved = pltpu.roll(ghosts, (dm.WE - 1 - shift) % dm.WE, 0) if shift > -1 else ghosts
        moved = jnp.where(live, moved, 0.0)
        for f in range(6):
            for side, edge in ((0, 3), (1, 1)):
                at = 16 * f + 8 * side
                z_ref[tap_of(f, edge, shift), at : at + 8] = moved[at : at + 8]

    def add_rows(edge, rows):
        j = lax.rem(lax.broadcasted_iota(jnp.int32, (dm.ROW, 1), 0), F)
        for shift in (-1, 0, 1):
            if shift == 0:
                moved = rows
            else:
                moved = pltpu.roll(rows, (-shift) % dm.ROW, 0)
                moved = jnp.where((j + shift >= 0) & (j + shift < F), moved, 0.0)
            for f in range(6):
                at = dm.WE + F * f
                z_ref[tap_of(f, edge, shift), at : at + F] = moved[F * f : F * (f + 1)]

    @pl.when(t == 0)
    def _():
        add_rows(0, top)

    @pl.when(t == dm.T - 1)
    def _():
        add_rows(2, bottom)


def adjoint(dm, t, taps_ref, z_ref, wt_ref, acc_ref):
    R, F, C, N = dm.R, dm.F, dm.C, dm.N
    for tap in range(9):
        taps_ref[N:, tap * C : (tap + 1) * C] = z_ref[tap].astype(BF)
    total = jnp.dot(taps_ref[...], wt_ref[...], preferred_element_type=F32)
    acc_ref[...] = total[:N]
    strips = total[N:]
    for f in range(6):
        for side in range(2):
            for r in range(R):
                at = (r * 6 + f) * F + side * (F - 1)
                row = 16 * f + 8 * side + r
                acc_ref[at : at + 1] += strips[row : row + 1]

    @pl.when(t == 0)
    def _():
        acc_ref[0 : dm.ROW] += strips[dm.WE :]

    @pl.when(t == dm.T - 1)
    def _():
        acc_ref[(R - 1) * dm.ROW : R * dm.ROW] += strips[dm.WE :]


def turn_kernel(w1_ref, w2_ref, w1s_ref, w1t_ref, w2t_ref):
    p = lax.axis_index("dp")
    half = w1_ref.shape[1] // 2
    for tap in range(9):
        w1t_ref[tap] = w1_ref[tap].T
        w2t_ref[tap] = w2_ref[tap].T
        w1s_ref[tap, :half] = w1_ref[tap, pl.ds(pl.multiple_of(p * half, half), half)]
        w1s_ref[tap, half:] = w1_ref[tap, pl.ds(pl.multiple_of((1 - p) * half, half), half)]


def put_taps(send_ref, keep_ref, first_tap, value):
    half = keep_ref.shape[1]
    for i in range(value.shape[0] // (2 * half)):
        keep_ref[first_tap + i] = value[2 * i * half : (2 * i + 1) * half]
        send_ref[first_tap + i] = value[(2 * i + 1) * half : (2 * i + 2) * half].astype(BF)


def first_kernel(dm, ep, x_ref, up_ref, w1_ref, bias_ref, w2t_ref, *refs):
    T, R, F, N, C = dm.T, dm.R, dm.F, dm.N, dm.C
    M = T + 1
    messages = refs[:M]
    send1_ref, keep1_ref, send2_ref, keep2_ref, hid_ref, inner_ref = refs[M : M + 6]
    out_messages = refs[M + 6 : 2 * M + 6]
    table_ref, frame_ref, xs_ref, us_ref, z_ref, before_ref, acc_ref, hcat_ref = refs[2 * M + 6 :]
    t, p = lax.axis_index("tile"), lax.axis_index("dp")
    own = (x_ref[...].reshape(N, C), up_ref[...].reshape(N, C))
    gx, gu = gather_ghosts(dm, ep, t, own, messages, table_ref)
    top, bottom = dm.WE, dm.WE + dm.ROW
    build_taps(dm, x_ref, gx[:top], gx[top:bottom], gx[bottom:], frame_ref, xs_ref, False, p)
    before = jnp.dot(xs_ref[...], w1_ref[...], preferred_element_type=F32) + bias_ref[...]
    before_ref[...] = before
    sig = 1.0 / (1.0 + jnp.exp(-before))
    acc_ref[...] = before * sig
    up_top = jnp.where(t == 0, 0.0, gu[top:bottom])
    up_bottom = jnp.where(t == T - 1, 0.0, gu[bottom:])
    build_taps(dm, up_ref, None, up_top, up_bottom, frame_ref, us_ref, True)
    build_strip_terms(dm, ep, t, gu[:top], gu[top:bottom], gu[bottom:], z_ref)
    hcat_ref[0:N] = acc_ref[...]
    hcat_ref[N:] = jnp.zeros((dm.S, C), F32)
    for f in range(6):
        for side in range(2):
            for r in range(R):
                at = (r * 6 + f) * F + side * (F - 1)
                row = N + 16 * f + 8 * side + r
                hcat_ref[row : row + 1] = acc_ref[at : at + 1]
    first_row = acc_ref[0 : dm.ROW]
    last_row = acc_ref[(R - 1) * dm.ROW : R * dm.ROW]
    hcat_ref[N + dm.WE :] = jnp.where(t == 0, first_row, last_row)
    for r in range(R):
        for f in range(6):
            at = (r * 6 + f) * F
            hid_ref[f * R + r] = acc_ref[at : at + F].astype(BF)
    adjoint(dm, t, us_ref, z_ref, w2t_ref, acc_ref)
    hidden_t = own_first(hcat_ref[...], p).astype(BF).T
    for tap in range(9):
        grad = jnp.dot(hidden_t, us_ref[:, tap * C : (tap + 1) * C], preferred_element_type=F32)
        put_taps(send2_ref, keep2_ref, tap, grad)
    before = before_ref[...]
    sig = 1.0 / (1.0 + jnp.exp(-before))
    before_grad = acc_ref[...] * (sig * (1.0 + before * (1.0 - sig)))
    acc_ref[...] = before_grad
    inner = before_grad.astype(BF)
    for tap in (0, 3, 6):
        grad = lax.dot_general(
            xs_ref[:, tap * C : (tap + 3) * C],
            inner,
            (((0,), (0,)), ((), ())),
            preferred_element_type=F32,
        )
        put_taps(send1_ref, keep1_ref, tap, grad)
    bias_sum = jnp.sum(before_grad, axis=0, keepdims=True)
    high = bias_sum.astype(BF).astype(F32)
    for k in range(T):
        for which, value in enumerate((high, bias_sum - high)):
            at = out_messages[k].shape[1] - EXTRA
            out_messages[k][which, at:] = jnp.broadcast_to(value, (EXTRA, C)).astype(BF)
    for r in range(R):
        for f in range(6):
            at = (r * 6 + f) * F
            inner_ref[f * R + r] = acc_ref[at : at + F].astype(BF)
    write_messages(
        dm, ep, t, (hid_ref[...].reshape(N, C), inner_ref[...].reshape(N, C)), out_messages
    )


def second_kernel(dm, ep, x_ref, d_ref, hid_ref, inner_ref, w1t_ref, w2_ref, *refs):
    T, R, F, N, C = dm.T, dm.R, dm.F, dm.N, dm.C
    messages = refs[: T + 1]
    state_ref, grad_ref, bias_ref = refs[T + 1 : T + 4]
    table_ref, frame_ref, hs_ref, is_ref, z_ref, acc_ref = refs[T + 4 :]
    bias_sum = jnp.zeros((1, C), F32)
    for k in range(T):
        at = messages[k].shape[1] - EXTRA
        for which in range(2):
            bias_sum = bias_sum + messages[k][which, at : at + 1].astype(F32)
    bias_ref[...] = jnp.broadcast_to(bias_sum, bias_ref.shape)
    t = lax.axis_index("tile")
    own = (hid_ref[...].reshape(N, C), inner_ref[...].reshape(N, C))
    gh, gi = gather_ghosts(dm, ep, t, own, messages, table_ref)
    top, bottom = dm.WE, dm.WE + dm.ROW
    build_taps(dm, hid_ref, gh[:top], gh[top:bottom], gh[bottom:], frame_ref, hs_ref, False)
    acc_ref[...] = jnp.dot(hs_ref[...], w2_ref[...], preferred_element_type=F32)
    for r in range(R):
        for f in range(6):
            at = (r * 6 + f) * F
            value = x_ref[f * R + r].astype(F32) + acc_ref[at : at + F]
            state_ref[f * R + r] = value.astype(BF)
    in_top = jnp.where(t == 0, 0.0, gi[top:bottom])
    in_bottom = jnp.where(t == T - 1, 0.0, gi[bottom:])
    build_taps(dm, inner_ref, None, in_top, in_bottom, frame_ref, is_ref, True)
    build_strip_terms(dm, ep, t, gi[:top], gi[top:bottom], gi[bottom:], z_ref)
    adjoint(dm, t, is_ref, z_ref, w1t_ref, acc_ref)
    for r in range(R):
        for f in range(6):
            at = (r * 6 + f) * F
            grad_ref[f * R + r] = d_ref[f * R + r].astype(F32) + acc_ref[at : at + F]


def half_kernel(zcount, keep2_ref, keep1_ref, recv2_ref, recv1_ref, out_keep, *out_sends):
    size = keep1_ref.shape[1] // 2
    own = lax.axis_index("tile") % 2
    mine = pl.ds(pl.multiple_of(own * size, size), size)
    far = pl.ds(pl.multiple_of((1 - own) * size, size), size)
    part = size // zcount
    for which, (keep_ref, recv_ref) in enumerate(((keep2_ref, recv2_ref), (keep1_ref, recv1_ref))):
        for tap in range(9):
            kept = keep_ref[tap, mine] + recv_ref[tap, mine].astype(F32)
            sent = keep_ref[tap, far] + recv_ref[tap, far].astype(F32)
            at = (9 * which + tap) * part
            for j in range(zcount):
                out_keep[j, at : at + part] = kept[j * part : (j + 1) * part]
                out_sends[j][at : at + part] = sent[j * part : (j + 1) * part].astype(BF)


def block_kernel(zcount, keep_ref, *refs):
    recvs, (out_keep, *out_sends), sum_ref = refs[:zcount], refs[zcount : 2 * zcount], refs[2 * zcount]
    own = lax.axis_index("tile") // 2
    for j in range(zcount):
        sum_ref[j] = keep_ref[j] + recvs[j][...].astype(F32)
    out_keep[...] = sum_ref[own]
    for j in range(1, zcount):
        out_sends[j - 1][...] = sum_ref[own ^ j].astype(BF)


def last_kernel(keep_ref, *refs):
    total = keep_ref[...]
    for ref in refs[:-1]:
        total = total + ref[...].astype(F32)
    refs[-1][...] = total.astype(BF)


def normal_kernel(zcount, bias1_ref, bias2_ref, *refs):
    sources, (second_ref, first_ref, bias_ref) = refs[:4], refs[4:]
    t, p = lax.axis_index("tile"), lax.axis_index("dp")
    rows = sources[0].shape[0] // zcount
    n = rows // 2
    size = n // 9
    for which, out_ref in enumerate((second_ref, first_ref)):
        square = None
        for ref in sources:
            for j in range(zcount):
                at = j * rows + which * n
                v = ref[at : at + n].astype(F32)
                part = jnp.sum(v * v, axis=0, keepdims=True)
                square = part if square is None else square + part
        mean = jnp.sum(square, keepdims=True) / (9 * out_ref.shape[1] * out_ref.shape[2])
        scale = lax.rsqrt(mean + 1e-06)
        for group, ref in enumerate(sources):
            block = (p ^ (group // 2)) * 2 + ((t % 2) ^ (group % 2))
            for j in range(zcount):
                at = pl.ds(pl.multiple_of((block * zcount + ((t // 2) ^ j)) * size, size), size)
                for tap in range(9):
                    row = j * rows + which * n + tap * size
                    out_ref[tap, at] = ref[row : row + size].astype(F32) * scale
    total = bias1_ref[0:1] + bias2_ref[0:1]
    bias_mean = jnp.mean(total * total, keepdims=True)
    bias_ref[...] = total * lax.rsqrt(bias_mean + 1e-06)


def call(kernel, out_shapes, scratch=(), smem_first=False, limit=16):
    def run(*args):
        vmem = pl.BlockSpec(memory_space=pltpu.VMEM)
        smem = pl.BlockSpec(memory_space=pltpu.SMEM)
        specs = [smem if smem_first and i == 0 else vmem for i in range(len(args))]
        return pl.pallas_call(
            kernel,
            out_shape=[jax.ShapeDtypeStruct(s, dt) for s, dt in out_shapes],
            in_specs=specs,
            out_specs=[vmem] * len(out_shapes),
            scratch_shapes=[pltpu.VMEM(s, dt) for s, dt in scratch],
            compiler_params=pltpu.CompilerParams(vmem_limit_bytes=limit << 20),
        )(*args)

    return run


def swap_dp(v):
    count = lax.axis_size("dp")
    return lax.ppermute(v, "dp", [(i, count - 1 - i) for i in range(count)])


def on_device(initial_state, state_cotangents, w_first, bias, w_second, edge_partner):
    tiles = lax.axis_size("tile")
    _, _, rows, face, channels = initial_state.shape
    dm = Dims(rows, face, tiles, channels)
    planes = (6 * rows, face, channels)
    x = initial_state.reshape(planes)
    d = state_cotangents[state_cotangents.shape[0] - 1].reshape(planes)
    taps = (9, channels, channels)
    w1 = w_first.reshape(9 * channels, channels)
    w2 = w_second.reshape(9 * channels, channels)
    w1s, w1t, w2t = call(turn_kernel, [(taps, BF)] * 3)(w_first.reshape(taps), w_second.reshape(taps))
    w1s = w1s.reshape(w1.shape)
    w1t = w1t.reshape(w1.shape)
    w2t = w2t.reshape(w2.shape)
    msg_shapes = [(shape, BF) for shape in dm.messages()]
    flat = (dm.N, channels)
    messages = call(functools.partial(pack_kernel, dm), msg_shapes, smem_first=True)(
        edge_partner, x.reshape(flat), d.reshape(flat)
    )
    pairs = dm.pairs()

    def send_message(messages, k):
        return messages[k] if k == 0 else lax.ppermute(messages[k], "tile", pairs[k])

    messages = [send_message(messages, k) for k in range(tiles + 1)]
    half = channels // 2
    wide = 9 * channels
    frame = (rows + 2, 6, face + 16, channels)
    outs = call(
        functools.partial(first_kernel, dm),
        [
            ((9, half, channels), BF),
            ((9, half, channels), F32),
            ((9, half, channels), BF),
            ((9, half, channels), F32),
            (planes, BF),
            (planes, BF),
        ]
        + [(shape, BF) for shape in dm.messages(EXTRA)],
        [
            ((dm.NT, channels), BF),
            (frame, F32),
            ((dm.N, wide), BF),
            ((dm.N + dm.S, wide), BF),
            ((9, dm.S, channels), F32),
            (flat, F32),
            (flat, F32),
            ((dm.N + dm.S, channels), F32),
        ],
        smem_first=True,
        limit=LIMIT,
    )(edge_partner, x, d, w1s, bias.reshape(1, channels), w2t, *messages)
    send1, keep1, send2, keep2, hidden, inner = outs[:6]
    packed = list(outs[6:])
    pairs = dm.pairs(True)

    zcount = tiles // 2
    block = (18 * half // tiles, channels)
    barrier = lax.optimization_barrier

    def along_y(v):
        return lax.ppermute(v, "tile", [(i, i ^ 1) for i in range(tiles)])

    def along_z(v, j):
        return lax.ppermute(v, "tile", [(i, i ^ (2 * j)) for i in range(tiles)])

    early = [k for k in range(2, tiles - 1) if k % 2 == 0]
    middle = [k for k in range(1, tiles - 1) if k % 2 == 1]
    late = [tiles - 1, tiles]
    messages = list(packed)

    keep, *sends = call(
        functools.partial(half_kernel, zcount), [((zcount,) + block, F32)] + [(block, BF)] * zcount
    )(keep2, keep1, swap_dp(send2), swap_dp(send1))
    recvs = [along_y(v) for v in sends]
    got = [lax.ppermute(packed[k], "tile", pairs[k]) for k in early]
    recvs, got = barrier((recvs, got))
    for k, v in zip(early, got):
        messages[k] = v

    keep, *sends = call(
        functools.partial(block_kernel, zcount),
        [(block, F32)] + [(block, BF)] * (zcount - 1),
        [((zcount,) + block, F32)],
    )(keep, *recvs)
    sends, todo = barrier((sends, [packed[k] for k in middle]))
    recvs = [along_z(v, j + 1) for j, v in enumerate(sends)]
    got = [lax.ppermute(v, "tile", pairs[k]) for k, v in zip(middle, todo)]
    recvs, got = barrier((recvs, got))
    for k, v in zip(middle, got):
        messages[k] = v

    (own,) = call(last_kernel, [(block, BF)])(keep, *recvs)
    own, todo = barrier((own, [packed[k] for k in late]))
    own = [own] + [along_z(own, j) for j in range(1, zcount)]
    got = [lax.ppermute(v, "tile", pairs[k]) for k, v in zip(late, todo)]
    own[-1], got = barrier((own[-1], got))
    for k, v in zip(late, got):
        messages[k] = v
    own = jnp.concatenate(own, axis=0)
    other = along_y(own)
    own, messages = barrier((own, messages))
    state, grad, bias_sum = call(
        functools.partial(second_kernel, dm),
        [(planes, BF), (planes, F32), ((8, channels), F32)],
        [
            ((dm.NT, channels), BF),
            (frame, F32),
            ((dm.N, wide), BF),
            ((dm.N + dm.S, wide), BF),
            ((9, dm.S, channels), F32),
            (flat, F32),
        ],
        smem_first=True,
        limit=LIMIT,
    )(edge_partner, x, d, hidden, inner, w1t, w2, *messages)
    other, bias_sum = barrier((other, bias_sum))
    second_step, first_step, bias_step = call(
        functools.partial(normal_kernel, zcount),
        [(taps, F32)] * 2 + [((1, channels), F32)],
        limit=24,
    )(bias_sum, swap_dp(bias_sum), own, other, swap_dp(own), swap_dp(other))
    return (
        state.reshape(initial_state.shape),
        grad.reshape(initial_state.shape),
        first_step.reshape(w_first.shape),
        bias_step.reshape(channels),
        second_step.reshape(w_second.shape),
    )


def solution(mesh):
    return jax.shard_map(
        on_device,
        mesh=mesh,
        in_specs=(
            P(("groups", "dp"), None, "tile", None, None),
            P(None, ("groups", "dp"), None, "tile", None, None),
            P(),
            P(),
            P(),
            P(),
        ),
        out_specs=(
            P(("groups", "dp"), None, "tile", None, None),
            P(("groups", "dp"), None, "tile", None, None),
            P("groups", None, None, None),
            P("groups"),
            P("groups", None, None, None),
        ),
        check_vma=False,
    )
```

```python
import functools

import jax
import jax.numpy as jnp
from jax import lax
from jax.experimental import pallas as pl
from jax.experimental.pallas import tpu as pltpu
from jax.sharding import PartitionSpec as P

BF = jnp.bfloat16
F32 = jnp.float32
EXTRA = 8
LIMIT = 24


class Dims:
    def __init__(self, rows, face, tiles, channels):
        self.R, self.F, self.T, self.C = rows, face, tiles, channels
        self.N = 6 * rows * face
        self.ROW = 6 * face
        self.SLOT = -(-(2 * rows + 2) // 8) * 8
        self.BASE = 6 * self.SLOT
        self.MIX = tiles // 2 - 1
        self.o_msg = self.N
        self.o_row = self.o_msg + tiles * self.BASE
        self.NT = self.o_row + 2 * self.ROW
        self.WE = 12 * 8
        self.S = self.WE + self.ROW

    def partner(self, t, k):
        if k == self.MIX:
            ends = (t == 0) | (t == self.MIX) | (t == self.MIX + 1) | (t == self.T - 1)
            return jnp.where(ends, t ^ k, self.T - 1 - t)
        return t ^ k

    def messages(self):
        rows = [self.BASE] * (self.T - 1) + [self.BASE + self.ROW]
        rows[1] += self.ROW
        return [(2, n, self.C) for n in rows]

    def pairs(self):
        T, mix = self.T, self.MIX

        def needed(i, d):
            return i in (0, T - 1) or d in (0, T - 1) or d in (T - 2 - i, T - i)

        out = [[(i, i ^ k) for i in range(T) if k == 1 or needed(i, i ^ k)] for k in range(T - 1)]
        out[mix] = [(i, i ^ mix if i in (0, mix, mix + 1, T - 1) else T - 1 - i) for i in range(T)]
        out.append([(i, (i + 1) % T if i % 2 else (i - 1) % T) for i in range(T)])
        return out


def col_iota(n):
    return lax.broadcasted_iota(jnp.int32, (n, 1), 0)


def one_hot(target, width):
    lanes = lax.broadcasted_iota(jnp.int32, (target.shape[0], width), 1)
    return jnp.where(lanes == target, 1.0, 0.0).astype(BF)


def strip_targets(dm, ep, t, d):
    R, F, T = dm.R, dm.F, dm.T
    at_edge = (t == 0) | (t == T - 1)
    to_edge = (d == 0) | (d == T - 1)
    own_edge = jnp.where(t == 0, 0, 2)
    far_edge = jnp.where(d == 0, 0, 2)
    side_row = jnp.where(d == T - 2 - t, R - 1, 0)
    i = col_iota(dm.SLOT)
    q = R * d - 1 + i
    inside = (q >= 0) & (q < F) & (i < R + 2)
    i2 = i - (R + 2)
    parts = []
    for f in range(6):
        far_low = (ep[f, own_edge] % 4) < 2
        reverse = far_low == (t == 0)
        p0 = jnp.where(reverse, F - 1, 0)
        sgn = jnp.where(reverse, -1, 1)
        row = jnp.where(t == 0, 0, R - 1)
        strip = jnp.where(inside, (f * R + row) * F + p0 + sgn * q, -1)
        sides = (f * R + side_row) * F
        low = jnp.where(at_edge, strip, sides + i * (F - 1))
        low = jnp.where(at_edge | (i < 2), low, -1)
        gvalue = ep[f, far_edge]
        column = jnp.where(gvalue % 4 == 1, F - 1, 0) + (gvalue // 4) * (R * F)
        high = jnp.where(to_edge, column + F * i2, jnp.where(i2 < 2, sides + i2 * (F - 1), -1))
        strips = jnp.where(i2 < 0, low, jnp.where(i2 < R, high, -1))
        parts.append(jnp.where(d == T - 1 - t, mirror_slot(dm, f), strips))
    return parts


def mirror_slot(dm, f):
    i = col_iota(dm.SLOT)
    return jnp.where(i < 2 * dm.R, (f * dm.R + i // 2) * dm.F + (i % 2) * (dm.F - 1), -1)


def row_targets(dm, row):
    j = col_iota(dm.F)
    return [(f * dm.R + row) * dm.F + j for f in range(6)]


def write_messages(dm, ep, t, sources, refs):
    R = dm.R
    for k in range(dm.T):
        if k < dm.T - 1:
            parts = strip_targets(dm, ep, t, dm.partner(t, k))
            if k == 1:
                parts = parts + row_targets(dm, jnp.where(t % 2 == 0, R - 1, 0))
        else:
            parts = [mirror_slot(dm, f) for f in range(6)]
            parts = parts + row_targets(dm, jnp.where(t % 2 == 1, R - 1, 0))
        hot = one_hot(jnp.concatenate(parts, axis=0), dm.N)
        for which in range(2):
            refs[k][which] = jnp.dot(hot, sources[which], preferred_element_type=F32).astype(BF)


def pack_kernel(dm, ep, x_ref, up_ref, *refs):
    write_messages(dm, ep, lax.axis_index("tile"), (x_ref[...], up_ref[...]), refs)


def ghost_targets(dm, ep, t):
    R, F, T = dm.R, dm.F, dm.T
    odd = t % 2
    parts = []
    m = col_iota(8)
    q = R * t - 1 + m
    inside = (q >= 0) & (q < F) & (m < R + 2)
    row_prev = dm.o_row + (1 - odd) * dm.ROW
    row_next = dm.o_row + odd * dm.ROW
    side_first = dm.o_msg + (t ^ (T - t)) * dm.BASE + jnp.where(t == 1, R + 2, 0)
    side_last = dm.o_msg + (t ^ (T - 2 - t)) * dm.BASE + jnp.where(t == T - 2, R + 2, 0)
    ends = (t == 0) | (t == dm.MIX) | (t == dm.MIX + 1) | (t == T - 1)
    mirror = dm.o_msg + jnp.where(ends, T - 1, dm.MIX) * dm.BASE
    for f in range(6):
        for edge in (3, 1):
            value = ep[f, edge]
            f2, e2 = value // 4, value % 4
            far_low = e2 < 2
            reverse = far_low if edge < 2 else e2 >= 2
            is_col = (e2 % 2) == 1
            side = jnp.where(e2 == 1, 1, 0)
            column = side * (F - 1)
            slot = f2 * dm.SLOT + side
            row = dm.o_msg + (t ^ jnp.where(e2 == 0, 0, T - 1)) * dm.BASE + f2 * dm.SLOT
            facing = jnp.where(e2 == 0, t == T - 1, t == 0)
            whole = dm.o_row + dm.ROW + f2 * F + jnp.where(reverse, F - R * t, R * t - 1)
            row = jnp.where(facing, whole, row)
            along = jnp.where(facing & reverse, -1, 1)
            i0 = jnp.where(is_col, jnp.where(reverse, side_first + slot, row_prev + f2 * F + column), row)
            i4 = jnp.where(
                is_col, jnp.where(reverse, side_last + slot, row_next + f2 * F + column), row + along * (R + 1)
            )
            base = jnp.where(
                is_col, jnp.where(reverse, mirror + 2 * R + slot, (f2 * R - 1) * F + column), row
            )
            step = jnp.where(is_col, jnp.where(reverse, -2, F), along)
            target = jnp.where(m == 0, i0, jnp.where(m == R + 1, i4, base + step * m))
            parts.append(jnp.where(inside, target, -1))
    j = col_iota(F)
    jt = jnp.zeros_like(j)
    for b in range(1, T):
        jt = jt + jnp.where(j >= b * R, 1, 0)
    jr = j - R * jt
    wrap = dm.o_row + dm.ROW
    for edge in (0, 2):
        at_edge = (t == 0) if edge == 0 else (t == T - 1)
        inner_base = row_prev if edge == 0 else row_next
        own_row = 0 if edge == 0 else R - 1
        for f in range(6):
            value = ep[f, edge]
            f2, e2 = value // 4, value % 4
            far_low = e2 < 2
            reverse = far_low if edge < 2 else e2 >= 2
            is_col = (e2 % 2) == 1
            same = e2 == edge
            row_base = jnp.where(same, (f2 * R + own_row) * F, wrap + f2 * F)
            lin_base = row_base + jnp.where(reverse, F - 1, 0)
            lin_step = jnp.where(reverse, -1, 1)
            k0 = jnp.where(reverse, T - 1, 0)
            ks = jnp.where(reverse, -1, 1)
            if edge == 2:
                k0 = T - 1 - k0
                ks = -ks
            col_base = dm.o_msg + k0 * dm.BASE + f * dm.SLOT + R + 2 + jnp.where(reverse, R - 1, 0)
            base = jnp.where(is_col, col_base, lin_base)
            sj = jnp.where(is_col, 0, lin_step)
            st = jnp.where(is_col, ks * dm.BASE, 0)
            sr = jnp.where(is_col, jnp.where(reverse, -1, 1), 0)
            base = jnp.where(at_edge, base, inner_base + f * F)
            sj = jnp.where(at_edge, sj, 1)
            st = jnp.where(at_edge, st, 0)
            sr = jnp.where(at_edge, sr, 0)
            target = base + sj * j + st * jt + sr * jr
            far_tile = T - 1 if edge == 0 else 0
            from_mirror = is_col & at_edge & (jnp.where(reverse, T - 1 - jt, jt) == far_tile)
            side = jnp.where(e2 == 1, 1, 0)
            cells = mirror + f2 * dm.SLOT + side + 2 * jnp.where(reverse, R - 1 - jr, jr)
            parts.append(jnp.where(from_mirror, cells, target))
    return jnp.concatenate(parts, axis=0)


def gather_ghosts(dm, ep, t, own, messages, table_ref):
    hot = one_hot(ghost_targets(dm, ep, t), dm.NT)
    out = []
    for which in range(2):
        table_ref[0 : dm.N] = own[which]
        for k in range(dm.T):
            at = dm.o_msg + k * dm.BASE
            table_ref[at : at + dm.BASE] = messages[k][which, : dm.BASE]
        table_ref[dm.o_row : dm.o_row + dm.ROW] = messages[1][which, dm.BASE :]
        table_ref[dm.o_row + dm.ROW :] = messages[dm.T - 1][which, dm.BASE :]
        out.append(jnp.dot(hot, table_ref[...], preferred_element_type=F32))
    return out


def own_first(value, p):
    half = value.shape[1] // 2
    low, high = value[:, :half], value[:, half:]
    return jnp.concatenate([jnp.where(p == 0, low, high), jnp.where(p == 0, high, low)], axis=1)


def build_taps(dm, field_ref, ghosts, top, bottom, frame_ref, taps_ref, adjoint, p=None):
    R, F, C = dm.R, dm.F, dm.C
    for f in range(6):
        for r in range(R):
            frame_ref[r + 1, f, 8 : 8 + F] = field_ref[f * R + r].astype(F32)
    frame_ref[0, :, 8 : 8 + F] = top.reshape(6, F, C)
    frame_ref[R + 1, :, 8 : 8 + F] = bottom.reshape(6, F, C)
    for m in range(R + 2):
        for f in range(6):
            if ghosts is None:
                west = jnp.zeros((1, C), F32)
                east = west
            else:
                west = ghosts[16 * f + m : 16 * f + m + 1]
                east = ghosts[16 * f + 8 + m : 16 * f + 8 + m + 1]
            frame_ref[m, f, 7:8] = west
            frame_ref[m, f, 8 + F : 9 + F] = east
    for m in range(R + 2):
        for b in range(3):
            plane = frame_ref[m, :, 7 + b : 7 + b + F].reshape(dm.ROW, C)
            if p is not None:
                plane = own_first(plane, p)
            plane = plane.astype(BF)
            for a in range(3):
                r = m - 2 + a if adjoint else m - a
                tap = 3 * a + (2 - b if adjoint else b)
                if 0 <= r < R:
                    taps_ref[r * dm.ROW : (r + 1) * dm.ROW, tap * C : (tap + 1) * C] = plane


def build_strip_terms(dm, ep, t, ghosts, top, bottom, z_ref):
    R, F = dm.R, dm.F
    z_ref[...] = jnp.zeros(z_ref.shape, F32)

    def tap_of(f, edge, shift):
        e2 = ep[f, edge] % 4
        reverse = e2 < 2 if edge < 2 else e2 >= 2
        along = 1 - jnp.where(reverse, -shift, shift)
        return jnp.where(
            e2 == 0, along, jnp.where(e2 == 2, 6 + along, jnp.where(e2 == 1, 3 * along + 2, 3 * along))
        )

    live = lax.rem(lax.broadcasted_iota(jnp.int32, (dm.WE, 1), 0), 8) < R
    for shift in (-1, 0, 1):
        moved = pltpu.roll(ghosts, (dm.WE - 1 - shift) % dm.WE, 0) if shift > -1 else ghosts
        moved = jnp.where(live, moved, 0.0)
        for f in range(6):
            for side, edge in ((0, 3), (1, 1)):
                at = 16 * f + 8 * side
                z_ref[tap_of(f, edge, shift), at : at + 8] = moved[at : at + 8]

    def add_rows(edge, rows):
        j = lax.rem(lax.broadcasted_iota(jnp.int32, (dm.ROW, 1), 0), F)
        for shift in (-1, 0, 1):
            if shift == 0:
                moved = rows
            else:
                moved = pltpu.roll(rows, (-shift) % dm.ROW, 0)
                moved = jnp.where((j + shift >= 0) & (j + shift < F), moved, 0.0)
            for f in range(6):
                at = dm.WE + F * f
                z_ref[tap_of(f, edge, shift), at : at + F] = moved[F * f : F * (f + 1)]

    @pl.when(t == 0)
    def _():
        add_rows(0, top)

    @pl.when(t == dm.T - 1)
    def _():
        add_rows(2, bottom)


def adjoint(dm, t, taps_ref, z_ref, wt_ref, acc_ref):
    R, F, C, N = dm.R, dm.F, dm.C, dm.N
    for tap in range(9):
        taps_ref[N:, tap * C : (tap + 1) * C] = z_ref[tap].astype(BF)
    total = jnp.dot(taps_ref[...], wt_ref[...], preferred_element_type=F32)
    acc_ref[...] = total[:N]
    strips = total[N:]
    for f in range(6):
        for side in range(2):
            for r in range(R):
                at = (r * 6 + f) * F + side * (F - 1)
                row = 16 * f + 8 * side + r
                acc_ref[at : at + 1] += strips[row : row + 1]

    @pl.when(t == 0)
    def _():
        acc_ref[0 : dm.ROW] += strips[dm.WE :]

    @pl.when(t == dm.T - 1)
    def _():
        acc_ref[(R - 1) * dm.ROW : R * dm.ROW] += strips[dm.WE :]


def turn_kernel(w1_ref, w2_ref, w1s_ref, w1t_ref, w2t_ref):
    p = lax.axis_index("dp")
    half = w1_ref.shape[1] // 2
    for tap in range(9):
        w1t_ref[tap] = w1_ref[tap].T
        w2t_ref[tap] = w2_ref[tap].T
        w1s_ref[tap, :half] = w1_ref[tap, pl.ds(pl.multiple_of(p * half, half), half)]
        w1s_ref[tap, half:] = w1_ref[tap, pl.ds(pl.multiple_of((1 - p) * half, half), half)]


def put_taps(send_ref, keep_ref, first_tap, value):
    half = keep_ref.shape[1]
    for i in range(value.shape[0] // (2 * half)):
        keep_ref[first_tap + i] = value[2 * i * half : (2 * i + 1) * half]
        send_ref[first_tap + i] = value[(2 * i + 1) * half : (2 * i + 2) * half].astype(BF)


def high_low(row):
    i = lax.broadcasted_iota(jnp.int32, (EXTRA, row.shape[1]), 0)
    high = row.astype(BF).astype(F32)
    return jnp.where(i == 0, high, jnp.where(i == 1, row - high, 0.0)).astype(BF)


def both(pair):
    return pair[0:1].astype(F32) + pair[1:2].astype(F32)


def first_kernel(dm, ep, x_ref, up_ref, w1_ref, bias_ref, w2t_ref, *refs):
    T, R, F, N, C = dm.T, dm.R, dm.F, dm.N, dm.C
    messages = refs[:T]
    send1_ref, keep1_ref, send2_ref, keep2_ref, hid_ref, inner_ref, bias_sum_ref, send_bias_ref = refs[T : T + 8]
    out_messages = refs[T + 8 : 2 * T + 8]
    table_ref, frame_ref, xs_ref, us_ref, z_ref, before_ref, acc_ref, hcat_ref = refs[2 * T + 8 :]
    t, p = lax.axis_index("tile"), lax.axis_index("dp")
    own = (x_ref[...].reshape(N, C), up_ref[...].reshape(N, C))
    gx, gu = gather_ghosts(dm, ep, t, own, messages, table_ref)
    top, bottom = dm.WE, dm.WE + dm.ROW
    build_taps(dm, x_ref, gx[:top], gx[top:bottom], gx[bottom:], frame_ref, xs_ref, False, p)
    before = jnp.dot(xs_ref[...], w1_ref[...], preferred_element_type=F32) + bias_ref[...]
    before_ref[...] = before
    sig = 1.0 / (1.0 + jnp.exp(-before))
    acc_ref[...] = before * sig
    up_top = jnp.where(t == 0, 0.0, gu[top:bottom])
    up_bottom = jnp.where(t == T - 1, 0.0, gu[bottom:])
    build_taps(dm, up_ref, None, up_top, up_bottom, frame_ref, us_ref, True)
    build_strip_terms(dm, ep, t, gu[:top], gu[top:bottom], gu[bottom:], z_ref)
    hcat_ref[0:N] = acc_ref[...]
    hcat_ref[N:] = jnp.zeros((dm.S, C), F32)
    for f in range(6):
        for side in range(2):
            for r in range(R):
                at = (r * 6 + f) * F + side * (F - 1)
                row = N + 16 * f + 8 * side + r
                hcat_ref[row : row + 1] = acc_ref[at : at + 1]
    first_row = acc_ref[0 : dm.ROW]
    last_row = acc_ref[(R - 1) * dm.ROW : R * dm.ROW]
    hcat_ref[N + dm.WE :] = jnp.where(t == 0, first_row, last_row)
    for r in range(R):
        for f in range(6):
            at = (r * 6 + f) * F
            hid_ref[f * R + r] = acc_ref[at : at + F].astype(BF)
    adjoint(dm, t, us_ref, z_ref, w2t_ref, acc_ref)
    hidden_t = own_first(hcat_ref[...], p).astype(BF).T
    for tap in range(9):
        grad = jnp.dot(hidden_t, us_ref[:, tap * C : (tap + 1) * C], preferred_element_type=F32)
        put_taps(send2_ref, keep2_ref, tap, grad)
    before = before_ref[...]
    sig = 1.0 / (1.0 + jnp.exp(-before))
    before_grad = acc_ref[...] * (sig * (1.0 + before * (1.0 - sig)))
    acc_ref[...] = before_grad
    inner = before_grad.astype(BF)
    for tap in (0, 3, 6):
        grad = lax.dot_general(
            xs_ref[:, tap * C : (tap + 3) * C],
            inner,
            (((0,), (0,)), ((), ())),
            preferred_element_type=F32,
        )
        put_taps(send1_ref, keep1_ref, tap, grad)
    bias_sum = jnp.sum(before_grad, axis=0, keepdims=True)
    bias_sum_ref[...] = bias_sum
    send_bias_ref[...] = high_low(bias_sum)
    for r in range(R):
        for f in range(6):
            at = (r * 6 + f) * F
            inner_ref[f * R + r] = acc_ref[at : at + F].astype(BF)
    write_messages(
        dm, ep, t, (hid_ref[...].reshape(N, C), inner_ref[...].reshape(N, C)), out_messages
    )


def second_kernel(dm, ep, x_ref, d_ref, hid_ref, inner_ref, w1t_ref, w2_ref, *refs):
    T, R, F, N, C = dm.T, dm.R, dm.F, dm.N, dm.C
    messages = refs[:T]
    state_ref, grad_ref = refs[T : T + 2]
    table_ref, frame_ref, hs_ref, is_ref, z_ref, acc_ref = refs[T + 2 :]
    t = lax.axis_index("tile")
    own = (hid_ref[...].reshape(N, C), inner_ref[...].reshape(N, C))
    gh, gi = gather_ghosts(dm, ep, t, own, messages, table_ref)
    top, bottom = dm.WE, dm.WE + dm.ROW
    build_taps(dm, hid_ref, gh[:top], gh[top:bottom], gh[bottom:], frame_ref, hs_ref, False)
    acc_ref[...] = jnp.dot(hs_ref[...], w2_ref[...], preferred_element_type=F32)
    for r in range(R):
        for f in range(6):
            at = (r * 6 + f) * F
            value = x_ref[f * R + r].astype(F32) + acc_ref[at : at + F]
            state_ref[f * R + r] = value.astype(BF)
    in_top = jnp.where(t == 0, 0.0, gi[top:bottom])
    in_bottom = jnp.where(t == T - 1, 0.0, gi[bottom:])
    build_taps(dm, inner_ref, None, in_top, in_bottom, frame_ref, is_ref, True)
    build_strip_terms(dm, ep, t, gi[:top], gi[top:bottom], gi[bottom:], z_ref)
    adjoint(dm, t, is_ref, z_ref, w1t_ref, acc_ref)
    for r in range(R):
        for f in range(6):
            at = (r * 6 + f) * F
            grad_ref[f * R + r] = d_ref[f * R + r].astype(F32) + acc_ref[at : at + F]


def half_kernel(zcount, keep_ref, recv_ref, *refs):
    size = keep_ref.shape[1] // 2
    own = lax.axis_index("tile") % 2
    mine = pl.ds(pl.multiple_of(own * size, size), size)
    far = pl.ds(pl.multiple_of((1 - own) * size, size), size)
    part = size // zcount
    if len(refs) > 2:
        bias_ref, recv_bias_ref, out_keep, out_send, out_bias = refs
        bias = bias_ref[...] + both(recv_bias_ref)
        out_bias[...] = bias
        out_send[9 * size :] = high_low(bias)
    else:
        out_keep, out_send = refs
    for tap in range(9):
        kept = keep_ref[tap, mine] + recv_ref[tap, mine].astype(F32)
        sent = keep_ref[tap, far] + recv_ref[tap, far].astype(F32)
        for j in range(zcount):
            at = j * 9 * part + tap * part
            out_keep[j, tap * part : (tap + 1) * part] = kept[j * part : (j + 1) * part]
            out_send[at : at + part] = sent[j * part : (j + 1) * part].astype(BF)


def block_kernel(zcount, keep_ref, recv_ref, *refs):
    own = lax.axis_index("tile") // 2
    n = keep_ref.shape[1]
    if len(refs) > zcount + 1:
        bias_ref, out_keep, *out_sends, out_bias, sum_ref = refs
        bias = bias_ref[...] + both(recv_ref[zcount * n : zcount * n + 2])
        out_bias[...] = bias
        tail = high_low(bias)
    else:
        out_keep, *out_sends, sum_ref = refs
        tail = None
    for j in range(zcount):
        sum_ref[j] = keep_ref[j] + recv_ref[j * n : (j + 1) * n].astype(F32)
    out_keep[...] = sum_ref[own]
    for j in range(1, zcount):
        out_sends[j - 1][0:n] = sum_ref[own ^ j].astype(BF)
        if tail is not None:
            out_sends[j - 1][n:] = tail


def last_kernel(zcount, keep_ref, *refs):
    recvs = refs[: zcount - 1]
    n = keep_ref.shape[0]
    total = keep_ref[...]
    for ref in recvs:
        total = total + ref[0:n].astype(F32)
    if len(refs) > zcount:
        bias_ref, block_ref, out_bias = refs[zcount - 1 :]
        bias = bias_ref[...]
        for ref in recvs:
            bias = bias + both(ref[n : n + 2])
        out_bias[...] = bias
    else:
        block_ref = refs[-1]
    block_ref[...] = total.astype(BF)


def normal_kernel(zcount, *refs):
    sources, out_ref = refs[:4], refs[4]
    if len(refs) > 5:
        bias_ref, out_ref, out_bias = refs[4:]
        bias = bias_ref[...]
        bias_mean = jnp.mean(bias * bias, keepdims=True)
        out_bias[...] = bias * lax.rsqrt(bias_mean + 1e-06)
    t, p = lax.axis_index("tile"), lax.axis_index("dp")
    n = sources[0].shape[0] // zcount
    size = n // 9
    square = None
    for ref in sources:
        for j in range(zcount):
            v = ref[j * n : (j + 1) * n].astype(F32)
            part = jnp.sum(v * v, axis=0, keepdims=True)
            square = part if square is None else square + part
    mean = jnp.sum(square, keepdims=True) / (9 * out_ref.shape[1] * out_ref.shape[2])
    scale = lax.rsqrt(mean + 1e-06)
    for group, ref in enumerate(sources):
        block = (p ^ (group // 2)) * 2 + ((t % 2) ^ (group % 2))
        for j in range(zcount):
            at = pl.ds(pl.multiple_of((block * zcount + ((t // 2) ^ j)) * size, size), size)
            for tap in range(9):
                row = j * n + tap * size
                out_ref[tap, at] = ref[row : row + size].astype(F32) * scale


def call(kernel, out_shapes, scratch=(), smem_first=False, limit=16):
    def run(*args):
        vmem = pl.BlockSpec(memory_space=pltpu.VMEM)
        smem = pl.BlockSpec(memory_space=pltpu.SMEM)
        specs = [smem if smem_first and i == 0 else vmem for i in range(len(args))]
        return pl.pallas_call(
            kernel,
            out_shape=[jax.ShapeDtypeStruct(s, dt) for s, dt in out_shapes],
            in_specs=specs,
            out_specs=[vmem] * len(out_shapes),
            scratch_shapes=[pltpu.VMEM(s, dt) for s, dt in scratch],
            compiler_params=pltpu.CompilerParams(vmem_limit_bytes=limit << 20),
        )(*args)

    return run


def swap_dp(v):
    count = lax.axis_size("dp")
    return lax.ppermute(v, "dp", [(i, count - 1 - i) for i in range(count)])


def on_device(initial_state, state_cotangents, w_first, bias, w_second, edge_partner):
    tiles = lax.axis_size("tile")
    _, _, rows, face, channels = initial_state.shape
    dm = Dims(rows, face, tiles, channels)
    planes = (6 * rows, face, channels)
    x = initial_state.reshape(planes)
    d = state_cotangents[state_cotangents.shape[0] - 1].reshape(planes)
    taps = (9, channels, channels)
    w1 = w_first.reshape(9 * channels, channels)
    w2 = w_second.reshape(9 * channels, channels)
    w1s, w1t, w2t = call(turn_kernel, [(taps, BF)] * 3)(w_first.reshape(taps), w_second.reshape(taps))
    w1s = w1s.reshape(w1.shape)
    w1t = w1t.reshape(w1.shape)
    w2t = w2t.reshape(w2.shape)
    msg_shapes = [(shape, BF) for shape in dm.messages()]
    flat = (dm.N, channels)
    messages = call(functools.partial(pack_kernel, dm), msg_shapes, smem_first=True)(
        edge_partner, x.reshape(flat), d.reshape(flat)
    )
    pairs = dm.pairs()

    def send_message(messages, k):
        return messages[k] if k == 0 else lax.ppermute(messages[k], "tile", pairs[k])

    messages = [send_message(messages, k) for k in range(tiles)]
    half = channels // 2
    wide = 9 * channels
    frame = (rows + 2, 6, face + 16, channels)
    outs = call(
        functools.partial(first_kernel, dm),
        [
            ((9, half, channels), BF),
            ((9, half, channels), F32),
            ((9, half, channels), BF),
            ((9, half, channels), F32),
            (planes, BF),
            (planes, BF),
            ((1, channels), F32),
            ((EXTRA, channels), BF),
        ]
        + msg_shapes,
        [
            ((dm.NT, channels), BF),
            (frame, F32),
            ((dm.N, wide), BF),
            ((dm.N + dm.S, wide), BF),
            ((9, dm.S, channels), F32),
            (flat, F32),
            (flat, F32),
            ((dm.N + dm.S, channels), F32),
        ],
        smem_first=True,
        limit=LIMIT,
    )(edge_partner, x, d, w1s, bias.reshape(1, channels), w2t, *messages)
    send1, keep1, send2, keep2, hidden, inner, bias_sum, send_bias = outs[:8]
    packed = list(outs[8:])

    zcount = tiles // 2
    n = 9 * half // tiles
    one = ((1, channels), F32)
    barrier = lax.optimization_barrier

    def along_y(v):
        return lax.ppermute(v, "tile", [(i, i ^ 1) for i in range(tiles)])

    def along_z(v, j):
        return lax.ppermute(v, "tile", [(i, i ^ (2 * j)) for i in range(tiles)])

    def sum_dp(keep, recv, *bias):
        extra = EXTRA if bias else 0
        return call(
            functools.partial(half_kernel, zcount),
            [((zcount, n, channels), F32), ((zcount * n + extra, channels), BF)] + [one] * bool(bias),
        )(keep, recv, *bias)

    def sum_y(keep, recv, *bias):
        extra = EXTRA if bias else 0
        keep, *out = call(
            functools.partial(block_kernel, zcount),
            [((n, channels), F32)] + [((n + extra, channels), BF)] * (zcount - 1) + [one] * bool(bias),
            [((zcount, n, channels), F32)],
        )(keep, recv, *bias)
        return keep, out[: zcount - 1], out[zcount - 1 :]

    def sum_z(keep, recvs, *bias):
        return call(
            functools.partial(last_kernel, zcount), [((n, channels), BF)] + [one] * bool(bias)
        )(keep, *recvs, *bias)

    early = [k for k in range(2, tiles - 1) if k % 2 == 0]
    middle = [k for k in range(1, tiles - 1) if k % 2 == 1]
    messages = list(packed)

    keep2, send2 = sum_dp(keep2, swap_dp(send2))
    recv2 = along_y(send2)
    keep1, send1, bias_sum = sum_dp(keep1, swap_dp(send1), bias_sum, swap_dp(send_bias))
    recv1 = along_y(send1)
    got = [lax.ppermute(packed[k], "tile", pairs[k]) for k in early]

    keep2, sends2, _ = sum_y(keep2, recv2)
    recvs2 = [along_z(v, j + 1) for j, v in enumerate(sends2)]
    recv1, got = barrier((recv1, got))
    for k, v in zip(early, got):
        messages[k] = v

    keep1, sends1, (bias_sum,) = sum_y(keep1, recv1, bias_sum)
    sends1, todo = barrier((sends1, [packed[k] for k in middle]))
    recvs1 = [along_z(v, j + 1) for j, v in enumerate(sends1)]
    got = [lax.ppermute(v, "tile", pairs[k]) for k, v in zip(middle, todo)]

    (own2,) = sum_z(keep2, recvs2)
    own2 = [own2] + [along_z(own2, j) for j in range(1, zcount)]
    recvs1, got = barrier((recvs1, got))
    for k, v in zip(middle, got):
        messages[k] = v

    own1, bias_sum = sum_z(keep1, recvs1, bias_sum)
    own1, last = barrier((own1, packed[tiles - 1]))
    own1 = [own1] + [along_z(own1, j) for j in range(1, zcount)]
    last = lax.ppermute(last, "tile", pairs[tiles - 1])
    own2 = jnp.concatenate(own2, axis=0)
    other2 = along_y(own2)
    own1[-1], messages[tiles - 1] = barrier((own1[-1], last))
    own1 = jnp.concatenate(own1, axis=0)
    other1 = along_y(own1)
    own1, messages = barrier((own1, messages))
    state, grad = call(
        functools.partial(second_kernel, dm),
        [(planes, BF), (planes, F32)],
        [
            ((dm.NT, channels), BF),
            (frame, F32),
            ((dm.N, wide), BF),
            ((dm.N + dm.S, wide), BF),
            ((9, dm.S, channels), F32),
            (flat, F32),
        ],
        smem_first=True,
        limit=LIMIT,
    )(edge_partner, x, d, hidden, inner, w1t, w2, *messages)
    other1, state, grad = barrier((other1, state, grad))
    (second_step,) = call(functools.partial(normal_kernel, zcount), [(taps, F32)])(
        own2, other2, swap_dp(own2), swap_dp(other2)
    )
    first_step, bias_step = call(functools.partial(normal_kernel, zcount), [(taps, F32), one])(
        own1, other1, swap_dp(own1), swap_dp(other1), bias_sum
    )
    return (
        state.reshape(initial_state.shape),
        grad.reshape(initial_state.shape),
        first_step.reshape(w_first.shape),
        bias_step.reshape(channels),
        second_step.reshape(w_second.shape),
    )


def solution(mesh):
    return jax.shard_map(
        on_device,
        mesh=mesh,
        in_specs=(
            P(("groups", "dp"), None, "tile", None, None),
            P(None, ("groups", "dp"), None, "tile", None, None),
            P(),
            P(),
            P(),
            P(),
        ),
        out_specs=(
            P(("groups", "dp"), None, "tile", None, None),
            P(("groups", "dp"), None, "tile", None, None),
            P("groups", None, None, None),
            P("groups"),
            P("groups", None, None, None),
        ),
        check_vma=False,
    )
```

```python
import functools

import jax
import jax.numpy as jnp
from jax import lax
from jax.experimental import pallas as pl
from jax.experimental.pallas import tpu as pltpu
from jax.sharding import PartitionSpec as P

BF = jnp.bfloat16
F32 = jnp.float32
EXTRA = 8
LIMIT = 24


class Dims:
    def __init__(self, rows, face, tiles, channels):
        self.R, self.F, self.T, self.C = rows, face, tiles, channels
        self.N = 6 * rows * face
        self.ROW = 6 * face
        self.SLOT = -(-(2 * rows + 2) // 8) * 8
        self.BASE = 6 * self.SLOT
        self.MIX = tiles // 2 - 1
        self.o_msg = self.N
        self.o_row = self.o_msg + tiles * self.BASE
        self.NT = self.o_row + 2 * self.ROW
        self.WE = 12 * 8
        self.S = self.WE + self.ROW

    def partner(self, t, k):
        if k == self.MIX:
            ends = (t == 0) | (t == self.MIX) | (t == self.MIX + 1) | (t == self.T - 1)
            return jnp.where(ends, t ^ k, self.T - 1 - t)
        return t ^ k

    def steps(self):
        rest = [k for k in range(2, self.T - 1)]
        evens = [k for k in rest if k % 2 == 0]
        odds = [k for k in rest if k % 2 == 1]
        rest = evens + odds
        if len(rest) % 2:
            rest = rest[:-1] + [None, rest[-1]]
        return [(1, self.T - 1)] + [(rest[i], rest[i + 1]) for i in range(0, len(rest), 2)]

    def rows(self, step):
        return self.BASE + (self.ROW if step == 0 else 0)

    def pairs(self):
        T, mix = self.T, self.MIX

        def needed(i, d):
            return i in (0, T - 1) or d in (0, T - 1) or d in (T - 2 - i, T - i)

        out = [[(i, i ^ k) for i in range(T) if k == 1 or needed(i, i ^ k)] for k in range(T - 1)]
        out[mix] = [(i, i ^ mix if i in (0, mix, mix + 1, T - 1) else T - 1 - i) for i in range(T)]
        out.append([(i, (i + 1) % T if i % 2 else (i - 1) % T) for i in range(T)])
        return [
            [(2 * i + core, 2 * d + core) for core in range(2) if ks[core] is not None for i, d in out[ks[core]]]
            for ks in self.steps()
        ]


def col_iota(n):
    return lax.broadcasted_iota(jnp.int32, (n, 1), 0)


def one_hot(target, width):
    lanes = lax.broadcasted_iota(jnp.int32, (target.shape[0], width), 1)
    return jnp.where(lanes == target, 1.0, 0.0).astype(BF)


def strip_targets(dm, ep, t, d):
    R, F, T = dm.R, dm.F, dm.T
    at_edge = (t == 0) | (t == T - 1)
    to_edge = (d == 0) | (d == T - 1)
    own_edge = jnp.where(t == 0, 0, 2)
    far_edge = jnp.where(d == 0, 0, 2)
    side_row = jnp.where(d == T - 2 - t, R - 1, 0)
    i = col_iota(dm.SLOT)
    q = R * d - 1 + i
    inside = (q >= 0) & (q < F) & (i < R + 2)
    i2 = i - (R + 2)
    parts = []
    for f in range(6):
        far_low = (ep[f, own_edge] % 4) < 2
        reverse = far_low == (t == 0)
        p0 = jnp.where(reverse, F - 1, 0)
        sgn = jnp.where(reverse, -1, 1)
        row = jnp.where(t == 0, 0, R - 1)
        strip = jnp.where(inside, (f * R + row) * F + p0 + sgn * q, -1)
        sides = (f * R + side_row) * F
        low = jnp.where(at_edge, strip, sides + i * (F - 1))
        low = jnp.where(at_edge | (i < 2), low, -1)
        gvalue = ep[f, far_edge]
        column = jnp.where(gvalue % 4 == 1, F - 1, 0) + (gvalue // 4) * (R * F)
        high = jnp.where(to_edge, column + F * i2, jnp.where(i2 < 2, sides + i2 * (F - 1), -1))
        strips = jnp.where(i2 < 0, low, jnp.where(i2 < R, high, -1))
        parts.append(jnp.where(d == T - 1 - t, mirror_slot(dm, f), strips))
    return parts


def mirror_slot(dm, f):
    i = col_iota(dm.SLOT)
    return jnp.where(i < 2 * dm.R, (f * dm.R + i // 2) * dm.F + (i % 2) * (dm.F - 1), -1)


def row_targets(dm, row):
    j = col_iota(dm.F)
    return [(f * dm.R + row) * dm.F + j for f in range(6)]


def write_messages(dm, ep, t, p, sources, refs):
    R = dm.R
    steps = dm.steps()
    for other in range(2):
        core = p ^ other
        for step, ks in enumerate(steps):
            if step == 0:
                strips = strip_targets(dm, ep, t, t ^ 1)
                parts = [jnp.where(core == 0, strips[f], mirror_slot(dm, f)) for f in range(6)]
                parts = parts + row_targets(dm, jnp.where((t + core) % 2 == 0, R - 1, 0))
            else:
                ds = [dm.partner(t, k) for k in ks if k is not None]
                parts = strip_targets(dm, ep, t, jnp.where(core == 0, ds[0], ds[-1]))
            hot = one_hot(jnp.concatenate(parts, axis=0), dm.N)
            for which in range(2):
                rows = jnp.dot(hot, sources[which], preferred_element_type=F32).astype(BF)
                refs[other * len(steps) + step][which] = rows


def write_self(dm, ep, t, sources, ref):
    hot = one_hot(jnp.concatenate(strip_targets(dm, ep, t, t), axis=0), dm.N)
    for which in range(2):
        ref[which] = jnp.dot(hot, sources[which], preferred_element_type=F32).astype(BF)


def pack_kernel(dm, ep, x_hbm, up_hbm, *refs):
    *refs, self_ref, x_ref, up_ref, sems = refs
    copies = [
        pltpu.make_async_copy(x_hbm, x_ref, sems.at[0]),
        pltpu.make_async_copy(up_hbm, up_ref, sems.at[1]),
    ]
    for copy in copies:
        copy.start()
    for copy in copies:
        copy.wait()
    t, p = lax.axis_index("tile"), lax.axis_index("dp")
    write_messages(dm, ep, t, p, (x_ref[...], up_ref[...]), refs)
    write_self(dm, ep, t, (x_ref[...], up_ref[...]), self_ref)


def merge_kernel(count, *refs):
    for i in range(count):
        refs[2 * count + i][0] = refs[i][...]
        refs[2 * count + i][1] = refs[count + i][...]


def ghost_targets(dm, ep, t):
    R, F, T = dm.R, dm.F, dm.T
    odd = t % 2
    parts = []
    m = col_iota(8)
    q = R * t - 1 + m
    inside = (q >= 0) & (q < F) & (m < R + 2)
    row_prev = dm.o_row + (1 - odd) * dm.ROW
    row_next = dm.o_row + odd * dm.ROW
    side_first = dm.o_msg + (t ^ (T - t)) * dm.BASE + jnp.where(t == 1, R + 2, 0)
    side_last = dm.o_msg + (t ^ (T - 2 - t)) * dm.BASE + jnp.where(t == T - 2, R + 2, 0)
    ends = (t == 0) | (t == dm.MIX) | (t == dm.MIX + 1) | (t == T - 1)
    mirror = dm.o_msg + jnp.where(ends, T - 1, dm.MIX) * dm.BASE
    for f in range(6):
        for edge in (3, 1):
            value = ep[f, edge]
            f2, e2 = value // 4, value % 4
            far_low = e2 < 2
            reverse = far_low if edge < 2 else e2 >= 2
            is_col = (e2 % 2) == 1
            side = jnp.where(e2 == 1, 1, 0)
            column = side * (F - 1)
            slot = f2 * dm.SLOT + side
            row = dm.o_msg + (t ^ jnp.where(e2 == 0, 0, T - 1)) * dm.BASE + f2 * dm.SLOT
            facing = jnp.where(e2 == 0, t == T - 1, t == 0)
            whole = dm.o_row + dm.ROW + f2 * F + jnp.where(reverse, F - R * t, R * t - 1)
            row = jnp.where(facing, whole, row)
            along = jnp.where(facing & reverse, -1, 1)
            i0 = jnp.where(is_col, jnp.where(reverse, side_first + slot, row_prev + f2 * F + column), row)
            i4 = jnp.where(
                is_col, jnp.where(reverse, side_last + slot, row_next + f2 * F + column), row + along * (R + 1)
            )
            base = jnp.where(
                is_col, jnp.where(reverse, mirror + 2 * R + slot, (f2 * R - 1) * F + column), row
            )
            step = jnp.where(is_col, jnp.where(reverse, -2, F), along)
            target = jnp.where(m == 0, i0, jnp.where(m == R + 1, i4, base + step * m))
            parts.append(jnp.where(inside, target, -1))
    j = col_iota(F)
    jt = jnp.zeros_like(j)
    for b in range(1, T):
        jt = jt + jnp.where(j >= b * R, 1, 0)
    jr = j - R * jt
    wrap = dm.o_row + dm.ROW
    for edge in (0, 2):
        at_edge = (t == 0) if edge == 0 else (t == T - 1)
        inner_base = row_prev if edge == 0 else row_next
        own_row = 0 if edge == 0 else R - 1
        for f in range(6):
            value = ep[f, edge]
            f2, e2 = value // 4, value % 4
            far_low = e2 < 2
            reverse = far_low if edge < 2 else e2 >= 2
            is_col = (e2 % 2) == 1
            same = e2 == edge
            row_base = jnp.where(same, (f2 * R + own_row) * F, wrap + f2 * F)
            lin_base = row_base + jnp.where(reverse, F - 1, 0)
            lin_step = jnp.where(reverse, -1, 1)
            k0 = jnp.where(reverse, T - 1, 0)
            ks = jnp.where(reverse, -1, 1)
            if edge == 2:
                k0 = T - 1 - k0
                ks = -ks
            col_base = dm.o_msg + k0 * dm.BASE + f * dm.SLOT + R + 2 + jnp.where(reverse, R - 1, 0)
            base = jnp.where(is_col, col_base, lin_base)
            sj = jnp.where(is_col, 0, lin_step)
            st = jnp.where(is_col, ks * dm.BASE, 0)
            sr = jnp.where(is_col, jnp.where(reverse, -1, 1), 0)
            base = jnp.where(at_edge, base, inner_base + f * F)
            sj = jnp.where(at_edge, sj, 1)
            st = jnp.where(at_edge, st, 0)
            sr = jnp.where(at_edge, sr, 0)
            target = base + sj * j + st * jt + sr * jr
            far_tile = T - 1 if edge == 0 else 0
            from_mirror = is_col & at_edge & (jnp.where(reverse, T - 1 - jt, jt) == far_tile)
            side = jnp.where(e2 == 1, 1, 0)
            cells = mirror + f2 * dm.SLOT + side + 2 * jnp.where(reverse, R - 1 - jr, jr)
            parts.append(jnp.where(from_mirror, cells, target))
    return jnp.concatenate(parts, axis=0)


def gather_ghosts(dm, ep, t, p, own, messages, table_ref):
    hot = one_hot(ghost_targets(dm, ep, t), dm.NT)
    out = []
    for which in range(2):
        table_ref[0 : dm.N] = own[which]
        table_ref[dm.o_msg : dm.o_msg + dm.BASE] = messages[-1][which]
        for step, ks in enumerate(dm.steps()):
            here = messages[2 * step][0, which].astype(F32)
            there = messages[2 * step + 1][1, which].astype(F32)
            for core, k in enumerate(ks):
                if k is None:
                    continue
                value = jnp.where(p == core, here, there).astype(BF)
                at = dm.o_msg + k * dm.BASE
                table_ref[at : at + dm.BASE] = value[: dm.BASE]
                if step == 0:
                    at = dm.o_row + core * dm.ROW
                    table_ref[at : at + dm.ROW] = value[dm.BASE :]
        out.append(jnp.dot(hot, table_ref[...], preferred_element_type=F32))
    return out


def own_first(value, p):
    half = value.shape[1] // 2
    low, high = value[:, :half], value[:, half:]
    return jnp.concatenate([jnp.where(p == 0, low, high), jnp.where(p == 0, high, low)], axis=1)


def build_taps(dm, field_ref, ghosts, top, bottom, frame_ref, taps_ref, adjoint, p=None):
    R, F, C = dm.R, dm.F, dm.C
    for f in range(6):
        for r in range(R):
            frame_ref[r + 1, f, 8 : 8 + F] = field_ref[f * R + r].astype(F32)
    frame_ref[0, :, 8 : 8 + F] = top.reshape(6, F, C)
    frame_ref[R + 1, :, 8 : 8 + F] = bottom.reshape(6, F, C)
    for m in range(R + 2):
        for f in range(6):
            if ghosts is None:
                west = jnp.zeros((1, C), F32)
                east = west
            else:
                west = ghosts[16 * f + m : 16 * f + m + 1]
                east = ghosts[16 * f + 8 + m : 16 * f + 8 + m + 1]
            frame_ref[m, f, 7:8] = west
            frame_ref[m, f, 8 + F : 9 + F] = east
    for m in range(R + 2):
        for b in range(3):
            plane = frame_ref[m, :, 7 + b : 7 + b + F].reshape(dm.ROW, C)
            if p is not None:
                plane = own_first(plane, p)
            plane = plane.astype(BF)
            for a in range(3):
                r = m - 2 + a if adjoint else m - a
                tap = 3 * a + (2 - b if adjoint else b)
                if 0 <= r < R:
                    taps_ref[r * dm.ROW : (r + 1) * dm.ROW, tap * C : (tap + 1) * C] = plane


def build_strip_terms(dm, ep, t, ghosts, top, bottom, z_ref):
    R, F = dm.R, dm.F
    z_ref[...] = jnp.zeros(z_ref.shape, F32)

    def tap_of(f, edge, shift):
        e2 = ep[f, edge] % 4
        reverse = e2 < 2 if edge < 2 else e2 >= 2
        along = 1 - jnp.where(reverse, -shift, shift)
        return jnp.where(
            e2 == 0, along, jnp.where(e2 == 2, 6 + along, jnp.where(e2 == 1, 3 * along + 2, 3 * along))
        )

    live = lax.rem(lax.broadcasted_iota(jnp.int32, (dm.WE, 1), 0), 8) < R
    for shift in (-1, 0, 1):
        moved = pltpu.roll(ghosts, (dm.WE - 1 - shift) % dm.WE, 0) if shift > -1 else ghosts
        moved = jnp.where(live, moved, 0.0)
        for f in range(6):
            for side, edge in ((0, 3), (1, 1)):
                at = 16 * f + 8 * side
                z_ref[tap_of(f, edge, shift), at : at + 8] = moved[at : at + 8]

    def add_rows(edge, rows):
        j = lax.rem(lax.broadcasted_iota(jnp.int32, (dm.ROW, 1), 0), F)
        for shift in (-1, 0, 1):
            if shift == 0:
                moved = rows
            else:
                moved = pltpu.roll(rows, (-shift) % dm.ROW, 0)
                moved = jnp.where((j + shift >= 0) & (j + shift < F), moved, 0.0)
            for f in range(6):
                at = dm.WE + F * f
                z_ref[tap_of(f, edge, shift), at : at + F] = moved[F * f : F * (f + 1)]

    @pl.when(t == 0)
    def _():
        add_rows(0, top)

    @pl.when(t == dm.T - 1)
    def _():
        add_rows(2, bottom)


def adjoint(dm, t, taps_ref, z_ref, wt_ref, acc_ref):
    R, F, C, N = dm.R, dm.F, dm.C, dm.N
    for tap in range(9):
        taps_ref[N:, tap * C : (tap + 1) * C] = z_ref[tap].astype(BF)
    total = jnp.dot(taps_ref[...], wt_ref[...], preferred_element_type=F32)
    acc_ref[...] = total[:N]
    strips = total[N:]
    for f in range(6):
        for side in range(2):
            for r in range(R):
                at = (r * 6 + f) * F + side * (F - 1)
                row = 16 * f + 8 * side + r
                acc_ref[at : at + 1] += strips[row : row + 1]

    @pl.when(t == 0)
    def _():
        acc_ref[0 : dm.ROW] += strips[dm.WE :]

    @pl.when(t == dm.T - 1)
    def _():
        acc_ref[(R - 1) * dm.ROW : R * dm.ROW] += strips[dm.WE :]


def turn_kernel(w1_ref, w2_ref, w1s_ref, w1t_ref, w2t_ref):
    p = lax.axis_index("dp")
    half = w1_ref.shape[1] // 2
    for tap in range(9):
        w1t_ref[tap] = w1_ref[tap].T
        w2t_ref[tap] = w2_ref[tap].T
        w1s_ref[tap, :half] = w1_ref[tap, pl.ds(pl.multiple_of(p * half, half), half)]
        w1s_ref[tap, half:] = w1_ref[tap, pl.ds(pl.multiple_of((1 - p) * half, half), half)]


def put_taps(send_ref, keep_ref, first_tap, value):
    half = keep_ref.shape[1]
    for i in range(value.shape[0] // (2 * half)):
        keep_ref[first_tap + i] = value[2 * i * half : (2 * i + 1) * half]
        send_ref[first_tap + i] = value[(2 * i + 1) * half : (2 * i + 2) * half].astype(BF)


def high_low(row):
    i = lax.broadcasted_iota(jnp.int32, (EXTRA, row.shape[1]), 0)
    high = row.astype(BF).astype(F32)
    return jnp.where(i == 0, high, jnp.where(i == 1, row - high, 0.0)).astype(BF)


def both(pair):
    return pair[0:1].astype(F32) + pair[1:2].astype(F32)


def first_kernel(dm, ep, x_ref, up_ref, w1_ref, bias_ref, w2t_ref, *refs):
    T, R, F, N, C = dm.T, dm.R, dm.F, dm.N, dm.C
    M = 2 * len(dm.steps())
    messages = refs[: M + 1]
    refs = refs[M + 1 :]
    send1_ref, keep1_ref, send2_ref, keep2_ref, hid_ref, inner_ref, bias_sum_ref, send_bias_ref = refs[:8]
    out_messages, self_ref = refs[8 : M + 8], refs[M + 8]
    table_ref, frame_ref, xs_ref, us_ref, z_ref, before_ref, acc_ref, hcat_ref = refs[M + 9 :]
    t, p = lax.axis_index("tile"), lax.axis_index("dp")
    own = (x_ref[...].reshape(N, C), up_ref[...].reshape(N, C))
    gx, gu = gather_ghosts(dm, ep, t, p, own, messages, table_ref)
    top, bottom = dm.WE, dm.WE + dm.ROW
    build_taps(dm, x_ref, gx[:top], gx[top:bottom], gx[bottom:], frame_ref, xs_ref, False, p)
    before = jnp.dot(xs_ref[...], w1_ref[...], preferred_element_type=F32) + bias_ref[...]
    before_ref[...] = before
    sig = 1.0 / (1.0 + jnp.exp(-before))
    acc_ref[...] = before * sig
    up_top = jnp.where(t == 0, 0.0, gu[top:bottom])
    up_bottom = jnp.where(t == T - 1, 0.0, gu[bottom:])
    build_taps(dm, up_ref, None, up_top, up_bottom, frame_ref, us_ref, True)
    build_strip_terms(dm, ep, t, gu[:top], gu[top:bottom], gu[bottom:], z_ref)
    hcat_ref[0:N] = acc_ref[...]
    hcat_ref[N:] = jnp.zeros((dm.S, C), F32)
    for f in range(6):
        for side in range(2):
            for r in range(R):
                at = (r * 6 + f) * F + side * (F - 1)
                row = N + 16 * f + 8 * side + r
                hcat_ref[row : row + 1] = acc_ref[at : at + 1]
    first_row = acc_ref[0 : dm.ROW]
    last_row = acc_ref[(R - 1) * dm.ROW : R * dm.ROW]
    hcat_ref[N + dm.WE :] = jnp.where(t == 0, first_row, last_row)
    for r in range(R):
        for f in range(6):
            at = (r * 6 + f) * F
            hid_ref[f * R + r] = acc_ref[at : at + F].astype(BF)
    adjoint(dm, t, us_ref, z_ref, w2t_ref, acc_ref)
    hidden_t = own_first(hcat_ref[...], p).astype(BF).T
    for tap in range(9):
        grad = jnp.dot(hidden_t, us_ref[:, tap * C : (tap + 1) * C], preferred_element_type=F32)
        put_taps(send2_ref, keep2_ref, tap, grad)
    before = before_ref[...]
    sig = 1.0 / (1.0 + jnp.exp(-before))
    before_grad = acc_ref[...] * (sig * (1.0 + before * (1.0 - sig)))
    acc_ref[...] = before_grad
    inner = before_grad.astype(BF)
    for tap in (0, 3, 6):
        grad = lax.dot_general(
            xs_ref[:, tap * C : (tap + 3) * C],
            inner,
            (((0,), (0,)), ((), ())),
            preferred_element_type=F32,
        )
        put_taps(send1_ref, keep1_ref, tap, grad)
    bias_sum = jnp.sum(before_grad, axis=0, keepdims=True)
    bias_sum_ref[...] = bias_sum
    send_bias_ref[...] = high_low(bias_sum)
    for r in range(R):
        for f in range(6):
            at = (r * 6 + f) * F
            inner_ref[f * R + r] = acc_ref[at : at + F].astype(BF)
    fields = (hid_ref[...].reshape(N, C), inner_ref[...].reshape(N, C))
    write_messages(dm, ep, t, p, fields, out_messages)
    write_self(dm, ep, t, fields, self_ref)


def second_kernel(dm, ep, x_ref, d_ref, hid_ref, inner_ref, w1t_ref, w2_ref, *refs):
    T, R, F, N, C = dm.T, dm.R, dm.F, dm.N, dm.C
    M = 2 * len(dm.steps()) + 1
    messages = refs[:M]
    state_ref, grad_ref = refs[M : M + 2]
    table_ref, frame_ref, hs_ref, is_ref, z_ref, acc_ref = refs[M + 2 :]
    t, p = lax.axis_index("tile"), lax.axis_index("dp")
    own = (hid_ref[...].reshape(N, C), inner_ref[...].reshape(N, C))
    gh, gi = gather_ghosts(dm, ep, t, p, own, messages, table_ref)
    top, bottom = dm.WE, dm.WE + dm.ROW
    build_taps(dm, hid_ref, gh[:top], gh[top:bottom], gh[bottom:], frame_ref, hs_ref, False)
    acc_ref[...] = jnp.dot(hs_ref[...], w2_ref[...], preferred_element_type=F32)
    for r in range(R):
        for f in range(6):
            at = (r * 6 + f) * F
            value = x_ref[f * R + r].astype(F32) + acc_ref[at : at + F]
            state_ref[f * R + r] = value.astype(BF)
    in_top = jnp.where(t == 0, 0.0, gi[top:bottom])
    in_bottom = jnp.where(t == T - 1, 0.0, gi[bottom:])
    build_taps(dm, inner_ref, None, in_top, in_bottom, frame_ref, is_ref, True)
    build_strip_terms(dm, ep, t, gi[:top], gi[top:bottom], gi[bottom:], z_ref)
    adjoint(dm, t, is_ref, z_ref, w1t_ref, acc_ref)
    for r in range(R):
        for f in range(6):
            at = (r * 6 + f) * F
            grad_ref[f * R + r] = d_ref[f * R + r].astype(F32) + acc_ref[at : at + F]


def half_kernel(zcount, keep_ref, recv_ref, *refs):
    size = keep_ref.shape[1] // 2
    own = lax.axis_index("tile") % 2
    mine = pl.ds(pl.multiple_of(own * size, size), size)
    far = pl.ds(pl.multiple_of((1 - own) * size, size), size)
    part = size // zcount
    if len(refs) > 2:
        bias_ref, recv_bias_ref, out_keep, out_send, out_bias = refs
        bias = bias_ref[...] + both(recv_bias_ref)
        out_bias[...] = bias
        out_send[9 * size :] = high_low(bias)
    else:
        out_keep, out_send = refs
    for tap in range(9):
        kept = keep_ref[tap, mine] + recv_ref[tap, mine].astype(F32)
        sent = keep_ref[tap, far] + recv_ref[tap, far].astype(F32)
        for j in range(zcount):
            at = j * 9 * part + tap * part
            out_keep[j, tap * part : (tap + 1) * part] = kept[j * part : (j + 1) * part]
            out_send[at : at + part] = sent[j * part : (j + 1) * part].astype(BF)


def block_kernel(zcount, keep_ref, recv_ref, *refs):
    own = lax.axis_index("tile") // 2
    n = keep_ref.shape[1]
    if len(refs) > zcount + 1:
        bias_ref, out_keep, *out_sends, out_bias, sum_ref = refs
        bias = bias_ref[...] + both(recv_ref[zcount * n : zcount * n + 2])
        out_bias[...] = bias
        tail = high_low(bias)
    else:
        out_keep, *out_sends, sum_ref = refs
        tail = None
    for j in range(zcount):
        sum_ref[j] = keep_ref[j] + recv_ref[j * n : (j + 1) * n].astype(F32)
    out_keep[...] = sum_ref[own]
    for j in range(1, zcount):
        out_sends[j - 1][0:n] = sum_ref[own ^ j].astype(BF)
        if tail is not None:
            out_sends[j - 1][n:] = tail


def last_kernel(zcount, keep_ref, *refs):
    recvs = refs[: zcount - 1]
    n = keep_ref.shape[0]
    total = keep_ref[...]
    for ref in recvs:
        total = total + ref[0:n].astype(F32)
    if len(refs) > zcount:
        bias_ref, block_ref, out_bias = refs[zcount - 1 :]
        bias = bias_ref[...]
        for ref in recvs:
            bias = bias + both(ref[n : n + 2])
        out_bias[...] = bias
    else:
        block_ref = refs[-1]
    block_ref[...] = total.astype(BF)


def normal_kernel(zcount, *refs):
    sources, out_ref = refs[:4], refs[4]
    if len(refs) > 5:
        bias_ref, out_ref, out_bias = refs[4:]
        bias = bias_ref[...]
        bias_mean = jnp.mean(bias * bias, keepdims=True)
        out_bias[...] = bias * lax.rsqrt(bias_mean + 1e-06)
    t, p = lax.axis_index("tile"), lax.axis_index("dp")
    n = sources[0].shape[0] // zcount
    size = n // 9
    square = None
    for ref in sources:
        for j in range(zcount):
            v = ref[j * n : (j + 1) * n].astype(F32)
            part = jnp.sum(v * v, axis=0, keepdims=True)
            square = part if square is None else square + part
    mean = jnp.sum(square, keepdims=True) / (9 * out_ref.shape[1] * out_ref.shape[2])
    scale = lax.rsqrt(mean + 1e-06)
    for group, ref in enumerate(sources):
        block = (p ^ (group // 2)) * 2 + ((t % 2) ^ (group % 2))
        for j in range(zcount):
            at = pl.ds(pl.multiple_of((block * zcount + ((t // 2) ^ j)) * size, size), size)
            for tap in range(9):
                row = j * n + tap * size
                out_ref[tap, at] = ref[row : row + size].astype(F32) * scale


def call(kernel, out_shapes, scratch=(), smem_first=False, limit=16, raw=()):
    def run(*args):
        vmem = pl.BlockSpec(memory_space=pltpu.VMEM)
        smem = pl.BlockSpec(memory_space=pltpu.SMEM)
        hbm = pl.BlockSpec(memory_space=pl.ANY)
        specs = [smem if smem_first and i == 0 else hbm if i in raw else vmem for i in range(len(args))]
        return pl.pallas_call(
            kernel,
            out_shape=[jax.ShapeDtypeStruct(s, dt) for s, dt in out_shapes],
            in_specs=specs,
            out_specs=[vmem] * len(out_shapes),
            scratch_shapes=[pltpu.VMEM(s, dt) for s, dt in scratch] + [pltpu.SemaphoreType.DMA((2,))] * bool(raw),
            compiler_params=pltpu.CompilerParams(vmem_limit_bytes=limit << 20),
        )(*args)

    return run


def swap_dp(v):
    count = lax.axis_size("dp")
    return lax.ppermute(v, "dp", [(i, count - 1 - i) for i in range(count)])


def on_device(initial_state, state_cotangents, w_first, bias, w_second, edge_partner):
    tiles = lax.axis_size("tile")
    _, _, rows, face, channels = initial_state.shape
    dm = Dims(rows, face, tiles, channels)
    planes = (6 * rows, face, channels)
    x = initial_state.reshape(planes)
    d = state_cotangents[state_cotangents.shape[0] - 1].reshape(planes)
    taps = (9, channels, channels)
    w1 = w_first.reshape(9 * channels, channels)
    w2 = w_second.reshape(9 * channels, channels)
    w1s, w1t, w2t = call(turn_kernel, [(taps, BF)] * 3)(w_first.reshape(taps), w_second.reshape(taps))
    w1s = w1s.reshape(w1.shape)
    w1t = w1t.reshape(w1.shape)
    w2t = w2t.reshape(w2.shape)
    steps = range(len(dm.steps()))
    pairs = dm.pairs()
    msg_shapes = [((2, dm.rows(i), channels), BF) for i in steps] * 2 + [((2, dm.BASE, channels), BF)]
    flat = (dm.N, channels)

    def merged(packed):
        count = len(steps)
        own, give = packed[:count], [swap_dp(v) for v in packed[count : 2 * count]]
        return call(
            functools.partial(merge_kernel, count), [((2,) + v.shape, BF) for v in own]
        )(*own, *give)

    def across(v, step):
        return lax.ppermute(v, ("tile", "dp"), pairs[step])

    packed = call(
        functools.partial(pack_kernel, dm), msg_shapes, [(flat, BF)] * 2, smem_first=True, raw=(1, 2)
    )(edge_partner, x.reshape(flat), d.reshape(flat))
    messages = []
    for i, v in enumerate(merged(packed)):
        v = across(v, i)
        messages += [v, swap_dp(v)]
    messages.append(packed[-1])
    half = channels // 2
    wide = 9 * channels
    frame = (rows + 2, 6, face + 16, channels)
    outs = call(
        functools.partial(first_kernel, dm),
        [
            ((9, half, channels), BF),
            ((9, half, channels), F32),
            ((9, half, channels), BF),
            ((9, half, channels), F32),
            (planes, BF),
            (planes, BF),
            ((1, channels), F32),
            ((EXTRA, channels), BF),
        ]
        + msg_shapes,
        [
            ((dm.NT, channels), BF),
            (frame, F32),
            ((dm.N, wide), BF),
            ((dm.N + dm.S, wide), BF),
            ((9, dm.S, channels), F32),
            (flat, F32),
            (flat, F32),
            ((dm.N + dm.S, channels), F32),
        ],
        smem_first=True,
        limit=LIMIT,
    )(edge_partner, x, d, w1s, bias.reshape(1, channels), w2t, *messages)
    send1, keep1, send2, keep2, hidden, inner, bias_sum, send_bias = outs[:8]
    packed = list(outs[8:])

    zcount = tiles // 2
    n = 9 * half // tiles
    one = ((1, channels), F32)
    barrier = lax.optimization_barrier

    def along_y(v):
        return lax.ppermute(v, "tile", [(i, i ^ 1) for i in range(tiles)])

    def along_z(v, j):
        return lax.ppermute(v, "tile", [(i, i ^ (2 * j)) for i in range(tiles)])

    def sum_dp(keep, recv, *bias):
        extra = EXTRA if bias else 0
        return call(
            functools.partial(half_kernel, zcount),
            [((zcount, n, channels), F32), ((zcount * n + extra, channels), BF)] + [one] * bool(bias),
        )(keep, recv, *bias)

    def sum_y(keep, recv, *bias):
        extra = EXTRA if bias else 0
        keep, *out = call(
            functools.partial(block_kernel, zcount),
            [((n, channels), F32)] + [((n + extra, channels), BF)] * (zcount - 1) + [one] * bool(bias),
            [((zcount, n, channels), F32)],
        )(keep, recv, *bias)
        return keep, out[: zcount - 1], out[zcount - 1 :]

    def sum_z(keep, recvs, *bias):
        return call(
            functools.partial(last_kernel, zcount), [((n, channels), BF)] + [one] * bool(bias)
        )(keep, *recvs, *bias)

    joined = merged(packed)
    early = list(steps)[1 : 1 + len(steps) // 2]
    middle = [i for i in steps if i not in early]
    came = {}

    keep2, send2 = sum_dp(keep2, swap_dp(send2))
    recv2 = along_y(send2)
    keep1, send1, bias_sum = sum_dp(keep1, swap_dp(send1), bias_sum, swap_dp(send_bias))
    recv1 = along_y(send1)
    got = [across(joined[i], i) for i in early]

    keep2, sends2, _ = sum_y(keep2, recv2)
    recvs2 = [along_z(v, j + 1) for j, v in enumerate(sends2)]
    recv1, got = barrier((recv1, got))
    came.update(zip(early, got))

    keep1, sends1, (bias_sum,) = sum_y(keep1, recv1, bias_sum)
    sends1, todo = barrier((sends1, [joined[i] for i in middle]))
    recvs1 = [along_z(v, j + 1) for j, v in enumerate(sends1)]
    got = [across(v, i) for i, v in zip(middle, todo)]

    (own2,) = sum_z(keep2, recvs2)
    own2 = [own2] + [along_z(own2, j) for j in range(1, zcount)]
    recvs1, got = barrier((recvs1, got))
    came.update(zip(middle, got))

    own1, bias_sum = sum_z(keep1, recvs1, bias_sum)
    own1 = [own1] + [along_z(own1, j) for j in range(1, zcount)]
    own2 = jnp.concatenate(own2, axis=0)
    other2 = along_y(own2)
    own1 = jnp.concatenate(own1, axis=0)
    other1 = along_y(own1)
    messages = []
    for i in steps:
        messages += [came[i], swap_dp(came[i])]
    messages.append(packed[-1])
    own1, messages = barrier((own1, messages))
    state, grad = call(
        functools.partial(second_kernel, dm),
        [(planes, BF), (planes, F32)],
        [
            ((dm.NT, channels), BF),
            (frame, F32),
            ((dm.N, wide), BF),
            ((dm.N + dm.S, wide), BF),
            ((9, dm.S, channels), F32),
            (flat, F32),
        ],
        smem_first=True,
        limit=LIMIT,
    )(edge_partner, x, d, hidden, inner, w1t, w2, *messages)
    other1, state, grad = barrier((other1, state, grad))
    (second_step,) = call(functools.partial(normal_kernel, zcount), [(taps, F32)])(
        own2, other2, swap_dp(own2), swap_dp(other2)
    )
    first_step, bias_step = call(functools.partial(normal_kernel, zcount), [(taps, F32), one])(
        own1, other1, swap_dp(own1), swap_dp(other1), bias_sum
    )
    return (
        state.reshape(initial_state.shape),
        grad.reshape(initial_state.shape),
        first_step.reshape(w_first.shape),
        bias_step.reshape(channels),
        second_step.reshape(w_second.shape),
    )


def solution(mesh):
    return jax.shard_map(
        on_device,
        mesh=mesh,
        in_specs=(
            P(("groups", "dp"), None, "tile", None, None),
            P(None, ("groups", "dp"), None, "tile", None, None),
            P(),
            P(),
            P(),
            P(),
        ),
        out_specs=(
            P(("groups", "dp"), None, "tile", None, None),
            P(("groups", "dp"), None, "tile", None, None),
            P("groups", None, None, None),
            P("groups"),
            P("groups", None, None, None),
        ),
        check_vma=False,
    )
```

```python
import functools

import jax
import jax.numpy as jnp
from jax import lax
from jax.experimental import pallas as pl
from jax.experimental.pallas import tpu as pltpu
from jax.sharding import PartitionSpec as P

BF = jnp.bfloat16
F32 = jnp.float32
EXTRA = 8
LIMIT = 24


class Dims:
    def __init__(self, rows, face, tiles, channels):
        self.R, self.F, self.T, self.C = rows, face, tiles, channels
        self.N = 6 * rows * face
        self.ROW = 6 * face
        self.SLOT = -(-(2 * rows + 2) // 8) * 8
        self.BASE = 6 * self.SLOT
        self.MIX = tiles // 2 - 1
        self.o_msg = self.N
        self.o_row = self.o_msg + tiles * self.BASE
        self.NT = self.o_row + 2 * self.ROW
        self.WE = 12 * 8
        self.S = self.WE + self.ROW

    def partner(self, t, k):
        if k == self.MIX:
            ends = (t == 0) | (t == self.MIX) | (t == self.MIX + 1) | (t == self.T - 1)
            return jnp.where(ends, t ^ k, self.T - 1 - t)
        return t ^ k

    def steps(self):
        rest = [k for k in range(2, self.T - 1)]
        evens = [k for k in rest if k % 2 == 0]
        odds = [k for k in rest if k % 2 == 1]
        rest = evens + odds
        if len(rest) % 2:
            rest = rest[:-1] + [None, rest[-1]]
        return [(1, self.T - 1)] + [(rest[i], rest[i + 1]) for i in range(0, len(rest), 2)]

    def rows(self, step):
        return self.BASE + (self.ROW if step == 0 else 0)

    def pairs(self):
        T, mix = self.T, self.MIX

        def needed(i, d):
            return i in (0, T - 1) or d in (0, T - 1) or d in (T - 2 - i, T - i)

        out = [[(i, i ^ k) for i in range(T) if k == 1 or needed(i, i ^ k)] for k in range(T - 1)]
        out[mix] = [(i, i ^ mix if i in (0, mix, mix + 1, T - 1) else T - 1 - i) for i in range(T)]
        out.append([(i, (i + 1) % T if i % 2 else (i - 1) % T) for i in range(T)])
        return [
            [(2 * i + core, 2 * d + core) for core in range(2) if ks[core] is not None for i, d in out[ks[core]]]
            for ks in self.steps()
        ]


def col_iota(n):
    return lax.broadcasted_iota(jnp.int32, (n, 1), 0)


def one_hot(target, width):
    lanes = lax.broadcasted_iota(jnp.int32, (target.shape[0], width), 1)
    return jnp.where(lanes == target, 1.0, 0.0).astype(BF)


def strip_targets(dm, ep, t, d):
    R, F, T = dm.R, dm.F, dm.T
    at_edge = (t == 0) | (t == T - 1)
    to_edge = (d == 0) | (d == T - 1)
    own_edge = jnp.where(t == 0, 0, 2)
    far_edge = jnp.where(d == 0, 0, 2)
    side_row = jnp.where(d == T - 2 - t, R - 1, 0)
    i = col_iota(dm.SLOT)
    q = R * d - 1 + i
    inside = (q >= 0) & (q < F) & (i < R + 2)
    i2 = i - (R + 2)
    parts = []
    for f in range(6):
        far_low = (ep[f, own_edge] % 4) < 2
        reverse = far_low == (t == 0)
        p0 = jnp.where(reverse, F - 1, 0)
        sgn = jnp.where(reverse, -1, 1)
        row = jnp.where(t == 0, 0, R - 1)
        strip = jnp.where(inside, (f * R + row) * F + p0 + sgn * q, -1)
        sides = (f * R + side_row) * F
        low = jnp.where(at_edge, strip, sides + i * (F - 1))
        low = jnp.where(at_edge | (i < 2), low, -1)
        gvalue = ep[f, far_edge]
        column = jnp.where(gvalue % 4 == 1, F - 1, 0) + (gvalue // 4) * (R * F)
        high = jnp.where(to_edge, column + F * i2, jnp.where(i2 < 2, sides + i2 * (F - 1), -1))
        strips = jnp.where(i2 < 0, low, jnp.where(i2 < R, high, -1))
        parts.append(jnp.where(d == T - 1 - t, mirror_slot(dm, f), strips))
    return parts


def mirror_slot(dm, f):
    i = col_iota(dm.SLOT)
    return jnp.where(i < 2 * dm.R, (f * dm.R + i // 2) * dm.F + (i % 2) * (dm.F - 1), -1)


def row_targets(dm, row):
    j = col_iota(dm.F)
    return [(f * dm.R + row) * dm.F + j for f in range(6)]


def write_messages(dm, ep, t, p, sources, refs):
    R = dm.R
    steps = dm.steps()
    for other in range(2):
        core = p ^ other
        for step, ks in enumerate(steps):
            if step == 0:
                strips = strip_targets(dm, ep, t, t ^ 1)
                parts = [jnp.where(core == 0, strips[f], mirror_slot(dm, f)) for f in range(6)]
                parts = parts + row_targets(dm, jnp.where((t + core) % 2 == 0, R - 1, 0))
            else:
                ds = [dm.partner(t, k) for k in ks if k is not None]
                parts = strip_targets(dm, ep, t, jnp.where(core == 0, ds[0], ds[-1]))
            hot = one_hot(jnp.concatenate(parts, axis=0), dm.N)
            for which in range(2):
                rows = jnp.dot(hot, sources[which], preferred_element_type=F32).astype(BF)
                refs[other * len(steps) + step][which] = rows


def write_self(dm, ep, t, sources, ref):
    hot = one_hot(jnp.concatenate(strip_targets(dm, ep, t, t), axis=0), dm.N)
    for which in range(2):
        ref[which] = jnp.dot(hot, sources[which], preferred_element_type=F32).astype(BF)


def pack_kernel(dm, ep, x_ref, up_ref, *refs):
    t, p = lax.axis_index("tile"), lax.axis_index("dp")
    fields = (x_ref[...], up_ref[...])
    write_messages(dm, ep, t, p, fields, refs[:-1])
    write_self(dm, ep, t, fields, refs[-1])


def merge_kernel(count, *refs):
    for i in range(count):
        refs[2 * count + i][0] = refs[i][...]
        refs[2 * count + i][1] = refs[count + i][...]


def ghost_targets(dm, ep, t):
    R, F, T = dm.R, dm.F, dm.T
    odd = t % 2
    parts = []
    m = col_iota(8)
    q = R * t - 1 + m
    inside = (q >= 0) & (q < F) & (m < R + 2)
    row_prev = dm.o_row + (1 - odd) * dm.ROW
    row_next = dm.o_row + odd * dm.ROW
    side_first = dm.o_msg + (t ^ (T - t)) * dm.BASE + jnp.where(t == 1, R + 2, 0)
    side_last = dm.o_msg + (t ^ (T - 2 - t)) * dm.BASE + jnp.where(t == T - 2, R + 2, 0)
    ends = (t == 0) | (t == dm.MIX) | (t == dm.MIX + 1) | (t == T - 1)
    mirror = dm.o_msg + jnp.where(ends, T - 1, dm.MIX) * dm.BASE
    for f in range(6):
        for edge in (3, 1):
            value = ep[f, edge]
            f2, e2 = value // 4, value % 4
            far_low = e2 < 2
            reverse = far_low if edge < 2 else e2 >= 2
            is_col = (e2 % 2) == 1
            side = jnp.where(e2 == 1, 1, 0)
            column = side * (F - 1)
            slot = f2 * dm.SLOT + side
            row = dm.o_msg + (t ^ jnp.where(e2 == 0, 0, T - 1)) * dm.BASE + f2 * dm.SLOT
            facing = jnp.where(e2 == 0, t == T - 1, t == 0)
            whole = dm.o_row + dm.ROW + f2 * F + jnp.where(reverse, F - R * t, R * t - 1)
            row = jnp.where(facing, whole, row)
            along = jnp.where(facing & reverse, -1, 1)
            i0 = jnp.where(is_col, jnp.where(reverse, side_first + slot, row_prev + f2 * F + column), row)
            i4 = jnp.where(
                is_col, jnp.where(reverse, side_last + slot, row_next + f2 * F + column), row + along * (R + 1)
            )
            base = jnp.where(
                is_col, jnp.where(reverse, mirror + 2 * R + slot, (f2 * R - 1) * F + column), row
            )
            step = jnp.where(is_col, jnp.where(reverse, -2, F), along)
            target = jnp.where(m == 0, i0, jnp.where(m == R + 1, i4, base + step * m))
            parts.append(jnp.where(inside, target, -1))
    j = col_iota(F)
    jt = jnp.zeros_like(j)
    for b in range(1, T):
        jt = jt + jnp.where(j >= b * R, 1, 0)
    jr = j - R * jt
    wrap = dm.o_row + dm.ROW
    for edge in (0, 2):
        at_edge = (t == 0) if edge == 0 else (t == T - 1)
        inner_base = row_prev if edge == 0 else row_next
        own_row = 0 if edge == 0 else R - 1
        for f in range(6):
            value = ep[f, edge]
            f2, e2 = value // 4, value % 4
            far_low = e2 < 2
            reverse = far_low if edge < 2 else e2 >= 2
            is_col = (e2 % 2) == 1
            same = e2 == edge
            row_base = jnp.where(same, (f2 * R + own_row) * F, wrap + f2 * F)
            lin_base = row_base + jnp.where(reverse, F - 1, 0)
            lin_step = jnp.where(reverse, -1, 1)
            k0 = jnp.where(reverse, T - 1, 0)
            ks = jnp.where(reverse, -1, 1)
            if edge == 2:
                k0 = T - 1 - k0
                ks = -ks
            col_base = dm.o_msg + k0 * dm.BASE + f * dm.SLOT + R + 2 + jnp.where(reverse, R - 1, 0)
            base = jnp.where(is_col, col_base, lin_base)
            sj = jnp.where(is_col, 0, lin_step)
            st = jnp.where(is_col, ks * dm.BASE, 0)
            sr = jnp.where(is_col, jnp.where(reverse, -1, 1), 0)
            base = jnp.where(at_edge, base, inner_base + f * F)
            sj = jnp.where(at_edge, sj, 1)
            st = jnp.where(at_edge, st, 0)
            sr = jnp.where(at_edge, sr, 0)
            target = base + sj * j + st * jt + sr * jr
            far_tile = T - 1 if edge == 0 else 0
            from_mirror = is_col & at_edge & (jnp.where(reverse, T - 1 - jt, jt) == far_tile)
            side = jnp.where(e2 == 1, 1, 0)
            cells = mirror + f2 * dm.SLOT + side + 2 * jnp.where(reverse, R - 1 - jr, jr)
            parts.append(jnp.where(from_mirror, cells, target))
    return jnp.concatenate(parts, axis=0)


def gather_ghosts(dm, ep, t, p, own, messages, table_ref):
    hot = one_hot(ghost_targets(dm, ep, t), dm.NT)
    out = []
    for which in range(2):
        table_ref[0 : dm.N] = own[which]
        table_ref[dm.o_msg : dm.o_msg + dm.BASE] = messages[-1][which]
        for step, ks in enumerate(dm.steps()):
            here = messages[2 * step][0, which].astype(F32)
            there = messages[2 * step + 1][1, which].astype(F32)
            for core, k in enumerate(ks):
                if k is None:
                    continue
                value = jnp.where(p == core, here, there).astype(BF)
                at = dm.o_msg + k * dm.BASE
                table_ref[at : at + dm.BASE] = value[: dm.BASE]
                if step == 0:
                    at = dm.o_row + core * dm.ROW
                    table_ref[at : at + dm.ROW] = value[dm.BASE :]
        out.append(jnp.dot(hot, table_ref[...], preferred_element_type=F32))
    return out


def own_first(value, p):
    half = value.shape[1] // 2
    low, high = value[:, :half], value[:, half:]
    return jnp.concatenate([jnp.where(p == 0, low, high), jnp.where(p == 0, high, low)], axis=1)


def build_taps(dm, field_ref, ghosts, top, bottom, frame_ref, taps_ref, adjoint, p=None):
    R, F, C = dm.R, dm.F, dm.C
    for f in range(6):
        for r in range(R):
            frame_ref[r + 1, f, 8 : 8 + F] = field_ref[f * R + r].astype(F32)
    frame_ref[0, :, 8 : 8 + F] = top.reshape(6, F, C)
    frame_ref[R + 1, :, 8 : 8 + F] = bottom.reshape(6, F, C)
    for m in range(R + 2):
        for f in range(6):
            if ghosts is None:
                west = jnp.zeros((1, C), F32)
                east = west
            else:
                west = ghosts[16 * f + m : 16 * f + m + 1]
                east = ghosts[16 * f + 8 + m : 16 * f + 8 + m + 1]
            frame_ref[m, f, 7:8] = west
            frame_ref[m, f, 8 + F : 9 + F] = east
    for m in range(R + 2):
        for b in range(3):
            plane = frame_ref[m, :, 7 + b : 7 + b + F].reshape(dm.ROW, C)
            if p is not None:
                plane = own_first(plane, p)
            plane = plane.astype(BF)
            for a in range(3):
                r = m - 2 + a if adjoint else m - a
                tap = 3 * a + (2 - b if adjoint else b)
                if 0 <= r < R:
                    taps_ref[r * dm.ROW : (r + 1) * dm.ROW, tap * C : (tap + 1) * C] = plane


def build_strip_terms(dm, ep, t, ghosts, top, bottom, z_ref):
    R, F = dm.R, dm.F
    z_ref[...] = jnp.zeros(z_ref.shape, F32)

    def tap_of(f, edge, shift):
        e2 = ep[f, edge] % 4
        reverse = e2 < 2 if edge < 2 else e2 >= 2
        along = 1 - jnp.where(reverse, -shift, shift)
        return jnp.where(
            e2 == 0, along, jnp.where(e2 == 2, 6 + along, jnp.where(e2 == 1, 3 * along + 2, 3 * along))
        )

    live = lax.rem(lax.broadcasted_iota(jnp.int32, (dm.WE, 1), 0), 8) < R
    for shift in (-1, 0, 1):
        moved = pltpu.roll(ghosts, (dm.WE - 1 - shift) % dm.WE, 0) if shift > -1 else ghosts
        moved = jnp.where(live, moved, 0.0)
        for f in range(6):
            for side, edge in ((0, 3), (1, 1)):
                at = 16 * f + 8 * side
                z_ref[tap_of(f, edge, shift), at : at + 8] = moved[at : at + 8]

    def add_rows(edge, rows):
        j = lax.rem(lax.broadcasted_iota(jnp.int32, (dm.ROW, 1), 0), F)
        for shift in (-1, 0, 1):
            if shift == 0:
                moved = rows
            else:
                moved = pltpu.roll(rows, (-shift) % dm.ROW, 0)
                moved = jnp.where((j + shift >= 0) & (j + shift < F), moved, 0.0)
            for f in range(6):
                at = dm.WE + F * f
                z_ref[tap_of(f, edge, shift), at : at + F] = moved[F * f : F * (f + 1)]

    @pl.when(t == 0)
    def _():
        add_rows(0, top)

    @pl.when(t == dm.T - 1)
    def _():
        add_rows(2, bottom)


def adjoint(dm, t, taps_ref, z_ref, wt_ref, acc_ref):
    R, F, C, N = dm.R, dm.F, dm.C, dm.N
    for tap in range(9):
        taps_ref[N:, tap * C : (tap + 1) * C] = z_ref[tap].astype(BF)
    total = jnp.dot(taps_ref[...], wt_ref[...], preferred_element_type=F32)
    acc_ref[...] = total[:N]
    strips = total[N:]
    for f in range(6):
        for side in range(2):
            for r in range(R):
                at = (r * 6 + f) * F + side * (F - 1)
                row = 16 * f + 8 * side + r
                acc_ref[at : at + 1] += strips[row : row + 1]

    @pl.when(t == 0)
    def _():
        acc_ref[0 : dm.ROW] += strips[dm.WE :]

    @pl.when(t == dm.T - 1)
    def _():
        acc_ref[(R - 1) * dm.ROW : R * dm.ROW] += strips[dm.WE :]


def turn_kernel(w1_ref, w2_ref, w1s_ref, w1t_ref, w2t_ref):
    p = lax.axis_index("dp")
    half = w1_ref.shape[1] // 2
    for tap in range(9):
        w1t_ref[tap] = w1_ref[tap].T
        w2t_ref[tap] = w2_ref[tap].T
        w1s_ref[tap, :half] = w1_ref[tap, pl.ds(pl.multiple_of(p * half, half), half)]
        w1s_ref[tap, half:] = w1_ref[tap, pl.ds(pl.multiple_of((1 - p) * half, half), half)]


def put_taps(send_ref, keep_ref, first_tap, value):
    half = keep_ref.shape[1]
    for i in range(value.shape[0] // (2 * half)):
        keep_ref[first_tap + i] = value[2 * i * half : (2 * i + 1) * half]
        send_ref[first_tap + i] = value[(2 * i + 1) * half : (2 * i + 2) * half].astype(BF)


def high_low(row):
    i = lax.broadcasted_iota(jnp.int32, (EXTRA, row.shape[1]), 0)
    high = row.astype(BF).astype(F32)
    return jnp.where(i == 0, high, jnp.where(i == 1, row - high, 0.0)).astype(BF)


def both(pair):
    return pair[0:1].astype(F32) + pair[1:2].astype(F32)


def first_kernel(dm, ep, x_ref, up_ref, w1_ref, bias_ref, w2t_ref, *refs):
    T, R, F, N, C = dm.T, dm.R, dm.F, dm.N, dm.C
    M = 2 * len(dm.steps())
    messages = refs[: M + 1]
    refs = refs[M + 1 :]
    send1_ref, keep1_ref, send2_ref, keep2_ref, hid_ref, inner_ref, bias_sum_ref, send_bias_ref = refs[:8]
    out_messages, self_ref = refs[8 : M + 8], refs[M + 8]
    table_ref, frame_ref, xs_ref, us_ref, z_ref, before_ref, acc_ref, hcat_ref = refs[M + 9 :]
    t, p = lax.axis_index("tile"), lax.axis_index("dp")
    own = (x_ref[...].reshape(N, C), up_ref[...].reshape(N, C))
    gx, gu = gather_ghosts(dm, ep, t, p, own, messages, table_ref)
    top, bottom = dm.WE, dm.WE + dm.ROW
    build_taps(dm, x_ref, gx[:top], gx[top:bottom], gx[bottom:], frame_ref, xs_ref, False, p)
    before = jnp.dot(xs_ref[...], w1_ref[...], preferred_element_type=F32) + bias_ref[...]
    before_ref[...] = before
    sig = 1.0 / (1.0 + jnp.exp(-before))
    acc_ref[...] = before * sig
    up_top = jnp.where(t == 0, 0.0, gu[top:bottom])
    up_bottom = jnp.where(t == T - 1, 0.0, gu[bottom:])
    build_taps(dm, up_ref, None, up_top, up_bottom, frame_ref, us_ref, True)
    build_strip_terms(dm, ep, t, gu[:top], gu[top:bottom], gu[bottom:], z_ref)
    hcat_ref[0:N] = acc_ref[...]
    hcat_ref[N:] = jnp.zeros((dm.S, C), F32)
    for f in range(6):
        for side in range(2):
            for r in range(R):
                at = (r * 6 + f) * F + side * (F - 1)
                row = N + 16 * f + 8 * side + r
                hcat_ref[row : row + 1] = acc_ref[at : at + 1]
    first_row = acc_ref[0 : dm.ROW]
    last_row = acc_ref[(R - 1) * dm.ROW : R * dm.ROW]
    hcat_ref[N + dm.WE :] = jnp.where(t == 0, first_row, last_row)
    for r in range(R):
        for f in range(6):
            at = (r * 6 + f) * F
            hid_ref[f * R + r] = acc_ref[at : at + F].astype(BF)
    adjoint(dm, t, us_ref, z_ref, w2t_ref, acc_ref)
    hidden_t = own_first(hcat_ref[...], p).astype(BF).T
    for tap in range(9):
        grad = jnp.dot(hidden_t, us_ref[:, tap * C : (tap + 1) * C], preferred_element_type=F32)
        put_taps(send2_ref, keep2_ref, tap, grad)
    before = before_ref[...]
    sig = 1.0 / (1.0 + jnp.exp(-before))
    before_grad = acc_ref[...] * (sig * (1.0 + before * (1.0 - sig)))
    acc_ref[...] = before_grad
    inner = before_grad.astype(BF)
    for tap in (0, 3, 6):
        grad = lax.dot_general(
            xs_ref[:, tap * C : (tap + 3) * C],
            inner,
            (((0,), (0,)), ((), ())),
            preferred_element_type=F32,
        )
        put_taps(send1_ref, keep1_ref, tap, grad)
    bias_sum = jnp.sum(before_grad, axis=0, keepdims=True)
    bias_sum_ref[...] = bias_sum
    send_bias_ref[...] = high_low(bias_sum)
    for r in range(R):
        for f in range(6):
            at = (r * 6 + f) * F
            inner_ref[f * R + r] = acc_ref[at : at + F].astype(BF)
    fields = (hid_ref[...].reshape(N, C), inner_ref[...].reshape(N, C))
    write_messages(dm, ep, t, p, fields, out_messages)
    write_self(dm, ep, t, fields, self_ref)


def second_kernel(dm, ep, x_ref, d_ref, hid_ref, inner_ref, w1t_ref, w2_ref, *refs):
    T, R, F, N, C = dm.T, dm.R, dm.F, dm.N, dm.C
    M = 2 * len(dm.steps()) + 1
    messages = refs[:M]
    state_ref, grad_ref = refs[M : M + 2]
    table_ref, frame_ref, hs_ref, is_ref, z_ref, acc_ref = refs[M + 2 :]
    t, p = lax.axis_index("tile"), lax.axis_index("dp")
    own = (hid_ref[...].reshape(N, C), inner_ref[...].reshape(N, C))
    gh, gi = gather_ghosts(dm, ep, t, p, own, messages, table_ref)
    top, bottom = dm.WE, dm.WE + dm.ROW
    build_taps(dm, hid_ref, gh[:top], gh[top:bottom], gh[bottom:], frame_ref, hs_ref, False)
    acc_ref[...] = jnp.dot(hs_ref[...], w2_ref[...], preferred_element_type=F32)
    for r in range(R):
        for f in range(6):
            at = (r * 6 + f) * F
            value = x_ref[f * R + r].astype(F32) + acc_ref[at : at + F]
            state_ref[f * R + r] = value.astype(BF)
    in_top = jnp.where(t == 0, 0.0, gi[top:bottom])
    in_bottom = jnp.where(t == T - 1, 0.0, gi[bottom:])
    build_taps(dm, inner_ref, None, in_top, in_bottom, frame_ref, is_ref, True)
    build_strip_terms(dm, ep, t, gi[:top], gi[top:bottom], gi[bottom:], z_ref)
    adjoint(dm, t, is_ref, z_ref, w1t_ref, acc_ref)
    for r in range(R):
        for f in range(6):
            at = (r * 6 + f) * F
            grad_ref[f * R + r] = d_ref[f * R + r].astype(F32) + acc_ref[at : at + F]


def half_kernel(zcount, keep_ref, recv_ref, *refs):
    size = keep_ref.shape[1] // 2
    own = lax.axis_index("tile") % 2
    mine = pl.ds(pl.multiple_of(own * size, size), size)
    far = pl.ds(pl.multiple_of((1 - own) * size, size), size)
    part = size // zcount
    if len(refs) > 2:
        bias_ref, recv_bias_ref, out_keep, out_send, out_bias = refs
        bias = bias_ref[...] + both(recv_bias_ref)
        out_bias[...] = bias
        out_send[9 * size :] = high_low(bias)
    else:
        out_keep, out_send = refs
    for tap in range(9):
        kept = keep_ref[tap, mine] + recv_ref[tap, mine].astype(F32)
        sent = keep_ref[tap, far] + recv_ref[tap, far].astype(F32)
        for j in range(zcount):
            at = j * 9 * part + tap * part
            out_keep[j, tap * part : (tap + 1) * part] = kept[j * part : (j + 1) * part]
            out_send[at : at + part] = sent[j * part : (j + 1) * part].astype(BF)


def block_kernel(zcount, keep_ref, recv_ref, *refs):
    own = lax.axis_index("tile") // 2
    n = keep_ref.shape[1]
    if len(refs) > zcount + 1:
        bias_ref, out_keep, *out_sends, out_bias, sum_ref = refs
        bias = bias_ref[...] + both(recv_ref[zcount * n : zcount * n + 2])
        out_bias[...] = bias
        tail = high_low(bias)
    else:
        out_keep, *out_sends, sum_ref = refs
        tail = None
    for j in range(zcount):
        sum_ref[j] = keep_ref[j] + recv_ref[j * n : (j + 1) * n].astype(F32)
    out_keep[...] = sum_ref[own]
    for j in range(1, zcount):
        out_sends[j - 1][0:n] = sum_ref[own ^ j].astype(BF)
        if tail is not None:
            out_sends[j - 1][n:] = tail


def last_kernel(zcount, keep_ref, *refs):
    recvs = refs[: zcount - 1]
    n = keep_ref.shape[0]
    total = keep_ref[...]
    for ref in recvs:
        total = total + ref[0:n].astype(F32)
    if len(refs) > zcount:
        bias_ref, block_ref, out_bias = refs[zcount - 1 :]
        bias = bias_ref[...]
        for ref in recvs:
            bias = bias + both(ref[n : n + 2])
        out_bias[...] = bias
    else:
        block_ref = refs[-1]
    block_ref[...] = total.astype(BF)


def normal_kernel(zcount, *refs):
    sources, out_ref = refs[:4], refs[4]
    if len(refs) > 5:
        bias_ref, out_ref, out_bias = refs[4:]
        bias = bias_ref[...]
        bias_mean = jnp.mean(bias * bias, keepdims=True)
        out_bias[...] = bias * lax.rsqrt(bias_mean + 1e-06)
    t, p = lax.axis_index("tile"), lax.axis_index("dp")
    n = sources[0].shape[0] // zcount
    size = n // 9
    square = None
    for ref in sources:
        for j in range(zcount):
            v = ref[j * n : (j + 1) * n].astype(F32)
            part = jnp.sum(v * v, axis=0, keepdims=True)
            square = part if square is None else square + part
    mean = jnp.sum(square, keepdims=True) / (9 * out_ref.shape[1] * out_ref.shape[2])
    scale = lax.rsqrt(mean + 1e-06)
    for group, ref in enumerate(sources):
        block = (p ^ (group // 2)) * 2 + ((t % 2) ^ (group % 2))
        for j in range(zcount):
            at = pl.ds(pl.multiple_of((block * zcount + ((t // 2) ^ j)) * size, size), size)
            for tap in range(9):
                row = j * n + tap * size
                out_ref[tap, at] = ref[row : row + size].astype(F32) * scale


def call(kernel, out_shapes, scratch=(), smem_first=False, limit=16):
    def run(*args):
        vmem = pl.BlockSpec(memory_space=pltpu.VMEM)
        smem = pl.BlockSpec(memory_space=pltpu.SMEM)
        specs = [smem if smem_first and i == 0 else vmem for i in range(len(args))]
        return pl.pallas_call(
            kernel,
            out_shape=[jax.ShapeDtypeStruct(s, dt) for s, dt in out_shapes],
            in_specs=specs,
            out_specs=[vmem] * len(out_shapes),
            scratch_shapes=[pltpu.VMEM(s, dt) for s, dt in scratch],
            compiler_params=pltpu.CompilerParams(vmem_limit_bytes=limit << 20),
        )(*args)

    return run


def swap_dp(v):
    count = lax.axis_size("dp")
    return lax.ppermute(v, "dp", [(i, count - 1 - i) for i in range(count)])


def on_device(initial_state, state_cotangents, w_first, bias, w_second, edge_partner):
    tiles = lax.axis_size("tile")
    _, _, rows, face, channels = initial_state.shape
    dm = Dims(rows, face, tiles, channels)
    planes = (6 * rows, face, channels)
    x = initial_state.reshape(planes)
    d = state_cotangents[state_cotangents.shape[0] - 1].reshape(planes)
    taps = (9, channels, channels)
    w1 = w_first.reshape(9 * channels, channels)
    w2 = w_second.reshape(9 * channels, channels)
    w1s, w1t, w2t = call(turn_kernel, [(taps, BF)] * 3)(w_first.reshape(taps), w_second.reshape(taps))
    w1s = w1s.reshape(w1.shape)
    w1t = w1t.reshape(w1.shape)
    w2t = w2t.reshape(w2.shape)
    steps = range(len(dm.steps()))
    pairs = dm.pairs()
    msg_shapes = [((2, dm.rows(i), channels), BF) for i in steps] * 2 + [((2, dm.BASE, channels), BF)]
    flat = (dm.N, channels)

    def merged(packed):
        count = len(steps)
        own, give = packed[:count], [swap_dp(v) for v in packed[count : 2 * count]]
        return call(
            functools.partial(merge_kernel, count), [((2,) + v.shape, BF) for v in own]
        )(*own, *give)

    def across(v, step):
        return lax.ppermute(v, ("tile", "dp"), pairs[step])

    packed = call(
        functools.partial(pack_kernel, dm), msg_shapes, smem_first=True
    )(edge_partner, x.reshape(flat), d.reshape(flat))
    came = [across(v, i) for i, v in enumerate(merged(packed))]
    came, w1s, w1t, w2t = lax.optimization_barrier((came, w1s, w1t, w2t))
    messages = []
    for v in came:
        messages += [v, swap_dp(v)]
    messages.append(packed[-1])
    half = channels // 2
    wide = 9 * channels
    frame = (rows + 2, 6, face + 16, channels)
    outs = call(
        functools.partial(first_kernel, dm),
        [
            ((9, half, channels), BF),
            ((9, half, channels), F32),
            ((9, half, channels), BF),
            ((9, half, channels), F32),
            (planes, BF),
            (planes, BF),
            ((1, channels), F32),
            ((EXTRA, channels), BF),
        ]
        + msg_shapes,
        [
            ((dm.NT, channels), BF),
            (frame, F32),
            ((dm.N, wide), BF),
            ((dm.N + dm.S, wide), BF),
            ((9, dm.S, channels), F32),
            (flat, F32),
            (flat, F32),
            ((dm.N + dm.S, channels), F32),
        ],
        smem_first=True,
        limit=LIMIT,
    )(edge_partner, x, d, w1s, bias.reshape(1, channels), w2t, *messages)
    send1, keep1, send2, keep2, hidden, inner, bias_sum, send_bias = outs[:8]
    packed = list(outs[8:])

    zcount = tiles // 2
    n = 9 * half // tiles
    one = ((1, channels), F32)
    barrier = lax.optimization_barrier

    def along_y(v):
        return lax.ppermute(v, "tile", [(i, i ^ 1) for i in range(tiles)])

    def along_z(v, j):
        return lax.ppermute(v, "tile", [(i, i ^ (2 * j)) for i in range(tiles)])

    def sum_dp(keep, recv, *bias):
        extra = EXTRA if bias else 0
        return call(
            functools.partial(half_kernel, zcount),
            [((zcount, n, channels), F32), ((zcount * n + extra, channels), BF)] + [one] * bool(bias),
        )(keep, recv, *bias)

    def sum_y(keep, recv, *bias):
        extra = EXTRA if bias else 0
        keep, *out = call(
            functools.partial(block_kernel, zcount),
            [((n, channels), F32)] + [((n + extra, channels), BF)] * (zcount - 1) + [one] * bool(bias),
            [((zcount, n, channels), F32)],
        )(keep, recv, *bias)
        return keep, out[: zcount - 1], out[zcount - 1 :]

    def sum_z(keep, recvs, *bias):
        return call(
            functools.partial(last_kernel, zcount), [((n, channels), BF)] + [one] * bool(bias)
        )(keep, *recvs, *bias)

    joined = merged(packed)
    early = list(steps)[1 : 1 + len(steps) // 2]
    middle = [i for i in steps if i not in early]
    came = {}

    keep2, send2 = sum_dp(keep2, swap_dp(send2))
    recv2 = along_y(send2)
    keep1, send1, bias_sum = sum_dp(keep1, swap_dp(send1), bias_sum, swap_dp(send_bias))
    recv1 = along_y(send1)
    got = [across(joined[i], i) for i in early]

    keep2, sends2, _ = sum_y(keep2, recv2)
    recvs2 = [along_z(v, j + 1) for j, v in enumerate(sends2)]
    recv1, got = barrier((recv1, got))
    came.update(zip(early, got))

    keep1, sends1, (bias_sum,) = sum_y(keep1, recv1, bias_sum)
    sends1, todo = barrier((sends1, [joined[i] for i in middle]))
    recvs1 = [along_z(v, j + 1) for j, v in enumerate(sends1)]
    got = [across(v, i) for i, v in zip(middle, todo)]

    (own2,) = sum_z(keep2, recvs2)
    own2 = [own2] + [along_z(own2, j) for j in range(1, zcount)]
    recvs1, got = barrier((recvs1, got))
    came.update(zip(middle, got))

    own1, bias_sum = sum_z(keep1, recvs1, bias_sum)
    own1 = [own1] + [along_z(own1, j) for j in range(1, zcount)]
    own2 = jnp.concatenate(own2, axis=0)
    other2 = along_y(own2)
    own1 = jnp.concatenate(own1, axis=0)
    other1 = along_y(own1)
    messages = []
    for i in steps:
        messages += [came[i], swap_dp(came[i])]
    messages.append(packed[-1])
    own1, messages = barrier((own1, messages))
    state, grad = call(
        functools.partial(second_kernel, dm),
        [(planes, BF), (planes, F32)],
        [
            ((dm.NT, channels), BF),
            (frame, F32),
            ((dm.N, wide), BF),
            ((dm.N + dm.S, wide), BF),
            ((9, dm.S, channels), F32),
            (flat, F32),
        ],
        smem_first=True,
        limit=LIMIT,
    )(edge_partner, x, d, hidden, inner, w1t, w2, *messages)
    other1, state, grad = barrier((other1, state, grad))
    (second_step,) = call(functools.partial(normal_kernel, zcount), [(taps, F32)])(
        own2, other2, swap_dp(own2), swap_dp(other2)
    )
    first_step, bias_step = call(functools.partial(normal_kernel, zcount), [(taps, F32), one])(
        own1, other1, swap_dp(own1), swap_dp(other1), bias_sum
    )
    return (
        state.reshape(initial_state.shape),
        grad.reshape(initial_state.shape),
        first_step.reshape(w_first.shape),
        bias_step.reshape(channels),
        second_step.reshape(w_second.shape),
    )


def solution(mesh):
    return jax.shard_map(
        on_device,
        mesh=mesh,
        in_specs=(
            P(("groups", "dp"), None, "tile", None, None),
            P(None, ("groups", "dp"), None, "tile", None, None),
            P(),
            P(),
            P(),
            P(),
        ),
        out_specs=(
            P(("groups", "dp"), None, "tile", None, None),
            P(("groups", "dp"), None, "tile", None, None),
            P("groups", None, None, None),
            P("groups"),
            P("groups", None, None, None),
        ),
        check_vma=False,
    )
```

```python
import functools

import jax
import jax.numpy as jnp
from jax import lax
from jax.experimental import pallas as pl
from jax.experimental.pallas import tpu as pltpu
from jax.sharding import PartitionSpec as P

BF = jnp.bfloat16
F32 = jnp.float32
EXTRA = 8
LIMIT = 24


class Dims:
    def __init__(self, rows, face, tiles, channels):
        self.R, self.F, self.T, self.C = rows, face, tiles, channels
        self.N = 6 * rows * face
        self.ROW = 6 * face
        self.SLOT = -(-(2 * rows + 2) // 8) * 8
        self.BASE = 6 * self.SLOT
        self.MIX = tiles // 2 - 1
        self.o_msg = self.N
        self.o_row = self.o_msg + tiles * self.BASE
        self.NT = self.o_row + 2 * self.ROW
        self.WE = 12 * 8
        self.S = self.WE + self.ROW

    def partner(self, t, k):
        if k == self.MIX:
            ends = (t == 0) | (t == self.MIX) | (t == self.MIX + 1) | (t == self.T - 1)
            return jnp.where(ends, t ^ k, self.T - 1 - t)
        return t ^ k

    def steps(self):
        rest = [k for k in range(2, self.T - 1)]
        evens = [k for k in rest if k % 2 == 0]
        odds = [k for k in rest if k % 2 == 1]
        rest = evens + odds
        if len(rest) % 2:
            rest = rest[:-1] + [None, rest[-1]]
        return [(1, self.T - 1)] + [(rest[i], rest[i + 1]) for i in range(0, len(rest), 2)]

    def rows(self, step):
        return self.BASE + (self.ROW if step == 0 else 0)

    def pairs(self):
        T, mix = self.T, self.MIX

        def needed(i, d):
            return i in (0, T - 1) or d in (0, T - 1) or d in (T - 2 - i, T - i)

        out = [[(i, i ^ k) for i in range(T) if k == 1 or needed(i, i ^ k)] for k in range(T - 1)]
        out[mix] = [(i, i ^ mix if i in (0, mix, mix + 1, T - 1) else T - 1 - i) for i in range(T)]
        out.append([(i, (i + 1) % T if i % 2 else (i - 1) % T) for i in range(T)])
        return [
            [(2 * i + core, 2 * d + core) for core in range(2) if ks[core] is not None for i, d in out[ks[core]]]
            for ks in self.steps()
        ]


def col_iota(n):
    return lax.broadcasted_iota(jnp.int32, (n, 1), 0)


def one_hot(target, width):
    lanes = lax.broadcasted_iota(jnp.int32, (target.shape[0], width), 1)
    return jnp.where(lanes == target, 1.0, 0.0).astype(BF)


def strip_targets(dm, ep, t, d):
    R, F, T = dm.R, dm.F, dm.T
    at_edge = (t == 0) | (t == T - 1)
    to_edge = (d == 0) | (d == T - 1)
    own_edge = jnp.where(t == 0, 0, 2)
    far_edge = jnp.where(d == 0, 0, 2)
    side_row = jnp.where(d == T - 2 - t, R - 1, 0)
    i = col_iota(dm.SLOT)
    q = R * d - 1 + i
    inside = (q >= 0) & (q < F) & (i < R + 2)
    i2 = i - (R + 2)
    parts = []
    for f in range(6):
        far_low = (ep[f, own_edge] % 4) < 2
        reverse = far_low == (t == 0)
        p0 = jnp.where(reverse, F - 1, 0)
        sgn = jnp.where(reverse, -1, 1)
        row = jnp.where(t == 0, 0, R - 1)
        strip = jnp.where(inside, (f * R + row) * F + p0 + sgn * q, -1)
        sides = (f * R + side_row) * F
        low = jnp.where(at_edge, strip, sides + i * (F - 1))
        low = jnp.where(at_edge | (i < 2), low, -1)
        gvalue = ep[f, far_edge]
        column = jnp.where(gvalue % 4 == 1, F - 1, 0) + (gvalue // 4) * (R * F)
        high = jnp.where(to_edge, column + F * i2, jnp.where(i2 < 2, sides + i2 * (F - 1), -1))
        strips = jnp.where(i2 < 0, low, jnp.where(i2 < R, high, -1))
        parts.append(jnp.where(d == T - 1 - t, mirror_slot(dm, f), strips))
    return parts


def mirror_slot(dm, f):
    i = col_iota(dm.SLOT)
    return jnp.where(i < 2 * dm.R, (f * dm.R + i // 2) * dm.F + (i % 2) * (dm.F - 1), -1)


def row_targets(dm, row):
    j = col_iota(dm.F)
    return [(f * dm.R + row) * dm.F + j for f in range(6)]


def write_messages(dm, ep, t, p, sources, refs):
    R = dm.R
    steps = dm.steps()
    for other in range(2):
        core = p ^ other
        for step, ks in enumerate(steps):
            if step == 0:
                strips = strip_targets(dm, ep, t, t ^ 1)
                parts = [jnp.where(core == 0, strips[f], mirror_slot(dm, f)) for f in range(6)]
                parts = parts + row_targets(dm, jnp.where((t + core) % 2 == 0, R - 1, 0))
            else:
                ds = [dm.partner(t, k) for k in ks if k is not None]
                parts = strip_targets(dm, ep, t, jnp.where(core == 0, ds[0], ds[-1]))
            hot = one_hot(jnp.concatenate(parts, axis=0), dm.N)
            for which in range(2):
                rows = jnp.dot(hot, sources[which], preferred_element_type=F32).astype(BF)
                refs[other * len(steps) + step][which] = rows


def write_self(dm, ep, t, sources, ref):
    hot = one_hot(jnp.concatenate(strip_targets(dm, ep, t, t), axis=0), dm.N)
    for which in range(2):
        ref[which] = jnp.dot(hot, sources[which], preferred_element_type=F32).astype(BF)


def pack_kernel(dm, ep, x_ref, up_ref, *refs):
    t, p = lax.axis_index("tile"), lax.axis_index("dp")
    fields = (x_ref[...], up_ref[...])
    write_messages(dm, ep, t, p, fields, refs[:-1])
    write_self(dm, ep, t, fields, refs[-1])


def merge_kernel(count, *refs):
    for i in range(count):
        refs[2 * count + i][0] = refs[i][...]
        refs[2 * count + i][1] = refs[count + i][...]


def ghost_targets(dm, ep, t):
    R, F, T = dm.R, dm.F, dm.T
    odd = t % 2
    parts = []
    m = col_iota(8)
    q = R * t - 1 + m
    inside = (q >= 0) & (q < F) & (m < R + 2)
    row_prev = dm.o_row + (1 - odd) * dm.ROW
    row_next = dm.o_row + odd * dm.ROW
    side_first = dm.o_msg + (t ^ (T - t)) * dm.BASE + jnp.where(t == 1, R + 2, 0)
    side_last = dm.o_msg + (t ^ (T - 2 - t)) * dm.BASE + jnp.where(t == T - 2, R + 2, 0)
    ends = (t == 0) | (t == dm.MIX) | (t == dm.MIX + 1) | (t == T - 1)
    mirror = dm.o_msg + jnp.where(ends, T - 1, dm.MIX) * dm.BASE
    for f in range(6):
        for edge in (3, 1):
            value = ep[f, edge]
            f2, e2 = value // 4, value % 4
            far_low = e2 < 2
            reverse = far_low if edge < 2 else e2 >= 2
            is_col = (e2 % 2) == 1
            side = jnp.where(e2 == 1, 1, 0)
            column = side * (F - 1)
            slot = f2 * dm.SLOT + side
            row = dm.o_msg + (t ^ jnp.where(e2 == 0, 0, T - 1)) * dm.BASE + f2 * dm.SLOT
            facing = jnp.where(e2 == 0, t == T - 1, t == 0)
            whole = dm.o_row + dm.ROW + f2 * F + jnp.where(reverse, F - R * t, R * t - 1)
            row = jnp.where(facing, whole, row)
            along = jnp.where(facing & reverse, -1, 1)
            i0 = jnp.where(is_col, jnp.where(reverse, side_first + slot, row_prev + f2 * F + column), row)
            i4 = jnp.where(
                is_col, jnp.where(reverse, side_last + slot, row_next + f2 * F + column), row + along * (R + 1)
            )
            base = jnp.where(
                is_col, jnp.where(reverse, mirror + 2 * R + slot, (f2 * R - 1) * F + column), row
            )
            step = jnp.where(is_col, jnp.where(reverse, -2, F), along)
            target = jnp.where(m == 0, i0, jnp.where(m == R + 1, i4, base + step * m))
            parts.append(jnp.where(inside, target, -1))
    j = col_iota(F)
    jt = jnp.zeros_like(j)
    for b in range(1, T):
        jt = jt + jnp.where(j >= b * R, 1, 0)
    jr = j - R * jt
    wrap = dm.o_row + dm.ROW
    for edge in (0, 2):
        at_edge = (t == 0) if edge == 0 else (t == T - 1)
        inner_base = row_prev if edge == 0 else row_next
        own_row = 0 if edge == 0 else R - 1
        for f in range(6):
            value = ep[f, edge]
            f2, e2 = value // 4, value % 4
            far_low = e2 < 2
            reverse = far_low if edge < 2 else e2 >= 2
            is_col = (e2 % 2) == 1
            same = e2 == edge
            row_base = jnp.where(same, (f2 * R + own_row) * F, wrap + f2 * F)
            lin_base = row_base + jnp.where(reverse, F - 1, 0)
            lin_step = jnp.where(reverse, -1, 1)
            k0 = jnp.where(reverse, T - 1, 0)
            ks = jnp.where(reverse, -1, 1)
            if edge == 2:
                k0 = T - 1 - k0
                ks = -ks
            col_base = dm.o_msg + k0 * dm.BASE + f * dm.SLOT + R + 2 + jnp.where(reverse, R - 1, 0)
            base = jnp.where(is_col, col_base, lin_base)
            sj = jnp.where(is_col, 0, lin_step)
            st = jnp.where(is_col, ks * dm.BASE, 0)
            sr = jnp.where(is_col, jnp.where(reverse, -1, 1), 0)
            base = jnp.where(at_edge, base, inner_base + f * F)
            sj = jnp.where(at_edge, sj, 1)
            st = jnp.where(at_edge, st, 0)
            sr = jnp.where(at_edge, sr, 0)
            target = base + sj * j + st * jt + sr * jr
            far_tile = T - 1 if edge == 0 else 0
            from_mirror = is_col & at_edge & (jnp.where(reverse, T - 1 - jt, jt) == far_tile)
            side = jnp.where(e2 == 1, 1, 0)
            cells = mirror + f2 * dm.SLOT + side + 2 * jnp.where(reverse, R - 1 - jr, jr)
            parts.append(jnp.where(from_mirror, cells, target))
    return jnp.concatenate(parts, axis=0)


def gather_ghosts(dm, ep, t, p, own, messages, table_ref):
    hot = one_hot(ghost_targets(dm, ep, t), dm.NT)
    out = []
    for which in range(2):
        table_ref[0 : dm.N] = own[which]
        table_ref[dm.o_msg : dm.o_msg + dm.BASE] = messages[-1][which]
        for step, ks in enumerate(dm.steps()):
            here = messages[2 * step][0, which].astype(F32)
            there = messages[2 * step + 1][1, which].astype(F32)
            for core, k in enumerate(ks):
                if k is None:
                    continue
                value = jnp.where(p == core, here, there).astype(BF)
                at = dm.o_msg + k * dm.BASE
                table_ref[at : at + dm.BASE] = value[: dm.BASE]
                if step == 0:
                    at = dm.o_row + core * dm.ROW
                    table_ref[at : at + dm.ROW] = value[dm.BASE :]
        out.append(jnp.dot(hot, table_ref[...], preferred_element_type=F32))
    return out


def own_first(value, p):
    half = value.shape[1] // 2
    low, high = value[:, :half], value[:, half:]
    return jnp.concatenate([jnp.where(p == 0, low, high), jnp.where(p == 0, high, low)], axis=1)


def build_taps(dm, field_ref, ghosts, top, bottom, frame_ref, taps_ref, adjoint, p=None):
    R, F, C = dm.R, dm.F, dm.C
    for f in range(6):
        for r in range(R):
            frame_ref[r + 1, f, 8 : 8 + F] = field_ref[f * R + r].astype(F32)
    frame_ref[0, :, 8 : 8 + F] = top.reshape(6, F, C)
    frame_ref[R + 1, :, 8 : 8 + F] = bottom.reshape(6, F, C)
    for m in range(R + 2):
        for f in range(6):
            if ghosts is None:
                west = jnp.zeros((1, C), F32)
                east = west
            else:
                west = ghosts[16 * f + m : 16 * f + m + 1]
                east = ghosts[16 * f + 8 + m : 16 * f + 8 + m + 1]
            frame_ref[m, f, 7:8] = west
            frame_ref[m, f, 8 + F : 9 + F] = east
    for m in range(R + 2):
        for b in range(3):
            plane = frame_ref[m, :, 7 + b : 7 + b + F].reshape(dm.ROW, C)
            if p is not None:
                plane = own_first(plane, p)
            plane = plane.astype(BF)
            for a in range(3):
                r = m - 2 + a if adjoint else m - a
                tap = 3 * a + (2 - b if adjoint else b)
                if 0 <= r < R:
                    taps_ref[r * dm.ROW : (r + 1) * dm.ROW, tap * C : (tap + 1) * C] = plane


def build_strip_terms(dm, ep, t, ghosts, top, bottom, z_ref):
    R, F = dm.R, dm.F
    z_ref[...] = jnp.zeros(z_ref.shape, F32)

    def tap_of(f, edge, shift):
        e2 = ep[f, edge] % 4
        reverse = e2 < 2 if edge < 2 else e2 >= 2
        along = 1 - jnp.where(reverse, -shift, shift)
        return jnp.where(
            e2 == 0, along, jnp.where(e2 == 2, 6 + along, jnp.where(e2 == 1, 3 * along + 2, 3 * along))
        )

    live = lax.rem(lax.broadcasted_iota(jnp.int32, (dm.WE, 1), 0), 8) < R
    for shift in (-1, 0, 1):
        moved = pltpu.roll(ghosts, (dm.WE - 1 - shift) % dm.WE, 0) if shift > -1 else ghosts
        moved = jnp.where(live, moved, 0.0)
        for f in range(6):
            for side, edge in ((0, 3), (1, 1)):
                at = 16 * f + 8 * side
                z_ref[tap_of(f, edge, shift), at : at + 8] = moved[at : at + 8]

    def add_rows(edge, rows):
        j = lax.rem(lax.broadcasted_iota(jnp.int32, (dm.ROW, 1), 0), F)
        for shift in (-1, 0, 1):
            if shift == 0:
                moved = rows
            else:
                moved = pltpu.roll(rows, (-shift) % dm.ROW, 0)
                moved = jnp.where((j + shift >= 0) & (j + shift < F), moved, 0.0)
            for f in range(6):
                at = dm.WE + F * f
                z_ref[tap_of(f, edge, shift), at : at + F] = moved[F * f : F * (f + 1)]

    @pl.when(t == 0)
    def _():
        add_rows(0, top)

    @pl.when(t == dm.T - 1)
    def _():
        add_rows(2, bottom)


def adjoint(dm, t, taps_ref, z_ref, wt_ref, acc_ref):
    R, F, C, N = dm.R, dm.F, dm.C, dm.N
    for tap in range(9):
        taps_ref[N:, tap * C : (tap + 1) * C] = z_ref[tap].astype(BF)
    total = jnp.dot(taps_ref[...], wt_ref[...], preferred_element_type=F32)
    acc_ref[...] = total[:N]
    strips = total[N:]
    for f in range(6):
        for side in range(2):
            for r in range(R):
                at = (r * 6 + f) * F + side * (F - 1)
                row = 16 * f + 8 * side + r
                acc_ref[at : at + 1] += strips[row : row + 1]

    @pl.when(t == 0)
    def _():
        acc_ref[0 : dm.ROW] += strips[dm.WE :]

    @pl.when(t == dm.T - 1)
    def _():
        acc_ref[(R - 1) * dm.ROW : R * dm.ROW] += strips[dm.WE :]


def turn_kernel(w1_ref, w2_ref, w1s_ref, w1t_ref, w2t_ref):
    p = lax.axis_index("dp")
    half = w1_ref.shape[1] // 2
    for tap in range(9):
        w1t_ref[tap] = w1_ref[tap].T
        w2t_ref[tap] = w2_ref[tap].T
        w1s_ref[tap, :half] = w1_ref[tap, pl.ds(pl.multiple_of(p * half, half), half)]
        w1s_ref[tap, half:] = w1_ref[tap, pl.ds(pl.multiple_of((1 - p) * half, half), half)]


def put_taps(send_ref, keep_ref, first_tap, value):
    half = keep_ref.shape[1]
    for i in range(value.shape[0] // (2 * half)):
        keep_ref[first_tap + i] = value[2 * i * half : (2 * i + 1) * half]
        send_ref[first_tap + i] = value[(2 * i + 1) * half : (2 * i + 2) * half].astype(BF)


def high_low(row):
    i = lax.broadcasted_iota(jnp.int32, (EXTRA, row.shape[1]), 0)
    high = row.astype(BF).astype(F32)
    return jnp.where(i == 0, high, jnp.where(i == 1, row - high, 0.0)).astype(BF)


def both(pair):
    return pair[0:1].astype(F32) + pair[1:2].astype(F32)


def first_kernel(dm, ep, x_ref, up_ref, w1_ref, bias_ref, w2t_ref, *refs):
    T, R, F, N, C = dm.T, dm.R, dm.F, dm.N, dm.C
    M = 2 * len(dm.steps())
    messages = refs[: M + 1]
    refs = refs[M + 1 :]
    send1_ref, keep1_ref, send2_ref, keep2_ref, hid_ref, inner_ref, bias_sum_ref, send_bias_ref = refs[:8]
    out_messages, self_ref = refs[8 : M + 8], refs[M + 8]
    table_ref, frame_ref, xs_ref, us_ref, z_ref, before_ref, acc_ref, hcat_ref = refs[M + 9 :]
    t, p = lax.axis_index("tile"), lax.axis_index("dp")
    own = (x_ref[...].reshape(N, C), up_ref[...].reshape(N, C))
    gx, gu = gather_ghosts(dm, ep, t, p, own, messages, table_ref)
    top, bottom = dm.WE, dm.WE + dm.ROW
    build_taps(dm, x_ref, gx[:top], gx[top:bottom], gx[bottom:], frame_ref, xs_ref, False, p)
    before = jnp.dot(xs_ref[...], w1_ref[...], preferred_element_type=F32) + bias_ref[...]
    before_ref[...] = before
    sig = 1.0 / (1.0 + jnp.exp(-before))
    acc_ref[...] = before * sig
    up_top = jnp.where(t == 0, 0.0, gu[top:bottom])
    up_bottom = jnp.where(t == T - 1, 0.0, gu[bottom:])
    build_taps(dm, up_ref, None, up_top, up_bottom, frame_ref, us_ref, True)
    build_strip_terms(dm, ep, t, gu[:top], gu[top:bottom], gu[bottom:], z_ref)
    hcat_ref[0:N] = acc_ref[...]
    hcat_ref[N:] = jnp.zeros((dm.S, C), F32)
    for f in range(6):
        for side in range(2):
            for r in range(R):
                at = (r * 6 + f) * F + side * (F - 1)
                row = N + 16 * f + 8 * side + r
                hcat_ref[row : row + 1] = acc_ref[at : at + 1]
    first_row = acc_ref[0 : dm.ROW]
    last_row = acc_ref[(R - 1) * dm.ROW : R * dm.ROW]
    hcat_ref[N + dm.WE :] = jnp.where(t == 0, first_row, last_row)
    for r in range(R):
        for f in range(6):
            at = (r * 6 + f) * F
            hid_ref[f * R + r] = acc_ref[at : at + F].astype(BF)
    adjoint(dm, t, us_ref, z_ref, w2t_ref, acc_ref)
    hidden_t = own_first(hcat_ref[...], p).astype(BF).T
    for tap in range(9):
        grad = jnp.dot(hidden_t, us_ref[:, tap * C : (tap + 1) * C], preferred_element_type=F32)
        put_taps(send2_ref, keep2_ref, tap, grad)
    before = before_ref[...]
    sig = 1.0 / (1.0 + jnp.exp(-before))
    before_grad = acc_ref[...] * (sig * (1.0 + before * (1.0 - sig)))
    acc_ref[...] = before_grad
    inner = before_grad.astype(BF)
    for tap in (0, 3, 6):
        grad = lax.dot_general(
            xs_ref[:, tap * C : (tap + 3) * C],
            inner,
            (((0,), (0,)), ((), ())),
            preferred_element_type=F32,
        )
        put_taps(send1_ref, keep1_ref, tap, grad)
    bias_sum = jnp.sum(before_grad, axis=0, keepdims=True)
    bias_sum_ref[...] = bias_sum
    send_bias_ref[...] = high_low(bias_sum)
    for r in range(R):
        for f in range(6):
            at = (r * 6 + f) * F
            inner_ref[f * R + r] = acc_ref[at : at + F].astype(BF)
    fields = (hid_ref[...].reshape(N, C), inner_ref[...].reshape(N, C))
    write_messages(dm, ep, t, p, fields, out_messages)
    write_self(dm, ep, t, fields, self_ref)


def second_kernel(dm, ep, x_ref, d_ref, hid_ref, inner_ref, w1t_ref, w2_ref, *refs):
    T, R, F, N, C = dm.T, dm.R, dm.F, dm.N, dm.C
    M = 2 * len(dm.steps()) + 1
    messages = refs[:M]
    state_ref, grad_ref = refs[M : M + 2]
    table_ref, frame_ref, hs_ref, is_ref, z_ref, acc_ref = refs[M + 2 :]
    t, p = lax.axis_index("tile"), lax.axis_index("dp")
    own = (hid_ref[...].reshape(N, C), inner_ref[...].reshape(N, C))
    gh, gi = gather_ghosts(dm, ep, t, p, own, messages, table_ref)
    top, bottom = dm.WE, dm.WE + dm.ROW
    build_taps(dm, hid_ref, gh[:top], gh[top:bottom], gh[bottom:], frame_ref, hs_ref, False)
    acc_ref[...] = jnp.dot(hs_ref[...], w2_ref[...], preferred_element_type=F32)
    for r in range(R):
        for f in range(6):
            at = (r * 6 + f) * F
            value = x_ref[f * R + r].astype(F32) + acc_ref[at : at + F]
            state_ref[f * R + r] = value.astype(BF)
    in_top = jnp.where(t == 0, 0.0, gi[top:bottom])
    in_bottom = jnp.where(t == T - 1, 0.0, gi[bottom:])
    build_taps(dm, inner_ref, None, in_top, in_bottom, frame_ref, is_ref, True)
    build_strip_terms(dm, ep, t, gi[:top], gi[top:bottom], gi[bottom:], z_ref)
    adjoint(dm, t, is_ref, z_ref, w1t_ref, acc_ref)
    for r in range(R):
        for f in range(6):
            at = (r * 6 + f) * F
            grad_ref[f * R + r] = d_ref[f * R + r].astype(F32) + acc_ref[at : at + F]


def half_kernel(zcount, keep_ref, recv_ref, *refs):
    size = keep_ref.shape[1] // 2
    own = lax.axis_index("tile") % 2
    mine = pl.ds(pl.multiple_of(own * size, size), size)
    far = pl.ds(pl.multiple_of((1 - own) * size, size), size)
    part = size // zcount
    if len(refs) > 2:
        bias_ref, recv_bias_ref, out_keep, out_send, out_bias = refs
        bias = bias_ref[...] + both(recv_bias_ref)
        out_bias[...] = bias
        out_send[9 * size :] = high_low(bias)
    else:
        out_keep, out_send = refs
    for tap in range(9):
        kept = keep_ref[tap, mine] + recv_ref[tap, mine].astype(F32)
        sent = keep_ref[tap, far] + recv_ref[tap, far].astype(F32)
        for j in range(zcount):
            at = j * 9 * part + tap * part
            out_keep[j, tap * part : (tap + 1) * part] = kept[j * part : (j + 1) * part]
            out_send[at : at + part] = sent[j * part : (j + 1) * part].astype(BF)


def block_kernel(zcount, keep_ref, recv_ref, *refs):
    own = lax.axis_index("tile") // 2
    n = keep_ref.shape[1]
    if len(refs) > zcount + 1:
        bias_ref, out_keep, *out_sends, out_bias, sum_ref = refs
        bias = bias_ref[...] + both(recv_ref[zcount * n : zcount * n + 2])
        out_bias[...] = bias
        tail = high_low(bias)
    else:
        out_keep, *out_sends, sum_ref = refs
        tail = None
    for j in range(zcount):
        sum_ref[j] = keep_ref[j] + recv_ref[j * n : (j + 1) * n].astype(F32)
    out_keep[...] = sum_ref[own]
    for j in range(1, zcount):
        out_sends[j - 1][0:n] = sum_ref[own ^ j].astype(BF)
        if tail is not None:
            out_sends[j - 1][n:] = tail


def last_kernel(zcount, keep_ref, *refs):
    recvs = refs[: zcount - 1]
    n = keep_ref.shape[0]
    total = keep_ref[...]
    for ref in recvs:
        total = total + ref[0:n].astype(F32)
    if len(refs) > zcount:
        bias_ref, block_ref, out_bias = refs[zcount - 1 :]
        bias = bias_ref[...]
        for ref in recvs:
            bias = bias + both(ref[n : n + 2])
        out_bias[...] = bias
    else:
        block_ref = refs[-1]
    block_ref[...] = total.astype(BF)


def normal_kernel(zcount, *refs):
    sources, out_ref = refs[:4], refs[4]
    if len(refs) > 5:
        bias_ref, out_ref, out_bias = refs[4:]
        bias = bias_ref[...]
        bias_mean = jnp.mean(bias * bias, keepdims=True)
        out_bias[...] = bias * lax.rsqrt(bias_mean + 1e-06)
    t, p = lax.axis_index("tile"), lax.axis_index("dp")
    n = sources[0].shape[0] // zcount
    size = n // 9
    square = None
    for ref in sources:
        for j in range(zcount):
            v = ref[j * n : (j + 1) * n].astype(F32)
            part = jnp.sum(v * v, axis=0, keepdims=True)
            square = part if square is None else square + part
    mean = jnp.sum(square, keepdims=True) / (9 * out_ref.shape[1] * out_ref.shape[2])
    scale = lax.rsqrt(mean + 1e-06)
    for group, ref in enumerate(sources):
        block = (p ^ (group // 2)) * 2 + ((t % 2) ^ (group % 2))
        for j in range(zcount):
            at = pl.ds(pl.multiple_of((block * zcount + ((t // 2) ^ j)) * size, size), size)
            for tap in range(9):
                row = j * n + tap * size
                out_ref[tap, at] = ref[row : row + size].astype(F32) * scale


def call(kernel, out_shapes, scratch=(), smem_first=False, limit=16):
    def run(*args):
        vmem = pl.BlockSpec(memory_space=pltpu.VMEM)
        smem = pl.BlockSpec(memory_space=pltpu.SMEM)
        specs = [smem if smem_first and i == 0 else vmem for i in range(len(args))]
        return pl.pallas_call(
            kernel,
            out_shape=[jax.ShapeDtypeStruct(s, dt) for s, dt in out_shapes],
            in_specs=specs,
            out_specs=[vmem] * len(out_shapes),
            scratch_shapes=[pltpu.VMEM(s, dt) for s, dt in scratch],
            compiler_params=pltpu.CompilerParams(vmem_limit_bytes=limit << 20),
        )(*args)

    return run


def swap_dp(v):
    count = lax.axis_size("dp")
    return lax.ppermute(v, "dp", [(i, count - 1 - i) for i in range(count)])


def on_device(initial_state, state_cotangents, w_first, bias, w_second, edge_partner):
    tiles = lax.axis_size("tile")
    _, _, rows, face, channels = initial_state.shape
    dm = Dims(rows, face, tiles, channels)
    planes = (6 * rows, face, channels)
    x = initial_state.reshape(planes)
    d = state_cotangents[state_cotangents.shape[0] - 1].reshape(planes)
    taps = (9, channels, channels)
    w1 = w_first.reshape(9 * channels, channels)
    w2 = w_second.reshape(9 * channels, channels)
    w1s, w1t, w2t = call(turn_kernel, [(taps, BF)] * 3)(w_first.reshape(taps), w_second.reshape(taps))
    w1s = w1s.reshape(w1.shape)
    w1t = w1t.reshape(w1.shape)
    w2t = w2t.reshape(w2.shape)
    steps = range(len(dm.steps()))
    pairs = dm.pairs()
    msg_shapes = [((2, dm.rows(i), channels), BF) for i in steps] * 2 + [((2, dm.BASE, channels), BF)]
    flat = (dm.N, channels)

    def merged(packed):
        count = len(steps)
        own, give = packed[:count], [swap_dp(v) for v in packed[count : 2 * count]]
        return call(
            functools.partial(merge_kernel, count), [((2,) + v.shape, BF) for v in own]
        )(*own, *give)

    def across(v, step):
        return lax.ppermute(v, ("tile", "dp"), pairs[step])

    packed = call(
        functools.partial(pack_kernel, dm), msg_shapes, smem_first=True
    )(edge_partner, x.reshape(flat), d.reshape(flat))
    came = [across(v, i) for i, v in enumerate(merged(packed))]
    came, w1s, w1t, w2t = lax.optimization_barrier((came, w1s, w1t, w2t))
    messages = []
    for v in came:
        messages += [v, swap_dp(v)]
    messages.append(packed[-1])
    half = channels // 2
    wide = 9 * channels
    frame = (rows + 2, 6, face + 16, channels)
    outs = call(
        functools.partial(first_kernel, dm),
        [
            ((9, half, channels), BF),
            ((9, half, channels), F32),
            ((9, half, channels), BF),
            ((9, half, channels), F32),
            (planes, BF),
            (planes, BF),
            ((1, channels), F32),
            ((EXTRA, channels), BF),
        ]
        + msg_shapes,
        [
            ((dm.NT, channels), BF),
            (frame, F32),
            ((dm.N, wide), BF),
            ((dm.N + dm.S, wide), BF),
            ((9, dm.S, channels), F32),
            (flat, F32),
            (flat, F32),
            ((dm.N + dm.S, channels), F32),
        ],
        smem_first=True,
        limit=LIMIT,
    )(edge_partner, x, d, w1s, bias.reshape(1, channels), w2t, *messages)
    send1, keep1, send2, keep2, hidden, inner, bias_sum, send_bias = outs[:8]
    packed = list(outs[8:])

    zcount = tiles // 2
    n = 9 * half // tiles
    one = ((1, channels), F32)
    barrier = lax.optimization_barrier

    def along_y(v):
        return lax.ppermute(v, "tile", [(i, i ^ 1) for i in range(tiles)])

    def along_z(v, j):
        return lax.ppermute(v, "tile", [(i, i ^ (2 * j)) for i in range(tiles)])

    def sum_dp(keep, recv, *bias):
        extra = EXTRA if bias else 0
        return call(
            functools.partial(half_kernel, zcount),
            [((zcount, n, channels), F32), ((zcount * n + extra, channels), BF)] + [one] * bool(bias),
        )(keep, recv, *bias)

    def sum_y(keep, recv, *bias):
        extra = EXTRA if bias else 0
        keep, *out = call(
            functools.partial(block_kernel, zcount),
            [((n, channels), F32)] + [((n + extra, channels), BF)] * (zcount - 1) + [one] * bool(bias),
            [((zcount, n, channels), F32)],
        )(keep, recv, *bias)
        return keep, out[: zcount - 1], out[zcount - 1 :]

    def sum_z(keep, recvs, *bias):
        return call(
            functools.partial(last_kernel, zcount), [((n, channels), BF)] + [one] * bool(bias)
        )(keep, *recvs, *bias)

    joined = merged(packed)
    early = list(steps)[1:]
    middle = [i for i in steps if i not in early]
    came = {}

    keep2, send2 = sum_dp(keep2, swap_dp(send2))
    recv2 = along_y(send2)
    keep1, send1, bias_sum = sum_dp(keep1, swap_dp(send1), bias_sum, swap_dp(send_bias))
    recv1 = along_y(send1)
    got = [across(joined[i], i) for i in early]

    keep2, sends2, _ = sum_y(keep2, recv2)
    recvs2 = [along_z(v, j + 1) for j, v in enumerate(sends2)]
    recv1, got = barrier((recv1, got))
    came.update(zip(early, got))

    keep1, sends1, (bias_sum,) = sum_y(keep1, recv1, bias_sum)
    sends1, todo = barrier((sends1, [joined[i] for i in middle]))
    recvs1 = [along_z(v, j + 1) for j, v in enumerate(sends1)]
    got = [across(v, i) for i, v in zip(middle, todo)]

    recvs2, recvs1 = barrier((recvs2, recvs1))
    (own2,) = sum_z(keep2, recvs2)
    own2 = [own2] + [along_z(own2, j) for j in range(1, zcount)]
    came.update(zip(middle, got))

    own1, bias_sum = sum_z(keep1, recvs1, bias_sum)
    own1 = [own1] + [along_z(own1, j) for j in range(1, zcount)]
    own2 = jnp.concatenate(own2, axis=0)
    other2 = along_y(own2)
    own1 = jnp.concatenate(own1, axis=0)
    other1 = along_y(own1)
    messages = []
    for i in steps:
        messages += [came[i], swap_dp(came[i])]
    messages.append(packed[-1])
    own1, messages = barrier((own1, messages))
    state, grad = call(
        functools.partial(second_kernel, dm),
        [(planes, BF), (planes, F32)],
        [
            ((dm.NT, channels), BF),
            (frame, F32),
            ((dm.N, wide), BF),
            ((dm.N + dm.S, wide), BF),
            ((9, dm.S, channels), F32),
            (flat, F32),
        ],
        smem_first=True,
        limit=LIMIT,
    )(edge_partner, x, d, hidden, inner, w1t, w2, *messages)
    other1, state, grad = barrier((other1, state, grad))
    (second_step,) = call(functools.partial(normal_kernel, zcount), [(taps, F32)])(
        own2, other2, swap_dp(own2), swap_dp(other2)
    )
    first_step, bias_step = call(functools.partial(normal_kernel, zcount), [(taps, F32), one])(
        own1, other1, swap_dp(own1), swap_dp(other1), bias_sum
    )
    return (
        state.reshape(initial_state.shape),
        grad.reshape(initial_state.shape),
        first_step.reshape(w_first.shape),
        bias_step.reshape(channels),
        second_step.reshape(w_second.shape),
    )


def solution(mesh):
    return jax.shard_map(
        on_device,
        mesh=mesh,
        in_specs=(
            P(("groups", "dp"), None, "tile", None, None),
            P(None, ("groups", "dp"), None, "tile", None, None),
            P(),
            P(),
            P(),
            P(),
        ),
        out_specs=(
            P(("groups", "dp"), None, "tile", None, None),
            P(("groups", "dp"), None, "tile", None, None),
            P("groups", None, None, None),
            P("groups"),
            P("groups", None, None, None),
        ),
        check_vma=False,
    )
```

```python
import functools

import jax
import jax.numpy as jnp
from jax import lax
from jax.experimental import pallas as pl
from jax.experimental.pallas import tpu as pltpu
from jax.sharding import PartitionSpec as P

BF = jnp.bfloat16
F32 = jnp.float32
EXTRA = 8
LIMIT = 24


class Dims:
    def __init__(self, rows, face, tiles, channels):
        self.R, self.F, self.T, self.C = rows, face, tiles, channels
        self.N = 6 * rows * face
        self.ROW = 6 * face
        self.SLOT = -(-(2 * rows + 2) // 8) * 8
        self.BASE = 6 * self.SLOT
        self.MIX = tiles // 2 - 1
        self.o_msg = self.N
        self.o_row = self.o_msg + tiles * self.BASE
        self.NT = self.o_row + 2 * self.ROW
        self.WE = 12 * 8
        self.S = self.WE + self.ROW

    def partner(self, t, k):
        if k == self.MIX:
            ends = (t == 0) | (t == self.MIX) | (t == self.MIX + 1) | (t == self.T - 1)
            return jnp.where(ends, t ^ k, self.T - 1 - t)
        return t ^ k

    def steps(self):
        rest = [k for k in range(2, self.T - 1)]
        evens = [k for k in rest if k % 2 == 0]
        odds = [k for k in rest if k % 2 == 1]
        rest = evens + odds
        if len(rest) % 2:
            rest = rest[:-1] + [None, rest[-1]]
        return [(1, self.T - 1)] + [(rest[i], rest[i + 1]) for i in range(0, len(rest), 2)]

    def rows(self, step):
        return self.BASE + (self.ROW if step == 0 else 0)

    def pairs(self):
        T, mix = self.T, self.MIX

        def needed(i, d):
            return i in (0, T - 1) or d in (0, T - 1) or d in (T - 2 - i, T - i)

        out = [[(i, i ^ k) for i in range(T) if k == 1 or needed(i, i ^ k)] for k in range(T - 1)]
        out[mix] = [(i, i ^ mix if i in (0, mix, mix + 1, T - 1) else T - 1 - i) for i in range(T)]
        out.append([(i, (i + 1) % T if i % 2 else (i - 1) % T) for i in range(T)])
        return [
            [(2 * i + core, 2 * d + core) for core in range(2) if ks[core] is not None for i, d in out[ks[core]]]
            for ks in self.steps()
        ]


def col_iota(n):
    return lax.broadcasted_iota(jnp.int32, (n, 1), 0)


def one_hot(target, width):
    lanes = lax.broadcasted_iota(jnp.int32, (target.shape[0], width), 1)
    return jnp.where(lanes == target, 1.0, 0.0).astype(BF)


def strip_targets(dm, ep, t, d):
    R, F, T = dm.R, dm.F, dm.T
    at_edge = (t == 0) | (t == T - 1)
    to_edge = (d == 0) | (d == T - 1)
    own_edge = jnp.where(t == 0, 0, 2)
    far_edge = jnp.where(d == 0, 0, 2)
    side_row = jnp.where(d == T - 2 - t, R - 1, 0)
    i = col_iota(dm.SLOT)
    q = R * d - 1 + i
    inside = (q >= 0) & (q < F) & (i < R + 2)
    i2 = i - (R + 2)
    parts = []
    for f in range(6):
        far_low = (ep[f, own_edge] % 4) < 2
        reverse = far_low == (t == 0)
        p0 = jnp.where(reverse, F - 1, 0)
        sgn = jnp.where(reverse, -1, 1)
        row = jnp.where(t == 0, 0, R - 1)
        strip = jnp.where(inside, (f * R + row) * F + p0 + sgn * q, -1)
        sides = (f * R + side_row) * F
        low = jnp.where(at_edge, strip, sides + i * (F - 1))
        low = jnp.where(at_edge | (i < 2), low, -1)
        gvalue = ep[f, far_edge]
        column = jnp.where(gvalue % 4 == 1, F - 1, 0) + (gvalue // 4) * (R * F)
        high = jnp.where(to_edge, column + F * i2, jnp.where(i2 < 2, sides + i2 * (F - 1), -1))
        strips = jnp.where(i2 < 0, low, jnp.where(i2 < R, high, -1))
        parts.append(jnp.where(d == T - 1 - t, mirror_slot(dm, f), strips))
    return parts


def mirror_slot(dm, f):
    i = col_iota(dm.SLOT)
    return jnp.where(i < 2 * dm.R, (f * dm.R + i // 2) * dm.F + (i % 2) * (dm.F - 1), -1)


def row_targets(dm, row):
    j = col_iota(dm.F)
    return [(f * dm.R + row) * dm.F + j for f in range(6)]


def write_messages(dm, ep, t, p, sources, refs):
    R = dm.R
    steps = dm.steps()
    for other in range(2):
        core = p ^ other
        for step, ks in enumerate(steps):
            if step == 0:
                strips = strip_targets(dm, ep, t, t ^ 1)
                parts = [jnp.where(core == 0, strips[f], mirror_slot(dm, f)) for f in range(6)]
                parts = parts + row_targets(dm, jnp.where((t + core) % 2 == 0, R - 1, 0))
            else:
                ds = [dm.partner(t, k) for k in ks if k is not None]
                parts = strip_targets(dm, ep, t, jnp.where(core == 0, ds[0], ds[-1]))
            hot = one_hot(jnp.concatenate(parts, axis=0), dm.N)
            for which in range(2):
                rows = jnp.dot(hot, sources[which], preferred_element_type=F32).astype(BF)
                refs[other * len(steps) + step][which] = rows


def write_self(dm, ep, t, sources, ref):
    hot = one_hot(jnp.concatenate(strip_targets(dm, ep, t, t), axis=0), dm.N)
    for which in range(2):
        ref[which] = jnp.dot(hot, sources[which], preferred_element_type=F32).astype(BF)


def pack_kernel(dm, ep, x_ref, up_ref, *refs):
    t, p = lax.axis_index("tile"), lax.axis_index("dp")
    fields = (x_ref[...], up_ref[...])
    write_messages(dm, ep, t, p, fields, refs[:-1])
    write_self(dm, ep, t, fields, refs[-1])


def merge_kernel(count, *refs):
    for i in range(count):
        refs[2 * count + i][0] = refs[i][...]
        refs[2 * count + i][1] = refs[count + i][...]


def ghost_targets(dm, ep, t):
    R, F, T = dm.R, dm.F, dm.T
    odd = t % 2
    parts = []
    m = col_iota(8)
    q = R * t - 1 + m
    inside = (q >= 0) & (q < F) & (m < R + 2)
    row_prev = dm.o_row + (1 - odd) * dm.ROW
    row_next = dm.o_row + odd * dm.ROW
    side_first = dm.o_msg + (t ^ (T - t)) * dm.BASE + jnp.where(t == 1, R + 2, 0)
    side_last = dm.o_msg + (t ^ (T - 2 - t)) * dm.BASE + jnp.where(t == T - 2, R + 2, 0)
    ends = (t == 0) | (t == dm.MIX) | (t == dm.MIX + 1) | (t == T - 1)
    mirror = dm.o_msg + jnp.where(ends, T - 1, dm.MIX) * dm.BASE
    for f in range(6):
        for edge in (3, 1):
            value = ep[f, edge]
            f2, e2 = value // 4, value % 4
            far_low = e2 < 2
            reverse = far_low if edge < 2 else e2 >= 2
            is_col = (e2 % 2) == 1
            side = jnp.where(e2 == 1, 1, 0)
            column = side * (F - 1)
            slot = f2 * dm.SLOT + side
            row = dm.o_msg + (t ^ jnp.where(e2 == 0, 0, T - 1)) * dm.BASE + f2 * dm.SLOT
            facing = jnp.where(e2 == 0, t == T - 1, t == 0)
            whole = dm.o_row + dm.ROW + f2 * F + jnp.where(reverse, F - R * t, R * t - 1)
            row = jnp.where(facing, whole, row)
            along = jnp.where(facing & reverse, -1, 1)
            i0 = jnp.where(is_col, jnp.where(reverse, side_first + slot, row_prev + f2 * F + column), row)
            i4 = jnp.where(
                is_col, jnp.where(reverse, side_last + slot, row_next + f2 * F + column), row + along * (R + 1)
            )
            base = jnp.where(
                is_col, jnp.where(reverse, mirror + 2 * R + slot, (f2 * R - 1) * F + column), row
            )
            step = jnp.where(is_col, jnp.where(reverse, -2, F), along)
            target = jnp.where(m == 0, i0, jnp.where(m == R + 1, i4, base + step * m))
            parts.append(jnp.where(inside, target, -1))
    j = col_iota(F)
    jt = jnp.zeros_like(j)
    for b in range(1, T):
        jt = jt + jnp.where(j >= b * R, 1, 0)
    jr = j - R * jt
    wrap = dm.o_row + dm.ROW
    for edge in (0, 2):
        at_edge = (t == 0) if edge == 0 else (t == T - 1)
        inner_base = row_prev if edge == 0 else row_next
        own_row = 0 if edge == 0 else R - 1
        for f in range(6):
            value = ep[f, edge]
            f2, e2 = value // 4, value % 4
            far_low = e2 < 2
            reverse = far_low if edge < 2 else e2 >= 2
            is_col = (e2 % 2) == 1
            same = e2 == edge
            row_base = jnp.where(same, (f2 * R + own_row) * F, wrap + f2 * F)
            lin_base = row_base + jnp.where(reverse, F - 1, 0)
            lin_step = jnp.where(reverse, -1, 1)
            k0 = jnp.where(reverse, T - 1, 0)
            ks = jnp.where(reverse, -1, 1)
            if edge == 2:
                k0 = T - 1 - k0
                ks = -ks
            col_base = dm.o_msg + k0 * dm.BASE + f * dm.SLOT + R + 2 + jnp.where(reverse, R - 1, 0)
            base = jnp.where(is_col, col_base, lin_base)
            sj = jnp.where(is_col, 0, lin_step)
            st = jnp.where(is_col, ks * dm.BASE, 0)
            sr = jnp.where(is_col, jnp.where(reverse, -1, 1), 0)
            base = jnp.where(at_edge, base, inner_base + f * F)
            sj = jnp.where(at_edge, sj, 1)
            st = jnp.where(at_edge, st, 0)
            sr = jnp.where(at_edge, sr, 0)
            target = base + sj * j + st * jt + sr * jr
            far_tile = T - 1 if edge == 0 else 0
            from_mirror = is_col & at_edge & (jnp.where(reverse, T - 1 - jt, jt) == far_tile)
            side = jnp.where(e2 == 1, 1, 0)
            cells = mirror + f2 * dm.SLOT + side + 2 * jnp.where(reverse, R - 1 - jr, jr)
            parts.append(jnp.where(from_mirror, cells, target))
    return jnp.concatenate(parts, axis=0)


def gather_ghosts(dm, ep, t, p, own, messages, table_ref):
    hot = one_hot(ghost_targets(dm, ep, t), dm.NT)
    out = []
    for which in range(2):
        table_ref[0 : dm.N] = own[which]
        table_ref[dm.o_msg : dm.o_msg + dm.BASE] = messages[-1][which]
        for step, ks in enumerate(dm.steps()):
            here = messages[2 * step][0, which].astype(F32)
            there = messages[2 * step + 1][1, which].astype(F32)
            for core, k in enumerate(ks):
                if k is None:
                    continue
                value = jnp.where(p == core, here, there).astype(BF)
                at = dm.o_msg + k * dm.BASE
                table_ref[at : at + dm.BASE] = value[: dm.BASE]
                if step == 0:
                    at = dm.o_row + core * dm.ROW
                    table_ref[at : at + dm.ROW] = value[dm.BASE :]
        out.append(jnp.dot(hot, table_ref[...], preferred_element_type=F32))
    return out


def own_first(value, p):
    half = value.shape[1] // 2
    low, high = value[:, :half], value[:, half:]
    return jnp.concatenate([jnp.where(p == 0, low, high), jnp.where(p == 0, high, low)], axis=1)


def build_taps(dm, field_ref, ghosts, top, bottom, frame_ref, taps_ref, adjoint, p=None):
    R, F, C = dm.R, dm.F, dm.C
    for f in range(6):
        for r in range(R):
            frame_ref[r + 1, f, 8 : 8 + F] = field_ref[f * R + r].astype(F32)
    frame_ref[0, :, 8 : 8 + F] = top.reshape(6, F, C)
    frame_ref[R + 1, :, 8 : 8 + F] = bottom.reshape(6, F, C)
    for m in range(R + 2):
        for f in range(6):
            if ghosts is None:
                west = jnp.zeros((1, C), F32)
                east = west
            else:
                west = ghosts[16 * f + m : 16 * f + m + 1]
                east = ghosts[16 * f + 8 + m : 16 * f + 8 + m + 1]
            frame_ref[m, f, 7:8] = west
            frame_ref[m, f, 8 + F : 9 + F] = east
    for m in range(R + 2):
        for b in range(3):
            plane = frame_ref[m, :, 7 + b : 7 + b + F].reshape(dm.ROW, C)
            if p is not None:
                plane = own_first(plane, p)
            plane = plane.astype(BF)
            for a in range(3):
                r = m - 2 + a if adjoint else m - a
                tap = 3 * a + (2 - b if adjoint else b)
                if 0 <= r < R:
                    taps_ref[r * dm.ROW : (r + 1) * dm.ROW, tap * C : (tap + 1) * C] = plane


def build_strip_terms(dm, ep, t, ghosts, top, bottom, z_ref):
    R, F = dm.R, dm.F
    z_ref[...] = jnp.zeros(z_ref.shape, F32)

    def tap_of(f, edge, shift):
        e2 = ep[f, edge] % 4
        reverse = e2 < 2 if edge < 2 else e2 >= 2
        along = 1 - jnp.where(reverse, -shift, shift)
        return jnp.where(
            e2 == 0, along, jnp.where(e2 == 2, 6 + along, jnp.where(e2 == 1, 3 * along + 2, 3 * along))
        )

    live = lax.rem(lax.broadcasted_iota(jnp.int32, (dm.WE, 1), 0), 8) < R
    for shift in (-1, 0, 1):
        moved = pltpu.roll(ghosts, (dm.WE - 1 - shift) % dm.WE, 0) if shift > -1 else ghosts
        moved = jnp.where(live, moved, 0.0)
        for f in range(6):
            for side, edge in ((0, 3), (1, 1)):
                at = 16 * f + 8 * side
                z_ref[tap_of(f, edge, shift), at : at + 8] = moved[at : at + 8]

    def add_rows(edge, rows):
        j = lax.rem(lax.broadcasted_iota(jnp.int32, (dm.ROW, 1), 0), F)
        for shift in (-1, 0, 1):
            if shift == 0:
                moved = rows
            else:
                moved = pltpu.roll(rows, (-shift) % dm.ROW, 0)
                moved = jnp.where((j + shift >= 0) & (j + shift < F), moved, 0.0)
            for f in range(6):
                at = dm.WE + F * f
                z_ref[tap_of(f, edge, shift), at : at + F] = moved[F * f : F * (f + 1)]

    @pl.when(t == 0)
    def _():
        add_rows(0, top)

    @pl.when(t == dm.T - 1)
    def _():
        add_rows(2, bottom)


def adjoint(dm, t, taps_ref, z_ref, wt_ref, acc_ref):
    R, F, C, N = dm.R, dm.F, dm.C, dm.N
    for tap in range(9):
        taps_ref[N:, tap * C : (tap + 1) * C] = z_ref[tap].astype(BF)
    total = jnp.dot(taps_ref[...], wt_ref[...], preferred_element_type=F32)
    acc_ref[...] = total[:N]
    strips = total[N:]
    for f in range(6):
        for side in range(2):
            for r in range(R):
                at = (r * 6 + f) * F + side * (F - 1)
                row = 16 * f + 8 * side + r
                acc_ref[at : at + 1] += strips[row : row + 1]

    @pl.when(t == 0)
    def _():
        acc_ref[0 : dm.ROW] += strips[dm.WE :]

    @pl.when(t == dm.T - 1)
    def _():
        acc_ref[(R - 1) * dm.ROW : R * dm.ROW] += strips[dm.WE :]


def turn_kernel(w1_ref, w2_ref, w1s_ref, w1t_ref, w2t_ref):
    p = lax.axis_index("dp")
    half = w1_ref.shape[1] // 2
    for tap in range(9):
        w1t_ref[tap] = w1_ref[tap].T
        w2t_ref[tap] = w2_ref[tap].T
        w1s_ref[tap, :half] = w1_ref[tap, pl.ds(pl.multiple_of(p * half, half), half)]
        w1s_ref[tap, half:] = w1_ref[tap, pl.ds(pl.multiple_of((1 - p) * half, half), half)]


def put_taps(send_ref, keep_ref, first_tap, value):
    half = keep_ref.shape[1]
    for i in range(value.shape[0] // (2 * half)):
        keep_ref[first_tap + i] = value[2 * i * half : (2 * i + 1) * half]
        send_ref[first_tap + i] = value[(2 * i + 1) * half : (2 * i + 2) * half].astype(BF)


def high_low(row):
    i = lax.broadcasted_iota(jnp.int32, (EXTRA, row.shape[1]), 0)
    high = row.astype(BF).astype(F32)
    return jnp.where(i == 0, high, jnp.where(i == 1, row - high, 0.0)).astype(BF)


def both(pair):
    return pair[0:1].astype(F32) + pair[1:2].astype(F32)


def first_kernel(dm, ep, x_ref, up_ref, w1_ref, bias_ref, w2t_ref, *refs):
    T, R, F, N, C = dm.T, dm.R, dm.F, dm.N, dm.C
    M = 2 * len(dm.steps())
    messages = refs[: M + 1]
    refs = refs[M + 1 :]
    send1_ref, keep1_ref, send2_ref, keep2_ref, hid_ref, inner_ref, bias_sum_ref, send_bias_ref = refs[:8]
    out_messages, self_ref = refs[8 : M + 8], refs[M + 8]
    table_ref, frame_ref, xs_ref, us_ref, z_ref, before_ref, acc_ref, hcat_ref = refs[M + 9 :]
    t, p = lax.axis_index("tile"), lax.axis_index("dp")
    own = (x_ref[...].reshape(N, C), up_ref[...].reshape(N, C))
    gx, gu = gather_ghosts(dm, ep, t, p, own, messages, table_ref)
    top, bottom = dm.WE, dm.WE + dm.ROW
    build_taps(dm, x_ref, gx[:top], gx[top:bottom], gx[bottom:], frame_ref, xs_ref, False, p)
    before = jnp.dot(xs_ref[...], w1_ref[...], preferred_element_type=F32) + bias_ref[...]
    before_ref[...] = before
    sig = 1.0 / (1.0 + jnp.exp(-before))
    acc_ref[...] = before * sig
    up_top = jnp.where(t == 0, 0.0, gu[top:bottom])
    up_bottom = jnp.where(t == T - 1, 0.0, gu[bottom:])
    build_taps(dm, up_ref, None, up_top, up_bottom, frame_ref, us_ref, True)
    build_strip_terms(dm, ep, t, gu[:top], gu[top:bottom], gu[bottom:], z_ref)
    hcat_ref[0:N] = acc_ref[...]
    hcat_ref[N:] = jnp.zeros((dm.S, C), F32)
    for f in range(6):
        for side in range(2):
            for r in range(R):
                at = (r * 6 + f) * F + side * (F - 1)
                row = N + 16 * f + 8 * side + r
                hcat_ref[row : row + 1] = acc_ref[at : at + 1]
    first_row = acc_ref[0 : dm.ROW]
    last_row = acc_ref[(R - 1) * dm.ROW : R * dm.ROW]
    hcat_ref[N + dm.WE :] = jnp.where(t == 0, first_row, last_row)
    for r in range(R):
        for f in range(6):
            at = (r * 6 + f) * F
            hid_ref[f * R + r] = acc_ref[at : at + F].astype(BF)
    adjoint(dm, t, us_ref, z_ref, w2t_ref, acc_ref)
    hidden_t = own_first(hcat_ref[...], p).astype(BF).T
    for tap in range(9):
        grad = jnp.dot(hidden_t, us_ref[:, tap * C : (tap + 1) * C], preferred_element_type=F32)
        put_taps(send2_ref, keep2_ref, tap, grad)
    before = before_ref[...]
    sig = 1.0 / (1.0 + jnp.exp(-before))
    before_grad = acc_ref[...] * (sig * (1.0 + before * (1.0 - sig)))
    acc_ref[...] = before_grad
    inner = before_grad.astype(BF)
    for tap in (0, 3, 6):
        grad = lax.dot_general(
            xs_ref[:, tap * C : (tap + 3) * C],
            inner,
            (((0,), (0,)), ((), ())),
            preferred_element_type=F32,
        )
        put_taps(send1_ref, keep1_ref, tap, grad)
    bias_sum = jnp.sum(before_grad, axis=0, keepdims=True)
    bias_sum_ref[...] = bias_sum
    send_bias_ref[...] = high_low(bias_sum)
    for r in range(R):
        for f in range(6):
            at = (r * 6 + f) * F
            inner_ref[f * R + r] = acc_ref[at : at + F].astype(BF)
    fields = (hid_ref[...].reshape(N, C), inner_ref[...].reshape(N, C))
    write_messages(dm, ep, t, p, fields, out_messages)
    write_self(dm, ep, t, fields, self_ref)


def second_kernel(dm, ep, x_ref, d_ref, hid_ref, inner_ref, w1t_ref, w2_ref, *refs):
    T, R, F, N, C = dm.T, dm.R, dm.F, dm.N, dm.C
    M = 2 * len(dm.steps()) + 1
    messages = refs[:M]
    state_ref, grad_ref = refs[M : M + 2]
    table_ref, frame_ref, hs_ref, is_ref, z_ref, acc_ref = refs[M + 2 :]
    t, p = lax.axis_index("tile"), lax.axis_index("dp")
    own = (hid_ref[...].reshape(N, C), inner_ref[...].reshape(N, C))
    gh, gi = gather_ghosts(dm, ep, t, p, own, messages, table_ref)
    top, bottom = dm.WE, dm.WE + dm.ROW
    build_taps(dm, hid_ref, gh[:top], gh[top:bottom], gh[bottom:], frame_ref, hs_ref, False)
    acc_ref[...] = jnp.dot(hs_ref[...], w2_ref[...], preferred_element_type=F32)
    for r in range(R):
        for f in range(6):
            at = (r * 6 + f) * F
            value = x_ref[f * R + r].astype(F32) + acc_ref[at : at + F]
            state_ref[f * R + r] = value.astype(BF)
    in_top = jnp.where(t == 0, 0.0, gi[top:bottom])
    in_bottom = jnp.where(t == T - 1, 0.0, gi[bottom:])
    build_taps(dm, inner_ref, None, in_top, in_bottom, frame_ref, is_ref, True)
    build_strip_terms(dm, ep, t, gi[:top], gi[top:bottom], gi[bottom:], z_ref)
    adjoint(dm, t, is_ref, z_ref, w1t_ref, acc_ref)
    for r in range(R):
        for f in range(6):
            at = (r * 6 + f) * F
            grad_ref[f * R + r] = d_ref[f * R + r].astype(F32) + acc_ref[at : at + F]


def half_kernel(zcount, keep_ref, recv_ref, *refs):
    size = keep_ref.shape[1] // 2
    own = lax.axis_index("tile") % 2
    mine = pl.ds(pl.multiple_of(own * size, size), size)
    far = pl.ds(pl.multiple_of((1 - own) * size, size), size)
    part = size // zcount
    if len(refs) > 2:
        bias_ref, recv_bias_ref, out_keep, out_send, out_bias = refs
        bias = bias_ref[...] + both(recv_bias_ref)
        out_bias[...] = bias
        out_send[9 * size :] = high_low(bias)
    else:
        out_keep, out_send = refs
    for tap in range(9):
        kept = keep_ref[tap, mine] + recv_ref[tap, mine].astype(F32)
        sent = keep_ref[tap, far] + recv_ref[tap, far].astype(F32)
        for j in range(zcount):
            at = j * 9 * part + tap * part
            out_keep[j, tap * part : (tap + 1) * part] = kept[j * part : (j + 1) * part]
            out_send[at : at + part] = sent[j * part : (j + 1) * part].astype(BF)


def block_kernel(zcount, keep_ref, recv_ref, *refs):
    own = lax.axis_index("tile") // 2
    n = keep_ref.shape[1]
    if len(refs) > zcount + 1:
        bias_ref, out_keep, *out_sends, out_bias, sum_ref = refs
        bias = bias_ref[...] + both(recv_ref[zcount * n : zcount * n + 2])
        out_bias[...] = bias
        tail = high_low(bias)
    else:
        out_keep, *out_sends, sum_ref = refs
        tail = None
    for j in range(zcount):
        sum_ref[j] = keep_ref[j] + recv_ref[j * n : (j + 1) * n].astype(F32)
    out_keep[...] = sum_ref[own]
    for j in range(1, zcount):
        out_sends[j - 1][0:n] = sum_ref[own ^ j].astype(BF)
        if tail is not None:
            out_sends[j - 1][n:] = tail


def last_kernel(zcount, keep_ref, *refs):
    recvs = refs[: zcount - 1]
    n = keep_ref.shape[0]
    total = keep_ref[...]
    for ref in recvs:
        total = total + ref[0:n].astype(F32)
    if len(refs) > zcount:
        bias_ref, block_ref, out_bias = refs[zcount - 1 :]
        bias = bias_ref[...]
        for ref in recvs:
            bias = bias + both(ref[n : n + 2])
        out_bias[...] = bias
    else:
        block_ref = refs[-1]
    block_ref[...] = total.astype(BF)


def normal_kernel(zcount, *refs):
    sources, out_ref = refs[:4], refs[4]
    if len(refs) > 5:
        bias_ref, out_ref, out_bias = refs[4:]
        bias = bias_ref[...]
        bias_mean = jnp.mean(bias * bias, keepdims=True)
        out_bias[...] = bias * lax.rsqrt(bias_mean + 1e-06)
    t, p = lax.axis_index("tile"), lax.axis_index("dp")
    n = sources[0].shape[0] // zcount
    size = n // 9
    square = None
    for ref in sources:
        for j in range(zcount):
            v = ref[j * n : (j + 1) * n].astype(F32)
            part = jnp.sum(v * v, axis=0, keepdims=True)
            square = part if square is None else square + part
    mean = jnp.sum(square, keepdims=True) / (9 * out_ref.shape[1] * out_ref.shape[2])
    scale = lax.rsqrt(mean + 1e-06)
    for group, ref in enumerate(sources):
        block = (p ^ (group // 2)) * 2 + ((t % 2) ^ (group % 2))
        for j in range(zcount):
            at = pl.ds(pl.multiple_of((block * zcount + ((t // 2) ^ j)) * size, size), size)
            for tap in range(9):
                row = j * n + tap * size
                out_ref[tap, at] = ref[row : row + size].astype(F32) * scale


def call(kernel, out_shapes, scratch=(), smem_first=False, limit=16):
    def run(*args):
        vmem = pl.BlockSpec(memory_space=pltpu.VMEM)
        smem = pl.BlockSpec(memory_space=pltpu.SMEM)
        specs = [smem if smem_first and i == 0 else vmem for i in range(len(args))]
        return pl.pallas_call(
            kernel,
            out_shape=[jax.ShapeDtypeStruct(s, dt) for s, dt in out_shapes],
            in_specs=specs,
            out_specs=[vmem] * len(out_shapes),
            scratch_shapes=[pltpu.VMEM(s, dt) for s, dt in scratch],
            compiler_params=pltpu.CompilerParams(vmem_limit_bytes=limit << 20),
        )(*args)

    return run


def swap_dp(v):
    count = lax.axis_size("dp")
    return lax.ppermute(v, "dp", [(i, count - 1 - i) for i in range(count)])


def on_device(initial_state, state_cotangents, w_first, bias, w_second, edge_partner):
    tiles = lax.axis_size("tile")
    _, _, rows, face, channels = initial_state.shape
    dm = Dims(rows, face, tiles, channels)
    planes = (6 * rows, face, channels)
    x = initial_state.reshape(planes)
    d = state_cotangents[state_cotangents.shape[0] - 1].reshape(planes)
    taps = (9, channels, channels)
    w1 = w_first.reshape(9 * channels, channels)
    w2 = w_second.reshape(9 * channels, channels)
    w1s, w1t, w2t = call(turn_kernel, [(taps, BF)] * 3)(w_first.reshape(taps), w_second.reshape(taps))
    w1s = w1s.reshape(w1.shape)
    w1t = w1t.reshape(w1.shape)
    w2t = w2t.reshape(w2.shape)
    steps = range(len(dm.steps()))
    pairs = dm.pairs()
    msg_shapes = [((2, dm.rows(i), channels), BF) for i in steps] * 2 + [((2, dm.BASE, channels), BF)]
    flat = (dm.N, channels)

    def merged(packed):
        count = len(steps)
        own, give = packed[:count], [swap_dp(v) for v in packed[count : 2 * count]]
        return call(
            functools.partial(merge_kernel, count), [((2,) + v.shape, BF) for v in own]
        )(*own, *give)

    def across(v, step):
        return lax.ppermute(v, ("tile", "dp"), pairs[step])

    packed = call(
        functools.partial(pack_kernel, dm), msg_shapes, smem_first=True
    )(edge_partner, x.reshape(flat), d.reshape(flat))
    came = [across(v, i) for i, v in enumerate(merged(packed))]
    came, w1s, w1t, w2t = lax.optimization_barrier((came, w1s, w1t, w2t))
    messages = []
    for v in came:
        messages += [v, swap_dp(v)]
    messages.append(packed[-1])
    half = channels // 2
    wide = 9 * channels
    frame = (rows + 2, 6, face + 16, channels)
    outs = call(
        functools.partial(first_kernel, dm),
        [
            ((9, half, channels), BF),
            ((9, half, channels), F32),
            ((9, half, channels), BF),
            ((9, half, channels), F32),
            (planes, BF),
            (planes, BF),
            ((1, channels), F32),
            ((EXTRA, channels), BF),
        ]
        + msg_shapes,
        [
            ((dm.NT, channels), BF),
            (frame, F32),
            ((dm.N, wide), BF),
            ((dm.N + dm.S, wide), BF),
            ((9, dm.S, channels), F32),
            (flat, F32),
            (flat, F32),
            ((dm.N + dm.S, channels), F32),
        ],
        smem_first=True,
        limit=LIMIT,
    )(edge_partner, x, d, w1s, bias.reshape(1, channels), w2t, *messages)
    send1, keep1, send2, keep2, hidden, inner, bias_sum, send_bias = outs[:8]
    packed = list(outs[8:])

    zcount = tiles // 2
    n = 9 * half // tiles
    one = ((1, channels), F32)
    barrier = lax.optimization_barrier

    def along_y(v):
        return lax.ppermute(v, "tile", [(i, i ^ 1) for i in range(tiles)])

    def along_z(v, j):
        return lax.ppermute(v, "tile", [(i, i ^ (2 * j)) for i in range(tiles)])

    def sum_dp(keep, recv, *bias):
        extra = EXTRA if bias else 0
        return call(
            functools.partial(half_kernel, zcount),
            [((zcount, n, channels), F32), ((zcount * n + extra, channels), BF)] + [one] * bool(bias),
        )(keep, recv, *bias)

    def sum_y(keep, recv, *bias):
        extra = EXTRA if bias else 0
        keep, *out = call(
            functools.partial(block_kernel, zcount),
            [((n, channels), F32)] + [((n + extra, channels), BF)] * (zcount - 1) + [one] * bool(bias),
            [((zcount, n, channels), F32)],
        )(keep, recv, *bias)
        return keep, out[: zcount - 1], out[zcount - 1 :]

    def sum_z(keep, recvs, *bias):
        return call(
            functools.partial(last_kernel, zcount), [((n, channels), BF)] + [one] * bool(bias)
        )(keep, *recvs, *bias)

    joined = merged(packed)
    early = list(steps)[1:]
    middle = [i for i in steps if i not in early]
    came = {}

    keep2, send2 = sum_dp(keep2, swap_dp(send2))
    recv2 = along_y(send2)
    keep1, send1, bias_sum = sum_dp(keep1, swap_dp(send1), bias_sum, swap_dp(send_bias))
    got = [across(joined[i], i) for i in early]
    recv2, send1, got = barrier((recv2, send1, got))
    came.update(zip(early, got))
    recv1 = along_y(send1)

    keep2, sends2, _ = sum_y(keep2, recv2)
    recvs2 = [along_z(v, j + 1) for j, v in enumerate(sends2)]

    keep1, sends1, (bias_sum,) = sum_y(keep1, recv1, bias_sum)
    sends1, todo = barrier((sends1, [joined[i] for i in middle]))
    recvs1 = [along_z(v, j + 1) for j, v in enumerate(sends1)]
    got = [across(v, i) for i, v in zip(middle, todo)]

    recvs2, recvs1 = barrier((recvs2, recvs1))
    (own2,) = sum_z(keep2, recvs2)
    own2 = [own2] + [along_z(own2, j) for j in range(1, zcount)]
    came.update(zip(middle, got))

    own1, bias_sum = sum_z(keep1, recvs1, bias_sum)
    own1 = [own1] + [along_z(own1, j) for j in range(1, zcount)]
    own2 = jnp.concatenate(own2, axis=0)
    other2 = along_y(own2)
    own1 = jnp.concatenate(own1, axis=0)
    other1 = along_y(own1)
    messages = []
    for i in steps:
        messages += [came[i], swap_dp(came[i])]
    messages.append(packed[-1])
    own1, messages = barrier((own1, messages))
    state, grad = call(
        functools.partial(second_kernel, dm),
        [(planes, BF), (planes, F32)],
        [
            ((dm.NT, channels), BF),
            (frame, F32),
            ((dm.N, wide), BF),
            ((dm.N + dm.S, wide), BF),
            ((9, dm.S, channels), F32),
            (flat, F32),
        ],
        smem_first=True,
        limit=LIMIT,
    )(edge_partner, x, d, hidden, inner, w1t, w2, *messages)
    other1, state, grad = barrier((other1, state, grad))
    (second_step,) = call(functools.partial(normal_kernel, zcount), [(taps, F32)])(
        own2, other2, swap_dp(own2), swap_dp(other2)
    )
    first_step, bias_step = call(functools.partial(normal_kernel, zcount), [(taps, F32), one])(
        own1, other1, swap_dp(own1), swap_dp(other1), bias_sum
    )
    return (
        state.reshape(initial_state.shape),
        grad.reshape(initial_state.shape),
        first_step.reshape(w_first.shape),
        bias_step.reshape(channels),
        second_step.reshape(w_second.shape),
    )


def solution(mesh):
    return jax.shard_map(
        on_device,
        mesh=mesh,
        in_specs=(
            P(("groups", "dp"), None, "tile", None, None),
            P(None, ("groups", "dp"), None, "tile", None, None),
            P(),
            P(),
            P(),
            P(),
        ),
        out_specs=(
            P(("groups", "dp"), None, "tile", None, None),
            P(("groups", "dp"), None, "tile", None, None),
            P("groups", None, None, None),
            P("groups"),
            P("groups", None, None, None),
        ),
        check_vma=False,
    )
```

```python
import functools

import jax
import jax.numpy as jnp
from jax import lax
from jax.experimental import pallas as pl
from jax.experimental.pallas import tpu as pltpu
from jax.sharding import PartitionSpec as P

BF = jnp.bfloat16
F32 = jnp.float32
EXTRA = 8
LIMIT = 24


class Dims:
    def __init__(self, rows, face, tiles, channels):
        self.R, self.F, self.T, self.C = rows, face, tiles, channels
        self.N = 6 * rows * face
        self.ROW = 6 * face
        self.SLOT = -(-(2 * rows + 2) // 8) * 8
        self.BASE = 6 * self.SLOT
        self.MIX = tiles // 2 - 1
        self.o_msg = self.N
        self.o_row = self.o_msg + tiles * self.BASE
        self.NT = self.o_row + 2 * self.ROW
        self.WE = 12 * 8
        self.S = self.WE + self.ROW

    def partner(self, t, k):
        if k == self.MIX:
            ends = (t == 0) | (t == self.MIX) | (t == self.MIX + 1) | (t == self.T - 1)
            return jnp.where(ends, t ^ k, self.T - 1 - t)
        return t ^ k

    def steps(self):
        rest = [k for k in range(2, self.T - 1)]
        evens = [k for k in rest if k % 2 == 0]
        odds = [k for k in rest if k % 2 == 1]
        rest = evens + odds
        if len(rest) % 2:
            rest = rest[:-1] + [None, rest[-1]]
        return [(1, self.T - 1)] + [(rest[i], rest[i + 1]) for i in range(0, len(rest), 2)]

    def rows(self, step):
        return self.BASE + (self.ROW if step == 0 else 0)

    def pairs(self):
        T, mix = self.T, self.MIX

        def needed(i, d):
            return i in (0, T - 1) or d in (0, T - 1) or d in (T - 2 - i, T - i)

        out = [[(i, i ^ k) for i in range(T) if k == 1 or needed(i, i ^ k)] for k in range(T - 1)]
        out[mix] = [(i, i ^ mix if i in (0, mix, mix + 1, T - 1) else T - 1 - i) for i in range(T)]
        out.append([(i, (i + 1) % T if i % 2 else (i - 1) % T) for i in range(T)])
        return [
            [(2 * i + core, 2 * d + core) for core in range(2) if ks[core] is not None for i, d in out[ks[core]]]
            for ks in self.steps()
        ]


def col_iota(n):
    return lax.broadcasted_iota(jnp.int32, (n, 1), 0)


def one_hot(target, width):
    lanes = lax.broadcasted_iota(jnp.int32, (target.shape[0], width), 1)
    return jnp.where(lanes == target, 1.0, 0.0).astype(BF)


def strip_targets(dm, ep, t, d):
    R, F, T = dm.R, dm.F, dm.T
    at_edge = (t == 0) | (t == T - 1)
    to_edge = (d == 0) | (d == T - 1)
    own_edge = jnp.where(t == 0, 0, 2)
    far_edge = jnp.where(d == 0, 0, 2)
    side_row = jnp.where(d == T - 2 - t, R - 1, 0)
    i = col_iota(dm.SLOT)
    q = R * d - 1 + i
    inside = (q >= 0) & (q < F) & (i < R + 2)
    i2 = i - (R + 2)
    parts = []
    for f in range(6):
        far_low = (ep[f, own_edge] % 4) < 2
        reverse = far_low == (t == 0)
        p0 = jnp.where(reverse, F - 1, 0)
        sgn = jnp.where(reverse, -1, 1)
        row = jnp.where(t == 0, 0, R - 1)
        strip = jnp.where(inside, (f * R + row) * F + p0 + sgn * q, -1)
        sides = (f * R + side_row) * F
        low = jnp.where(at_edge, strip, sides + i * (F - 1))
        low = jnp.where(at_edge | (i < 2), low, -1)
        gvalue = ep[f, far_edge]
        column = jnp.where(gvalue % 4 == 1, F - 1, 0) + (gvalue // 4) * (R * F)
        high = jnp.where(to_edge, column + F * i2, jnp.where(i2 < 2, sides + i2 * (F - 1), -1))
        strips = jnp.where(i2 < 0, low, jnp.where(i2 < R, high, -1))
        parts.append(jnp.where(d == T - 1 - t, mirror_slot(dm, f), strips))
    return parts


def mirror_slot(dm, f):
    i = col_iota(dm.SLOT)
    return jnp.where(i < 2 * dm.R, (f * dm.R + i // 2) * dm.F + (i % 2) * (dm.F - 1), -1)


def row_targets(dm, row):
    j = col_iota(dm.F)
    return [(f * dm.R + row) * dm.F + j for f in range(6)]


def write_messages(dm, ep, t, p, sources, refs):
    R = dm.R
    steps = dm.steps()
    for other in range(2):
        core = p ^ other
        for step, ks in enumerate(steps):
            if step == 0:
                strips = strip_targets(dm, ep, t, t ^ 1)
                parts = [jnp.where(core == 0, strips[f], mirror_slot(dm, f)) for f in range(6)]
                parts = parts + row_targets(dm, jnp.where((t + core) % 2 == 0, R - 1, 0))
            else:
                ds = [dm.partner(t, k) for k in ks if k is not None]
                parts = strip_targets(dm, ep, t, jnp.where(core == 0, ds[0], ds[-1]))
            hot = one_hot(jnp.concatenate(parts, axis=0), dm.N)
            for which in range(2):
                rows = jnp.dot(hot, sources[which], preferred_element_type=F32).astype(BF)
                refs[other * len(steps) + step][which] = rows


def write_self(dm, ep, t, sources, ref):
    hot = one_hot(jnp.concatenate(strip_targets(dm, ep, t, t), axis=0), dm.N)
    for which in range(2):
        ref[which] = jnp.dot(hot, sources[which], preferred_element_type=F32).astype(BF)


def pack_kernel(dm, ep, x_ref, up_ref, *refs):
    t, p = lax.axis_index("tile"), lax.axis_index("dp")
    fields = (x_ref[...], up_ref[...])
    write_messages(dm, ep, t, p, fields, refs[:-1])
    write_self(dm, ep, t, fields, refs[-1])


def merge_kernel(count, *refs):
    for i in range(count):
        refs[2 * count + i][0] = refs[i][...]
        refs[2 * count + i][1] = refs[count + i][...]


def ghost_targets(dm, ep, t):
    R, F, T = dm.R, dm.F, dm.T
    odd = t % 2
    parts = []
    m = col_iota(8)
    q = R * t - 1 + m
    inside = (q >= 0) & (q < F) & (m < R + 2)
    row_prev = dm.o_row + (1 - odd) * dm.ROW
    row_next = dm.o_row + odd * dm.ROW
    side_first = dm.o_msg + (t ^ (T - t)) * dm.BASE + jnp.where(t == 1, R + 2, 0)
    side_last = dm.o_msg + (t ^ (T - 2 - t)) * dm.BASE + jnp.where(t == T - 2, R + 2, 0)
    ends = (t == 0) | (t == dm.MIX) | (t == dm.MIX + 1) | (t == T - 1)
    mirror = dm.o_msg + jnp.where(ends, T - 1, dm.MIX) * dm.BASE
    for f in range(6):
        for edge in (3, 1):
            value = ep[f, edge]
            f2, e2 = value // 4, value % 4
            far_low = e2 < 2
            reverse = far_low if edge < 2 else e2 >= 2
            is_col = (e2 % 2) == 1
            side = jnp.where(e2 == 1, 1, 0)
            column = side * (F - 1)
            slot = f2 * dm.SLOT + side
            row = dm.o_msg + (t ^ jnp.where(e2 == 0, 0, T - 1)) * dm.BASE + f2 * dm.SLOT
            facing = jnp.where(e2 == 0, t == T - 1, t == 0)
            whole = dm.o_row + dm.ROW + f2 * F + jnp.where(reverse, F - R * t, R * t - 1)
            row = jnp.where(facing, whole, row)
            along = jnp.where(facing & reverse, -1, 1)
            i0 = jnp.where(is_col, jnp.where(reverse, side_first + slot, row_prev + f2 * F + column), row)
            i4 = jnp.where(
                is_col, jnp.where(reverse, side_last + slot, row_next + f2 * F + column), row + along * (R + 1)
            )
            base = jnp.where(
                is_col, jnp.where(reverse, mirror + 2 * R + slot, (f2 * R - 1) * F + column), row
            )
            step = jnp.where(is_col, jnp.where(reverse, -2, F), along)
            target = jnp.where(m == 0, i0, jnp.where(m == R + 1, i4, base + step * m))
            parts.append(jnp.where(inside, target, -1))
    j = col_iota(F)
    jt = jnp.zeros_like(j)
    for b in range(1, T):
        jt = jt + jnp.where(j >= b * R, 1, 0)
    jr = j - R * jt
    wrap = dm.o_row + dm.ROW
    for edge in (0, 2):
        at_edge = (t == 0) if edge == 0 else (t == T - 1)
        inner_base = row_prev if edge == 0 else row_next
        own_row = 0 if edge == 0 else R - 1
        for f in range(6):
            value = ep[f, edge]
            f2, e2 = value // 4, value % 4
            far_low = e2 < 2
            reverse = far_low if edge < 2 else e2 >= 2
            is_col = (e2 % 2) == 1
            same = e2 == edge
            row_base = jnp.where(same, (f2 * R + own_row) * F, wrap + f2 * F)
            lin_base = row_base + jnp.where(reverse, F - 1, 0)
            lin_step = jnp.where(reverse, -1, 1)
            k0 = jnp.where(reverse, T - 1, 0)
            ks = jnp.where(reverse, -1, 1)
            if edge == 2:
                k0 = T - 1 - k0
                ks = -ks
            col_base = dm.o_msg + k0 * dm.BASE + f * dm.SLOT + R + 2 + jnp.where(reverse, R - 1, 0)
            base = jnp.where(is_col, col_base, lin_base)
            sj = jnp.where(is_col, 0, lin_step)
            st = jnp.where(is_col, ks * dm.BASE, 0)
            sr = jnp.where(is_col, jnp.where(reverse, -1, 1), 0)
            base = jnp.where(at_edge, base, inner_base + f * F)
            sj = jnp.where(at_edge, sj, 1)
            st = jnp.where(at_edge, st, 0)
            sr = jnp.where(at_edge, sr, 0)
            target = base + sj * j + st * jt + sr * jr
            far_tile = T - 1 if edge == 0 else 0
            from_mirror = is_col & at_edge & (jnp.where(reverse, T - 1 - jt, jt) == far_tile)
            side = jnp.where(e2 == 1, 1, 0)
            cells = mirror + f2 * dm.SLOT + side + 2 * jnp.where(reverse, R - 1 - jr, jr)
            parts.append(jnp.where(from_mirror, cells, target))
    return jnp.concatenate(parts, axis=0)


def gather_ghosts(dm, ep, t, p, own, messages, table_ref):
    hot = one_hot(ghost_targets(dm, ep, t), dm.NT)
    out = []
    for which in range(2):
        table_ref[0 : dm.N] = own[which]
        table_ref[dm.o_msg : dm.o_msg + dm.BASE] = messages[-1][which]
        for step, ks in enumerate(dm.steps()):
            here = messages[2 * step][0, which].astype(F32)
            there = messages[2 * step + 1][1, which].astype(F32)
            for core, k in enumerate(ks):
                if k is None:
                    continue
                value = jnp.where(p == core, here, there).astype(BF)
                at = dm.o_msg + k * dm.BASE
                table_ref[at : at + dm.BASE] = value[: dm.BASE]
                if step == 0:
                    at = dm.o_row + core * dm.ROW
                    table_ref[at : at + dm.ROW] = value[dm.BASE :]
        out.append(jnp.dot(hot, table_ref[...], preferred_element_type=F32))
    return out


def own_first(value, p):
    half = value.shape[1] // 2
    low, high = value[:, :half], value[:, half:]
    return jnp.concatenate([jnp.where(p == 0, low, high), jnp.where(p == 0, high, low)], axis=1)


def build_taps(dm, field_ref, ghosts, top, bottom, frame_ref, taps_ref, adjoint, p=None):
    R, F, C = dm.R, dm.F, dm.C
    for f in range(6):
        for r in range(R):
            frame_ref[r + 1, f, 8 : 8 + F] = field_ref[f * R + r].astype(F32)
    frame_ref[0, :, 8 : 8 + F] = top.reshape(6, F, C)
    frame_ref[R + 1, :, 8 : 8 + F] = bottom.reshape(6, F, C)
    for m in range(R + 2):
        for f in range(6):
            if ghosts is None:
                west = jnp.zeros((1, C), F32)
                east = west
            else:
                west = ghosts[16 * f + m : 16 * f + m + 1]
                east = ghosts[16 * f + 8 + m : 16 * f + 8 + m + 1]
            frame_ref[m, f, 7:8] = west
            frame_ref[m, f, 8 + F : 9 + F] = east
    for m in range(R + 2):
        for b in range(3):
            plane = frame_ref[m, :, 7 + b : 7 + b + F].reshape(dm.ROW, C)
            if p is not None:
                plane = own_first(plane, p)
            plane = plane.astype(BF)
            for a in range(3):
                r = m - 2 + a if adjoint else m - a
                tap = 3 * a + (2 - b if adjoint else b)
                if 0 <= r < R:
                    taps_ref[r * dm.ROW : (r + 1) * dm.ROW, tap * C : (tap + 1) * C] = plane


def build_strip_terms(dm, ep, t, ghosts, top, bottom, z_ref):
    R, F = dm.R, dm.F
    z_ref[...] = jnp.zeros(z_ref.shape, F32)

    def tap_of(f, edge, shift):
        e2 = ep[f, edge] % 4
        reverse = e2 < 2 if edge < 2 else e2 >= 2
        along = 1 - jnp.where(reverse, -shift, shift)
        return jnp.where(
            e2 == 0, along, jnp.where(e2 == 2, 6 + along, jnp.where(e2 == 1, 3 * along + 2, 3 * along))
        )

    live = lax.rem(lax.broadcasted_iota(jnp.int32, (dm.WE, 1), 0), 8) < R
    for shift in (-1, 0, 1):
        moved = pltpu.roll(ghosts, (dm.WE - 1 - shift) % dm.WE, 0) if shift > -1 else ghosts
        moved = jnp.where(live, moved, 0.0)
        for f in range(6):
            for side, edge in ((0, 3), (1, 1)):
                at = 16 * f + 8 * side
                z_ref[tap_of(f, edge, shift), at : at + 8] = moved[at : at + 8]

    def add_rows(edge, rows):
        j = lax.rem(lax.broadcasted_iota(jnp.int32, (dm.ROW, 1), 0), F)
        for shift in (-1, 0, 1):
            if shift == 0:
                moved = rows
            else:
                moved = pltpu.roll(rows, (-shift) % dm.ROW, 0)
                moved = jnp.where((j + shift >= 0) & (j + shift < F), moved, 0.0)
            for f in range(6):
                at = dm.WE + F * f
                z_ref[tap_of(f, edge, shift), at : at + F] = moved[F * f : F * (f + 1)]

    @pl.when(t == 0)
    def _():
        add_rows(0, top)

    @pl.when(t == dm.T - 1)
    def _():
        add_rows(2, bottom)


def adjoint(dm, t, taps_ref, z_ref, wt_ref, acc_ref):
    R, F, C, N = dm.R, dm.F, dm.C, dm.N
    for tap in range(9):
        taps_ref[N:, tap * C : (tap + 1) * C] = z_ref[tap].astype(BF)
    total = jnp.dot(taps_ref[...], wt_ref[...], preferred_element_type=F32)
    acc_ref[...] = total[:N]
    strips = total[N:]
    for f in range(6):
        for side in range(2):
            for r in range(R):
                at = (r * 6 + f) * F + side * (F - 1)
                row = 16 * f + 8 * side + r
                acc_ref[at : at + 1] += strips[row : row + 1]

    @pl.when(t == 0)
    def _():
        acc_ref[0 : dm.ROW] += strips[dm.WE :]

    @pl.when(t == dm.T - 1)
    def _():
        acc_ref[(R - 1) * dm.ROW : R * dm.ROW] += strips[dm.WE :]


def turn_kernel(w1_ref, w2_ref, w1s_ref, w1t_ref, w2t_ref):
    p = lax.axis_index("dp")
    half = w1_ref.shape[1] // 2
    for tap in range(9):
        w1t_ref[tap] = w1_ref[tap].T
        w2t_ref[tap] = w2_ref[tap].T
        w1s_ref[tap, :half] = w1_ref[tap, pl.ds(pl.multiple_of(p * half, half), half)]
        w1s_ref[tap, half:] = w1_ref[tap, pl.ds(pl.multiple_of((1 - p) * half, half), half)]


def put_taps(send_ref, keep_ref, first_tap, value):
    half = keep_ref.shape[1]
    for i in range(value.shape[0] // (2 * half)):
        keep_ref[first_tap + i] = value[2 * i * half : (2 * i + 1) * half]
        send_ref[first_tap + i] = value[(2 * i + 1) * half : (2 * i + 2) * half].astype(BF)


def high_low(row):
    i = lax.broadcasted_iota(jnp.int32, (EXTRA, row.shape[1]), 0)
    high = row.astype(BF).astype(F32)
    return jnp.where(i == 0, high, jnp.where(i == 1, row - high, 0.0)).astype(BF)


def both(pair):
    return pair[0:1].astype(F32) + pair[1:2].astype(F32)


def first_kernel(dm, ep, x_ref, up_ref, w1_ref, bias_ref, w2t_ref, *refs):
    T, R, F, N, C = dm.T, dm.R, dm.F, dm.N, dm.C
    M = 2 * len(dm.steps())
    messages = refs[: M + 1]
    refs = refs[M + 1 :]
    send1_ref, keep1_ref, send2_ref, keep2_ref, hid_ref, inner_ref, bias_sum_ref, send_bias_ref = refs[:8]
    out_messages, self_ref = refs[8 : M + 8], refs[M + 8]
    table_ref, frame_ref, xs_ref, us_ref, z_ref, before_ref, acc_ref, hcat_ref = refs[M + 9 :]
    t, p = lax.axis_index("tile"), lax.axis_index("dp")
    own = (x_ref[...].reshape(N, C), up_ref[...].reshape(N, C))
    gx, gu = gather_ghosts(dm, ep, t, p, own, messages, table_ref)
    top, bottom = dm.WE, dm.WE + dm.ROW
    build_taps(dm, x_ref, gx[:top], gx[top:bottom], gx[bottom:], frame_ref, xs_ref, False, p)
    before = jnp.dot(xs_ref[...], w1_ref[...], preferred_element_type=F32) + bias_ref[...]
    before_ref[...] = before
    sig = 1.0 / (1.0 + jnp.exp(-before))
    acc_ref[...] = before * sig
    up_top = jnp.where(t == 0, 0.0, gu[top:bottom])
    up_bottom = jnp.where(t == T - 1, 0.0, gu[bottom:])
    build_taps(dm, up_ref, None, up_top, up_bottom, frame_ref, us_ref, True)
    build_strip_terms(dm, ep, t, gu[:top], gu[top:bottom], gu[bottom:], z_ref)
    hcat_ref[0:N] = acc_ref[...]
    hcat_ref[N:] = jnp.zeros((dm.S, C), F32)
    for f in range(6):
        for side in range(2):
            for r in range(R):
                at = (r * 6 + f) * F + side * (F - 1)
                row = N + 16 * f + 8 * side + r
                hcat_ref[row : row + 1] = acc_ref[at : at + 1]
    first_row = acc_ref[0 : dm.ROW]
    last_row = acc_ref[(R - 1) * dm.ROW : R * dm.ROW]
    hcat_ref[N + dm.WE :] = jnp.where(t == 0, first_row, last_row)
    for r in range(R):
        for f in range(6):
            at = (r * 6 + f) * F
            hid_ref[f * R + r] = acc_ref[at : at + F].astype(BF)
    adjoint(dm, t, us_ref, z_ref, w2t_ref, acc_ref)
    hidden_t = own_first(hcat_ref[...], p).astype(BF).T
    for tap in range(9):
        grad = jnp.dot(hidden_t, us_ref[:, tap * C : (tap + 1) * C], preferred_element_type=F32)
        put_taps(send2_ref, keep2_ref, tap, grad)
    before = before_ref[...]
    sig = 1.0 / (1.0 + jnp.exp(-before))
    before_grad = acc_ref[...] * (sig * (1.0 + before * (1.0 - sig)))
    acc_ref[...] = before_grad
    inner = before_grad.astype(BF)
    for tap in (0, 3, 6):
        grad = lax.dot_general(
            xs_ref[:, tap * C : (tap + 3) * C],
            inner,
            (((0,), (0,)), ((), ())),
            preferred_element_type=F32,
        )
        put_taps(send1_ref, keep1_ref, tap, grad)
    bias_sum = jnp.sum(before_grad, axis=0, keepdims=True)
    bias_sum_ref[...] = bias_sum
    send_bias_ref[...] = high_low(bias_sum)
    for r in range(R):
        for f in range(6):
            at = (r * 6 + f) * F
            inner_ref[f * R + r] = acc_ref[at : at + F].astype(BF)
    fields = (hid_ref[...].reshape(N, C), inner_ref[...].reshape(N, C))
    write_messages(dm, ep, t, p, fields, out_messages)
    write_self(dm, ep, t, fields, self_ref)


def second_kernel(dm, ep, x_ref, d_ref, hid_ref, inner_ref, w1t_ref, w2_ref, *refs):
    T, R, F, N, C = dm.T, dm.R, dm.F, dm.N, dm.C
    M = 2 * len(dm.steps()) + 1
    messages = refs[:M]
    state_ref, grad_ref = refs[M : M + 2]
    table_ref, frame_ref, hs_ref, is_ref, z_ref, acc_ref = refs[M + 2 :]
    t, p = lax.axis_index("tile"), lax.axis_index("dp")
    own = (hid_ref[...].reshape(N, C), inner_ref[...].reshape(N, C))
    gh, gi = gather_ghosts(dm, ep, t, p, own, messages, table_ref)
    top, bottom = dm.WE, dm.WE + dm.ROW
    build_taps(dm, hid_ref, gh[:top], gh[top:bottom], gh[bottom:], frame_ref, hs_ref, False)
    acc_ref[...] = jnp.dot(hs_ref[...], w2_ref[...], preferred_element_type=F32)
    for r in range(R):
        for f in range(6):
            at = (r * 6 + f) * F
            value = x_ref[f * R + r].astype(F32) + acc_ref[at : at + F]
            state_ref[f * R + r] = value.astype(BF)
    in_top = jnp.where(t == 0, 0.0, gi[top:bottom])
    in_bottom = jnp.where(t == T - 1, 0.0, gi[bottom:])
    build_taps(dm, inner_ref, None, in_top, in_bottom, frame_ref, is_ref, True)
    build_strip_terms(dm, ep, t, gi[:top], gi[top:bottom], gi[bottom:], z_ref)
    adjoint(dm, t, is_ref, z_ref, w1t_ref, acc_ref)
    for r in range(R):
        for f in range(6):
            at = (r * 6 + f) * F
            grad_ref[f * R + r] = d_ref[f * R + r].astype(F32) + acc_ref[at : at + F]


def half_kernel(zcount, keep_ref, recv_ref, *refs):
    size = keep_ref.shape[1] // 2
    own = lax.axis_index("tile") % 2
    mine = pl.ds(pl.multiple_of(own * size, size), size)
    far = pl.ds(pl.multiple_of((1 - own) * size, size), size)
    part = size // zcount
    if len(refs) > 2:
        bias_ref, recv_bias_ref, out_keep, out_send, out_bias = refs
        bias = bias_ref[...] + both(recv_bias_ref)
        out_bias[...] = bias
        out_send[9 * size :] = high_low(bias)
    else:
        out_keep, out_send = refs
    for tap in range(9):
        kept = keep_ref[tap, mine] + recv_ref[tap, mine].astype(F32)
        sent = keep_ref[tap, far] + recv_ref[tap, far].astype(F32)
        for j in range(zcount):
            at = j * 9 * part + tap * part
            out_keep[j, tap * part : (tap + 1) * part] = kept[j * part : (j + 1) * part]
            out_send[at : at + part] = sent[j * part : (j + 1) * part].astype(BF)


def block_kernel(zcount, keep_ref, recv_ref, *refs):
    own = lax.axis_index("tile") // 2
    n = keep_ref.shape[1]
    if len(refs) > zcount + 1:
        bias_ref, out_keep, *out_sends, out_bias, sum_ref = refs
        bias = bias_ref[...] + both(recv_ref[zcount * n : zcount * n + 2])
        out_bias[...] = bias
        tail = high_low(bias)
    else:
        out_keep, *out_sends, sum_ref = refs
        tail = None
    for j in range(zcount):
        sum_ref[j] = keep_ref[j] + recv_ref[j * n : (j + 1) * n].astype(F32)
    out_keep[...] = sum_ref[own]
    for j in range(1, zcount):
        out_sends[j - 1][0:n] = sum_ref[own ^ j].astype(BF)
        if tail is not None:
            out_sends[j - 1][n:] = tail


def last_kernel(zcount, keep_ref, *refs):
    recvs = refs[: zcount - 1]
    n = keep_ref.shape[0]
    total = keep_ref[...]
    for ref in recvs:
        total = total + ref[0:n].astype(F32)
    if len(refs) > zcount:
        bias_ref, block_ref, out_bias = refs[zcount - 1 :]
        bias = bias_ref[...]
        for ref in recvs:
            bias = bias + both(ref[n : n + 2])
        out_bias[...] = bias
    else:
        block_ref = refs[-1]
    block_ref[...] = total.astype(BF)


def normal_kernel(zcount, *refs):
    sources, out_ref = refs[:4], refs[4]
    if len(refs) > 5:
        bias_ref, out_ref, out_bias = refs[4:]
        bias = bias_ref[...]
        bias_mean = jnp.mean(bias * bias, keepdims=True)
        out_bias[...] = bias * lax.rsqrt(bias_mean + 1e-06)
    t, p = lax.axis_index("tile"), lax.axis_index("dp")
    n = sources[0].shape[0] // zcount
    size = n // 9
    square = None
    for ref in sources:
        for j in range(zcount):
            v = ref[j * n : (j + 1) * n].astype(F32)
            part = jnp.sum(v * v, axis=0, keepdims=True)
            square = part if square is None else square + part
    mean = jnp.sum(square, keepdims=True) / (9 * out_ref.shape[1] * out_ref.shape[2])
    scale = lax.rsqrt(mean + 1e-06)
    for group, ref in enumerate(sources):
        block = (p ^ (group // 2)) * 2 + ((t % 2) ^ (group % 2))
        for j in range(zcount):
            at = pl.ds(pl.multiple_of((block * zcount + ((t // 2) ^ j)) * size, size), size)
            for tap in range(9):
                row = j * n + tap * size
                out_ref[tap, at] = ref[row : row + size].astype(F32) * scale


def call(kernel, out_shapes, scratch=(), smem_first=False, limit=16):
    def run(*args):
        vmem = pl.BlockSpec(memory_space=pltpu.VMEM)
        smem = pl.BlockSpec(memory_space=pltpu.SMEM)
        specs = [smem if smem_first and i == 0 else vmem for i in range(len(args))]
        return pl.pallas_call(
            kernel,
            out_shape=[jax.ShapeDtypeStruct(s, dt) for s, dt in out_shapes],
            in_specs=specs,
            out_specs=[vmem] * len(out_shapes),
            scratch_shapes=[pltpu.VMEM(s, dt) for s, dt in scratch],
            compiler_params=pltpu.CompilerParams(vmem_limit_bytes=limit << 20),
        )(*args)

    return run


def swap_dp(v):
    count = lax.axis_size("dp")
    return lax.ppermute(v, "dp", [(i, count - 1 - i) for i in range(count)])


def on_device(initial_state, state_cotangents, w_first, bias, w_second, edge_partner):
    tiles = lax.axis_size("tile")
    _, _, rows, face, channels = initial_state.shape
    dm = Dims(rows, face, tiles, channels)
    planes = (6 * rows, face, channels)
    x = initial_state.reshape(planes)
    d = state_cotangents[state_cotangents.shape[0] - 1].reshape(planes)
    taps = (9, channels, channels)
    w1 = w_first.reshape(9 * channels, channels)
    w2 = w_second.reshape(9 * channels, channels)
    w1s, w1t, w2t = call(turn_kernel, [(taps, BF)] * 3)(w_first.reshape(taps), w_second.reshape(taps))
    w1s = w1s.reshape(w1.shape)
    w1t = w1t.reshape(w1.shape)
    w2t = w2t.reshape(w2.shape)
    steps = range(len(dm.steps()))
    pairs = dm.pairs()
    msg_shapes = [((2, dm.rows(i), channels), BF) for i in steps] * 2 + [((2, dm.BASE, channels), BF)]
    flat = (dm.N, channels)

    def merged(packed):
        count = len(steps)
        own, give = packed[:count], [swap_dp(v) for v in packed[count : 2 * count]]
        return call(
            functools.partial(merge_kernel, count), [((2,) + v.shape, BF) for v in own]
        )(*own, *give)

    def across(v, step):
        return lax.ppermute(v, ("tile", "dp"), pairs[step])

    packed = call(
        functools.partial(pack_kernel, dm), msg_shapes, smem_first=True
    )(edge_partner, x.reshape(flat), d.reshape(flat))
    came = [across(v, i) for i, v in enumerate(merged(packed))]
    came, w1s, w1t, w2t = lax.optimization_barrier((came, w1s, w1t, w2t))
    messages = []
    for v in came:
        messages += [v, swap_dp(v)]
    messages.append(packed[-1])
    half = channels // 2
    wide = 9 * channels
    frame = (rows + 2, 6, face + 16, channels)
    outs = call(
        functools.partial(first_kernel, dm),
        [
            ((9, half, channels), BF),
            ((9, half, channels), F32),
            ((9, half, channels), BF),
            ((9, half, channels), F32),
            (planes, BF),
            (planes, BF),
            ((1, channels), F32),
            ((EXTRA, channels), BF),
        ]
        + msg_shapes,
        [
            ((dm.NT, channels), BF),
            (frame, F32),
            ((dm.N, wide), BF),
            ((dm.N + dm.S, wide), BF),
            ((9, dm.S, channels), F32),
            (flat, F32),
            (flat, F32),
            ((dm.N + dm.S, channels), F32),
        ],
        smem_first=True,
        limit=LIMIT,
    )(edge_partner, x, d, w1s, bias.reshape(1, channels), w2t, *messages)
    send1, keep1, send2, keep2, hidden, inner, bias_sum, send_bias = outs[:8]
    packed = list(outs[8:])

    zcount = tiles // 2
    n = 9 * half // tiles
    one = ((1, channels), F32)
    barrier = lax.optimization_barrier

    def along_y(v):
        return lax.ppermute(v, "tile", [(i, i ^ 1) for i in range(tiles)])

    def along_z(v, j):
        return lax.ppermute(v, "tile", [(i, i ^ (2 * j)) for i in range(tiles)])

    def sum_dp(keep, recv, *bias):
        extra = EXTRA if bias else 0
        return call(
            functools.partial(half_kernel, zcount),
            [((zcount, n, channels), F32), ((zcount * n + extra, channels), BF)] + [one] * bool(bias),
        )(keep, recv, *bias)

    def sum_y(keep, recv, *bias):
        extra = EXTRA if bias else 0
        keep, *out = call(
            functools.partial(block_kernel, zcount),
            [((n, channels), F32)] + [((n + extra, channels), BF)] * (zcount - 1) + [one] * bool(bias),
            [((zcount, n, channels), F32)],
        )(keep, recv, *bias)
        return keep, out[: zcount - 1], out[zcount - 1 :]

    def sum_z(keep, recvs, *bias):
        return call(
            functools.partial(last_kernel, zcount), [((n, channels), BF)] + [one] * bool(bias)
        )(keep, *recvs, *bias)

    joined = merged(packed)
    early = list(steps)[1:]
    middle = [i for i in steps if i not in early]
    came = {}

    keep2, send2 = sum_dp(keep2, swap_dp(send2))
    recv2 = along_y(send2)
    keep1, send1, bias_sum = sum_dp(keep1, swap_dp(send1), bias_sum, swap_dp(send_bias))
    got = [across(joined[i], i) for i in early]
    recv2, send1, got = barrier((recv2, send1, got))
    came.update(zip(early, got))
    recv1 = along_y(send1)

    keep2, sends2, _ = sum_y(keep2, recv2)
    recvs2 = [along_z(v, j + 1) for j, v in enumerate(sends2)]
    recv1, recvs2 = barrier((recv1, recvs2))

    keep1, sends1, (bias_sum,) = sum_y(keep1, recv1, bias_sum)
    (own2,) = sum_z(keep2, recvs2)
    sends1, own2, todo = barrier((sends1, own2, [joined[i] for i in middle]))
    recvs1 = [along_z(v, j + 1) for j, v in enumerate(sends1)]
    own2 = [own2] + [along_z(own2, j) for j in range(1, zcount)]
    got = [across(v, i) for i, v in zip(middle, todo)]
    recvs1, own2, got = barrier((recvs1, own2, got))
    came.update(zip(middle, got))

    own1, bias_sum = sum_z(keep1, recvs1, bias_sum)
    own1 = [own1] + [along_z(own1, j) for j in range(1, zcount)]
    own2 = jnp.concatenate(own2, axis=0)
    other2 = along_y(own2)
    messages = []
    for i in steps:
        messages += [came[i], swap_dp(came[i])]
    messages.append(packed[-1])
    own1, other2, messages = barrier((own1, other2, messages))
    own1 = jnp.concatenate(own1, axis=0)
    other1 = along_y(own1)
    state, grad = call(
        functools.partial(second_kernel, dm),
        [(planes, BF), (planes, F32)],
        [
            ((dm.NT, channels), BF),
            (frame, F32),
            ((dm.N, wide), BF),
            ((dm.N + dm.S, wide), BF),
            ((9, dm.S, channels), F32),
            (flat, F32),
        ],
        smem_first=True,
        limit=LIMIT,
    )(edge_partner, x, d, hidden, inner, w1t, w2, *messages)
    other1, state, grad = barrier((other1, state, grad))
    (second_step,) = call(functools.partial(normal_kernel, zcount), [(taps, F32)])(
        own2, other2, swap_dp(own2), swap_dp(other2)
    )
    first_step, bias_step = call(functools.partial(normal_kernel, zcount), [(taps, F32), one])(
        own1, other1, swap_dp(own1), swap_dp(other1), bias_sum
    )
    return (
        state.reshape(initial_state.shape),
        grad.reshape(initial_state.shape),
        first_step.reshape(w_first.shape),
        bias_step.reshape(channels),
        second_step.reshape(w_second.shape),
    )


def solution(mesh):
    return jax.shard_map(
        on_device,
        mesh=mesh,
        in_specs=(
            P(("groups", "dp"), None, "tile", None, None),
            P(None, ("groups", "dp"), None, "tile", None, None),
            P(),
            P(),
            P(),
            P(),
        ),
        out_specs=(
            P(("groups", "dp"), None, "tile", None, None),
            P(("groups", "dp"), None, "tile", None, None),
            P("groups", None, None, None),
            P("groups"),
            P("groups", None, None, None),
        ),
        check_vma=False,
    )
```

```python
import functools

import jax
import jax.numpy as jnp
from jax import lax
from jax.experimental import pallas as pl
from jax.experimental.pallas import tpu as pltpu
from jax.sharding import PartitionSpec as P

BF = jnp.bfloat16
F32 = jnp.float32
EXTRA = 8
LIMIT = 24


class Dims:
    def __init__(self, rows, face, tiles, channels):
        self.R, self.F, self.T, self.C = rows, face, tiles, channels
        self.N = 6 * rows * face
        self.ROW = 6 * face
        self.SLOT = -(-(2 * rows + 2) // 8) * 8
        self.BASE = 6 * self.SLOT
        self.MIX = tiles // 2 - 1
        self.o_msg = self.N
        self.o_row = self.o_msg + tiles * self.BASE
        self.NT = self.o_row + 2 * self.ROW
        self.WE = 12 * 8
        self.S = self.WE + self.ROW

    def partner(self, t, k):
        if k == self.MIX:
            ends = (t == 0) | (t == self.MIX) | (t == self.MIX + 1) | (t == self.T - 1)
            return jnp.where(ends, t ^ k, self.T - 1 - t)
        return t ^ k

    def steps(self):
        rest = [k for k in range(2, self.T - 1)]
        evens = [k for k in rest if k % 2 == 0]
        odds = [k for k in rest if k % 2 == 1]
        rest = evens + odds
        if len(rest) % 2:
            rest = rest[:-1] + [None, rest[-1]]
        return [(1, self.T - 1)] + [(rest[i], rest[i + 1]) for i in range(0, len(rest), 2)]

    def rows(self, step):
        return self.BASE + (self.ROW if step == 0 else 0)

    def pairs(self):
        T, mix = self.T, self.MIX

        def needed(i, d):
            return i in (0, T - 1) or d in (0, T - 1) or d in (T - 2 - i, T - i)

        out = [[(i, i ^ k) for i in range(T) if k == 1 or needed(i, i ^ k)] for k in range(T - 1)]
        out[mix] = [(i, i ^ mix if i in (0, mix, mix + 1, T - 1) else T - 1 - i) for i in range(T)]
        out.append([(i, (i + 1) % T if i % 2 else (i - 1) % T) for i in range(T)])
        return [
            [(2 * i + core, 2 * d + core) for core in range(2) if ks[core] is not None for i, d in out[ks[core]]]
            for ks in self.steps()
        ]


def col_iota(n):
    return lax.broadcasted_iota(jnp.int32, (n, 1), 0)


def one_hot(target, width):
    lanes = lax.broadcasted_iota(jnp.int32, (target.shape[0], width), 1)
    return jnp.where(lanes == target, 1.0, 0.0).astype(BF)


def strip_targets(dm, ep, t, d):
    R, F, T = dm.R, dm.F, dm.T
    at_edge = (t == 0) | (t == T - 1)
    to_edge = (d == 0) | (d == T - 1)
    own_edge = jnp.where(t == 0, 0, 2)
    far_edge = jnp.where(d == 0, 0, 2)
    side_row = jnp.where(d == T - 2 - t, R - 1, 0)
    i = col_iota(dm.SLOT)
    q = R * d - 1 + i
    inside = (q >= 0) & (q < F) & (i < R + 2)
    i2 = i - (R + 2)
    parts = []
    for f in range(6):
        far_low = (ep[f, own_edge] % 4) < 2
        reverse = far_low == (t == 0)
        p0 = jnp.where(reverse, F - 1, 0)
        sgn = jnp.where(reverse, -1, 1)
        row = jnp.where(t == 0, 0, R - 1)
        strip = jnp.where(inside, (f * R + row) * F + p0 + sgn * q, -1)
        sides = (f * R + side_row) * F
        low = jnp.where(at_edge, strip, sides + i * (F - 1))
        low = jnp.where(at_edge | (i < 2), low, -1)
        gvalue = ep[f, far_edge]
        column = jnp.where(gvalue % 4 == 1, F - 1, 0) + (gvalue // 4) * (R * F)
        high = jnp.where(to_edge, column + F * i2, jnp.where(i2 < 2, sides + i2 * (F - 1), -1))
        strips = jnp.where(i2 < 0, low, jnp.where(i2 < R, high, -1))
        parts.append(jnp.where(d == T - 1 - t, mirror_slot(dm, f), strips))
    return parts


def mirror_slot(dm, f):
    i = col_iota(dm.SLOT)
    return jnp.where(i < 2 * dm.R, (f * dm.R + i // 2) * dm.F + (i % 2) * (dm.F - 1), -1)


def row_targets(dm, row):
    j = col_iota(dm.F)
    return [(f * dm.R + row) * dm.F + j for f in range(6)]


def write_messages(dm, ep, t, p, sources, refs):
    R = dm.R
    steps = dm.steps()
    for other in range(2):
        core = p ^ other
        for step, ks in enumerate(steps):
            if step == 0:
                strips = strip_targets(dm, ep, t, t ^ 1)
                parts = [jnp.where(core == 0, strips[f], mirror_slot(dm, f)) for f in range(6)]
                parts = parts + row_targets(dm, jnp.where((t + core) % 2 == 0, R - 1, 0))
            else:
                ds = [dm.partner(t, k) for k in ks if k is not None]
                parts = strip_targets(dm, ep, t, jnp.where(core == 0, ds[0], ds[-1]))
            hot = one_hot(jnp.concatenate(parts, axis=0), dm.N)
            for which in range(2):
                rows = jnp.dot(hot, sources[which], preferred_element_type=F32).astype(BF)
                refs[other * len(steps) + step][which] = rows


def write_self(dm, ep, t, sources, ref):
    hot = one_hot(jnp.concatenate(strip_targets(dm, ep, t, t), axis=0), dm.N)
    for which in range(2):
        ref[which] = jnp.dot(hot, sources[which], preferred_element_type=F32).astype(BF)


def pack_kernel(dm, ep, x_ref, up_ref, *refs):
    t, p = lax.axis_index("tile"), lax.axis_index("dp")
    fields = (x_ref[...], up_ref[...])
    write_messages(dm, ep, t, p, fields, refs[:-1])
    write_self(dm, ep, t, fields, refs[-1])


def merge_kernel(count, *refs):
    for i in range(count):
        refs[2 * count + i][0] = refs[i][...]
        refs[2 * count + i][1] = refs[count + i][...]


def ghost_targets(dm, ep, t):
    R, F, T = dm.R, dm.F, dm.T
    odd = t % 2
    parts = []
    m = col_iota(8)
    q = R * t - 1 + m
    inside = (q >= 0) & (q < F) & (m < R + 2)
    row_prev = dm.o_row + (1 - odd) * dm.ROW
    row_next = dm.o_row + odd * dm.ROW
    side_first = dm.o_msg + (t ^ (T - t)) * dm.BASE + jnp.where(t == 1, R + 2, 0)
    side_last = dm.o_msg + (t ^ (T - 2 - t)) * dm.BASE + jnp.where(t == T - 2, R + 2, 0)
    ends = (t == 0) | (t == dm.MIX) | (t == dm.MIX + 1) | (t == T - 1)
    mirror = dm.o_msg + jnp.where(ends, T - 1, dm.MIX) * dm.BASE
    for f in range(6):
        for edge in (3, 1):
            value = ep[f, edge]
            f2, e2 = value // 4, value % 4
            far_low = e2 < 2
            reverse = far_low if edge < 2 else e2 >= 2
            is_col = (e2 % 2) == 1
            side = jnp.where(e2 == 1, 1, 0)
            column = side * (F - 1)
            slot = f2 * dm.SLOT + side
            row = dm.o_msg + (t ^ jnp.where(e2 == 0, 0, T - 1)) * dm.BASE + f2 * dm.SLOT
            facing = jnp.where(e2 == 0, t == T - 1, t == 0)
            whole = dm.o_row + dm.ROW + f2 * F + jnp.where(reverse, F - R * t, R * t - 1)
            row = jnp.where(facing, whole, row)
            along = jnp.where(facing & reverse, -1, 1)
            i0 = jnp.where(is_col, jnp.where(reverse, side_first + slot, row_prev + f2 * F + column), row)
            i4 = jnp.where(
                is_col, jnp.where(reverse, side_last + slot, row_next + f2 * F + column), row + along * (R + 1)
            )
            base = jnp.where(
                is_col, jnp.where(reverse, mirror + 2 * R + slot, (f2 * R - 1) * F + column), row
            )
            step = jnp.where(is_col, jnp.where(reverse, -2, F), along)
            target = jnp.where(m == 0, i0, jnp.where(m == R + 1, i4, base + step * m))
            parts.append(jnp.where(inside, target, -1))
    j = col_iota(F)
    jt = jnp.zeros_like(j)
    for b in range(1, T):
        jt = jt + jnp.where(j >= b * R, 1, 0)
    jr = j - R * jt
    wrap = dm.o_row + dm.ROW
    for edge in (0, 2):
        at_edge = (t == 0) if edge == 0 else (t == T - 1)
        inner_base = row_prev if edge == 0 else row_next
        own_row = 0 if edge == 0 else R - 1
        for f in range(6):
            value = ep[f, edge]
            f2, e2 = value // 4, value % 4
            far_low = e2 < 2
            reverse = far_low if edge < 2 else e2 >= 2
            is_col = (e2 % 2) == 1
            same = e2 == edge
            row_base = jnp.where(same, (f2 * R + own_row) * F, wrap + f2 * F)
            lin_base = row_base + jnp.where(reverse, F - 1, 0)
            lin_step = jnp.where(reverse, -1, 1)
            k0 = jnp.where(reverse, T - 1, 0)
            ks = jnp.where(reverse, -1, 1)
            if edge == 2:
                k0 = T - 1 - k0
                ks = -ks
            col_base = dm.o_msg + k0 * dm.BASE + f * dm.SLOT + R + 2 + jnp.where(reverse, R - 1, 0)
            base = jnp.where(is_col, col_base, lin_base)
            sj = jnp.where(is_col, 0, lin_step)
            st = jnp.where(is_col, ks * dm.BASE, 0)
            sr = jnp.where(is_col, jnp.where(reverse, -1, 1), 0)
            base = jnp.where(at_edge, base, inner_base + f * F)
            sj = jnp.where(at_edge, sj, 1)
            st = jnp.where(at_edge, st, 0)
            sr = jnp.where(at_edge, sr, 0)
            target = base + sj * j + st * jt + sr * jr
            far_tile = T - 1 if edge == 0 else 0
            from_mirror = is_col & at_edge & (jnp.where(reverse, T - 1 - jt, jt) == far_tile)
            side = jnp.where(e2 == 1, 1, 0)
            cells = mirror + f2 * dm.SLOT + side + 2 * jnp.where(reverse, R - 1 - jr, jr)
            parts.append(jnp.where(from_mirror, cells, target))
    return jnp.concatenate(parts, axis=0)


def gather_ghosts(dm, ep, t, p, own, messages, table_ref):
    hot = one_hot(ghost_targets(dm, ep, t), dm.NT)
    out = []
    for which in range(2):
        table_ref[0 : dm.N] = own[which]
        table_ref[dm.o_msg : dm.o_msg + dm.BASE] = messages[-1][which]
        for step, ks in enumerate(dm.steps()):
            here = messages[2 * step][0, which].astype(F32)
            there = messages[2 * step + 1][1, which].astype(F32)
            for core, k in enumerate(ks):
                if k is None:
                    continue
                value = jnp.where(p == core, here, there).astype(BF)
                at = dm.o_msg + k * dm.BASE
                table_ref[at : at + dm.BASE] = value[: dm.BASE]
                if step == 0:
                    at = dm.o_row + core * dm.ROW
                    table_ref[at : at + dm.ROW] = value[dm.BASE :]
        out.append(jnp.dot(hot, table_ref[...], preferred_element_type=F32))
    return out


def own_first(value, p):
    half = value.shape[1] // 2
    low, high = value[:, :half], value[:, half:]
    return jnp.concatenate([jnp.where(p == 0, low, high), jnp.where(p == 0, high, low)], axis=1)


def build_taps(dm, field_ref, ghosts, top, bottom, frame_ref, taps_ref, adjoint, p=None):
    R, F, C = dm.R, dm.F, dm.C
    for f in range(6):
        for r in range(R):
            frame_ref[r + 1, f, 8 : 8 + F] = field_ref[f * R + r].astype(F32)
    frame_ref[0, :, 8 : 8 + F] = top.reshape(6, F, C)
    frame_ref[R + 1, :, 8 : 8 + F] = bottom.reshape(6, F, C)
    for m in range(R + 2):
        for f in range(6):
            if ghosts is None:
                west = jnp.zeros((1, C), F32)
                east = west
            else:
                west = ghosts[16 * f + m : 16 * f + m + 1]
                east = ghosts[16 * f + 8 + m : 16 * f + 8 + m + 1]
            frame_ref[m, f, 7:8] = west
            frame_ref[m, f, 8 + F : 9 + F] = east
    for m in range(R + 2):
        for b in range(3):
            plane = frame_ref[m, :, 7 + b : 7 + b + F].reshape(dm.ROW, C)
            if p is not None:
                plane = own_first(plane, p)
            plane = plane.astype(BF)
            for a in range(3):
                r = m - 2 + a if adjoint else m - a
                tap = 3 * a + (2 - b if adjoint else b)
                if 0 <= r < R:
                    taps_ref[r * dm.ROW : (r + 1) * dm.ROW, tap * C : (tap + 1) * C] = plane


def build_strip_terms(dm, ep, t, ghosts, top, bottom, z_ref):
    R, F = dm.R, dm.F
    z_ref[...] = jnp.zeros(z_ref.shape, F32)

    def tap_of(f, edge, shift):
        e2 = ep[f, edge] % 4
        reverse = e2 < 2 if edge < 2 else e2 >= 2
        along = 1 - jnp.where(reverse, -shift, shift)
        return jnp.where(
            e2 == 0, along, jnp.where(e2 == 2, 6 + along, jnp.where(e2 == 1, 3 * along + 2, 3 * along))
        )

    live = lax.rem(lax.broadcasted_iota(jnp.int32, (dm.WE, 1), 0), 8) < R
    for shift in (-1, 0, 1):
        moved = pltpu.roll(ghosts, (dm.WE - 1 - shift) % dm.WE, 0) if shift > -1 else ghosts
        moved = jnp.where(live, moved, 0.0)
        for f in range(6):
            for side, edge in ((0, 3), (1, 1)):
                at = 16 * f + 8 * side
                z_ref[tap_of(f, edge, shift), at : at + 8] = moved[at : at + 8]

    def add_rows(edge, rows):
        j = lax.rem(lax.broadcasted_iota(jnp.int32, (dm.ROW, 1), 0), F)
        for shift in (-1, 0, 1):
            if shift == 0:
                moved = rows
            else:
                moved = pltpu.roll(rows, (-shift) % dm.ROW, 0)
                moved = jnp.where((j + shift >= 0) & (j + shift < F), moved, 0.0)
            for f in range(6):
                at = dm.WE + F * f
                z_ref[tap_of(f, edge, shift), at : at + F] = moved[F * f : F * (f + 1)]

    @pl.when(t == 0)
    def _():
        add_rows(0, top)

    @pl.when(t == dm.T - 1)
    def _():
        add_rows(2, bottom)


def adjoint(dm, t, taps_ref, z_ref, wt_ref, acc_ref):
    R, F, C, N = dm.R, dm.F, dm.C, dm.N
    for tap in range(9):
        taps_ref[N:, tap * C : (tap + 1) * C] = z_ref[tap].astype(BF)
    total = jnp.dot(taps_ref[...], wt_ref[...], preferred_element_type=F32)
    acc_ref[...] = total[:N]
    strips = total[N:]
    for f in range(6):
        for side in range(2):
            for r in range(R):
                at = (r * 6 + f) * F + side * (F - 1)
                row = 16 * f + 8 * side + r
                acc_ref[at : at + 1] += strips[row : row + 1]

    @pl.when(t == 0)
    def _():
        acc_ref[0 : dm.ROW] += strips[dm.WE :]

    @pl.when(t == dm.T - 1)
    def _():
        acc_ref[(R - 1) * dm.ROW : R * dm.ROW] += strips[dm.WE :]


def turn_kernel(w1_ref, w2_ref, w1s_ref, w1t_ref, w2t_ref):
    p = lax.axis_index("dp")
    half = w1_ref.shape[1] // 2
    for tap in range(9):
        w1t_ref[tap] = w1_ref[tap].T
        w2t_ref[tap] = w2_ref[tap].T
        w1s_ref[tap, :half] = w1_ref[tap, pl.ds(pl.multiple_of(p * half, half), half)]
        w1s_ref[tap, half:] = w1_ref[tap, pl.ds(pl.multiple_of((1 - p) * half, half), half)]


def put_taps(send_ref, keep_ref, first_tap, value):
    half = keep_ref.shape[1]
    for i in range(value.shape[0] // (2 * half)):
        keep_ref[first_tap + i] = value[2 * i * half : (2 * i + 1) * half]
        send_ref[first_tap + i] = value[(2 * i + 1) * half : (2 * i + 2) * half].astype(BF)


def high_low(row):
    i = lax.broadcasted_iota(jnp.int32, (EXTRA, row.shape[1]), 0)
    high = row.astype(BF).astype(F32)
    return jnp.where(i == 0, high, jnp.where(i == 1, row - high, 0.0)).astype(BF)


def both(pair):
    return pair[0:1].astype(F32) + pair[1:2].astype(F32)


def first_kernel(dm, ep, x_ref, up_ref, w1_ref, bias_ref, w2t_ref, *refs):
    T, R, F, N, C = dm.T, dm.R, dm.F, dm.N, dm.C
    M = 2 * len(dm.steps())
    messages = refs[: M + 1]
    refs = refs[M + 1 :]
    send1_ref, keep1_ref, send2_ref, keep2_ref, hid_ref, inner_ref, bias_sum_ref, send_bias_ref = refs[:8]
    out_messages, self_ref = refs[8 : M + 8], refs[M + 8]
    table_ref, frame_ref, xs_ref, us_ref, z_ref, before_ref, acc_ref, hcat_ref = refs[M + 9 :]
    t, p = lax.axis_index("tile"), lax.axis_index("dp")
    own = (x_ref[...].reshape(N, C), up_ref[...].reshape(N, C))
    gx, gu = gather_ghosts(dm, ep, t, p, own, messages, table_ref)
    top, bottom = dm.WE, dm.WE + dm.ROW
    build_taps(dm, x_ref, gx[:top], gx[top:bottom], gx[bottom:], frame_ref, xs_ref, False, p)
    before = jnp.dot(xs_ref[...], w1_ref[...], preferred_element_type=F32) + bias_ref[...]
    before_ref[...] = before
    sig = 1.0 / (1.0 + jnp.exp(-before))
    acc_ref[...] = before * sig
    up_top = jnp.where(t == 0, 0.0, gu[top:bottom])
    up_bottom = jnp.where(t == T - 1, 0.0, gu[bottom:])
    build_taps(dm, up_ref, None, up_top, up_bottom, frame_ref, us_ref, True)
    build_strip_terms(dm, ep, t, gu[:top], gu[top:bottom], gu[bottom:], z_ref)
    hcat_ref[0:N] = acc_ref[...]
    hcat_ref[N:] = jnp.zeros((dm.S, C), F32)
    for f in range(6):
        for side in range(2):
            for r in range(R):
                at = (r * 6 + f) * F + side * (F - 1)
                row = N + 16 * f + 8 * side + r
                hcat_ref[row : row + 1] = acc_ref[at : at + 1]
    first_row = acc_ref[0 : dm.ROW]
    last_row = acc_ref[(R - 1) * dm.ROW : R * dm.ROW]
    hcat_ref[N + dm.WE :] = jnp.where(t == 0, first_row, last_row)
    for r in range(R):
        for f in range(6):
            at = (r * 6 + f) * F
            hid_ref[f * R + r] = acc_ref[at : at + F].astype(BF)
    adjoint(dm, t, us_ref, z_ref, w2t_ref, acc_ref)
    hidden_t = own_first(hcat_ref[...], p).astype(BF).T
    for tap in range(9):
        grad = jnp.dot(hidden_t, us_ref[:, tap * C : (tap + 1) * C], preferred_element_type=F32)
        put_taps(send2_ref, keep2_ref, tap, grad)
    before = before_ref[...]
    sig = 1.0 / (1.0 + jnp.exp(-before))
    before_grad = acc_ref[...] * (sig * (1.0 + before * (1.0 - sig)))
    acc_ref[...] = before_grad
    inner = before_grad.astype(BF)
    for tap in (0, 3, 6):
        grad = lax.dot_general(
            xs_ref[:, tap * C : (tap + 3) * C],
            inner,
            (((0,), (0,)), ((), ())),
            preferred_element_type=F32,
        )
        put_taps(send1_ref, keep1_ref, tap, grad)
    bias_sum = jnp.sum(before_grad, axis=0, keepdims=True)
    bias_sum_ref[...] = bias_sum
    send_bias_ref[...] = high_low(bias_sum)
    for r in range(R):
        for f in range(6):
            at = (r * 6 + f) * F
            inner_ref[f * R + r] = acc_ref[at : at + F].astype(BF)
    fields = (hid_ref[...].reshape(N, C), inner_ref[...].reshape(N, C))
    write_messages(dm, ep, t, p, fields, out_messages)
    write_self(dm, ep, t, fields, self_ref)


def second_kernel(dm, ep, x_ref, d_ref, hid_ref, inner_ref, w1t_ref, w2_ref, *refs):
    T, R, F, N, C = dm.T, dm.R, dm.F, dm.N, dm.C
    M = 2 * len(dm.steps()) + 1
    messages = refs[:M]
    state_ref, grad_ref = refs[M : M + 2]
    table_ref, frame_ref, hs_ref, is_ref, z_ref, acc_ref = refs[M + 2 :]
    t, p = lax.axis_index("tile"), lax.axis_index("dp")
    own = (hid_ref[...].reshape(N, C), inner_ref[...].reshape(N, C))
    gh, gi = gather_ghosts(dm, ep, t, p, own, messages, table_ref)
    top, bottom = dm.WE, dm.WE + dm.ROW
    build_taps(dm, hid_ref, gh[:top], gh[top:bottom], gh[bottom:], frame_ref, hs_ref, False)
    acc_ref[...] = jnp.dot(hs_ref[...], w2_ref[...], preferred_element_type=F32)
    for r in range(R):
        for f in range(6):
            at = (r * 6 + f) * F
            value = x_ref[f * R + r].astype(F32) + acc_ref[at : at + F]
            state_ref[f * R + r] = value.astype(BF)
    in_top = jnp.where(t == 0, 0.0, gi[top:bottom])
    in_bottom = jnp.where(t == T - 1, 0.0, gi[bottom:])
    build_taps(dm, inner_ref, None, in_top, in_bottom, frame_ref, is_ref, True)
    build_strip_terms(dm, ep, t, gi[:top], gi[top:bottom], gi[bottom:], z_ref)
    adjoint(dm, t, is_ref, z_ref, w1t_ref, acc_ref)
    for r in range(R):
        for f in range(6):
            at = (r * 6 + f) * F
            grad_ref[f * R + r] = d_ref[f * R + r].astype(F32) + acc_ref[at : at + F]


def half_kernel(zcount, keep_ref, recv_ref, *refs):
    size = keep_ref.shape[1] // 2
    own = lax.axis_index("tile") % 2
    mine = pl.ds(pl.multiple_of(own * size, size), size)
    far = pl.ds(pl.multiple_of((1 - own) * size, size), size)
    part = size // zcount
    if len(refs) > 2:
        bias_ref, recv_bias_ref, out_keep, out_send, out_bias = refs
        bias = bias_ref[...] + both(recv_bias_ref)
        out_bias[...] = bias
        out_send[9 * size :] = high_low(bias)
    else:
        out_keep, out_send = refs
    for tap in range(9):
        kept = keep_ref[tap, mine] + recv_ref[tap, mine].astype(F32)
        sent = keep_ref[tap, far] + recv_ref[tap, far].astype(F32)
        for j in range(zcount):
            at = j * 9 * part + tap * part
            out_keep[j, tap * part : (tap + 1) * part] = kept[j * part : (j + 1) * part]
            out_send[at : at + part] = sent[j * part : (j + 1) * part].astype(BF)


def block_kernel(zcount, keep_ref, recv_ref, *refs):
    own = lax.axis_index("tile") // 2
    n = keep_ref.shape[1]
    if len(refs) > zcount + 1:
        bias_ref, out_keep, *out_sends, out_bias, sum_ref = refs
        bias = bias_ref[...] + both(recv_ref[zcount * n : zcount * n + 2])
        out_bias[...] = bias
        tail = high_low(bias)
    else:
        out_keep, *out_sends, sum_ref = refs
        tail = None
    for j in range(zcount):
        sum_ref[j] = keep_ref[j] + recv_ref[j * n : (j + 1) * n].astype(F32)
    out_keep[...] = sum_ref[own]
    for j in range(1, zcount):
        out_sends[j - 1][0:n] = sum_ref[own ^ j].astype(BF)
        if tail is not None:
            out_sends[j - 1][n:] = tail


def last_kernel(zcount, keep_ref, *refs):
    recvs = refs[: zcount - 1]
    n = keep_ref.shape[0]
    total = keep_ref[...]
    for ref in recvs:
        total = total + ref[0:n].astype(F32)
    if len(refs) > zcount:
        bias_ref, block_ref, out_bias = refs[zcount - 1 :]
        bias = bias_ref[...]
        for ref in recvs:
            bias = bias + both(ref[n : n + 2])
        out_bias[...] = bias
    else:
        block_ref = refs[-1]
    block_ref[...] = total.astype(BF)


def normal_kernel(zcount, *refs):
    sources, out_ref = refs[:4], refs[4]
    if len(refs) > 5:
        bias_ref, out_ref, out_bias = refs[4:]
        bias = bias_ref[...]
        bias_mean = jnp.mean(bias * bias, keepdims=True)
        out_bias[...] = bias * lax.rsqrt(bias_mean + 1e-06)
    t, p = lax.axis_index("tile"), lax.axis_index("dp")
    n = sources[0].shape[0] // zcount
    size = n // 9
    square = None
    for ref in sources:
        for j in range(zcount):
            v = ref[j * n : (j + 1) * n].astype(F32)
            part = jnp.sum(v * v, axis=0, keepdims=True)
            square = part if square is None else square + part
    mean = jnp.sum(square, keepdims=True) / (9 * out_ref.shape[1] * out_ref.shape[2])
    scale = lax.rsqrt(mean + 1e-06)
    for group, ref in enumerate(sources):
        block = (p ^ (group // 2)) * 2 + ((t % 2) ^ (group % 2))
        for j in range(zcount):
            at = pl.ds(pl.multiple_of((block * zcount + ((t // 2) ^ j)) * size, size), size)
            for tap in range(9):
                row = j * n + tap * size
                out_ref[tap, at] = ref[row : row + size].astype(F32) * scale


def call(kernel, out_shapes, scratch=(), smem_first=False, limit=16):
    def run(*args):
        vmem = pl.BlockSpec(memory_space=pltpu.VMEM)
        smem = pl.BlockSpec(memory_space=pltpu.SMEM)
        specs = [smem if smem_first and i == 0 else vmem for i in range(len(args))]
        return pl.pallas_call(
            kernel,
            out_shape=[jax.ShapeDtypeStruct(s, dt) for s, dt in out_shapes],
            in_specs=specs,
            out_specs=[vmem] * len(out_shapes),
            scratch_shapes=[pltpu.VMEM(s, dt) for s, dt in scratch],
            compiler_params=pltpu.CompilerParams(vmem_limit_bytes=limit << 20),
        )(*args)

    return run


def swap_dp(v):
    count = lax.axis_size("dp")
    return lax.ppermute(v, "dp", [(i, count - 1 - i) for i in range(count)])


def on_device(initial_state, state_cotangents, w_first, bias, w_second, edge_partner):
    tiles = lax.axis_size("tile")
    _, _, rows, face, channels = initial_state.shape
    dm = Dims(rows, face, tiles, channels)
    planes = (6 * rows, face, channels)
    x = initial_state.reshape(planes)
    d = state_cotangents[state_cotangents.shape[0] - 1].reshape(planes)
    taps = (9, channels, channels)
    w1 = w_first.reshape(9 * channels, channels)
    w2 = w_second.reshape(9 * channels, channels)
    w1s, w1t, w2t = call(turn_kernel, [(taps, BF)] * 3)(w_first.reshape(taps), w_second.reshape(taps))
    w1s = w1s.reshape(w1.shape)
    w1t = w1t.reshape(w1.shape)
    w2t = w2t.reshape(w2.shape)
    steps = range(len(dm.steps()))
    pairs = dm.pairs()
    msg_shapes = [((2, dm.rows(i), channels), BF) for i in steps] * 2 + [((2, dm.BASE, channels), BF)]
    flat = (dm.N, channels)

    def merged(packed):
        count = len(steps)
        own, give = packed[:count], [swap_dp(v) for v in packed[count : 2 * count]]
        return call(
            functools.partial(merge_kernel, count), [((2,) + v.shape, BF) for v in own]
        )(*own, *give)

    def across(v, step):
        return lax.ppermute(v, ("tile", "dp"), pairs[step])

    packed = call(
        functools.partial(pack_kernel, dm), msg_shapes, smem_first=True
    )(edge_partner, x.reshape(flat), d.reshape(flat))
    came = [across(v, i) for i, v in enumerate(merged(packed))]
    came, w1s, w1t, w2t = lax.optimization_barrier((came, w1s, w1t, w2t))
    messages = []
    for v in came:
        messages += [v, swap_dp(v)]
    messages.append(packed[-1])
    half = channels // 2
    wide = 9 * channels
    frame = (rows + 2, 6, face + 16, channels)
    outs = call(
        functools.partial(first_kernel, dm),
        [
            ((9, half, channels), BF),
            ((9, half, channels), F32),
            ((9, half, channels), BF),
            ((9, half, channels), F32),
            (planes, BF),
            (planes, BF),
            ((1, channels), F32),
            ((EXTRA, channels), BF),
        ]
        + msg_shapes,
        [
            ((dm.NT, channels), BF),
            (frame, F32),
            ((dm.N, wide), BF),
            ((dm.N + dm.S, wide), BF),
            ((9, dm.S, channels), F32),
            (flat, F32),
            (flat, F32),
            ((dm.N + dm.S, channels), F32),
        ],
        smem_first=True,
        limit=LIMIT,
    )(edge_partner, x, d, w1s, bias.reshape(1, channels), w2t, *messages)
    send1, keep1, send2, keep2, hidden, inner, bias_sum, send_bias = outs[:8]
    packed = list(outs[8:])

    zcount = tiles // 2
    n = 9 * half // tiles
    one = ((1, channels), F32)
    barrier = lax.optimization_barrier

    def along_y(v):
        return lax.ppermute(v, "tile", [(i, i ^ 1) for i in range(tiles)])

    def along_z(v, j):
        return lax.ppermute(v, "tile", [(i, i ^ (2 * j)) for i in range(tiles)])

    def sum_dp(keep, recv, *bias):
        extra = EXTRA if bias else 0
        return call(
            functools.partial(half_kernel, zcount),
            [((zcount, n, channels), F32), ((zcount * n + extra, channels), BF)] + [one] * bool(bias),
        )(keep, recv, *bias)

    def sum_y(keep, recv, *bias):
        extra = EXTRA if bias else 0
        keep, *out = call(
            functools.partial(block_kernel, zcount),
            [((n, channels), F32)] + [((n + extra, channels), BF)] * (zcount - 1) + [one] * bool(bias),
            [((zcount, n, channels), F32)],
        )(keep, recv, *bias)
        return keep, out[: zcount - 1], out[zcount - 1 :]

    def sum_z(keep, recvs, *bias):
        return call(
            functools.partial(last_kernel, zcount), [((n, channels), BF)] + [one] * bool(bias)
        )(keep, *recvs, *bias)

    joined = merged(packed)
    early = list(steps)[1 : 1 + len(steps) // 2]
    middle = [i for i in steps if i not in early]
    came = {}

    keep2, send2 = sum_dp(keep2, swap_dp(send2))
    recv2 = along_y(send2)
    keep1, send1, bias_sum = sum_dp(keep1, swap_dp(send1), bias_sum, swap_dp(send_bias))
    recv1 = along_y(send1)
    got = [across(joined[i], i) for i in early]

    keep2, sends2, _ = sum_y(keep2, recv2)
    recvs2 = [along_z(v, j + 1) for j, v in enumerate(sends2)]
    recv1, got = barrier((recv1, got))
    came.update(zip(early, got))

    keep1, sends1, (bias_sum,) = sum_y(keep1, recv1, bias_sum)
    sends1, todo = barrier((sends1, [joined[i] for i in middle]))
    recvs1 = [along_z(v, j + 1) for j, v in enumerate(sends1)]
    got = [across(v, i) for i, v in zip(middle, todo)]

    (own2,) = sum_z(keep2, recvs2)
    own2 = [own2] + [along_z(own2, j) for j in range(1, zcount)]
    recvs1, got = barrier((recvs1, got))
    came.update(zip(middle, got))

    own1, bias_sum = sum_z(keep1, recvs1, bias_sum)
    own1 = [own1] + [along_z(own1, j) for j in range(1, zcount)]
    back = {i: swap_dp(came[i]) for i in steps}
    own1[-1], back = barrier((own1[-1], back))
    own2 = jnp.concatenate(own2, axis=0)
    other2 = along_y(own2)
    own1 = jnp.concatenate(own1, axis=0)
    other1 = along_y(own1)
    messages = []
    for i in steps:
        messages += [came[i], back[i]]
    messages.append(packed[-1])
    own1, messages = barrier((own1, messages))
    state, grad = call(
        functools.partial(second_kernel, dm),
        [(planes, BF), (planes, F32)],
        [
            ((dm.NT, channels), BF),
            (frame, F32),
            ((dm.N, wide), BF),
            ((dm.N + dm.S, wide), BF),
            ((9, dm.S, channels), F32),
            (flat, F32),
        ],
        smem_first=True,
        limit=LIMIT,
    )(edge_partner, x, d, hidden, inner, w1t, w2, *messages)
    other1, state, grad = barrier((other1, state, grad))
    (second_step,) = call(functools.partial(normal_kernel, zcount), [(taps, F32)])(
        own2, other2, swap_dp(own2), swap_dp(other2)
    )
    first_step, bias_step = call(functools.partial(normal_kernel, zcount), [(taps, F32), one])(
        own1, other1, swap_dp(own1), swap_dp(other1), bias_sum
    )
    return (
        state.reshape(initial_state.shape),
        grad.reshape(initial_state.shape),
        first_step.reshape(w_first.shape),
        bias_step.reshape(channels),
        second_step.reshape(w_second.shape),
    )


def solution(mesh):
    return jax.shard_map(
        on_device,
        mesh=mesh,
        in_specs=(
            P(("groups", "dp"), None, "tile", None, None),
            P(None, ("groups", "dp"), None, "tile", None, None),
            P(),
            P(),
            P(),
            P(),
        ),
        out_specs=(
            P(("groups", "dp"), None, "tile", None, None),
            P(("groups", "dp"), None, "tile", None, None),
            P("groups", None, None, None),
            P("groups"),
            P("groups", None, None, None),
        ),
        check_vma=False,
    )
```

```python
import functools

import jax
import jax.numpy as jnp
from jax import lax
from jax.experimental import pallas as pl
from jax.experimental.pallas import tpu as pltpu
from jax.sharding import PartitionSpec as P

BF = jnp.bfloat16
F32 = jnp.float32
EXTRA = 8
LIMIT = 24


class Dims:
    def __init__(self, rows, face, tiles, channels):
        self.R, self.F, self.T, self.C = rows, face, tiles, channels
        self.N = 6 * rows * face
        self.ROW = 6 * face
        self.SLOT = -(-(2 * rows + 2) // 8) * 8
        self.BASE = 6 * self.SLOT
        self.MIX = tiles // 2 - 1
        self.o_msg = self.N
        self.o_row = self.o_msg + tiles * self.BASE
        self.NT = self.o_row + 2 * self.ROW
        self.WE = 12 * 8
        self.S = self.WE + self.ROW

    def partner(self, t, k):
        if k == self.MIX:
            ends = (t == 0) | (t == self.MIX) | (t == self.MIX + 1) | (t == self.T - 1)
            return jnp.where(ends, t ^ k, self.T - 1 - t)
        return t ^ k

    def steps(self):
        rest = [k for k in range(2, self.T - 1)]
        evens = [k for k in rest if k % 2 == 0]
        odds = [k for k in rest if k % 2 == 1]
        rest = evens + odds
        if len(rest) % 2:
            rest = rest[:-1] + [None, rest[-1]]
        return [(1, self.T - 1)] + [(rest[i], rest[i + 1]) for i in range(0, len(rest), 2)]

    def rows(self, step):
        return self.BASE + (self.ROW if step == 0 else 0)

    def pairs(self):
        T, mix = self.T, self.MIX

        def needed(i, d):
            return i in (0, T - 1) or d in (0, T - 1) or d in (T - 2 - i, T - i)

        out = [[(i, i ^ k) for i in range(T) if k == 1 or needed(i, i ^ k)] for k in range(T - 1)]
        out[mix] = [(i, i ^ mix if i in (0, mix, mix + 1, T - 1) else T - 1 - i) for i in range(T)]
        out.append([(i, (i + 1) % T if i % 2 else (i - 1) % T) for i in range(T)])
        return [
            [(2 * i + core, 2 * d + core) for core in range(2) if ks[core] is not None for i, d in out[ks[core]]]
            for ks in self.steps()
        ]


def col_iota(n):
    return lax.broadcasted_iota(jnp.int32, (n, 1), 0)


def one_hot(target, width):
    lanes = lax.broadcasted_iota(jnp.int32, (target.shape[0], width), 1)
    return jnp.where(lanes == target, 1.0, 0.0).astype(BF)


def strip_targets(dm, ep, t, d):
    R, F, T = dm.R, dm.F, dm.T
    at_edge = (t == 0) | (t == T - 1)
    to_edge = (d == 0) | (d == T - 1)
    own_edge = jnp.where(t == 0, 0, 2)
    far_edge = jnp.where(d == 0, 0, 2)
    side_row = jnp.where(d == T - 2 - t, R - 1, 0)
    i = col_iota(dm.SLOT)
    q = R * d - 1 + i
    inside = (q >= 0) & (q < F) & (i < R + 2)
    i2 = i - (R + 2)
    parts = []
    for f in range(6):
        far_low = (ep[f, own_edge] % 4) < 2
        reverse = far_low == (t == 0)
        p0 = jnp.where(reverse, F - 1, 0)
        sgn = jnp.where(reverse, -1, 1)
        row = jnp.where(t == 0, 0, R - 1)
        strip = jnp.where(inside, (f * R + row) * F + p0 + sgn * q, -1)
        sides = (f * R + side_row) * F
        low = jnp.where(at_edge, strip, sides + i * (F - 1))
        low = jnp.where(at_edge | (i < 2), low, -1)
        gvalue = ep[f, far_edge]
        column = jnp.where(gvalue % 4 == 1, F - 1, 0) + (gvalue // 4) * (R * F)
        high = jnp.where(to_edge, column + F * i2, jnp.where(i2 < 2, sides + i2 * (F - 1), -1))
        strips = jnp.where(i2 < 0, low, jnp.where(i2 < R, high, -1))
        parts.append(jnp.where(d == T - 1 - t, mirror_slot(dm, f), strips))
    return parts


def mirror_slot(dm, f):
    i = col_iota(dm.SLOT)
    return jnp.where(i < 2 * dm.R, (f * dm.R + i // 2) * dm.F + (i % 2) * (dm.F - 1), -1)


def row_targets(dm, row):
    j = col_iota(dm.F)
    return [(f * dm.R + row) * dm.F + j for f in range(6)]


def write_messages(dm, ep, t, p, sources, refs):
    R = dm.R
    steps = dm.steps()
    for other in range(2):
        core = p ^ other
        for step, ks in enumerate(steps):
            if step == 0:
                strips = strip_targets(dm, ep, t, t ^ 1)
                parts = [jnp.where(core == 0, strips[f], mirror_slot(dm, f)) for f in range(6)]
                parts = parts + row_targets(dm, jnp.where((t + core) % 2 == 0, R - 1, 0))
            else:
                ds = [dm.partner(t, k) for k in ks if k is not None]
                parts = strip_targets(dm, ep, t, jnp.where(core == 0, ds[0], ds[-1]))
            hot = one_hot(jnp.concatenate(parts, axis=0), dm.N)
            for which in range(2):
                rows = jnp.dot(hot, sources[which], preferred_element_type=F32).astype(BF)
                refs[other * len(steps) + step][which] = rows


def write_self(dm, ep, t, sources, ref):
    hot = one_hot(jnp.concatenate(strip_targets(dm, ep, t, t), axis=0), dm.N)
    for which in range(2):
        ref[which] = jnp.dot(hot, sources[which], preferred_element_type=F32).astype(BF)


def pack_kernel(dm, ep, fields_ref, *refs):
    t, p = lax.axis_index("tile"), lax.axis_index("dp")
    fields = (fields_ref[0], fields_ref[1])
    write_messages(dm, ep, t, p, fields, refs[:-1])
    write_self(dm, ep, t, fields, refs[-1])


def merge_kernel(count, *refs):
    for i in range(count):
        refs[2 * count + i][0] = refs[i][...]
        refs[2 * count + i][1] = refs[count + i][...]


def ghost_targets(dm, ep, t):
    R, F, T = dm.R, dm.F, dm.T
    odd = t % 2
    parts = []
    m = col_iota(8)
    q = R * t - 1 + m
    inside = (q >= 0) & (q < F) & (m < R + 2)
    row_prev = dm.o_row + (1 - odd) * dm.ROW
    row_next = dm.o_row + odd * dm.ROW
    side_first = dm.o_msg + (t ^ (T - t)) * dm.BASE + jnp.where(t == 1, R + 2, 0)
    side_last = dm.o_msg + (t ^ (T - 2 - t)) * dm.BASE + jnp.where(t == T - 2, R + 2, 0)
    ends = (t == 0) | (t == dm.MIX) | (t == dm.MIX + 1) | (t == T - 1)
    mirror = dm.o_msg + jnp.where(ends, T - 1, dm.MIX) * dm.BASE
    for f in range(6):
        for edge in (3, 1):
            value = ep[f, edge]
            f2, e2 = value // 4, value % 4
            far_low = e2 < 2
            reverse = far_low if edge < 2 else e2 >= 2
            is_col = (e2 % 2) == 1
            side = jnp.where(e2 == 1, 1, 0)
            column = side * (F - 1)
            slot = f2 * dm.SLOT + side
            row = dm.o_msg + (t ^ jnp.where(e2 == 0, 0, T - 1)) * dm.BASE + f2 * dm.SLOT
            facing = jnp.where(e2 == 0, t == T - 1, t == 0)
            whole = dm.o_row + dm.ROW + f2 * F + jnp.where(reverse, F - R * t, R * t - 1)
            row = jnp.where(facing, whole, row)
            along = jnp.where(facing & reverse, -1, 1)
            i0 = jnp.where(is_col, jnp.where(reverse, side_first + slot, row_prev + f2 * F + column), row)
            i4 = jnp.where(
                is_col, jnp.where(reverse, side_last + slot, row_next + f2 * F + column), row + along * (R + 1)
            )
            base = jnp.where(
                is_col, jnp.where(reverse, mirror + 2 * R + slot, (f2 * R - 1) * F + column), row
            )
            step = jnp.where(is_col, jnp.where(reverse, -2, F), along)
            target = jnp.where(m == 0, i0, jnp.where(m == R + 1, i4, base + step * m))
            parts.append(jnp.where(inside, target, -1))
    j = col_iota(F)
    jt = jnp.zeros_like(j)
    for b in range(1, T):
        jt = jt + jnp.where(j >= b * R, 1, 0)
    jr = j - R * jt
    wrap = dm.o_row + dm.ROW
    for edge in (0, 2):
        at_edge = (t == 0) if edge == 0 else (t == T - 1)
        inner_base = row_prev if edge == 0 else row_next
        own_row = 0 if edge == 0 else R - 1
        for f in range(6):
            value = ep[f, edge]
            f2, e2 = value // 4, value % 4
            far_low = e2 < 2
            reverse = far_low if edge < 2 else e2 >= 2
            is_col = (e2 % 2) == 1
            same = e2 == edge
            row_base = jnp.where(same, (f2 * R + own_row) * F, wrap + f2 * F)
            lin_base = row_base + jnp.where(reverse, F - 1, 0)
            lin_step = jnp.where(reverse, -1, 1)
            k0 = jnp.where(reverse, T - 1, 0)
            ks = jnp.where(reverse, -1, 1)
            if edge == 2:
                k0 = T - 1 - k0
                ks = -ks
            col_base = dm.o_msg + k0 * dm.BASE + f * dm.SLOT + R + 2 + jnp.where(reverse, R - 1, 0)
            base = jnp.where(is_col, col_base, lin_base)
            sj = jnp.where(is_col, 0, lin_step)
            st = jnp.where(is_col, ks * dm.BASE, 0)
            sr = jnp.where(is_col, jnp.where(reverse, -1, 1), 0)
            base = jnp.where(at_edge, base, inner_base + f * F)
            sj = jnp.where(at_edge, sj, 1)
            st = jnp.where(at_edge, st, 0)
            sr = jnp.where(at_edge, sr, 0)
            target = base + sj * j + st * jt + sr * jr
            far_tile = T - 1 if edge == 0 else 0
            from_mirror = is_col & at_edge & (jnp.where(reverse, T - 1 - jt, jt) == far_tile)
            side = jnp.where(e2 == 1, 1, 0)
            cells = mirror + f2 * dm.SLOT + side + 2 * jnp.where(reverse, R - 1 - jr, jr)
            parts.append(jnp.where(from_mirror, cells, target))
    return jnp.concatenate(parts, axis=0)


def gather_ghosts(dm, ep, t, p, own, messages, table_ref):
    hot = one_hot(ghost_targets(dm, ep, t), dm.NT)
    out = []
    for which in range(2):
        table_ref[0 : dm.N] = own[which]
        table_ref[dm.o_msg : dm.o_msg + dm.BASE] = messages[-1][which]
        for step, ks in enumerate(dm.steps()):
            here = messages[2 * step][0, which].astype(F32)
            there = messages[2 * step + 1][1, which].astype(F32)
            for core, k in enumerate(ks):
                if k is None:
                    continue
                value = jnp.where(p == core, here, there).astype(BF)
                at = dm.o_msg + k * dm.BASE
                table_ref[at : at + dm.BASE] = value[: dm.BASE]
                if step == 0:
                    at = dm.o_row + core * dm.ROW
                    table_ref[at : at + dm.ROW] = value[dm.BASE :]
        out.append(jnp.dot(hot, table_ref[...], preferred_element_type=F32))
    return out


def own_first(value, p):
    half = value.shape[1] // 2
    low, high = value[:, :half], value[:, half:]
    return jnp.concatenate([jnp.where(p == 0, low, high), jnp.where(p == 0, high, low)], axis=1)


def build_taps(dm, field_ref, ghosts, top, bottom, frame_ref, taps_ref, adjoint, p=None):
    R, F, C = dm.R, dm.F, dm.C
    for f in range(6):
        for r in range(R):
            frame_ref[r + 1, f, 8 : 8 + F] = field_ref[f * R + r].astype(F32)
    frame_ref[0, :, 8 : 8 + F] = top.reshape(6, F, C)
    frame_ref[R + 1, :, 8 : 8 + F] = bottom.reshape(6, F, C)
    for m in range(R + 2):
        for f in range(6):
            if ghosts is None:
                west = jnp.zeros((1, C), F32)
                east = west
            else:
                west = ghosts[16 * f + m : 16 * f + m + 1]
                east = ghosts[16 * f + 8 + m : 16 * f + 8 + m + 1]
            frame_ref[m, f, 7:8] = west
            frame_ref[m, f, 8 + F : 9 + F] = east
    for m in range(R + 2):
        for b in range(3):
            plane = frame_ref[m, :, 7 + b : 7 + b + F].reshape(dm.ROW, C)
            if p is not None:
                plane = own_first(plane, p)
            plane = plane.astype(BF)
            for a in range(3):
                r = m - 2 + a if adjoint else m - a
                tap = 3 * a + (2 - b if adjoint else b)
                if 0 <= r < R:
                    taps_ref[r * dm.ROW : (r + 1) * dm.ROW, tap * C : (tap + 1) * C] = plane


def build_strip_terms(dm, ep, t, ghosts, top, bottom, z_ref):
    R, F = dm.R, dm.F
    z_ref[...] = jnp.zeros(z_ref.shape, F32)

    def tap_of(f, edge, shift):
        e2 = ep[f, edge] % 4
        reverse = e2 < 2 if edge < 2 else e2 >= 2
        along = 1 - jnp.where(reverse, -shift, shift)
        return jnp.where(
            e2 == 0, along, jnp.where(e2 == 2, 6 + along, jnp.where(e2 == 1, 3 * along + 2, 3 * along))
        )

    live = lax.rem(lax.broadcasted_iota(jnp.int32, (dm.WE, 1), 0), 8) < R
    for shift in (-1, 0, 1):
        moved = pltpu.roll(ghosts, (dm.WE - 1 - shift) % dm.WE, 0) if shift > -1 else ghosts
        moved = jnp.where(live, moved, 0.0)
        for f in range(6):
            for side, edge in ((0, 3), (1, 1)):
                at = 16 * f + 8 * side
                z_ref[tap_of(f, edge, shift), at : at + 8] = moved[at : at + 8]

    def add_rows(edge, rows):
        j = lax.rem(lax.broadcasted_iota(jnp.int32, (dm.ROW, 1), 0), F)
        for shift in (-1, 0, 1):
            if shift == 0:
                moved = rows
            else:
                moved = pltpu.roll(rows, (-shift) % dm.ROW, 0)
                moved = jnp.where((j + shift >= 0) & (j + shift < F), moved, 0.0)
            for f in range(6):
                at = dm.WE + F * f
                z_ref[tap_of(f, edge, shift), at : at + F] = moved[F * f : F * (f + 1)]

    @pl.when(t == 0)
    def _():
        add_rows(0, top)

    @pl.when(t == dm.T - 1)
    def _():
        add_rows(2, bottom)


def adjoint(dm, t, taps_ref, z_ref, wt_ref, acc_ref):
    R, F, C, N = dm.R, dm.F, dm.C, dm.N
    for tap in range(9):
        taps_ref[N:, tap * C : (tap + 1) * C] = z_ref[tap].astype(BF)
    total = jnp.dot(taps_ref[...], wt_ref[...], preferred_element_type=F32)
    acc_ref[...] = total[:N]
    strips = total[N:]
    for f in range(6):
        for side in range(2):
            for r in range(R):
                at = (r * 6 + f) * F + side * (F - 1)
                row = 16 * f + 8 * side + r
                acc_ref[at : at + 1] += strips[row : row + 1]

    @pl.when(t == 0)
    def _():
        acc_ref[0 : dm.ROW] += strips[dm.WE :]

    @pl.when(t == dm.T - 1)
    def _():
        acc_ref[(R - 1) * dm.ROW : R * dm.ROW] += strips[dm.WE :]


def turn_kernel(w1_ref, w2_ref, w1s_ref, w1t_ref, w2t_ref):
    p = lax.axis_index("dp")
    half = w1_ref.shape[1] // 2
    for tap in range(9):
        w1t_ref[tap] = w1_ref[tap].T
        w2t_ref[tap] = w2_ref[tap].T
        w1s_ref[tap, :half] = w1_ref[tap, pl.ds(pl.multiple_of(p * half, half), half)]
        w1s_ref[tap, half:] = w1_ref[tap, pl.ds(pl.multiple_of((1 - p) * half, half), half)]


def put_taps(send_ref, keep_ref, first_tap, value):
    half = keep_ref.shape[1]
    for i in range(value.shape[0] // (2 * half)):
        keep_ref[first_tap + i] = value[2 * i * half : (2 * i + 1) * half]
        send_ref[first_tap + i] = value[(2 * i + 1) * half : (2 * i + 2) * half].astype(BF)


def high_low(row):
    i = lax.broadcasted_iota(jnp.int32, (EXTRA, row.shape[1]), 0)
    high = row.astype(BF).astype(F32)
    return jnp.where(i == 0, high, jnp.where(i == 1, row - high, 0.0)).astype(BF)


def both(pair):
    return pair[0:1].astype(F32) + pair[1:2].astype(F32)


def first_kernel(dm, ep, x_ref, up_ref, w1_ref, bias_ref, w2t_ref, *refs):
    T, R, F, N, C = dm.T, dm.R, dm.F, dm.N, dm.C
    M = 2 * len(dm.steps())
    messages = refs[: M + 1]
    refs = refs[M + 1 :]
    send1_ref, keep1_ref, send2_ref, keep2_ref, hid_ref, inner_ref, bias_sum_ref, send_bias_ref = refs[:8]
    out_messages, self_ref = refs[8 : M + 8], refs[M + 8]
    table_ref, frame_ref, xs_ref, us_ref, z_ref, before_ref, acc_ref, hcat_ref = refs[M + 9 :]
    t, p = lax.axis_index("tile"), lax.axis_index("dp")
    own = (x_ref[...].reshape(N, C), up_ref[...].reshape(N, C))
    gx, gu = gather_ghosts(dm, ep, t, p, own, messages, table_ref)
    top, bottom = dm.WE, dm.WE + dm.ROW
    build_taps(dm, x_ref, gx[:top], gx[top:bottom], gx[bottom:], frame_ref, xs_ref, False, p)
    before = jnp.dot(xs_ref[...], w1_ref[...], preferred_element_type=F32) + bias_ref[...]
    before_ref[...] = before
    sig = 1.0 / (1.0 + jnp.exp(-before))
    acc_ref[...] = before * sig
    up_top = jnp.where(t == 0, 0.0, gu[top:bottom])
    up_bottom = jnp.where(t == T - 1, 0.0, gu[bottom:])
    build_taps(dm, up_ref, None, up_top, up_bottom, frame_ref, us_ref, True)
    build_strip_terms(dm, ep, t, gu[:top], gu[top:bottom], gu[bottom:], z_ref)
    hcat_ref[0:N] = acc_ref[...]
    hcat_ref[N:] = jnp.zeros((dm.S, C), F32)
    for f in range(6):
        for side in range(2):
            for r in range(R):
                at = (r * 6 + f) * F + side * (F - 1)
                row = N + 16 * f + 8 * side + r
                hcat_ref[row : row + 1] = acc_ref[at : at + 1]
    first_row = acc_ref[0 : dm.ROW]
    last_row = acc_ref[(R - 1) * dm.ROW : R * dm.ROW]
    hcat_ref[N + dm.WE :] = jnp.where(t == 0, first_row, last_row)
    for r in range(R):
        for f in range(6):
            at = (r * 6 + f) * F
            hid_ref[f * R + r] = acc_ref[at : at + F].astype(BF)
    adjoint(dm, t, us_ref, z_ref, w2t_ref, acc_ref)
    hidden_t = own_first(hcat_ref[...], p).astype(BF).T
    for tap in range(9):
        grad = jnp.dot(hidden_t, us_ref[:, tap * C : (tap + 1) * C], preferred_element_type=F32)
        put_taps(send2_ref, keep2_ref, tap, grad)
    before = before_ref[...]
    sig = 1.0 / (1.0 + jnp.exp(-before))
    before_grad = acc_ref[...] * (sig * (1.0 + before * (1.0 - sig)))
    acc_ref[...] = before_grad
    inner = before_grad.astype(BF)
    for tap in (0, 3, 6):
        grad = lax.dot_general(
            xs_ref[:, tap * C : (tap + 3) * C],
            inner,
            (((0,), (0,)), ((), ())),
            preferred_element_type=F32,
        )
        put_taps(send1_ref, keep1_ref, tap, grad)
    bias_sum = jnp.sum(before_grad, axis=0, keepdims=True)
    bias_sum_ref[...] = bias_sum
    send_bias_ref[...] = high_low(bias_sum)
    for r in range(R):
        for f in range(6):
            at = (r * 6 + f) * F
            inner_ref[f * R + r] = acc_ref[at : at + F].astype(BF)
    fields = (hid_ref[...].reshape(N, C), inner_ref[...].reshape(N, C))
    write_messages(dm, ep, t, p, fields, out_messages)
    write_self(dm, ep, t, fields, self_ref)


def second_kernel(dm, ep, x_ref, d_ref, hid_ref, inner_ref, w1t_ref, w2_ref, *refs):
    T, R, F, N, C = dm.T, dm.R, dm.F, dm.N, dm.C
    M = 2 * len(dm.steps()) + 1
    messages = refs[:M]
    state_ref, grad_ref = refs[M : M + 2]
    table_ref, frame_ref, hs_ref, is_ref, z_ref, acc_ref = refs[M + 2 :]
    t, p = lax.axis_index("tile"), lax.axis_index("dp")
    own = (hid_ref[...].reshape(N, C), inner_ref[...].reshape(N, C))
    gh, gi = gather_ghosts(dm, ep, t, p, own, messages, table_ref)
    top, bottom = dm.WE, dm.WE + dm.ROW
    build_taps(dm, hid_ref, gh[:top], gh[top:bottom], gh[bottom:], frame_ref, hs_ref, False)
    acc_ref[...] = jnp.dot(hs_ref[...], w2_ref[...], preferred_element_type=F32)
    for r in range(R):
        for f in range(6):
            at = (r * 6 + f) * F
            value = x_ref[f * R + r].astype(F32) + acc_ref[at : at + F]
            state_ref[f * R + r] = value.astype(BF)
    in_top = jnp.where(t == 0, 0.0, gi[top:bottom])
    in_bottom = jnp.where(t == T - 1, 0.0, gi[bottom:])
    build_taps(dm, inner_ref, None, in_top, in_bottom, frame_ref, is_ref, True)
    build_strip_terms(dm, ep, t, gi[:top], gi[top:bottom], gi[bottom:], z_ref)
    adjoint(dm, t, is_ref, z_ref, w1t_ref, acc_ref)
    for r in range(R):
        for f in range(6):
            at = (r * 6 + f) * F
            grad_ref[f * R + r] = d_ref[f * R + r].astype(F32) + acc_ref[at : at + F]


def half_kernel(zcount, keep_ref, recv_ref, *refs):
    size = keep_ref.shape[1] // 2
    own = lax.axis_index("tile") % 2
    mine = pl.ds(pl.multiple_of(own * size, size), size)
    far = pl.ds(pl.multiple_of((1 - own) * size, size), size)
    part = size // zcount
    if len(refs) > 2:
        bias_ref, recv_bias_ref, out_keep, out_send, out_bias = refs
        bias = bias_ref[...] + both(recv_bias_ref)
        out_bias[...] = bias
        out_send[9 * size :] = high_low(bias)
    else:
        out_keep, out_send = refs
    for tap in range(9):
        kept = keep_ref[tap, mine] + recv_ref[tap, mine].astype(F32)
        sent = keep_ref[tap, far] + recv_ref[tap, far].astype(F32)
        for j in range(zcount):
            at = j * 9 * part + tap * part
            out_keep[j, tap * part : (tap + 1) * part] = kept[j * part : (j + 1) * part]
            out_send[at : at + part] = sent[j * part : (j + 1) * part].astype(BF)


def block_kernel(zcount, keep_ref, recv_ref, *refs):
    own = lax.axis_index("tile") // 2
    n = keep_ref.shape[1]
    if len(refs) > zcount + 1:
        bias_ref, out_keep, *out_sends, out_bias, sum_ref = refs
        bias = bias_ref[...] + both(recv_ref[zcount * n : zcount * n + 2])
        out_bias[...] = bias
        tail = high_low(bias)
    else:
        out_keep, *out_sends, sum_ref = refs
        tail = None
    for j in range(zcount):
        sum_ref[j] = keep_ref[j] + recv_ref[j * n : (j + 1) * n].astype(F32)
    out_keep[...] = sum_ref[own]
    for j in range(1, zcount):
        out_sends[j - 1][0:n] = sum_ref[own ^ j].astype(BF)
        if tail is not None:
            out_sends[j - 1][n:] = tail


def last_kernel(zcount, keep_ref, *refs):
    recvs = refs[: zcount - 1]
    n = keep_ref.shape[0]
    total = keep_ref[...]
    for ref in recvs:
        total = total + ref[0:n].astype(F32)
    if len(refs) > zcount:
        bias_ref, block_ref, out_bias = refs[zcount - 1 :]
        bias = bias_ref[...]
        for ref in recvs:
            bias = bias + both(ref[n : n + 2])
        out_bias[...] = bias
    else:
        block_ref = refs[-1]
    block_ref[...] = total.astype(BF)


def normal_kernel(zcount, *refs):
    sources, out_ref = refs[:4], refs[4]
    if len(refs) > 5:
        bias_ref, out_ref, out_bias = refs[4:]
        bias = bias_ref[...]
        bias_mean = jnp.mean(bias * bias, keepdims=True)
        out_bias[...] = bias * lax.rsqrt(bias_mean + 1e-06)
    t, p = lax.axis_index("tile"), lax.axis_index("dp")
    n = sources[0].shape[0] // zcount
    size = n // 9
    square = None
    for ref in sources:
        for j in range(zcount):
            v = ref[j * n : (j + 1) * n].astype(F32)
            part = jnp.sum(v * v, axis=0, keepdims=True)
            square = part if square is None else square + part
    mean = jnp.sum(square, keepdims=True) / (9 * out_ref.shape[1] * out_ref.shape[2])
    scale = lax.rsqrt(mean + 1e-06)
    for group, ref in enumerate(sources):
        block = (p ^ (group // 2)) * 2 + ((t % 2) ^ (group % 2))
        for j in range(zcount):
            at = pl.ds(pl.multiple_of((block * zcount + ((t // 2) ^ j)) * size, size), size)
            for tap in range(9):
                row = j * n + tap * size
                out_ref[tap, at] = ref[row : row + size].astype(F32) * scale


def call(kernel, out_shapes, scratch=(), smem_first=False, limit=16):
    def run(*args):
        vmem = pl.BlockSpec(memory_space=pltpu.VMEM)
        smem = pl.BlockSpec(memory_space=pltpu.SMEM)
        specs = [smem if smem_first and i == 0 else vmem for i in range(len(args))]
        return pl.pallas_call(
            kernel,
            out_shape=[jax.ShapeDtypeStruct(s, dt) for s, dt in out_shapes],
            in_specs=specs,
            out_specs=[vmem] * len(out_shapes),
            scratch_shapes=[pltpu.VMEM(s, dt) for s, dt in scratch],
            compiler_params=pltpu.CompilerParams(vmem_limit_bytes=limit << 20),
        )(*args)

    return run


def swap_dp(v):
    count = lax.axis_size("dp")
    return lax.ppermute(v, "dp", [(i, count - 1 - i) for i in range(count)])


def on_device(initial_state, state_cotangents, w_first, bias, w_second, edge_partner):
    tiles = lax.axis_size("tile")
    _, _, rows, face, channels = initial_state.shape
    dm = Dims(rows, face, tiles, channels)
    planes = (6 * rows, face, channels)
    x = initial_state.reshape(planes)
    d = state_cotangents[state_cotangents.shape[0] - 1].reshape(planes)
    taps = (9, channels, channels)
    w1 = w_first.reshape(9 * channels, channels)
    w2 = w_second.reshape(9 * channels, channels)
    w1s, w1t, w2t = call(turn_kernel, [(taps, BF)] * 3)(w_first.reshape(taps), w_second.reshape(taps))
    w1s = w1s.reshape(w1.shape)
    w1t = w1t.reshape(w1.shape)
    w2t = w2t.reshape(w2.shape)
    steps = range(len(dm.steps()))
    pairs = dm.pairs()
    msg_shapes = [((2, dm.rows(i), channels), BF) for i in steps] * 2 + [((2, dm.BASE, channels), BF)]
    flat = (dm.N, channels)

    def merged(packed):
        count = len(steps)
        own, give = packed[:count], [swap_dp(v) for v in packed[count : 2 * count]]
        return call(
            functools.partial(merge_kernel, count), [((2,) + v.shape, BF) for v in own]
        )(*own, *give)

    def across(v, step):
        return lax.ppermute(v, ("tile", "dp"), pairs[step])

    packed = call(
        functools.partial(pack_kernel, dm), msg_shapes, smem_first=True
    )(edge_partner, jnp.stack([x.reshape(flat), d.reshape(flat)]))
    came = [across(v, i) for i, v in enumerate(merged(packed))]
    came, w1s, w1t, w2t = lax.optimization_barrier((came, w1s, w1t, w2t))
    messages = []
    for v in came:
        messages += [v, swap_dp(v)]
    messages.append(packed[-1])
    half = channels // 2
    wide = 9 * channels
    frame = (rows + 2, 6, face + 16, channels)
    outs = call(
        functools.partial(first_kernel, dm),
        [
            ((9, half, channels), BF),
            ((9, half, channels), F32),
            ((9, half, channels), BF),
            ((9, half, channels), F32),
            (planes, BF),
            (planes, BF),
            ((1, channels), F32),
            ((EXTRA, channels), BF),
        ]
        + msg_shapes,
        [
            ((dm.NT, channels), BF),
            (frame, F32),
            ((dm.N, wide), BF),
            ((dm.N + dm.S, wide), BF),
            ((9, dm.S, channels), F32),
            (flat, F32),
            (flat, F32),
            ((dm.N + dm.S, channels), F32),
        ],
        smem_first=True,
        limit=LIMIT,
    )(edge_partner, x, d, w1s, bias.reshape(1, channels), w2t, *messages)
    send1, keep1, send2, keep2, hidden, inner, bias_sum, send_bias = outs[:8]
    packed = list(outs[8:])

    zcount = tiles // 2
    n = 9 * half // tiles
    one = ((1, channels), F32)
    barrier = lax.optimization_barrier

    def along_y(v):
        return lax.ppermute(v, "tile", [(i, i ^ 1) for i in range(tiles)])

    def along_z(v, j):
        return lax.ppermute(v, "tile", [(i, i ^ (2 * j)) for i in range(tiles)])

    def sum_dp(keep, recv, *bias):
        extra = EXTRA if bias else 0
        return call(
            functools.partial(half_kernel, zcount),
            [((zcount, n, channels), F32), ((zcount * n + extra, channels), BF)] + [one] * bool(bias),
        )(keep, recv, *bias)

    def sum_y(keep, recv, *bias):
        extra = EXTRA if bias else 0
        keep, *out = call(
            functools.partial(block_kernel, zcount),
            [((n, channels), F32)] + [((n + extra, channels), BF)] * (zcount - 1) + [one] * bool(bias),
            [((zcount, n, channels), F32)],
        )(keep, recv, *bias)
        return keep, out[: zcount - 1], out[zcount - 1 :]

    def sum_z(keep, recvs, *bias):
        return call(
            functools.partial(last_kernel, zcount), [((n, channels), BF)] + [one] * bool(bias)
        )(keep, *recvs, *bias)

    joined = merged(packed)
    early = list(steps)[1 : 1 + len(steps) // 2]
    middle = [i for i in steps if i not in early]
    came = {}

    keep2, send2 = sum_dp(keep2, swap_dp(send2))
    recv2 = along_y(send2)
    keep1, send1, bias_sum = sum_dp(keep1, swap_dp(send1), bias_sum, swap_dp(send_bias))
    recv1 = along_y(send1)
    got = [across(joined[i], i) for i in early]

    keep2, sends2, _ = sum_y(keep2, recv2)
    recvs2 = [along_z(v, j + 1) for j, v in enumerate(sends2)]
    recv1, got = barrier((recv1, got))
    came.update(zip(early, got))

    keep1, sends1, (bias_sum,) = sum_y(keep1, recv1, bias_sum)
    sends1, todo = barrier((sends1, [joined[i] for i in middle]))
    recvs1 = [along_z(v, j + 1) for j, v in enumerate(sends1)]
    got = [across(v, i) for i, v in zip(middle, todo)]

    (own2,) = sum_z(keep2, recvs2)
    own2 = [own2] + [along_z(own2, j) for j in range(1, zcount)]
    recvs1, got = barrier((recvs1, got))
    came.update(zip(middle, got))

    own1, bias_sum = sum_z(keep1, recvs1, bias_sum)
    own1 = [own1] + [along_z(own1, j) for j in range(1, zcount)]
    own2 = jnp.concatenate(own2, axis=0)
    other2 = along_y(own2)
    own1 = jnp.concatenate(own1, axis=0)
    other1 = along_y(own1)
    messages = []
    for i in steps:
        messages += [came[i], swap_dp(came[i])]
    messages.append(packed[-1])
    own1, messages = barrier((own1, messages))
    state, grad = call(
        functools.partial(second_kernel, dm),
        [(planes, BF), (planes, F32)],
        [
            ((dm.NT, channels), BF),
            (frame, F32),
            ((dm.N, wide), BF),
            ((dm.N + dm.S, wide), BF),
            ((9, dm.S, channels), F32),
            (flat, F32),
        ],
        smem_first=True,
        limit=LIMIT,
    )(edge_partner, x, d, hidden, inner, w1t, w2, *messages)
    other1, state, grad = barrier((other1, state, grad))
    (second_step,) = call(functools.partial(normal_kernel, zcount), [(taps, F32)])(
        own2, other2, swap_dp(own2), swap_dp(other2)
    )
    first_step, bias_step = call(functools.partial(normal_kernel, zcount), [(taps, F32), one])(
        own1, other1, swap_dp(own1), swap_dp(other1), bias_sum
    )
    return (
        state.reshape(initial_state.shape),
        grad.reshape(initial_state.shape),
        first_step.reshape(w_first.shape),
        bias_step.reshape(channels),
        second_step.reshape(w_second.shape),
    )


def solution(mesh):
    return jax.shard_map(
        on_device,
        mesh=mesh,
        in_specs=(
            P(("groups", "dp"), None, "tile", None, None),
            P(None, ("groups", "dp"), None, "tile", None, None),
            P(),
            P(),
            P(),
            P(),
        ),
        out_specs=(
            P(("groups", "dp"), None, "tile", None, None),
            P(("groups", "dp"), None, "tile", None, None),
            P("groups", None, None, None),
            P("groups"),
            P("groups", None, None, None),
        ),
        check_vma=False,
    )
```
